32 devices in a mesh: ctx: 4 (over z), fsdp: 4 (over y, x), grp: 2 (over core).
Axes of the slice: x: 2, y: 2, z: 4, core: 2. Of those that a mesh axis runs over, the one named last changes fastest.
Arguments:
- tokens: bfloat16 [8, 2048, 1536], P(('fsdp', 'grp'), 'ctx'), may hold values from -6 to 6
- seq_lengths: int32 [8, 2], P(('fsdp', 'grp')), may hold values from 1024 to 1024, as said below
- dealing: int32 [8, 4, 4], P(('fsdp', 'grp')), may hold values from 0 to 3, each once within a row
- first_gain: bfloat16 [1536], P('fsdp'), may hold values from 0.5 to 1.5
- query_weight: bfloat16 [1536, 1536], P('fsdp'), may hold values from -0.21875 to 0.21875
- key_matrix: bfloat16 [1536, 768], P('fsdp'), may hold values from -0.21875 to 0.21875
- value_matrix: bfloat16 [1536, 768], P('fsdp'), may hold values from -0.15625 to 0.15625
- out_weight: bfloat16 [1536, 1536], P('fsdp'), may hold values from -2.5 to 2.5
- second_gain: bfloat16 [1536], P('fsdp'), may hold values from 0.5 to 1.5
- gate_weight: bfloat16 [1536, 4096], P('fsdp'), may hold values from -0.15625 to 0.15625
- up_weight: bfloat16 [1536, 4096], P('fsdp'), may hold values from -0.15625 to 0.15625
- down_weight: bfloat16 [4096, 1536], P('fsdp'), may hold values from -0.09375 to 0.09375
- cotangent: bfloat16 [8, 2048, 1536], P(('fsdp', 'grp'), 'ctx'), may hold values from -6 to 6
Outputs:
- layer_out: bfloat16 [8, 2048, 1536], P(('fsdp', 'grp'), 'ctx')
- tokens_grad: bfloat16 [8, 2048, 1536], P(('fsdp', 'grp'), 'ctx')
- softmax_totals: float32 [8, 16, 2048], P(('fsdp', 'grp'), None, 'ctx')
- first_gain_grad: float32 [1536], P('fsdp')
- query_grad: float32 [1536, 1536], P('fsdp')
- key_grad: float32 [1536, 768], P('fsdp')
- value_grad: float32 [1536, 768], P('fsdp')
- out_proj_grad: float32 [1536, 1536], P('fsdp')
- second_gain_grad: float32 [1536], P('fsdp')
- gate_grad: float32 [1536, 4096], P('fsdp')
- up_grad: float32 [1536, 4096], P('fsdp')
- down_grad: float32 [4096, 1536], P('fsdp')
The draws below stay inside these ranges and needn't reach their ends.
Inputs may be any that keep to these rules, and one draw needn't show every extreme that they name: `seq_lengths`: each row holds the lengths of the 2 sequences packed one after another into one pack; they sum to 2048. For pack g and r < 4, dealing[g, r] is a permutation: block r * 4 + i of 128 tokens goes to the ctx device of index dealing[g, r, i], where it stands r-th among that device's blocks.
All inputs are finite; a program needn't handle non-finite values.
Results may differ from the reference program's by a relative error of at most 0.023.
Values may be sent and summed in bfloat16 or wider, within the bound.
A program may use at most 256 MiB of HBM per device.

```python
import math
import jax
import jax.numpy as jnp
from jax import lax

MODEL_WIDTH = 1536
QUERY_HEADS = 16
KEY_VALUE_HEADS = 8
HEAD_SIZE = 96
FF = 4096
BLK = 128
BPD = 4
MINLEN = 1024
PACK_TOKENS = 2048
GROUPS = 8
N_CTX = 4


def draw_seq_lengths(key, part):
    first_key, pick_key = jax.random.split(jax.random.fold_in(key, 17))
    first_len = jax.random.randint(first_key, (GROUPS,), MINLEN, PACK_TOKENS - MINLEN + 1)
    chosen = jax.random.randint(pick_key, (), 0, GROUPS)
    first_len = jnp.where(jnp.arange(GROUPS) == chosen, PACK_TOKENS - MINLEN, first_len)
    return jnp.stack([first_len, PACK_TOKENS - first_len], axis=1).astype(jnp.int32)


def strengthened(entries, stream_key, source, target, parts, factor):
    def block_of(dim):
        return (jnp.arange(entries.shape[dim]) // (entries.shape[dim] // parts)).reshape((-1,) + (1,) * (entries.ndim - 1 - dim))

    first = jax.random.permutation(stream_key, parts)[block_of(target)]
    second = (block_of(target) + parts // 2) % parts
    return jnp.where((block_of(source) == first) | (block_of(source) == second), factor * entries, entries)


def steps_of(key, shape, shards, low, largest):
    loudness = 1.0
    for axis_at, shards_of in shards:
        heights = jax.random.uniform(jax.random.fold_in(jax.random.fold_in(key, 6), axis_at), (shards_of,), jnp.float32, low / len(shards), largest / len(shards))
        loudness = loudness * jnp.repeat(jnp.exp(heights), shape[axis_at] // shards_of).reshape((-1,) + (1,) * (len(shape) - 1 - axis_at))
    return loudness


def bell_draw(key, shape, spread, bound, cuts=(), kind=jnp.bfloat16):
    values = jax.random.normal(key, shape, jnp.float32) * spread
    if len(cuts) > 0:
        values = steps_of(key, shape, cuts, -0.22, 0.18) * values
    return jnp.clip(values, min=-bound, max=bound).astype(kind)


def heavy_noise(stream_key, dims, spread, most, shards, heavy, held_as=jnp.bfloat16):
    entries = spread * jax.random.normal(stream_key, dims, jnp.float32)
    if shards:
        entries = entries * steps_of(stream_key, dims, shards, -0.22, 0.18)
    return jnp.clip(strengthened(entries, jax.random.fold_in(stream_key, 3), *heavy), -most, most).astype(held_as)


def setup_inputs(seed: int = 0) -> dict:
    arg_keys = jax.random.split(jax.random.key(seed), 14)
    return {
        "tokens": bell_draw(arg_keys[0], (GROUPS, PACK_TOKENS, MODEL_WIDTH), 1.0, 6.0, ((0, 8), (1, 4))),
        "seq_lengths": draw_seq_lengths(jax.random.fold_in(arg_keys[13], 71), 0),
        "dealing": jax.vmap(lambda own: jax.random.permutation(own, N_CTX))(jax.random.split(arg_keys[2], GROUPS * BPD)).reshape((GROUPS, BPD, N_CTX)).astype(jnp.int32),
        "first_gain": jnp.clip(1.0 + 0.1 * jax.random.normal(arg_keys[3], (MODEL_WIDTH,), jnp.float32), 0.5, 1.5).astype(jnp.bfloat16),
        "query_weight": bell_draw(arg_keys[4], (MODEL_WIDTH, QUERY_HEADS * HEAD_SIZE), (MODEL_WIDTH // 2) ** -0.5, 0.21875, ((0, 4),)),
        "key_matrix": bell_draw(arg_keys[5], (MODEL_WIDTH, KEY_VALUE_HEADS * HEAD_SIZE), (MODEL_WIDTH // 2) ** -0.5, 0.21875, ((0, 4),)),
        "value_matrix": bell_draw(arg_keys[6], (MODEL_WIDTH, KEY_VALUE_HEADS * HEAD_SIZE), MODEL_WIDTH ** -0.5, 0.15625, ((0, 4),)),
        "out_weight": bell_draw(arg_keys[7], (QUERY_HEADS * HEAD_SIZE, MODEL_WIDTH), (max(1, QUERY_HEADS * HEAD_SIZE // 256)) ** -0.5, 2.5, ((0, 4),)),
        "second_gain": jnp.clip(1.0 + 0.1 * jax.random.normal(arg_keys[8], (MODEL_WIDTH,), jnp.float32), 0.5, 1.5).astype(jnp.bfloat16),
        "gate_weight": bell_draw(arg_keys[9], (MODEL_WIDTH, FF), MODEL_WIDTH ** -0.5, 0.15625, ((0, 4),)),
        "up_weight": bell_draw(arg_keys[10], (MODEL_WIDTH, FF), MODEL_WIDTH ** -0.5, 0.15625, ((0, 4),)),
        "down_weight": bell_draw(arg_keys[11], (FF, MODEL_WIDTH), FF ** -0.5, 0.09375, ((0, 4),)),
        "cotangent": heavy_noise(arg_keys[12], (GROUPS, PACK_TOKENS, MODEL_WIDTH), 1.0, 6.0, ((0, 8), (1, 4)), (0, 2, 8, 2.0)),
    }


EPS = 1e-05
ROPE_BASE = 100000.0
MASKED = -1e+30

@jax.custom_vjp
def low(v):
    return lax.optimization_barrier(v.astype(jnp.bfloat16)).astype(jnp.float32)

@jax.custom_vjp
def low_back(v):
    return v

def low_keep(v):
    return (low(v), None)

def low_pass(kept, grad):
    return (grad,)

def back_keep(v):
    return (v, None)

def back_low(kept, grad):
    return (low(grad),)
low.defvjp(low_keep, low_pass)
low_back.defvjp(back_keep, back_low)

def matmul(left, right):
    return jnp.dot(left, right, precision=lax.Precision.HIGHEST, preferred_element_type=jnp.float32)

def place_rows(positions, lengths):
    ends = jnp.cumsum(lengths, axis=-1)
    before = positions[..., :, None] >= ends[..., None, :]
    segment = lax.optimization_barrier(jnp.sum(before.astype(jnp.int32), axis=-1))
    offset = lax.optimization_barrier(jnp.sum(jnp.where(before, lengths[..., None, :], 0), axis=-1))
    return (segment, positions - offset)

def rotation(relative, half_size):
    frequency = ROPE_BASE ** (-(2.0 * jnp.arange(half_size, dtype=jnp.float32)) / (2 * half_size))
    angles = relative.astype(jnp.float32)[:, None] * frequency[None, :]
    return (jnp.cos(angles), jnp.sin(angles))

def rotate(field, cosine, sine_part):
    row_count = field.shape[0]
    half_size = cosine.shape[-1]
    split_heads = field.reshape(row_count, -1, 2 * half_size)
    front_half = split_heads[..., :half_size]
    back_half = split_heads[..., half_size:]
    cos_rows = cosine[:, None, :]
    sin_rows = sine_part[:, None, :]
    turned = jnp.concatenate([front_half * cos_rows - back_half * sin_rows, back_half * cos_rows + front_half * sin_rows], axis=-1)
    return turned.reshape(row_count, -1)

def norm_rows(field, gain):
    scale = lax.rsqrt(lax.optimization_barrier(jnp.mean(field * field, axis=-1, keepdims=True)) + EPS)
    return low(field * scale * gain)

def layer(params, inputs, lengths):
    gain_one, query_weight, key_matrix, value_matrix, out_weight, gain_two, gate_weight, up_weight, down_weight = params
    positions = jnp.arange(PACK_TOKENS, dtype=jnp.int32)
    segment, relative = place_rows(positions, lengths)
    cosine, sine_part = rotation(relative, HEAD_SIZE // 2)
    xn_one = norm_rows(inputs, gain_one)
    query_rows = low(rotate(low_back(matmul(xn_one, query_weight)), cosine, sine_part))
    rows_of_keys = low(rotate(low_back(matmul(xn_one, key_matrix)), cosine, sine_part))
    rows_of_values = low(low_back(matmul(xn_one, value_matrix)))
    query_group_width = QUERY_HEADS // KEY_VALUE_HEADS
    rows_per_block = math.gcd(PACK_TOKENS, 512)
    blocks_of_queries = query_rows.reshape(PACK_TOKENS // rows_per_block, rows_per_block, KEY_VALUE_HEADS, query_group_width, HEAD_SIZE)
    heads_of_keys = rows_of_keys.reshape(PACK_TOKENS, KEY_VALUE_HEADS, HEAD_SIZE)
    heads_of_values = rows_of_values.reshape(PACK_TOKENS, KEY_VALUE_HEADS, HEAD_SIZE)

    def attend(block_item):
        query_part, query_pos, query_seg = block_item
        scores = low_back(jnp.einsum('qhgd,khd->hgqk', query_part, heads_of_keys, precision=lax.Precision.HIGHEST)) * HEAD_SIZE ** (-0.5)
        visible = (query_seg[:, None] == segment[None, :]) & (positions[None, :] <= query_pos[:, None])
        scores = jnp.where(visible[None, None], scores, MASKED)
        row_top = lax.optimization_barrier(jnp.max(scores, axis=-1, keepdims=True))
        exp_scores = jnp.exp(scores - row_top)
        row_total = lax.optimization_barrier(jnp.sum(exp_scores, axis=-1, keepdims=True))
        probabilities = low(exp_scores / row_total)
        attended_heads = jnp.einsum('hgqk,khd->qhgd', probabilities, heads_of_values, precision=lax.Precision.HIGHEST)
        return (attended_heads, (row_top + jnp.log(row_total))[..., 0])
    attended_heads, totals = lax.map(jax.checkpoint(attend), (blocks_of_queries, positions.reshape(-1, rows_per_block), segment.reshape(-1, rows_per_block)))
    attended = low(low_back(attended_heads.reshape(PACK_TOKENS, QUERY_HEADS * HEAD_SIZE)))
    hidden_in = inputs + low_back(matmul(attended, out_weight))
    xn_two = norm_rows(hidden_in, gain_two)
    gate_val = low_back(matmul(xn_two, gate_weight))
    up_val = low_back(matmul(xn_two, up_weight))
    hidden = low(jax.nn.silu(gate_val) * up_val)
    result = hidden_in + low_back(matmul(hidden, down_weight))
    log_totals = jnp.transpose(totals, (1, 2, 0, 3)).reshape(QUERY_HEADS, PACK_TOKENS)
    return (result, log_totals)

def reference(tokens, seq_lengths, dealing, first_gain, query_weight, key_matrix, value_matrix, out_weight, second_gain, gate_weight, up_weight, down_weight, cotangent):
    params = (first_gain.astype(jnp.float32), query_weight.astype(jnp.float32), key_matrix.astype(jnp.float32), value_matrix.astype(jnp.float32), out_weight.astype(jnp.float32), second_gain.astype(jnp.float32), gate_weight.astype(jnp.float32), up_weight.astype(jnp.float32), down_weight.astype(jnp.float32))
    inputs = tokens.astype(jnp.float32)
    upstream = cotangent.astype(jnp.float32)

    def forward(weights, packs_in):

        def one_pack(carry, pack_item):
            pack_tokens, pack_lengths = pack_item
            result, log_totals = layer(weights, pack_tokens, pack_lengths)
            return (carry, (result, log_totals))
        unused, (results, totals) = lax.scan(one_pack, jnp.float32(0.0), (packs_in, seq_lengths))
        return (results, totals)
    results, pullback, totals = jax.vjp(forward, params, inputs, has_aux=True)
    param_grads, input_grad = pullback(upstream)
    ctx_range = jnp.arange(N_CTX, dtype=jnp.int32)
    matches = (dealing[..., None] == ctx_range).astype(jnp.int32)
    slot_of = lax.optimization_barrier(jnp.sum(matches * ctx_range[:, None], axis=2))
    block_of = jnp.arange(BPD, dtype=jnp.int32)[None, :, None] * N_CTX + slot_of
    order = (jnp.transpose(block_of, (0, 2, 1))[..., None] * BLK + jnp.arange(BLK, dtype=jnp.int32)).reshape(GROUPS, PACK_TOKENS)
    dealt = jnp.take_along_axis(totals, jnp.broadcast_to(order[:, None, :], totals.shape), axis=2)
    return (results.astype(jnp.bfloat16), input_grad.astype(jnp.bfloat16), dealt, param_grads[0], param_grads[1], param_grads[2], param_grads[3], param_grads[4], param_grads[5], param_grads[6], param_grads[7], param_grads[8])
```

```python
import jax
import jax.numpy as jnp
from jax import lax
from jax.experimental import pallas as pl
from jax.experimental.pallas import tpu as pltpu
from jax.sharding import PartitionSpec as P

QUERY_HEADS = 16
KEY_VALUE_HEADS = 8
HEAD_SIZE = 96
BLK = 128


EPS = 1e-05
ROPE_BASE = 100000.0
MASKED = -1e30


def place_rows(positions, lengths):
    ends = jnp.cumsum(lengths, axis=-1)
    before = positions[..., :, None] >= ends[..., None, :]
    segment = jnp.sum(before.astype(jnp.int32), axis=-1)
    offset = jnp.sum(jnp.where(before, lengths[..., None, :], 0), axis=-1)
    return (segment, positions - offset)


def rotation(relative, half_size):
    frequency = ROPE_BASE ** (-(2.0 * jnp.arange(half_size, dtype=jnp.float32)) / (2 * half_size))
    angles = relative.astype(jnp.float32)[:, None] * frequency[None, :]
    return (jnp.cos(angles), jnp.sin(angles))


def rotate(field, cosine, sine_part):
    row_count = field.shape[0]
    half_size = cosine.shape[-1]
    split_heads = field.reshape(row_count, -1, 2 * half_size)
    front_half = split_heads[..., :half_size]
    back_half = split_heads[..., half_size:]
    cos_rows = cosine[:, None, :]
    sin_rows = sine_part[:, None, :]
    turned = jnp.concatenate(
        [
            front_half * cos_rows - back_half * sin_rows,
            back_half * cos_rows + front_half * sin_rows,
        ],
        axis=-1,
    )
    return turned.reshape(row_count, -1)


def rms_back(d_normed, normed, scale):
    return scale * (d_normed - normed * jnp.mean(d_normed * normed, axis=-1, keepdims=True))


def score_block(query_part, key_part, visible):
    scores = jnp.einsum(
        "rgd,kd->grk", query_part, key_part, preferred_element_type=jnp.float32
    ) * HEAD_SIZE ** (-0.5)
    return jnp.where(visible[None], scores, MASKED)


def attend_pack(query_pack, key_pack, value_pack, visible_list):
    token_count = query_pack.shape[0]
    rounds = len(visible_list)
    query_group_width = QUERY_HEADS // KEY_VALUE_HEADS
    context_count = key_pack.shape[0] // token_count

    def width_per_head(head_index, carry):
        out_buf, total_buf = carry
        query_head = lax.dynamic_slice_in_dim(
            query_pack, head_index * query_group_width * HEAD_SIZE, query_group_width * HEAD_SIZE, 1
        ).reshape(token_count, query_group_width, HEAD_SIZE)
        key_head = lax.dynamic_slice_in_dim(key_pack, head_index * HEAD_SIZE, HEAD_SIZE, 1).reshape(
            context_count, rounds, BLK, HEAD_SIZE
        )
        value_head = lax.dynamic_slice_in_dim(
            value_pack, head_index * HEAD_SIZE, HEAD_SIZE, 1
        ).reshape(context_count, rounds, BLK, HEAD_SIZE)
        running_top = jnp.full((query_group_width, token_count), MASKED, jnp.float32)
        running_sum = jnp.zeros((query_group_width, token_count), jnp.float32)
        for round_index in range(rounds):
            first_row = round_index * BLK
            scores = score_block(
                query_head[first_row:],
                key_head[:, round_index].reshape(-1, HEAD_SIZE),
                visible_list[round_index],
            )
            new_top = jnp.maximum(running_top[:, first_row:], jnp.max(scores, axis=-1))
            weights = jnp.where(
                visible_list[round_index][None], jnp.exp(scores - new_top[..., None]), 0.0
            )
            new_sum = running_sum[:, first_row:] * jnp.exp(
                running_top[:, first_row:] - new_top
            ) + jnp.sum(weights, axis=-1)
            running_top = running_top.at[:, first_row:].set(new_top)
            running_sum = running_sum.at[:, first_row:].set(new_sum)
        log_totals = running_top + jnp.log(running_sum)
        mixture = jnp.zeros((token_count, query_group_width, HEAD_SIZE), jnp.float32)
        for round_index in range(rounds):
            first_row = round_index * BLK
            scores = score_block(
                query_head[first_row:],
                key_head[:, round_index].reshape(-1, HEAD_SIZE),
                visible_list[round_index],
            )
            prob_bf = jnp.where(
                visible_list[round_index][None],
                jnp.exp(scores - log_totals[:, first_row:, None]),
                0.0,
            ).astype(jnp.bfloat16)
            mixture = mixture.at[first_row:].add(
                jnp.einsum(
                    "grk,kd->rgd",
                    prob_bf,
                    value_head[:, round_index].reshape(-1, HEAD_SIZE),
                    preferred_element_type=jnp.float32,
                )
            )
        out_buf = lax.dynamic_update_slice_in_dim(
            out_buf,
            mixture.astype(jnp.bfloat16).reshape(token_count, -1),
            head_index * query_group_width * HEAD_SIZE,
            1,
        )
        total_buf = lax.dynamic_update_slice_in_dim(
            total_buf, log_totals, head_index * query_group_width, 0
        )
        return (out_buf, total_buf)

    start_offsets = (
        jnp.zeros((token_count, QUERY_HEADS * HEAD_SIZE), jnp.bfloat16),
        jnp.zeros((QUERY_HEADS, token_count), jnp.float32),
    )
    return lax.fori_loop(0, KEY_VALUE_HEADS, width_per_head, start_offsets)


def attend_back(
    query_pack, key_pack, value_pack, grad_pack, attended_pack, total_pack, visible_list
):
    token_count = query_pack.shape[0]
    rounds = len(visible_list)
    query_group_width = QUERY_HEADS // KEY_VALUE_HEADS
    context_count = key_pack.shape[0] // token_count

    def width_per_head(head_index, carry):
        query_buf, key_buf, value_buf = carry
        query_head = lax.dynamic_slice_in_dim(
            query_pack, head_index * query_group_width * HEAD_SIZE, query_group_width * HEAD_SIZE, 1
        ).reshape(token_count, query_group_width, HEAD_SIZE)
        grad_head = lax.dynamic_slice_in_dim(
            grad_pack, head_index * query_group_width * HEAD_SIZE, query_group_width * HEAD_SIZE, 1
        ).reshape(token_count, query_group_width, HEAD_SIZE)
        output_head = lax.dynamic_slice_in_dim(
            attended_pack,
            head_index * query_group_width * HEAD_SIZE,
            query_group_width * HEAD_SIZE,
            1,
        ).reshape(token_count, query_group_width, HEAD_SIZE)
        key_head = lax.dynamic_slice_in_dim(key_pack, head_index * HEAD_SIZE, HEAD_SIZE, 1).reshape(
            context_count, rounds, BLK, HEAD_SIZE
        )
        value_head = lax.dynamic_slice_in_dim(
            value_pack, head_index * HEAD_SIZE, HEAD_SIZE, 1
        ).reshape(context_count, rounds, BLK, HEAD_SIZE)
        log_totals = lax.dynamic_slice_in_dim(
            total_pack, head_index * query_group_width, query_group_width, 0
        )
        delta = jnp.sum(grad_head.astype(jnp.float32) * output_head.astype(jnp.float32), axis=-1).T
        query_grad = jnp.zeros((token_count, query_group_width, HEAD_SIZE), jnp.float32)
        key_parts = []
        value_parts = []
        for round_index in range(rounds):
            first_row = round_index * BLK
            key_round = key_head[:, round_index].reshape(-1, HEAD_SIZE)
            value_round = value_head[:, round_index].reshape(-1, HEAD_SIZE)
            scores = score_block(query_head[first_row:], key_round, visible_list[round_index])
            probs_full = jnp.where(
                visible_list[round_index][None],
                jnp.exp(scores - log_totals[:, first_row:, None]),
                0.0,
            )
            d_probs = jnp.einsum(
                "rgd,kd->grk",
                grad_head[first_row:],
                value_round,
                preferred_element_type=jnp.float32,
            )
            d_scores = (
                HEAD_SIZE ** (-0.5) * probs_full * (d_probs - delta[:, first_row:, None])
            ).astype(jnp.bfloat16)
            value_parts.append(
                jnp.einsum(
                    "grk,rgd->kd",
                    probs_full.astype(jnp.bfloat16),
                    grad_head[first_row:],
                    preferred_element_type=jnp.float32,
                )
            )
            key_parts.append(
                jnp.einsum(
                    "grk,rgd->kd",
                    d_scores,
                    query_head[first_row:],
                    preferred_element_type=jnp.float32,
                )
            )
            query_grad = query_grad.at[first_row:].add(
                jnp.einsum("grk,kd->rgd", d_scores, key_round, preferred_element_type=jnp.float32)
            )
        key_block = jnp.stack(
            [part.reshape(context_count, BLK, HEAD_SIZE) for part in key_parts], axis=1
        ).reshape(-1, HEAD_SIZE)
        value_block = jnp.stack(
            [part.reshape(context_count, BLK, HEAD_SIZE) for part in value_parts], axis=1
        ).reshape(-1, HEAD_SIZE)
        query_buf = lax.dynamic_update_slice_in_dim(
            query_buf,
            query_grad.reshape(token_count, -1),
            head_index * query_group_width * HEAD_SIZE,
            1,
        )
        key_buf = lax.dynamic_update_slice_in_dim(key_buf, key_block, head_index * HEAD_SIZE, 1)
        value_buf = lax.dynamic_update_slice_in_dim(
            value_buf, value_block, head_index * HEAD_SIZE, 1
        )
        return (query_buf, key_buf, value_buf)

    start_offsets = (
        jnp.zeros((token_count, QUERY_HEADS * HEAD_SIZE), jnp.float32),
        jnp.zeros((context_count * token_count, KEY_VALUE_HEADS * HEAD_SIZE), jnp.float32),
        jnp.zeros((context_count * token_count, KEY_VALUE_HEADS * HEAD_SIZE), jnp.float32),
    )
    return lax.fori_loop(0, KEY_VALUE_HEADS, width_per_head, start_offsets)


def local(
    tokens,
    seq_lengths,
    dealing,
    first_gain,
    query_weight,
    key_matrix,
    value_matrix,
    out_weight,
    second_gain,
    gate_weight,
    up_weight,
    down_weight,
    cotangent,
):
    context_count = lax.axis_size("ctx")
    my_index = lax.axis_index("ctx")
    pack_count, token_count, model_dim = tokens.shape
    rounds = token_count // BLK
    spread = context_count // rounds
    ctx_range = jnp.arange(context_count, dtype=jnp.int32)
    matches = (dealing[..., None] == ctx_range).astype(jnp.int32)
    slot_of = jnp.sum(matches * ctx_range[:, None], axis=2)
    block_of = jnp.arange(rounds, dtype=jnp.int32)[None, :, None] * context_count + slot_of
    key_pos = (
        jnp.transpose(block_of, (0, 2, 1))[..., None] * BLK + jnp.arange(BLK, dtype=jnp.int32)
    ).reshape(pack_count, -1)
    key_seg = place_rows(key_pos, seq_lengths)[0]
    query_pos = lax.dynamic_slice_in_dim(key_pos, my_index * token_count, token_count, 1)
    query_seg, query_rel = place_rows(query_pos, seq_lengths)
    home_row = lax.dynamic_index_in_dim(dealing, my_index // spread, 1, False)
    targets = lax.dynamic_slice_in_dim(home_row, my_index % spread * rounds, rounds, 1)
    picker = (targets[:, None, :] == ctx_range[None, :, None]).astype(jnp.bfloat16)
    my_slots = lax.dynamic_index_in_dim(slot_of, my_index, 2, False)
    owner_index = (
        jnp.arange(rounds, dtype=jnp.int32)[None, :] * context_count + my_slots
    ) // rounds
    keep_slot = jnp.repeat(owner_index, spread, axis=1) == ctx_range[None, :]

    def spread_out(field):
        blocks = field.reshape(pack_count, rounds, BLK, model_dim)
        return jnp.einsum(
            "pkj,pjtd->pktd", picker, blocks, preferred_element_type=jnp.float32
        ).astype(jnp.bfloat16)

    def collect(received):
        grouped = received.reshape(pack_count, rounds, spread, BLK, model_dim)
        return (
            jnp.sum(grouped, axis=2, dtype=jnp.float32)
            .astype(jnp.bfloat16)
            .reshape(pack_count * token_count, model_dim)
        )

    def send_home(field):
        blocks = jnp.repeat(field.reshape(pack_count, rounds, BLK, model_dim), spread, axis=1)
        return jnp.where(keep_slot[:, :, None, None], blocks, jnp.zeros_like(blocks))

    def restore(returned):
        placed = jnp.einsum("pkj,pktd->pjtd", picker, returned, preferred_element_type=jnp.float32)
        return placed.astype(jnp.bfloat16).reshape(pack_count, token_count, model_dim)

    dealt_tokens, dealt_upstream = (
        lax.all_to_all(spread_out(tokens), "ctx", split_axis=1, concat_axis=1, tiled=True),
        lax.all_to_all(spread_out(cotangent), "ctx", split_axis=1, concat_axis=1, tiled=True),
    )
    inputs = collect(dealt_tokens)
    upstream = collect(dealt_upstream)
    gain_one, query_full, key_full, value_full, out_full = (
        lax.all_gather(first_gain, "fsdp", axis=0, tiled=True),
        lax.all_gather(query_weight, "fsdp", axis=0, tiled=True),
        lax.all_gather(key_matrix, "fsdp", axis=0, tiled=True),
        lax.all_gather(value_matrix, "fsdp", axis=0, tiled=True),
        lax.all_gather(out_weight, "fsdp", axis=0, tiled=True),
    )
    gain_two, gate_full, up_full, down_full = (
        lax.all_gather(second_gain, "fsdp", axis=0, tiled=True),
        lax.all_gather(gate_weight, "fsdp", axis=0, tiled=True),
        lax.all_gather(up_weight, "fsdp", axis=0, tiled=True),
        lax.all_gather(down_weight, "fsdp", axis=0, tiled=True),
    )
    gain_one32 = gain_one.astype(jnp.float32)
    gain_two32 = gain_two.astype(jnp.float32)
    cosine, sine_part = rotation(query_rel.reshape(-1), HEAD_SIZE // 2)
    inputs32 = inputs.astype(jnp.float32)
    scale_one = lax.rsqrt(jnp.mean(inputs32 * inputs32, axis=-1, keepdims=True) + EPS)
    normed_one = inputs32 * scale_one
    xn_one = (normed_one * gain_one32).astype(jnp.bfloat16)
    query_rot = rotate(
        jnp.dot(xn_one, query_full, preferred_element_type=jnp.float32), cosine, sine_part
    ).astype(jnp.bfloat16)
    key_rot = rotate(
        jnp.dot(xn_one, key_full, preferred_element_type=jnp.float32), cosine, sine_part
    ).astype(jnp.bfloat16)
    rows_of_values = jnp.dot(xn_one, value_full, preferred_element_type=jnp.float32).astype(
        jnp.bfloat16
    )
    key_local = key_rot.reshape(pack_count, token_count, -1)
    value_local = rows_of_values.reshape(pack_count, token_count, -1)
    gathered_keys, gathered_values = (
        lax.all_gather(key_local, "ctx", axis=1, tiled=True),
        lax.all_gather(value_local, "ctx", axis=1, tiled=True),
    )
    key_pos_rounds = key_pos.reshape(pack_count, context_count, rounds, BLK)
    key_seg_rounds = key_seg.reshape(pack_count, context_count, rounds, BLK)
    visible = []
    for round_index in range(rounds):
        first_row = round_index * BLK
        round_pos = key_pos_rounds[:, :, round_index].reshape(pack_count, -1)
        round_seg = key_seg_rounds[:, :, round_index].reshape(pack_count, -1)
        same_seq = query_seg[:, first_row:, None] == round_seg[:, None, :]
        earlier = round_pos[:, None, :] <= query_pos[:, first_row:, None]
        visible.append(same_seq & earlier)
    query_packs = query_rot.reshape(pack_count, token_count, -1)
    pack_index = 0
    pack_visible = [mask[pack_index] for mask in visible]
    attended_pack, total_pack = attend_pack(
        query_packs[pack_index],
        gathered_keys[pack_index],
        gathered_values[pack_index],
        pack_visible,
    )
    total_list = [total_pack]
    softmax_totals = jnp.stack(total_list, axis=0)
    hidden_in = inputs32 + jnp.dot(attended_pack, out_full, preferred_element_type=jnp.float32)
    scale_two = lax.rsqrt(jnp.mean(hidden_in * hidden_in, axis=-1, keepdims=True) + EPS)
    normed_two = hidden_in * scale_two
    xn_two = (normed_two * gain_two32).astype(jnp.bfloat16)
    gate_val = jnp.dot(xn_two, gate_full, preferred_element_type=jnp.float32)
    up_val = jnp.dot(xn_two, up_full, preferred_element_type=jnp.float32)
    activated = jax.nn.silu(gate_val)
    hidden = (activated * up_val).astype(jnp.bfloat16)
    result = (hidden_in + jnp.dot(hidden, down_full, preferred_element_type=jnp.float32)).astype(
        jnp.bfloat16
    )
    down_grad = jnp.dot(hidden.T, upstream, preferred_element_type=jnp.float32)
    d_hidden = jnp.dot(upstream, down_full.T, preferred_element_type=jnp.float32)
    sigmoid_gate = jax.nn.sigmoid(gate_val)
    d_gate = (d_hidden * up_val * sigmoid_gate * (1.0 + gate_val * (1.0 - sigmoid_gate))).astype(
        jnp.bfloat16
    )
    d_up = (d_hidden * activated).astype(jnp.bfloat16)
    gate_grad = jnp.dot(xn_two.T, d_gate, preferred_element_type=jnp.float32)
    up_grad = jnp.dot(xn_two.T, d_up, preferred_element_type=jnp.float32)
    d_norm_two = jnp.dot(d_gate, gate_full.T, preferred_element_type=jnp.float32) + jnp.dot(
        d_up, up_full.T, preferred_element_type=jnp.float32
    )
    gain_two_grad = jnp.sum(d_norm_two * normed_two, axis=0)
    d_hidden_in = upstream.astype(jnp.float32) + rms_back(
        d_norm_two * gain_two32, normed_two, scale_two
    )
    mlp_parts = (
        lax.psum_scatter(
            gain_two_grad.astype(jnp.bfloat16), "fsdp", scatter_dimension=0, tiled=True
        ).astype(jnp.float32),
        lax.psum_scatter(
            gate_grad.astype(jnp.bfloat16), "fsdp", scatter_dimension=0, tiled=True
        ).astype(jnp.float32),
        lax.psum_scatter(
            up_grad.astype(jnp.bfloat16), "fsdp", scatter_dimension=0, tiled=True
        ).astype(jnp.float32),
        lax.psum_scatter(
            down_grad.astype(jnp.bfloat16), "fsdp", scatter_dimension=0, tiled=True
        ).astype(jnp.float32),
    )
    d_branch = d_hidden_in.astype(jnp.bfloat16)
    out_grad = jnp.dot(attended_pack.T, d_branch, preferred_element_type=jnp.float32)
    d_attended = jnp.dot(d_branch, out_full.T, preferred_element_type=jnp.float32).astype(
        jnp.bfloat16
    )
    back_keys, back_values = (gathered_keys, gathered_values)
    grad_packs = d_attended.reshape(pack_count, token_count, -1)
    out_packs = attended_pack.reshape(pack_count, token_count, -1)
    pack_index = 0
    pack_visible = [mask[pack_index] for mask in visible]
    query_part, key_part, value_part = attend_back(
        query_packs[pack_index],
        back_keys[pack_index],
        back_values[pack_index],
        grad_packs[pack_index],
        out_packs[pack_index],
        softmax_totals[pack_index],
        pack_visible,
    )
    key_list = [key_part]
    value_list = [value_part]
    d_keys, d_values = (
        lax.psum_scatter(
            jnp.stack(key_list, axis=0).astype(jnp.bfloat16), "ctx", scatter_dimension=1, tiled=True
        ).astype(jnp.float32),
        lax.psum_scatter(
            jnp.stack(value_list, axis=0).astype(jnp.bfloat16),
            "ctx",
            scatter_dimension=1,
            tiled=True,
        ).astype(jnp.float32),
    )
    d_query = rotate(query_part, cosine, -sine_part).astype(jnp.bfloat16)
    d_key = rotate(d_keys.reshape(pack_count * token_count, -1), cosine, -sine_part).astype(
        jnp.bfloat16
    )
    d_value = d_values.reshape(pack_count * token_count, -1).astype(jnp.bfloat16)
    query_grad = jnp.dot(xn_one.T, d_query, preferred_element_type=jnp.float32)
    key_grad = jnp.dot(xn_one.T, d_key, preferred_element_type=jnp.float32)
    value_grad = jnp.dot(xn_one.T, d_value, preferred_element_type=jnp.float32)
    d_norm_one = (
        jnp.dot(d_query, query_full.T, preferred_element_type=jnp.float32)
        + jnp.dot(d_key, key_full.T, preferred_element_type=jnp.float32)
        + jnp.dot(d_value, value_full.T, preferred_element_type=jnp.float32)
    )
    gain_one_grad = jnp.sum(d_norm_one * normed_one, axis=0)
    d_inputs = d_hidden_in + rms_back(d_norm_one * gain_one32, normed_one, scale_one)
    attn_parts = (
        lax.psum_scatter(
            gain_one_grad.astype(jnp.bfloat16), "fsdp", scatter_dimension=0, tiled=True
        ).astype(jnp.float32),
        lax.psum_scatter(
            query_grad.astype(jnp.bfloat16), "fsdp", scatter_dimension=0, tiled=True
        ).astype(jnp.float32),
        lax.psum_scatter(
            key_grad.astype(jnp.bfloat16), "fsdp", scatter_dimension=0, tiled=True
        ).astype(jnp.float32),
        lax.psum_scatter(
            value_grad.astype(jnp.bfloat16), "fsdp", scatter_dimension=0, tiled=True
        ).astype(jnp.float32),
        lax.psum_scatter(
            out_grad.astype(jnp.bfloat16), "fsdp", scatter_dimension=0, tiled=True
        ).astype(jnp.float32),
    )
    finished = (
        lax.psum(attn_parts[0].astype(jnp.bfloat16), ("ctx", "grp")).astype(jnp.float32),
        lax.psum(attn_parts[1].astype(jnp.bfloat16), ("ctx", "grp")).astype(jnp.float32),
        lax.psum(attn_parts[2].astype(jnp.bfloat16), ("ctx", "grp")).astype(jnp.float32),
        lax.psum(attn_parts[3].astype(jnp.bfloat16), ("ctx", "grp")).astype(jnp.float32),
        lax.psum(attn_parts[4].astype(jnp.bfloat16), ("ctx", "grp")).astype(jnp.float32),
        lax.psum(mlp_parts[0].astype(jnp.bfloat16), ("ctx", "grp")).astype(jnp.float32),
        lax.psum(mlp_parts[1].astype(jnp.bfloat16), ("ctx", "grp")).astype(jnp.float32),
        lax.psum(mlp_parts[2].astype(jnp.bfloat16), ("ctx", "grp")).astype(jnp.float32),
        lax.psum(mlp_parts[3].astype(jnp.bfloat16), ("ctx", "grp")).astype(jnp.float32),
    )
    home_out, home_grad = (
        lax.all_to_all(send_home(result), "ctx", split_axis=1, concat_axis=1, tiled=True),
        lax.all_to_all(
            send_home(d_inputs.astype(jnp.bfloat16)), "ctx", split_axis=1, concat_axis=1, tiled=True
        ),
    )
    return (
        restore(home_out),
        restore(home_grad),
        softmax_totals,
        finished[0],
        finished[1],
        finished[2],
        finished[3],
        finished[4],
        finished[5],
        finished[6],
        finished[7],
        finished[8],
    )


MINLEN = 1024
QB = 256
VMEM_LIMIT = 56 * 1024 * 1024


def attend_kernel(q_ref, k_ref, v_ref, c_ref, s_ref, o_ref, lse_ref, qr_ref, kr_ref, vr_ref):
    cosine = c_ref[...]
    sine = s_ref[...]
    half = HEAD_SIZE // 2
    seq = cosine.shape[1]

    def turn(field):
        front, back = field[:half], field[half:]
        return jnp.concatenate(
            [front * cosine - back * sine, back * cosine + front * sine], axis=0
        )

    k_rot = turn(k_ref[...])
    kr_ref[...] = k_rot.astype(jnp.bfloat16)
    key = k_rot.T.astype(jnp.bfloat16)
    val_t = v_ref[...].astype(jnp.bfloat16)
    vr_ref[...] = val_t
    q0 = turn(q_ref[:HEAD_SIZE]).astype(jnp.bfloat16)
    q1 = turn(q_ref[HEAD_SIZE:]).astype(jnp.bfloat16)
    qr_ref[:HEAD_SIZE] = q0
    qr_ref[HEAD_SIZE:] = q1
    rows = lax.broadcasted_iota(jnp.int32, (QB, 2 * QB), 0)
    cols = lax.broadcasted_iota(jnp.int32, (QB, 2 * QB), 1)
    keep = rows <= jnp.where(cols >= QB, cols - QB, cols)
    for b in range(seq // QB):
        lo, n = b * QB, (b + 1) * QB
        q_t = jnp.concatenate([q0[:, lo:n], q1[:, lo:n]], axis=1)
        scores = jnp.dot(key[:n], q_t, preferred_element_type=jnp.float32) * HEAD_SIZE ** (-0.5)
        diag = jnp.where(keep, scores[lo:], MASKED)
        top = jnp.max(diag, axis=0, keepdims=True)
        if b > 0:
            top = jnp.maximum(top, jnp.max(scores[:lo], axis=0, keepdims=True))
        e_diag = jnp.exp(diag - top)
        total = jnp.sum(e_diag, axis=0, keepdims=True)
        out = jnp.dot(val_t[:, lo:n], e_diag.astype(jnp.bfloat16), preferred_element_type=jnp.float32)
        if b > 0:
            e_rest = jnp.exp(scores[:lo] - top)
            total = total + jnp.sum(e_rest, axis=0, keepdims=True)
            out = out + jnp.dot(
                val_t[:, :lo], e_rest.astype(jnp.bfloat16), preferred_element_type=jnp.float32
            )
        out = (out / total).astype(jnp.bfloat16)
        o_ref[:HEAD_SIZE, lo:n] = out[:, :QB]
        o_ref[HEAD_SIZE:, lo:n] = out[:, QB:]
        lse = top + jnp.log(total)
        lse_ref[0, 0:1, lo:n] = lse[:, :QB]
        lse_ref[0, 1:2, lo:n] = lse[:, QB:]


def attend_seq(qkv_t, cosine, sine):
    rows, seq = qkv_t.shape
    kv = rows // (4 * HEAD_SIZE)
    group = pl.BlockSpec((2 * HEAD_SIZE, seq), lambda j: (j, 0))

    def head(base):
        return pl.BlockSpec((HEAD_SIZE, seq), lambda j: (base + j, 0))

    table = pl.BlockSpec((HEAD_SIZE // 2, seq), lambda j: (0, 0))
    return pl.pallas_call(
        attend_kernel,
        grid=(kv,),
        in_specs=[group, head(2 * kv), head(3 * kv), table, table],
        out_specs=[
            group,
            pl.BlockSpec((1, 2, seq), lambda j: (j, 0, 0)),
            group,
            head(0),
            head(0),
        ],
        out_shape=[
            jax.ShapeDtypeStruct((2 * kv * HEAD_SIZE, seq), jnp.bfloat16),
            jax.ShapeDtypeStruct((kv, 2, seq), jnp.float32),
            jax.ShapeDtypeStruct((2 * kv * HEAD_SIZE, seq), jnp.bfloat16),
            jax.ShapeDtypeStruct((kv * HEAD_SIZE, seq), jnp.bfloat16),
            jax.ShapeDtypeStruct((kv * HEAD_SIZE, seq), jnp.bfloat16),
        ],
        compiler_params=pltpu.CompilerParams(vmem_limit_bytes=VMEM_LIMIT),
        cost_estimate=pl.CostEstimate(
            flops=4 * kv * 2 * seq * seq * HEAD_SIZE, bytes_accessed=10 * rows * seq, transcendentals=kv * seq * seq
        ),
        name="attend",
    )(qkv_t, qkv_t, qkv_t, cosine, sine)


def attend_back_kernel(
    q_ref, k_ref, v_ref, g_ref, lse_ref, c_ref, s_ref, dq_ref, dk_ref, dv_ref, dk_acc, dv_acc
):
    half = HEAD_SIZE // 2
    cosine = c_ref[...]
    sine = s_ref[...]
    seq = cosine.shape[1]

    def turn_back(field, cos, sin):
        front, back = field[:half], field[half:]
        return jnp.concatenate([front * cos + back * sin, back * cos - front * sin], axis=0)

    def flip(field):
        return field.astype(jnp.float32).T.astype(jnp.bfloat16)

    key_t = k_ref[...]
    key = flip(key_t)
    val = flip(v_ref[...])
    q0_t, q1_t = q_ref[:HEAD_SIZE], q_ref[HEAD_SIZE:]
    g0_t, g1_t = g_ref[:HEAD_SIZE], g_ref[HEAD_SIZE:]
    q0, q1, g0, g1 = flip(q0_t), flip(q1_t), flip(g0_t), flip(g1_t)
    dk_acc[...] = jnp.zeros_like(dk_acc)
    dv_acc[...] = jnp.zeros_like(dv_acc)
    rows = lax.broadcasted_iota(jnp.int32, (QB, 2 * QB), 0)
    cols = lax.broadcasted_iota(jnp.int32, (QB, 2 * QB), 1)
    keep = rows <= jnp.where(cols >= QB, cols - QB, cols)
    for b in range(seq // QB):
        lo, n = b * QB, (b + 1) * QB
        q_t = jnp.concatenate([q0_t[:, lo:n], q1_t[:, lo:n]], axis=1)
        g_t = jnp.concatenate([g0_t[:, lo:n], g1_t[:, lo:n]], axis=1)
        q_n = jnp.concatenate([q0[lo:n], q1[lo:n]], axis=0)
        g_n = jnp.concatenate([g0[lo:n], g1[lo:n]], axis=0)
        lse = jnp.concatenate([lse_ref[0, 0:1, lo:n], lse_ref[0, 1:2, lo:n]], axis=1)
        parts = []
        delta = None
        for start, stop in ([(0, lo)] if b > 0 else []) + [(lo, n)]:
            scores = jnp.dot(key[start:stop], q_t, preferred_element_type=jnp.float32) * HEAD_SIZE ** (-0.5)
            prob = jnp.exp(scores - lse)
            if start == lo:
                prob = jnp.where(keep, prob, 0.0)
            d_prob = jnp.dot(val[start:stop], g_t, preferred_element_type=jnp.float32)
            part = jnp.sum(prob * d_prob, axis=0, keepdims=True)
            delta = part if delta is None else delta + part
            dv_acc[start:stop] += jnp.dot(prob.astype(jnp.bfloat16), g_n, preferred_element_type=jnp.float32)
            parts.append((start, stop, prob, d_prob))
        dq_t = None
        for start, stop, prob, d_prob in parts:
            d_score = (prob * (d_prob - delta) * HEAD_SIZE ** (-0.5)).astype(jnp.bfloat16)
            dk_acc[start:stop] += jnp.dot(d_score, q_n, preferred_element_type=jnp.float32)
            part = jnp.dot(key_t[:, start:stop], d_score, preferred_element_type=jnp.float32)
            dq_t = part if dq_t is None else dq_t + part
        cos, sin = cosine[:, lo:n], sine[:, lo:n]
        dq_ref[:HEAD_SIZE, lo:n] = turn_back(dq_t[:, :QB], cos, sin).astype(jnp.bfloat16)
        dq_ref[HEAD_SIZE:, lo:n] = turn_back(dq_t[:, QB:], cos, sin).astype(jnp.bfloat16)
    dk_ref[...] = turn_back(dk_acc[...].T, cosine, sine).astype(jnp.bfloat16)
    dv_ref[...] = dv_acc[...].T.astype(jnp.bfloat16)


def attend_seq_back(q_t, k_t, v_t, g_t, lse, cosine, sine):
    rows, seq = k_t.shape
    kv = rows // HEAD_SIZE
    group = pl.BlockSpec((2 * HEAD_SIZE, seq), lambda j: (j, 0))
    head = pl.BlockSpec((HEAD_SIZE, seq), lambda j: (j, 0))
    table = pl.BlockSpec((HEAD_SIZE // 2, seq), lambda j: (0, 0))
    return pl.pallas_call(
        attend_back_kernel,
        grid=(kv,),
        in_specs=[group, head, head, group, pl.BlockSpec((1, 2, seq), lambda j: (j, 0, 0)), table, table],
        out_specs=[group, head, head],
        out_shape=[
            jax.ShapeDtypeStruct((2 * rows, seq), jnp.bfloat16),
            jax.ShapeDtypeStruct((rows, seq), jnp.bfloat16),
            jax.ShapeDtypeStruct((rows, seq), jnp.bfloat16),
        ],
        scratch_shapes=[
            pltpu.VMEM((seq, HEAD_SIZE), jnp.float32),
            pltpu.VMEM((seq, HEAD_SIZE), jnp.float32),
        ],
        compiler_params=pltpu.CompilerParams(vmem_limit_bytes=VMEM_LIMIT),
        cost_estimate=pl.CostEstimate(
            flops=10 * kv * 2 * seq * seq * HEAD_SIZE, bytes_accessed=20 * rows * seq, transcendentals=kv * seq * seq
        ),
        name="attend_back",
    )(q_t, k_t, v_t, g_t, lse, cosine, sine)


def fp32(field):
    return field.astype(jnp.float32)


def mm(left, right, dims=((1,), (0,)), out=jnp.float32):
    return lax.dot_general(left, right, (dims, ((), ())), preferred_element_type=out)


def chip_local(
    tokens,
    seq_lengths,
    dealing,
    first_gain,
    query_weight,
    key_matrix,
    value_matrix,
    out_weight,
    second_gain,
    gate_weight,
    up_weight,
    down_weight,
    cotangent,
):
    ctx = lax.axis_size("ctx")
    z = lax.axis_index("ctx")
    f = lax.axis_index("fsdp")
    g = lax.axis_index("grp")
    parity_core = (g == z % 2)
    width = tokens.shape[2]
    tok = tokens.shape[1]
    seq = 2 * tok

    def over_x(field):
        return lax.ppermute(field, "fsdp", [(i, i ^ 1) for i in range(4)])

    def over_y(field):
        return lax.ppermute(field, "fsdp", [(i, i ^ 2) for i in range(4)])

    def over_core(field):
        return lax.ppermute(field, "grp", [(0, 1), (1, 0)])

    swap_pairs = [(2 * i + (1 - i % 2), 2 * (i ^ 1) + i % 2) for i in range(ctx)]

    def swap(field):
        got = lax.ppermute(field, ("ctx", "grp"), swap_pairs)
        return jnp.where(parity_core, field, got)

    def along(field, pairs):
        return lax.ppermute(field, "ctx", pairs)

    def cut(field, start, size, axis):
        return lax.dynamic_slice_in_dim(field, start, size, axis)

    def in_order(mine, other, axis=0):
        first = jnp.where(g == 0, mine, other)
        second = jnp.where(g == 0, other, mine)
        return jnp.concatenate([first, second], axis=axis)

    def gather(piece):
        rows = piece.shape[0]
        from_x, from_y = over_x(piece), over_y(piece)
        top, bottom = over_y(from_x[: rows // 2]), over_x(from_y[rows // 2 :])
        whole = jnp.zeros((4 * rows, piece.shape[1]), piece.dtype)
        for part, at in (
            (piece, f * rows),
            (from_x, (f ^ 1) * rows),
            (from_y, (f ^ 2) * rows),
            (top, (f ^ 3) * rows),
            (bottom, (f ^ 3) * rows + rows // 2),
        ):
            whole = lax.dynamic_update_slice_in_dim(whole, part, at, 0)
        return whole

    def add(left, right):
        return (fp32(left) + fp32(right)).astype(jnp.bfloat16)

    def scatter(grad):
        rows = grad.shape[0] // 4
        mid = rows // 2

        def block(j, low):
            return cut(grad, (f ^ j) * rows + low, mid, 0)

        got = over_x(jnp.concatenate([block(1, 0), block(3, 0)], axis=0))
        top = add(block(0, 0), got[:mid])
        top = add(top, over_y(add(block(2, 0), got[mid:])))
        got = over_y(jnp.concatenate([block(2, mid), block(3, mid)], axis=0))
        low = add(block(0, mid), got[:mid])
        low = add(low, over_x(add(block(1, mid), got[mid:])))
        both = jnp.concatenate([top, low], axis=0)
        both = add(both, along(both, [(0, 1), (3, 2)]))
        first, second = both[:mid], both[mid:]
        left = z == 1
        middle = [(1, 2), (2, 1)]
        got = along(jnp.where(left, second, first), middle)
        done = add(jnp.where(left, first, second), got)
        other = along(done, middle)
        total = jnp.concatenate(
            [jnp.where(left, done, other), jnp.where(left, other, done)], axis=0
        )
        got = along(total, [(1, 0), (2, 3)])
        return jnp.where((z == 1) | (z == 2), total, got)

    heads_q = query_weight.shape[1] // 2
    heads_k = key_matrix.shape[1] // 2
    qkv_own = jnp.concatenate(
        [
            cut(query_weight, g * heads_q, heads_q, 1),
            cut(key_matrix, g * heads_k, heads_k, 1),
            cut(value_matrix, g * heads_k, heads_k, 1),
        ],
        axis=1,
    )
    out_own = cut(out_weight, g * (width // 2), width // 2, 1)
    part_ff = down_weight.shape[0] // 2
    rows_in = gate_weight.shape[0]

    def ff_half(weight):
        return lax.dynamic_index_in_dim(
            weight.reshape(rows_in, 4, 2, part_ff), g, 2, False
        ).reshape(rows_in, 4 * part_ff)

    gate_own, up_own = ff_half(gate_weight), ff_half(up_weight)
    down_own = cut(down_weight, g * part_ff, part_ff, 0)

    x_mine = swap(tokens[0])
    x_other = over_core(x_mine)
    gain_one = fp32(lax.all_gather(first_gain, "fsdp", axis=0, tiled=True))
    gain_two = fp32(lax.all_gather(second_gain, "fsdp", axis=0, tiled=True))
    qkv_w = gather(qkv_own)
    out_half = gather(out_own)
    out_w = in_order(out_half, over_core(out_half), axis=1)
    gate_w = gather(gate_own)
    up_w = gather(up_own)
    down_w = gather(down_own)
    dy_mine = swap(cotangent[0])
    dy_all = jnp.concatenate([dy_mine, over_core(dy_mine)], axis=0)

    positions = jnp.arange(seq, dtype=jnp.int32)
    cosine, sine = rotation(positions, HEAD_SIZE // 2)
    cosine, sine = cosine.T, sine.T

    x_seq = fp32(in_order(x_mine, x_other))
    scale_one = lax.rsqrt(jnp.mean(x_seq * x_seq, axis=-1, keepdims=True) + EPS)
    xn_one = (x_seq * scale_one * gain_one).astype(jnp.bfloat16)
    qkv_t = mm(qkv_w, xn_one, ((0,), (1,)))
    attn_t, lse, q_t, k_t, v_t = attend_seq(qkv_t, cosine, sine)
    attn_keep = cut(attn_t, g * tok, tok, 1)
    attn_send = cut(attn_t, (1 - g) * tok, tok, 1)
    attn_mine = in_order(attn_keep, over_core(attn_send))
    x_own = fp32(x_mine)
    h_own = x_own + mm(attn_mine, out_w, ((0,), (0,)))
    scale_two = lax.rsqrt(jnp.mean(h_own * h_own, axis=-1, keepdims=True) + EPS)
    hat_two = h_own * scale_two
    xn_two_own = (hat_two * gain_two).astype(jnp.bfloat16)
    xn_two = jnp.concatenate([xn_two_own, over_core(xn_two_own)], axis=0)
    gate = mm(xn_two, gate_w)
    up = mm(xn_two, up_w)
    d_hidden = mm(dy_all, down_w, ((1,), (1,)))
    sig = jax.nn.sigmoid(gate)
    act = gate * sig
    hidden = (act * up).astype(jnp.bfloat16)
    d_gate = (d_hidden * up * sig * (1.0 + gate * (1.0 - sig))).astype(jnp.bfloat16)
    d_up = (d_hidden * act).astype(jnp.bfloat16)
    back = ((1,), (1,))
    dn_send = mm(d_gate[tok:], gate_w, back) + mm(d_up[tok:], up_w, back)
    dn_got = over_core(dn_send.astype(jnp.bfloat16))
    dn_own = mm(d_gate[:tok], gate_w, back) + mm(d_up[:tok], up_w, back) + fp32(dn_got)
    gain_two_part = jnp.sum(dn_own * hat_two, axis=0)
    dh_own = fp32(dy_mine) + rms_back(dn_own * gain_two, hat_two, scale_two)
    da = dh_own.astype(jnp.bfloat16)
    dattn_t = mm(out_w, da, back, jnp.bfloat16)
    heads = out_w.shape[0] // 2
    dattn_keep = cut(dattn_t, g * heads, heads, 0)
    dattn_send = cut(dattn_t, (1 - g) * heads, heads, 0)
    dattn_all = in_order(dattn_keep, over_core(dattn_send), axis=1)
    dq_t, dk_t, dv_t = attend_seq_back(q_t, k_t, v_t, dattn_all, lse, cosine, sine)
    dqkv_t = jnp.concatenate([dq_t, dk_t, dv_t], axis=0)

    tokens_in = ((0,), (0,))
    bf = jnp.bfloat16
    down_grad = mm(hidden, dy_all, tokens_in, bf)
    gate_grad = mm(xn_two, d_gate, tokens_in, bf)
    up_grad = mm(xn_two, d_up, tokens_in, bf)
    out_part = mm(attn_mine, da, ((1,), (0,)), bf)
    out_grad = add(
        cut(out_part, g * (width // 2), width // 2, 1),
        over_core(cut(out_part, (1 - g) * (width // 2), width // 2, 1)),
    )
    qkv_grad = mm(xn_one, dqkv_t, ((0,), (1,)), bf)

    res_send = mm(hidden[tok:], down_w).astype(jnp.bfloat16)
    res = h_own + mm(hidden[:tok], down_w) + fp32(over_core(res_send))
    layer_out = swap(res.astype(jnp.bfloat16))

    d1 = mm(dqkv_t, qkv_w, ((0,), (1,)))
    d1_own = cut(d1, g * tok, tok, 0) + fp32(
        over_core(cut(d1, (1 - g) * tok, tok, 0).astype(jnp.bfloat16))
    )
    scale_own = lax.rsqrt(jnp.mean(x_own * x_own, axis=-1, keepdims=True) + EPS)
    hat_one = x_own * scale_own
    gain_one_part = jnp.sum(d1_own * hat_one, axis=0)
    dx = dh_own + rms_back(d1_own * gain_one, hat_one, scale_own)
    tokens_grad = swap(dx.astype(jnp.bfloat16))

    def widen(half, axis=1):
        return fp32(in_order(half, over_core(half), axis=axis))

    down_out = widen(scatter(down_grad), 0)

    def ff_out(grad):
        half = scatter(grad).reshape(rows_in, 4, 1, part_ff)
        return widen(half, 2).reshape(rows_in, 8 * part_ff)

    gate_out, up_out = ff_out(gate_grad), ff_out(up_grad)
    out_out = widen(scatter(out_grad))
    qkv_half = scatter(qkv_grad)
    query_out = widen(qkv_half[:, :heads_q])
    key_out = widen(qkv_half[:, heads_q : heads_q + heads_k])
    value_out = widen(qkv_half[:, heads_q + heads_k :])

    gains = lax.psum(jnp.stack([gain_one_part, gain_two_part]), ("ctx", "fsdp", "grp"))
    gains = cut(gains, f * (width // 4), width // 4, 1)

    all_lse = lax.all_gather(lse.reshape(1, -1, seq), ("ctx", "grp"), axis=0, tiled=True)
    all_lse = all_lse.reshape(ctx // 2, 2, QUERY_HEADS, seq)
    pack_lse = lax.dynamic_index_in_dim(all_lse, g, 1, False)
    pack_lse = jnp.transpose(pack_lse, (1, 0, 2)).reshape(QUERY_HEADS, ctx, tok // BLK, BLK)
    mine = (dealing[0] == z).astype(jnp.float32)
    totals = jnp.sum(pack_lse * mine[None, :, :, None], axis=2).reshape(1, QUERY_HEADS, tok)

    return (
        layer_out[None],
        tokens_grad[None],
        totals,
        gains[0],
        query_out,
        key_out,
        value_out,
        out_out,
        gains[1],
        gate_out,
        up_out,
        down_out,
    )


def chip_holds_sequence(mesh, tokens, seq_lengths):
    sizes = dict(mesh.shape)
    packs, length, _ = tokens.shape
    count = seq_lengths.shape[1]
    return (
        sizes["fsdp"] == 4
        and sizes["grp"] == 2
        and sizes["ctx"] == 4
        and packs == sizes["fsdp"] * sizes["grp"]
        and length == count * MINLEN
        and 2 * length == sizes["ctx"] * MINLEN
    )


def solution(mesh):
    placed = (
        P(("fsdp", "grp"), "ctx", None),
        P(("fsdp", "grp"), None),
        P(("fsdp", "grp"), None, None),
        P("fsdp"),
        P("fsdp", None),
        P("fsdp", None),
        P("fsdp", None),
        P("fsdp", None),
        P("fsdp"),
        P("fsdp", None),
        P("fsdp", None),
        P("fsdp", None),
        P(("fsdp", "grp"), "ctx", None),
    )
    results = (
        P(("fsdp", "grp"), "ctx", None),
        P(("fsdp", "grp"), "ctx", None),
        P(("fsdp", "grp"), None, "ctx"),
        P("fsdp"),
        P("fsdp", None),
        P("fsdp", None),
        P("fsdp", None),
        P("fsdp", None),
        P("fsdp"),
        P("fsdp", None),
        P("fsdp", None),
        P("fsdp", None),
    )

    def program(*arrays):
        body = chip_local if chip_holds_sequence(mesh, arrays[0], arrays[1]) else local
        return jax.shard_map(
            body, mesh=mesh, in_specs=placed, out_specs=results, check_vma=False
        )(*arrays)

    return program
```

```python
import jax
import jax.numpy as jnp
from jax import lax
from jax.experimental import pallas as pl
from jax.experimental.pallas import tpu as pltpu
from jax.sharding import PartitionSpec as P

QUERY_HEADS = 16
KEY_VALUE_HEADS = 8
HEAD_SIZE = 96
BLK = 128


EPS = 1e-05
ROPE_BASE = 100000.0
MASKED = -1e30


def place_rows(positions, lengths):
    ends = jnp.cumsum(lengths, axis=-1)
    before = positions[..., :, None] >= ends[..., None, :]
    segment = jnp.sum(before.astype(jnp.int32), axis=-1)
    offset = jnp.sum(jnp.where(before, lengths[..., None, :], 0), axis=-1)
    return (segment, positions - offset)


def rotation(relative, half_size):
    frequency = ROPE_BASE ** (-(2.0 * jnp.arange(half_size, dtype=jnp.float32)) / (2 * half_size))
    angles = relative.astype(jnp.float32)[:, None] * frequency[None, :]
    return (jnp.cos(angles), jnp.sin(angles))


def rotate(field, cosine, sine_part):
    row_count = field.shape[0]
    half_size = cosine.shape[-1]
    split_heads = field.reshape(row_count, -1, 2 * half_size)
    front_half = split_heads[..., :half_size]
    back_half = split_heads[..., half_size:]
    cos_rows = cosine[:, None, :]
    sin_rows = sine_part[:, None, :]
    turned = jnp.concatenate(
        [
            front_half * cos_rows - back_half * sin_rows,
            back_half * cos_rows + front_half * sin_rows,
        ],
        axis=-1,
    )
    return turned.reshape(row_count, -1)


def rms_back(d_normed, normed, scale):
    return scale * (d_normed - normed * jnp.mean(d_normed * normed, axis=-1, keepdims=True))


def score_block(query_part, key_part, visible):
    scores = jnp.einsum(
        "rgd,kd->grk", query_part, key_part, preferred_element_type=jnp.float32
    ) * HEAD_SIZE ** (-0.5)
    return jnp.where(visible[None], scores, MASKED)


def attend_pack(query_pack, key_pack, value_pack, visible_list):
    token_count = query_pack.shape[0]
    rounds = len(visible_list)
    query_group_width = QUERY_HEADS // KEY_VALUE_HEADS
    context_count = key_pack.shape[0] // token_count

    def width_per_head(head_index, carry):
        out_buf, total_buf = carry
        query_head = lax.dynamic_slice_in_dim(
            query_pack, head_index * query_group_width * HEAD_SIZE, query_group_width * HEAD_SIZE, 1
        ).reshape(token_count, query_group_width, HEAD_SIZE)
        key_head = lax.dynamic_slice_in_dim(key_pack, head_index * HEAD_SIZE, HEAD_SIZE, 1).reshape(
            context_count, rounds, BLK, HEAD_SIZE
        )
        value_head = lax.dynamic_slice_in_dim(
            value_pack, head_index * HEAD_SIZE, HEAD_SIZE, 1
        ).reshape(context_count, rounds, BLK, HEAD_SIZE)
        running_top = jnp.full((query_group_width, token_count), MASKED, jnp.float32)
        running_sum = jnp.zeros((query_group_width, token_count), jnp.float32)
        for round_index in range(rounds):
            first_row = round_index * BLK
            scores = score_block(
                query_head[first_row:],
                key_head[:, round_index].reshape(-1, HEAD_SIZE),
                visible_list[round_index],
            )
            new_top = jnp.maximum(running_top[:, first_row:], jnp.max(scores, axis=-1))
            weights = jnp.where(
                visible_list[round_index][None], jnp.exp(scores - new_top[..., None]), 0.0
            )
            new_sum = running_sum[:, first_row:] * jnp.exp(
                running_top[:, first_row:] - new_top
            ) + jnp.sum(weights, axis=-1)
            running_top = running_top.at[:, first_row:].set(new_top)
            running_sum = running_sum.at[:, first_row:].set(new_sum)
        log_totals = running_top + jnp.log(running_sum)
        mixture = jnp.zeros((token_count, query_group_width, HEAD_SIZE), jnp.float32)
        for round_index in range(rounds):
            first_row = round_index * BLK
            scores = score_block(
                query_head[first_row:],
                key_head[:, round_index].reshape(-1, HEAD_SIZE),
                visible_list[round_index],
            )
            prob_bf = jnp.where(
                visible_list[round_index][None],
                jnp.exp(scores - log_totals[:, first_row:, None]),
                0.0,
            ).astype(jnp.bfloat16)
            mixture = mixture.at[first_row:].add(
                jnp.einsum(
                    "grk,kd->rgd",
                    prob_bf,
                    value_head[:, round_index].reshape(-1, HEAD_SIZE),
                    preferred_element_type=jnp.float32,
                )
            )
        out_buf = lax.dynamic_update_slice_in_dim(
            out_buf,
            mixture.astype(jnp.bfloat16).reshape(token_count, -1),
            head_index * query_group_width * HEAD_SIZE,
            1,
        )
        total_buf = lax.dynamic_update_slice_in_dim(
            total_buf, log_totals, head_index * query_group_width, 0
        )
        return (out_buf, total_buf)

    start_offsets = (
        jnp.zeros((token_count, QUERY_HEADS * HEAD_SIZE), jnp.bfloat16),
        jnp.zeros((QUERY_HEADS, token_count), jnp.float32),
    )
    return lax.fori_loop(0, KEY_VALUE_HEADS, width_per_head, start_offsets)


def attend_back(
    query_pack, key_pack, value_pack, grad_pack, attended_pack, total_pack, visible_list
):
    token_count = query_pack.shape[0]
    rounds = len(visible_list)
    query_group_width = QUERY_HEADS // KEY_VALUE_HEADS
    context_count = key_pack.shape[0] // token_count

    def width_per_head(head_index, carry):
        query_buf, key_buf, value_buf = carry
        query_head = lax.dynamic_slice_in_dim(
            query_pack, head_index * query_group_width * HEAD_SIZE, query_group_width * HEAD_SIZE, 1
        ).reshape(token_count, query_group_width, HEAD_SIZE)
        grad_head = lax.dynamic_slice_in_dim(
            grad_pack, head_index * query_group_width * HEAD_SIZE, query_group_width * HEAD_SIZE, 1
        ).reshape(token_count, query_group_width, HEAD_SIZE)
        output_head = lax.dynamic_slice_in_dim(
            attended_pack,
            head_index * query_group_width * HEAD_SIZE,
            query_group_width * HEAD_SIZE,
            1,
        ).reshape(token_count, query_group_width, HEAD_SIZE)
        key_head = lax.dynamic_slice_in_dim(key_pack, head_index * HEAD_SIZE, HEAD_SIZE, 1).reshape(
            context_count, rounds, BLK, HEAD_SIZE
        )
        value_head = lax.dynamic_slice_in_dim(
            value_pack, head_index * HEAD_SIZE, HEAD_SIZE, 1
        ).reshape(context_count, rounds, BLK, HEAD_SIZE)
        log_totals = lax.dynamic_slice_in_dim(
            total_pack, head_index * query_group_width, query_group_width, 0
        )
        delta = jnp.sum(grad_head.astype(jnp.float32) * output_head.astype(jnp.float32), axis=-1).T
        query_grad = jnp.zeros((token_count, query_group_width, HEAD_SIZE), jnp.float32)
        key_parts = []
        value_parts = []
        for round_index in range(rounds):
            first_row = round_index * BLK
            key_round = key_head[:, round_index].reshape(-1, HEAD_SIZE)
            value_round = value_head[:, round_index].reshape(-1, HEAD_SIZE)
            scores = score_block(query_head[first_row:], key_round, visible_list[round_index])
            probs_full = jnp.where(
                visible_list[round_index][None],
                jnp.exp(scores - log_totals[:, first_row:, None]),
                0.0,
            )
            d_probs = jnp.einsum(
                "rgd,kd->grk",
                grad_head[first_row:],
                value_round,
                preferred_element_type=jnp.float32,
            )
            d_scores = (
                HEAD_SIZE ** (-0.5) * probs_full * (d_probs - delta[:, first_row:, None])
            ).astype(jnp.bfloat16)
            value_parts.append(
                jnp.einsum(
                    "grk,rgd->kd",
                    probs_full.astype(jnp.bfloat16),
                    grad_head[first_row:],
                    preferred_element_type=jnp.float32,
                )
            )
            key_parts.append(
                jnp.einsum(
                    "grk,rgd->kd",
                    d_scores,
                    query_head[first_row:],
                    preferred_element_type=jnp.float32,
                )
            )
            query_grad = query_grad.at[first_row:].add(
                jnp.einsum("grk,kd->rgd", d_scores, key_round, preferred_element_type=jnp.float32)
            )
        key_block = jnp.stack(
            [part.reshape(context_count, BLK, HEAD_SIZE) for part in key_parts], axis=1
        ).reshape(-1, HEAD_SIZE)
        value_block = jnp.stack(
            [part.reshape(context_count, BLK, HEAD_SIZE) for part in value_parts], axis=1
        ).reshape(-1, HEAD_SIZE)
        query_buf = lax.dynamic_update_slice_in_dim(
            query_buf,
            query_grad.reshape(token_count, -1),
            head_index * query_group_width * HEAD_SIZE,
            1,
        )
        key_buf = lax.dynamic_update_slice_in_dim(key_buf, key_block, head_index * HEAD_SIZE, 1)
        value_buf = lax.dynamic_update_slice_in_dim(
            value_buf, value_block, head_index * HEAD_SIZE, 1
        )
        return (query_buf, key_buf, value_buf)

    start_offsets = (
        jnp.zeros((token_count, QUERY_HEADS * HEAD_SIZE), jnp.float32),
        jnp.zeros((context_count * token_count, KEY_VALUE_HEADS * HEAD_SIZE), jnp.float32),
        jnp.zeros((context_count * token_count, KEY_VALUE_HEADS * HEAD_SIZE), jnp.float32),
    )
    return lax.fori_loop(0, KEY_VALUE_HEADS, width_per_head, start_offsets)


def local(
    tokens,
    seq_lengths,
    dealing,
    first_gain,
    query_weight,
    key_matrix,
    value_matrix,
    out_weight,
    second_gain,
    gate_weight,
    up_weight,
    down_weight,
    cotangent,
):
    context_count = lax.axis_size("ctx")
    my_index = lax.axis_index("ctx")
    pack_count, token_count, model_dim = tokens.shape
    rounds = token_count // BLK
    spread = context_count // rounds
    ctx_range = jnp.arange(context_count, dtype=jnp.int32)
    matches = (dealing[..., None] == ctx_range).astype(jnp.int32)
    slot_of = jnp.sum(matches * ctx_range[:, None], axis=2)
    block_of = jnp.arange(rounds, dtype=jnp.int32)[None, :, None] * context_count + slot_of
    key_pos = (
        jnp.transpose(block_of, (0, 2, 1))[..., None] * BLK + jnp.arange(BLK, dtype=jnp.int32)
    ).reshape(pack_count, -1)
    key_seg = place_rows(key_pos, seq_lengths)[0]
    query_pos = lax.dynamic_slice_in_dim(key_pos, my_index * token_count, token_count, 1)
    query_seg, query_rel = place_rows(query_pos, seq_lengths)
    home_row = lax.dynamic_index_in_dim(dealing, my_index // spread, 1, False)
    targets = lax.dynamic_slice_in_dim(home_row, my_index % spread * rounds, rounds, 1)
    picker = (targets[:, None, :] == ctx_range[None, :, None]).astype(jnp.bfloat16)
    my_slots = lax.dynamic_index_in_dim(slot_of, my_index, 2, False)
    owner_index = (
        jnp.arange(rounds, dtype=jnp.int32)[None, :] * context_count + my_slots
    ) // rounds
    keep_slot = jnp.repeat(owner_index, spread, axis=1) == ctx_range[None, :]

    def spread_out(field):
        blocks = field.reshape(pack_count, rounds, BLK, model_dim)
        return jnp.einsum(
            "pkj,pjtd->pktd", picker, blocks, preferred_element_type=jnp.float32
        ).astype(jnp.bfloat16)

    def collect(received):
        grouped = received.reshape(pack_count, rounds, spread, BLK, model_dim)
        return (
            jnp.sum(grouped, axis=2, dtype=jnp.float32)
            .astype(jnp.bfloat16)
            .reshape(pack_count * token_count, model_dim)
        )

    def send_home(field):
        blocks = jnp.repeat(field.reshape(pack_count, rounds, BLK, model_dim), spread, axis=1)
        return jnp.where(keep_slot[:, :, None, None], blocks, jnp.zeros_like(blocks))

    def restore(returned):
        placed = jnp.einsum("pkj,pktd->pjtd", picker, returned, preferred_element_type=jnp.float32)
        return placed.astype(jnp.bfloat16).reshape(pack_count, token_count, model_dim)

    dealt_tokens, dealt_upstream = (
        lax.all_to_all(spread_out(tokens), "ctx", split_axis=1, concat_axis=1, tiled=True),
        lax.all_to_all(spread_out(cotangent), "ctx", split_axis=1, concat_axis=1, tiled=True),
    )
    inputs = collect(dealt_tokens)
    upstream = collect(dealt_upstream)
    gain_one, query_full, key_full, value_full, out_full = (
        lax.all_gather(first_gain, "fsdp", axis=0, tiled=True),
        lax.all_gather(query_weight, "fsdp", axis=0, tiled=True),
        lax.all_gather(key_matrix, "fsdp", axis=0, tiled=True),
        lax.all_gather(value_matrix, "fsdp", axis=0, tiled=True),
        lax.all_gather(out_weight, "fsdp", axis=0, tiled=True),
    )
    gain_two, gate_full, up_full, down_full = (
        lax.all_gather(second_gain, "fsdp", axis=0, tiled=True),
        lax.all_gather(gate_weight, "fsdp", axis=0, tiled=True),
        lax.all_gather(up_weight, "fsdp", axis=0, tiled=True),
        lax.all_gather(down_weight, "fsdp", axis=0, tiled=True),
    )
    gain_one32 = gain_one.astype(jnp.float32)
    gain_two32 = gain_two.astype(jnp.float32)
    cosine, sine_part = rotation(query_rel.reshape(-1), HEAD_SIZE // 2)
    inputs32 = inputs.astype(jnp.float32)
    scale_one = lax.rsqrt(jnp.mean(inputs32 * inputs32, axis=-1, keepdims=True) + EPS)
    normed_one = inputs32 * scale_one
    xn_one = (normed_one * gain_one32).astype(jnp.bfloat16)
    query_rot = rotate(
        jnp.dot(xn_one, query_full, preferred_element_type=jnp.float32), cosine, sine_part
    ).astype(jnp.bfloat16)
    key_rot = rotate(
        jnp.dot(xn_one, key_full, preferred_element_type=jnp.float32), cosine, sine_part
    ).astype(jnp.bfloat16)
    rows_of_values = jnp.dot(xn_one, value_full, preferred_element_type=jnp.float32).astype(
        jnp.bfloat16
    )
    key_local = key_rot.reshape(pack_count, token_count, -1)
    value_local = rows_of_values.reshape(pack_count, token_count, -1)
    gathered_keys, gathered_values = (
        lax.all_gather(key_local, "ctx", axis=1, tiled=True),
        lax.all_gather(value_local, "ctx", axis=1, tiled=True),
    )
    key_pos_rounds = key_pos.reshape(pack_count, context_count, rounds, BLK)
    key_seg_rounds = key_seg.reshape(pack_count, context_count, rounds, BLK)
    visible = []
    for round_index in range(rounds):
        first_row = round_index * BLK
        round_pos = key_pos_rounds[:, :, round_index].reshape(pack_count, -1)
        round_seg = key_seg_rounds[:, :, round_index].reshape(pack_count, -1)
        same_seq = query_seg[:, first_row:, None] == round_seg[:, None, :]
        earlier = round_pos[:, None, :] <= query_pos[:, first_row:, None]
        visible.append(same_seq & earlier)
    query_packs = query_rot.reshape(pack_count, token_count, -1)
    pack_index = 0
    pack_visible = [mask[pack_index] for mask in visible]
    attended_pack, total_pack = attend_pack(
        query_packs[pack_index],
        gathered_keys[pack_index],
        gathered_values[pack_index],
        pack_visible,
    )
    total_list = [total_pack]
    softmax_totals = jnp.stack(total_list, axis=0)
    hidden_in = inputs32 + jnp.dot(attended_pack, out_full, preferred_element_type=jnp.float32)
    scale_two = lax.rsqrt(jnp.mean(hidden_in * hidden_in, axis=-1, keepdims=True) + EPS)
    normed_two = hidden_in * scale_two
    xn_two = (normed_two * gain_two32).astype(jnp.bfloat16)
    gate_val = jnp.dot(xn_two, gate_full, preferred_element_type=jnp.float32)
    up_val = jnp.dot(xn_two, up_full, preferred_element_type=jnp.float32)
    activated = jax.nn.silu(gate_val)
    hidden = (activated * up_val).astype(jnp.bfloat16)
    result = (hidden_in + jnp.dot(hidden, down_full, preferred_element_type=jnp.float32)).astype(
        jnp.bfloat16
    )
    down_grad = jnp.dot(hidden.T, upstream, preferred_element_type=jnp.float32)
    d_hidden = jnp.dot(upstream, down_full.T, preferred_element_type=jnp.float32)
    sigmoid_gate = jax.nn.sigmoid(gate_val)
    d_gate = (d_hidden * up_val * sigmoid_gate * (1.0 + gate_val * (1.0 - sigmoid_gate))).astype(
        jnp.bfloat16
    )
    d_up = (d_hidden * activated).astype(jnp.bfloat16)
    gate_grad = jnp.dot(xn_two.T, d_gate, preferred_element_type=jnp.float32)
    up_grad = jnp.dot(xn_two.T, d_up, preferred_element_type=jnp.float32)
    d_norm_two = jnp.dot(d_gate, gate_full.T, preferred_element_type=jnp.float32) + jnp.dot(
        d_up, up_full.T, preferred_element_type=jnp.float32
    )
    gain_two_grad = jnp.sum(d_norm_two * normed_two, axis=0)
    d_hidden_in = upstream.astype(jnp.float32) + rms_back(
        d_norm_two * gain_two32, normed_two, scale_two
    )
    mlp_parts = (
        lax.psum_scatter(
            gain_two_grad.astype(jnp.bfloat16), "fsdp", scatter_dimension=0, tiled=True
        ).astype(jnp.float32),
        lax.psum_scatter(
            gate_grad.astype(jnp.bfloat16), "fsdp", scatter_dimension=0, tiled=True
        ).astype(jnp.float32),
        lax.psum_scatter(
            up_grad.astype(jnp.bfloat16), "fsdp", scatter_dimension=0, tiled=True
        ).astype(jnp.float32),
        lax.psum_scatter(
            down_grad.astype(jnp.bfloat16), "fsdp", scatter_dimension=0, tiled=True
        ).astype(jnp.float32),
    )
    d_branch = d_hidden_in.astype(jnp.bfloat16)
    out_grad = jnp.dot(attended_pack.T, d_branch, preferred_element_type=jnp.float32)
    d_attended = jnp.dot(d_branch, out_full.T, preferred_element_type=jnp.float32).astype(
        jnp.bfloat16
    )
    back_keys, back_values = (gathered_keys, gathered_values)
    grad_packs = d_attended.reshape(pack_count, token_count, -1)
    out_packs = attended_pack.reshape(pack_count, token_count, -1)
    pack_index = 0
    pack_visible = [mask[pack_index] for mask in visible]
    query_part, key_part, value_part = attend_back(
        query_packs[pack_index],
        back_keys[pack_index],
        back_values[pack_index],
        grad_packs[pack_index],
        out_packs[pack_index],
        softmax_totals[pack_index],
        pack_visible,
    )
    key_list = [key_part]
    value_list = [value_part]
    d_keys, d_values = (
        lax.psum_scatter(
            jnp.stack(key_list, axis=0).astype(jnp.bfloat16), "ctx", scatter_dimension=1, tiled=True
        ).astype(jnp.float32),
        lax.psum_scatter(
            jnp.stack(value_list, axis=0).astype(jnp.bfloat16),
            "ctx",
            scatter_dimension=1,
            tiled=True,
        ).astype(jnp.float32),
    )
    d_query = rotate(query_part, cosine, -sine_part).astype(jnp.bfloat16)
    d_key = rotate(d_keys.reshape(pack_count * token_count, -1), cosine, -sine_part).astype(
        jnp.bfloat16
    )
    d_value = d_values.reshape(pack_count * token_count, -1).astype(jnp.bfloat16)
    query_grad = jnp.dot(xn_one.T, d_query, preferred_element_type=jnp.float32)
    key_grad = jnp.dot(xn_one.T, d_key, preferred_element_type=jnp.float32)
    value_grad = jnp.dot(xn_one.T, d_value, preferred_element_type=jnp.float32)
    d_norm_one = (
        jnp.dot(d_query, query_full.T, preferred_element_type=jnp.float32)
        + jnp.dot(d_key, key_full.T, preferred_element_type=jnp.float32)
        + jnp.dot(d_value, value_full.T, preferred_element_type=jnp.float32)
    )
    gain_one_grad = jnp.sum(d_norm_one * normed_one, axis=0)
    d_inputs = d_hidden_in + rms_back(d_norm_one * gain_one32, normed_one, scale_one)
    attn_parts = (
        lax.psum_scatter(
            gain_one_grad.astype(jnp.bfloat16), "fsdp", scatter_dimension=0, tiled=True
        ).astype(jnp.float32),
        lax.psum_scatter(
            query_grad.astype(jnp.bfloat16), "fsdp", scatter_dimension=0, tiled=True
        ).astype(jnp.float32),
        lax.psum_scatter(
            key_grad.astype(jnp.bfloat16), "fsdp", scatter_dimension=0, tiled=True
        ).astype(jnp.float32),
        lax.psum_scatter(
            value_grad.astype(jnp.bfloat16), "fsdp", scatter_dimension=0, tiled=True
        ).astype(jnp.float32),
        lax.psum_scatter(
            out_grad.astype(jnp.bfloat16), "fsdp", scatter_dimension=0, tiled=True
        ).astype(jnp.float32),
    )
    finished = (
        lax.psum(attn_parts[0].astype(jnp.bfloat16), ("ctx", "grp")).astype(jnp.float32),
        lax.psum(attn_parts[1].astype(jnp.bfloat16), ("ctx", "grp")).astype(jnp.float32),
        lax.psum(attn_parts[2].astype(jnp.bfloat16), ("ctx", "grp")).astype(jnp.float32),
        lax.psum(attn_parts[3].astype(jnp.bfloat16), ("ctx", "grp")).astype(jnp.float32),
        lax.psum(attn_parts[4].astype(jnp.bfloat16), ("ctx", "grp")).astype(jnp.float32),
        lax.psum(mlp_parts[0].astype(jnp.bfloat16), ("ctx", "grp")).astype(jnp.float32),
        lax.psum(mlp_parts[1].astype(jnp.bfloat16), ("ctx", "grp")).astype(jnp.float32),
        lax.psum(mlp_parts[2].astype(jnp.bfloat16), ("ctx", "grp")).astype(jnp.float32),
        lax.psum(mlp_parts[3].astype(jnp.bfloat16), ("ctx", "grp")).astype(jnp.float32),
    )
    home_out, home_grad = (
        lax.all_to_all(send_home(result), "ctx", split_axis=1, concat_axis=1, tiled=True),
        lax.all_to_all(
            send_home(d_inputs.astype(jnp.bfloat16)), "ctx", split_axis=1, concat_axis=1, tiled=True
        ),
    )
    return (
        restore(home_out),
        restore(home_grad),
        softmax_totals,
        finished[0],
        finished[1],
        finished[2],
        finished[3],
        finished[4],
        finished[5],
        finished[6],
        finished[7],
        finished[8],
    )


MINLEN = 1024
QB = 256
VMEM_LIMIT = 56 * 1024 * 1024


def attend_kernel(q_ref, k_ref, v_ref, c_ref, s_ref, o_ref, lse_ref, qr_ref, kr_ref, vr_ref):
    cosine = c_ref[...]
    sine = s_ref[...]
    half = HEAD_SIZE // 2
    seq = cosine.shape[1]

    def turn(field):
        front, back = field[:half], field[half:]
        return jnp.concatenate(
            [front * cosine - back * sine, back * cosine + front * sine], axis=0
        )

    k_rot = turn(k_ref[...])
    kr_ref[...] = k_rot.astype(jnp.bfloat16)
    key = k_rot.T.astype(jnp.bfloat16)
    val_t = v_ref[...].astype(jnp.bfloat16)
    vr_ref[...] = val_t
    q0 = turn(q_ref[:HEAD_SIZE]).astype(jnp.bfloat16)
    q1 = turn(q_ref[HEAD_SIZE:]).astype(jnp.bfloat16)
    qr_ref[:HEAD_SIZE] = q0
    qr_ref[HEAD_SIZE:] = q1
    rows = lax.broadcasted_iota(jnp.int32, (QB, 2 * QB), 0)
    cols = lax.broadcasted_iota(jnp.int32, (QB, 2 * QB), 1)
    keep = rows <= jnp.where(cols >= QB, cols - QB, cols)
    for b in range(seq // QB):
        lo, n = b * QB, (b + 1) * QB
        q_t = jnp.concatenate([q0[:, lo:n], q1[:, lo:n]], axis=1)
        scores = jnp.dot(key[:n], q_t, preferred_element_type=jnp.float32) * HEAD_SIZE ** (-0.5)
        diag = jnp.where(keep, scores[lo:], MASKED)
        top = jnp.max(diag, axis=0, keepdims=True)
        if b > 0:
            top = jnp.maximum(top, jnp.max(scores[:lo], axis=0, keepdims=True))
        e_diag = jnp.exp(diag - top)
        total = jnp.sum(e_diag, axis=0, keepdims=True)
        out = jnp.dot(val_t[:, lo:n], e_diag.astype(jnp.bfloat16), preferred_element_type=jnp.float32)
        if b > 0:
            e_rest = jnp.exp(scores[:lo] - top)
            total = total + jnp.sum(e_rest, axis=0, keepdims=True)
            out = out + jnp.dot(
                val_t[:, :lo], e_rest.astype(jnp.bfloat16), preferred_element_type=jnp.float32
            )
        out = (out / total).astype(jnp.bfloat16)
        o_ref[:HEAD_SIZE, lo:n] = out[:, :QB]
        o_ref[HEAD_SIZE:, lo:n] = out[:, QB:]
        lse = top + jnp.log(total)
        lse_ref[0, 0:1, lo:n] = lse[:, :QB]
        lse_ref[0, 1:2, lo:n] = lse[:, QB:]


def attend_seq(qkv_t, cosine, sine):
    rows, seq = qkv_t.shape
    kv = rows // (4 * HEAD_SIZE)
    group = pl.BlockSpec((2 * HEAD_SIZE, seq), lambda j: (j, 0))

    def head(base):
        return pl.BlockSpec((HEAD_SIZE, seq), lambda j: (base + j, 0))

    table = pl.BlockSpec((HEAD_SIZE // 2, seq), lambda j: (0, 0))
    return pl.pallas_call(
        attend_kernel,
        grid=(kv,),
        in_specs=[group, head(2 * kv), head(3 * kv), table, table],
        out_specs=[
            group,
            pl.BlockSpec((1, 2, seq), lambda j: (j, 0, 0)),
            group,
            head(0),
            head(0),
        ],
        out_shape=[
            jax.ShapeDtypeStruct((2 * kv * HEAD_SIZE, seq), jnp.bfloat16),
            jax.ShapeDtypeStruct((kv, 2, seq), jnp.float32),
            jax.ShapeDtypeStruct((2 * kv * HEAD_SIZE, seq), jnp.bfloat16),
            jax.ShapeDtypeStruct((kv * HEAD_SIZE, seq), jnp.bfloat16),
            jax.ShapeDtypeStruct((kv * HEAD_SIZE, seq), jnp.bfloat16),
        ],
        compiler_params=pltpu.CompilerParams(vmem_limit_bytes=VMEM_LIMIT),
        cost_estimate=pl.CostEstimate(
            flops=4 * kv * 2 * seq * seq * HEAD_SIZE, bytes_accessed=10 * rows * seq, transcendentals=kv * seq * seq
        ),
        name="attend",
    )(qkv_t, qkv_t, qkv_t, cosine, sine)


def attend_back_kernel(
    q_ref, k_ref, v_ref, g_ref, lse_ref, c_ref, s_ref, dq_ref, dk_ref, dv_ref, dk_acc, dv_acc
):
    half = HEAD_SIZE // 2
    cosine = c_ref[...]
    sine = s_ref[...]
    seq = cosine.shape[1]

    def turn_back(field, cos, sin):
        front, back = field[:half], field[half:]
        return jnp.concatenate([front * cos + back * sin, back * cos - front * sin], axis=0)

    def flip(field):
        return field.astype(jnp.float32).T.astype(jnp.bfloat16)

    key_t = k_ref[...]
    key = flip(key_t)
    val = flip(v_ref[...])
    q0_t, q1_t = q_ref[:HEAD_SIZE], q_ref[HEAD_SIZE:]
    g0_t, g1_t = g_ref[:HEAD_SIZE], g_ref[HEAD_SIZE:]
    q0, q1, g0, g1 = flip(q0_t), flip(q1_t), flip(g0_t), flip(g1_t)
    dk_acc[...] = jnp.zeros_like(dk_acc)
    dv_acc[...] = jnp.zeros_like(dv_acc)
    rows = lax.broadcasted_iota(jnp.int32, (QB, 2 * QB), 0)
    cols = lax.broadcasted_iota(jnp.int32, (QB, 2 * QB), 1)
    keep = rows <= jnp.where(cols >= QB, cols - QB, cols)
    for b in range(seq // QB):
        lo, n = b * QB, (b + 1) * QB
        q_t = jnp.concatenate([q0_t[:, lo:n], q1_t[:, lo:n]], axis=1)
        g_t = jnp.concatenate([g0_t[:, lo:n], g1_t[:, lo:n]], axis=1)
        q_n = jnp.concatenate([q0[lo:n], q1[lo:n]], axis=0)
        g_n = jnp.concatenate([g0[lo:n], g1[lo:n]], axis=0)
        lse = jnp.concatenate([lse_ref[0, 0:1, lo:n], lse_ref[0, 1:2, lo:n]], axis=1)
        parts = []
        delta = None
        for start, stop in ([(0, lo)] if b > 0 else []) + [(lo, n)]:
            scores = jnp.dot(key[start:stop], q_t, preferred_element_type=jnp.float32) * HEAD_SIZE ** (-0.5)
            prob = jnp.exp(scores - lse)
            if start == lo:
                prob = jnp.where(keep, prob, 0.0)
            d_prob = jnp.dot(val[start:stop], g_t, preferred_element_type=jnp.float32)
            part = jnp.sum(prob * d_prob, axis=0, keepdims=True)
            delta = part if delta is None else delta + part
            dv_acc[start:stop] += jnp.dot(prob.astype(jnp.bfloat16), g_n, preferred_element_type=jnp.float32)
            parts.append((start, stop, prob, d_prob))
        dq_t = None
        for start, stop, prob, d_prob in parts:
            d_score = (prob * (d_prob - delta) * HEAD_SIZE ** (-0.5)).astype(jnp.bfloat16)
            dk_acc[start:stop] += jnp.dot(d_score, q_n, preferred_element_type=jnp.float32)
            part = jnp.dot(key_t[:, start:stop], d_score, preferred_element_type=jnp.float32)
            dq_t = part if dq_t is None else dq_t + part
        cos, sin = cosine[:, lo:n], sine[:, lo:n]
        dq_ref[:HEAD_SIZE, lo:n] = turn_back(dq_t[:, :QB], cos, sin).astype(jnp.bfloat16)
        dq_ref[HEAD_SIZE:, lo:n] = turn_back(dq_t[:, QB:], cos, sin).astype(jnp.bfloat16)
    dk_ref[...] = turn_back(dk_acc[...].T, cosine, sine).astype(jnp.bfloat16)
    dv_ref[...] = dv_acc[...].T.astype(jnp.bfloat16)


def attend_seq_back(q_t, k_t, v_t, g_t, lse, cosine, sine):
    rows, seq = k_t.shape
    kv = rows // HEAD_SIZE
    group = pl.BlockSpec((2 * HEAD_SIZE, seq), lambda j: (j, 0))
    head = pl.BlockSpec((HEAD_SIZE, seq), lambda j: (j, 0))
    table = pl.BlockSpec((HEAD_SIZE // 2, seq), lambda j: (0, 0))
    return pl.pallas_call(
        attend_back_kernel,
        grid=(kv,),
        in_specs=[group, head, head, group, pl.BlockSpec((1, 2, seq), lambda j: (j, 0, 0)), table, table],
        out_specs=[group, head, head],
        out_shape=[
            jax.ShapeDtypeStruct((2 * rows, seq), jnp.bfloat16),
            jax.ShapeDtypeStruct((rows, seq), jnp.bfloat16),
            jax.ShapeDtypeStruct((rows, seq), jnp.bfloat16),
        ],
        scratch_shapes=[
            pltpu.VMEM((seq, HEAD_SIZE), jnp.float32),
            pltpu.VMEM((seq, HEAD_SIZE), jnp.float32),
        ],
        compiler_params=pltpu.CompilerParams(vmem_limit_bytes=VMEM_LIMIT),
        cost_estimate=pl.CostEstimate(
            flops=10 * kv * 2 * seq * seq * HEAD_SIZE, bytes_accessed=20 * rows * seq, transcendentals=kv * seq * seq
        ),
        name="attend_back",
    )(q_t, k_t, v_t, g_t, lse, cosine, sine)


def fp32(field):
    return field.astype(jnp.float32)


def mm(left, right, dims=((1,), (0,)), out=jnp.float32):
    return lax.dot_general(left, right, (dims, ((), ())), preferred_element_type=out)


ANY = pl.BlockSpec(memory_space=pl.ANY)
SMEM = pl.BlockSpec(memory_space=pltpu.SMEM)
VM = pl.BlockSpec(memory_space=pltpu.VMEM)
PARAMS = pltpu.CompilerParams(vmem_limit_bytes=VMEM_LIMIT)
MESH = pl.DeviceIdType.MESH
TILE = 256


def bf16_like(*dims):
    return jax.ShapeDtypeStruct(dims, jnp.bfloat16)


def f32_like(*dims):
    return jax.ShapeDtypeStruct(dims, jnp.float32)


def cost(flops, moved):
    return pl.CostEstimate(flops=int(flops), bytes_accessed=int(moved), transcendentals=0)


class Spots:
    def __init__(self):
        z, f, g = lax.axis_index("ctx"), lax.axis_index("fsdp"), lax.axis_index("grp")
        self.z, self.f, self.g = z, f, g
        self.parity = z % 2
        self.fx = f + 1 - 2 * (f % 2)
        self.fy = f + 2 - 4 * (f // 2)
        self.fd = 3 - f
        across = z + 1 - 2 * self.parity
        self.x = (z, self.fx, g)
        self.y = (z, self.fy, g)
        self.diag = (z, self.fd, g)
        self.core = (z, f, 1 - g)
        self.across = (across, f, g)
        self.swap = (across, f, 1 - g)


def greet(*partners):
    barrier = pltpu.get_barrier_semaphore()
    for partner in partners:
        pl.semaphore_signal(barrier, inc=1, device_id=partner, device_id_type=MESH)
    pl.semaphore_wait(barrier, len(partners))


def rows_at(start, size):
    return pl.ds(pl.multiple_of(start, size), size)


def gather_kernel(
    tokens, cotangent, wq, wk, wv, wo, gate, up, down, gain,
    qkv_o, out_o, pair_o, down_o, x_o, dy_o, gain_o,
    send, recv, near, far, qkv_v, out_v, pair_v, down_v, tok_v, gain_v,
):
    at = Spots()
    g, f, parity = at.g, at.f, at.parity
    greet(at.x, at.y, at.diag, at.core, at.across, at.swap)
    taken = [0, 0]

    def remote(src, dst, device):
        i = taken[0]
        taken[0] += 1
        return pltpu.make_async_remote_copy(
            src_ref=src, dst_ref=dst, send_sem=send.at[i], recv_sem=recv.at[i],
            device_id=device, device_id_type=MESH,
        )

    class Bounce:
        def __init__(self, src, via, dst):
            i = taken[1]
            taken[1] += 1
            self.first = pltpu.make_async_copy(src, via, near.at[i])
            self.second = pltpu.make_async_copy(via, dst, far.at[i])

        def start(self):
            self.first.start()

        def turn(self):
            self.first.wait()
            self.second.start()

        def wait(self):
            self.second.wait()

    def start(copies):
        for copy in copies:
            copy.start()
        return copies

    def arrive(copies):
        for copy in copies:
            copy.wait_recv()

    tok = tokens.shape[1]
    feat = wq.shape[0]
    mid = feat // 2
    nq, nk, nv = (w.shape[1] // 2 for w in (wq, wk, wv))
    nf = down.shape[0] // 2
    wide = wo.shape[1] // 2
    count = 4
    top, low = slice(0, mid), slice(mid, feat)

    mine = rows_at(g * tok, tok)
    swaps = [
        remote(tokens.at[0], x_o.at[mine], at.swap),
        remote(cotangent.at[0], dy_o.at[mine], at.swap),
    ]
    keeps = [
        Bounce(tokens.at[0], tok_v.at[0], x_o.at[mine]),
        Bounce(cotangent.at[0], tok_v.at[1], dy_o.at[mine]),
    ]
    away = rows_at((1 - g) * tok, tok)
    swaps_out = [
        pltpu.make_async_remote_copy(
            src_ref=array.at[0], dst_ref=into.at[away], send_sem=send.at[i], recv_sem=recv.at[i],
            device_id=at.swap, device_id_type=MESH,
        )
        for i, (array, into) in enumerate(((tokens, x_o), (cotangent, dy_o)))
    ]
    shares = [remote(x_o.at[mine], x_o.at[mine], at.core), remote(dy_o.at[mine], dy_o.at[mine], at.core)]

    @pl.when(g != parity)
    def _():
        start(swaps_out)

    @pl.when(g == parity)
    def _():
        start(keeps)
        for copy in keeps:
            copy.turn()

    own_rows = f * feat

    def pair_sends(array, device, part):
        return [
            (
                array.at[part, rows_at((2 * k + g) * nf, nf)],
                pair_o.at[parity, rows_at(own_rows + part.start, mid), rows_at(k * nf, nf)],
                device,
            )
            for k in range(count)
        ]

    def pair_direct(part, device):
        first = taken[0]
        taken[0] += count

        def made(array):
            return [
                pltpu.make_async_remote_copy(
                    src_ref=src, dst_ref=dst, send_sem=send.at[first + k], recv_sem=recv.at[first + k],
                    device_id=to, device_id_type=MESH,
                )
                for k, (src, dst, to) in enumerate(pair_sends(array, device, part))
            ]

        @pl.when(parity == 0)
        def _():
            start(made(gate))

        @pl.when(parity == 1)
        def _():
            start(made(up))

        return made(gate)

    pair_xt = pair_direct(top, at.x)
    pair_yl = pair_direct(low, at.y)
    pair_xl = pair_direct(low, at.x)
    pair_yt = pair_direct(top, at.y)

    def qkv_direct(part, device):
        copies = []
        for array, width, column in ((wq, nq, 0), (wk, nk, nq), (wv, nv, nq + nk)):
            copies.append(
                remote(
                    array.at[part, rows_at(g * width, width)],
                    qkv_o.at[rows_at(own_rows + part.start, mid), column : column + width],
                    device,
                )
            )
        return start(copies)

    qkv_xt = qkv_direct(top, at.x)
    qkv_yl = qkv_direct(low, at.y)
    qkv_xl = qkv_direct(low, at.x)
    qkv_yt = qkv_direct(top, at.y)

    own = rows_at(own_rows, feat)
    locals_ = [
        Bounce(
            array.at[:, rows_at(g * width, width)],
            qkv_v.at[:, column : column + width],
            qkv_o.at[own, column : column + width],
        )
        for array, width, column in ((wq, nq, 0), (wk, nk, nq), (wv, nv, nq + nk))
    ]
    locals_.append(Bounce(wo, out_v, out_o.at[own]))
    locals_.append(Bounce(down.at[rows_at(g * nf, nf)], down_v, down_o.at[rows_at(f * nf, nf)]))
    for array, index in ((gate, 0), (up, 1)):
        for k in range(count):
            locals_.append(
                Bounce(
                    array.at[:, rows_at((2 * k + g) * nf, nf)],
                    pair_v.at[index, :, rows_at(k * nf, nf)],
                    pair_o.at[index, own, rows_at(k * nf, nf)],
                )
            )
    gain_place = gain_o.at[pl.ds(f, 1)]
    locals_.append(Bounce(gain, gain_v, gain_place))
    start(locals_)
    for copy in locals_:
        copy.turn()
    gains = start([remote(gain, gain_place, to) for to in (at.x, at.y, at.diag)])

    def forward(array_at, rows_x, rows_y):
        return remote(array_at(rows_x), array_at(rows_x), at.y), remote(
            array_at(rows_y), array_at(rows_y), at.x
        )

    x_top, y_low = rows_at(at.fx * feat, mid), rows_at(at.fy * feat + mid, mid)
    x_low, y_top = rows_at(at.fx * feat + mid, mid), rows_at(at.fy * feat, mid)
    d_top, d_low = rows_at(at.fd * feat, mid), rows_at(at.fd * feat + mid, mid)

    def pair_view(rows):
        return pair_o.at[parity, rows]

    def out_view(rows):
        return out_o.at[rows, rows_at(g * wide, wide)]

    pair_fy, pair_fx = forward(pair_view, x_top, y_low)
    sends = [pair_fy, pair_fx]

    def across(rows):
        copy = remote(pair_view(rows), pair_view(rows), at.across)
        copy.start()
        sends.append(copy)
        return copy

    arrive(pair_xt)
    pair_fy.start()
    z_copies = [across(x_top)]
    arrive(pair_yl)
    pair_fx.start()
    z_copies.append(across(y_low))

    def out_direct(part, device):
        copy = remote(
            wo.at[part, rows_at(g * wide, wide)],
            out_o.at[rows_at(own_rows + part.start, mid), rows_at(g * wide, wide)],
            device,
        )
        copy.start()
        return copy

    out_xt, out_yl = out_direct(top, at.x), out_direct(low, at.y)
    out_xl, out_yt = out_direct(low, at.x), out_direct(top, at.y)

    arrive(pair_xl)
    z_copies.append(across(x_low))
    arrive(pair_yt)
    z_copies.append(across(y_top))

    def qkv_view(rows):
        return qkv_o.at[rows]

    qkv_fy, qkv_fx = forward(qkv_view, x_top, y_low)
    arrive(qkv_xt)
    qkv_fy.start()
    arrive(qkv_yl)
    qkv_fx.start()

    dmid = nf // 2

    def down_direct(lower, device):
        copy = remote(
            down.at[rows_at(g * nf + lower, dmid)], down_o.at[rows_at(f * nf + lower, dmid)], device
        )
        copy.start()
        return copy

    down_xt, down_yl = down_direct(0, at.x), down_direct(dmid, at.y)
    down_xl, down_yt = down_direct(dmid, at.x), down_direct(0, at.y)

    pair_fy.wait_recv()
    z_copies.append(across(d_top))
    pair_fx.wait_recv()
    z_copies.append(across(d_low))

    for i in range(2):

        @pl.when(g != parity)
        def _():
            swaps[i].wait_recv()
            swaps_out[i].wait_send()

        @pl.when(g == parity)
        def _():
            keeps[i].wait()

        shares[i].start()

    out_fy, out_fx = forward(out_view, x_top, y_low)
    out_xt.wait_recv()
    out_fy.start()
    out_yl.wait_recv()
    out_fx.start()
    out_xl.wait_recv()
    out_yt.wait_recv()

    def share(rows):
        copy = remote(out_view(rows), out_view(rows), at.core)
        copy.start()
        return copy

    shared = [share(x_top), share(x_low), share(y_top), share(y_low)]

    def down_view(rows):
        return down_o.at[rows]

    down_fy, down_fx = forward(
        down_view, rows_at(at.fx * nf, dmid), rows_at(at.fy * nf + dmid, dmid)
    )
    down_xt.wait_recv()
    down_fy.start()
    down_yl.wait_recv()
    down_fx.start()

    out_fy.wait_recv()
    shared.append(share(d_top))
    out_fx.wait_recv()
    shared.append(share(d_low))

    arrive(qkv_xl)
    arrive(qkv_yt)
    arrive([qkv_fy, qkv_fx, down_xl, down_yt, down_fy, down_fx])
    arrive(gains)
    arrive(shares)
    arrive(shared)
    arrive(z_copies)
    for copy in locals_:
        copy.wait()
    for copy in (
        pair_xt + pair_yl + pair_xl + pair_yt + qkv_xt + qkv_yl + qkv_xl + qkv_yt + gains
        + sends + shares + shared
        + [out_xt, out_yl, out_xl, out_yt, out_fy, out_fx, qkv_fy, qkv_fx]
        + [down_xt, down_yl, down_xl, down_yt, down_fy, down_fx]
    ):
        copy.wait_send()


def gather_all(tokens, cotangent, wq, wk, wv, wo, gate, up, down, gain):
    tok, width = tokens.shape[1:]
    nf = down.shape[0] // 2
    cols = (wq.shape[1] + wk.shape[1] + wv.shape[1]) // 2
    return pl.pallas_call(
        gather_kernel,
        in_specs=[ANY] * 10,
        out_specs=[ANY] * 7,
        out_shape=[
            bf16_like(width, cols),
            bf16_like(4 * wo.shape[0], width),
            bf16_like(2, width, 4 * nf),
            bf16_like(4 * nf, width),
            bf16_like(2 * tok, width),
            bf16_like(2 * tok, width),
            jax.ShapeDtypeStruct((4,) + gain.shape[1:], gain.dtype),
        ],
        scratch_shapes=[
            pltpu.SemaphoreType.DMA((64,)),
            pltpu.SemaphoreType.DMA((64,)),
            pltpu.SemaphoreType.DMA((20,)),
            pltpu.SemaphoreType.DMA((20,)),
            pltpu.VMEM((width // 4, cols), jnp.bfloat16),
            pltpu.VMEM(wo.shape, jnp.bfloat16),
            pltpu.VMEM((2, width // 4, 4 * nf), jnp.bfloat16),
            pltpu.VMEM((nf, width), jnp.bfloat16),
            pltpu.VMEM((2, tok, width), jnp.bfloat16),
            pltpu.VMEM(gain.shape, gain.dtype),
        ],
        compiler_params=pltpu.CompilerParams(
            collective_id=0, has_side_effects=True, vmem_limit_bytes=VMEM_LIMIT
        ),
        cost_estimate=cost(0, 500e6),
        name="gather",
    )(tokens, cotangent, wq, wk, wv, wo, gate, up, down, gain)


def norm_scale(field):
    return lax.rsqrt(jnp.mean(field * field, axis=-1, keepdims=True) + EPS)


def project_kernel(x_ref, gain, w_ref, xn_ref, out_ref):
    seq = x_ref.shape[0]

    @pl.when(pl.program_id(0) == 0)
    def _():
        for part in range(seq // TILE):
            rows = slice(part * TILE, (part + 1) * TILE)
            field = fp32(x_ref[rows, :])
            xn_ref[rows, :] = (field * norm_scale(field) * gain[0:1, :]).astype(jnp.bfloat16)

    out_ref[...] = mm(w_ref[...].T, xn_ref[...], ((1,), (1,)))


def project(x_seq, gains, weight):
    seq, width = x_seq.shape
    cols = weight.shape[1]
    return pl.pallas_call(
        project_kernel,
        grid=(cols // TILE,),
        in_specs=[VM, VM, pl.BlockSpec((width, TILE), lambda n: (0, n))],
        out_specs=[VM, pl.BlockSpec((TILE, seq), lambda n: (n, 0))],
        out_shape=[bf16_like(seq, width), f32_like(cols, seq)],
        compiler_params=PARAMS,
        cost_estimate=cost(2 * seq * width * cols, 20e6),
        name="project",
    )(x_seq, gains, weight)


def residual_kernel(place, x_ref, attn_keep, attn_got, gain, w_ref, h_ref, xn_ref):
    core = place[0]
    heads = attn_keep.shape[0]
    keep_at, got_at = rows_at(core * heads, heads), rows_at((1 - core) * heads, heads)
    tok = h_ref.shape[0]
    field = mm(attn_keep[...].T, w_ref[keep_at, :])
    field = field + mm(attn_got[...].T, w_ref[got_at, :])
    h_ref[...] = field + fp32(x_ref[rows_at(core * tok, tok), :])
    for part in range(tok // TILE):
        rows = slice(part * TILE, (part + 1) * TILE)
        field = h_ref[rows, :]
        xn_ref[rows, :] = (field * norm_scale(field) * gain[1:2, :]).astype(jnp.bfloat16)


def residual(place, x_seq, attn_keep, attn_got, gains, weight):
    seq, width = x_seq.shape
    tok = seq // 2
    return pl.pallas_call(
        residual_kernel,
        in_specs=[SMEM] + [VM] * 5,
        out_specs=[VM, VM],
        out_shape=[f32_like(tok, width), bf16_like(tok, width)],
        compiler_params=PARAMS,
        cost_estimate=cost(2 * tok * width * weight.shape[0], 14e6),
        name="residual",
    )(place, x_seq, attn_keep, attn_got, gains, weight)


def hidden_kernel(xn_ref, dy_ref, gate_w, up_w, down_w, hid_ref, dgate_ref, dup_ref):
    gate = mm(xn_ref[...], gate_w[0])
    up = mm(xn_ref[...], up_w[0])
    d_hidden = mm(dy_ref[...], down_w[...], ((1,), (1,)))
    sig = 1.0 / (1.0 + jnp.exp(-gate))
    act = gate * sig
    hid_ref[...] = (act * up).astype(jnp.bfloat16)
    dgate_ref[...] = (d_hidden * up * (sig + act * (1.0 - sig))).astype(jnp.bfloat16)
    dup_ref[...] = (d_hidden * act).astype(jnp.bfloat16)


def hidden_step(xn, dy, pair, down):
    seq, width = xn.shape
    ff = down.shape[0]
    block = pl.BlockSpec((seq, TILE), lambda n: (0, n))
    return pl.pallas_call(
        hidden_kernel,
        grid=(ff // TILE,),
        in_specs=[
            VM,
            VM,
            pl.BlockSpec((1, width, TILE), lambda n: (0, 0, n)),
            pl.BlockSpec((1, width, TILE), lambda n: (1, 0, n)),
            pl.BlockSpec((TILE, width), lambda n: (n, 0)),
        ],
        out_specs=[block] * 3,
        out_shape=[bf16_like(seq, ff)] * 3,
        compiler_params=PARAMS,
        cost_estimate=cost(6 * seq * width * ff, 38e6),
        name="hidden",
    )(xn, dy, pair, pair, down)


def back_kernel(place, dgate_ref, dup_ref, gate_w, up_w, own_ref, send_ref):
    field = mm(dgate_ref[...], gate_w[0], ((1,), (1,)))
    field = field + mm(dup_ref[...], up_w[0], ((1,), (1,)))
    tok = own_ref.shape[0]

    @pl.when(place[0] == 0)
    def _():
        own_ref[...] = field[:tok]
        send_ref[...] = field[tok:].astype(jnp.bfloat16)

    @pl.when(place[0] == 1)
    def _():
        own_ref[...] = field[tok:]
        send_ref[...] = field[:tok].astype(jnp.bfloat16)


def back_step(place, d_gate, d_up, pair):
    seq, ff = d_gate.shape
    width = pair.shape[1]
    out = pl.BlockSpec((seq // 2, TILE), lambda n: (0, n))
    return pl.pallas_call(
        back_kernel,
        grid=(width // TILE,),
        in_specs=[
            SMEM,
            VM,
            VM,
            pl.BlockSpec((1, TILE, ff), lambda n: (0, n, 0)),
            pl.BlockSpec((1, TILE, ff), lambda n: (1, n, 0)),
        ],
        out_specs=[out, out],
        out_shape=[f32_like(seq // 2, width), bf16_like(seq // 2, width)],
        compiler_params=PARAMS,
        cost_estimate=cost(4 * seq * width * ff, 26e6),
        name="back",
    )(place, d_gate, d_up, pair, pair)


def result_kernel(place, hid_ref, h_ref, down_w, own_ref, send_ref):
    field = mm(hid_ref[...], down_w[...])
    tok = own_ref.shape[0]

    @pl.when(place[0] == 0)
    def _():
        own_ref[...] = field[:tok] + h_ref[...]
        send_ref[...] = field[tok:].astype(jnp.bfloat16)

    @pl.when(place[0] == 1)
    def _():
        own_ref[...] = field[tok:] + h_ref[...]
        send_ref[...] = field[:tok].astype(jnp.bfloat16)


def result_step(place, hidden, h_own, down):
    tok, width = h_own.shape
    ff = hidden.shape[1]
    out = pl.BlockSpec((tok, TILE), lambda n: (0, n))
    return pl.pallas_call(
        result_kernel,
        grid=(width // TILE,),
        in_specs=[SMEM, VM, out, pl.BlockSpec((ff, TILE), lambda n: (0, n))],
        out_specs=[out, out],
        out_shape=[f32_like(tok, width), bf16_like(tok, width)],
        compiler_params=PARAMS,
        cost_estimate=cost(4 * tok * width * ff, 20e6),
        name="result",
    )(place, hidden, h_own, down)


def entry_kernel(place, dn_own, dn_got, h_ref, dy_ref, gain, w_ref, dh_ref, da_ref, keep_ref, send_ref, part_ref):
    core = place[0]
    tok = dh_ref.shape[0]
    part_ref[...] = jnp.zeros_like(part_ref)
    for part in range(tok // TILE):
        rows = slice(part * TILE, (part + 1) * TILE)
        field = h_ref[rows, :]
        scale = norm_scale(field)
        hat = field * scale
        grad = dn_own[rows, :] + fp32(dn_got[rows, :])
        part_ref[...] += jnp.sum(grad * hat, axis=0, keepdims=True)
        dy = fp32(dy_ref[rows_at(core * tok + part * TILE, TILE), :])
        total = dy + rms_back(grad * gain[1:2, :], hat, scale)
        dh_ref[rows, :] = total
        da_ref[rows, :] = total.astype(jnp.bfloat16)
    heads = keep_ref.shape[0]
    for ref, at in ((send_ref, 1 - core), (keep_ref, core)):
        ref[...] = mm(w_ref[rows_at(at * heads, heads), :], da_ref[...], ((1,), (1,))).astype(jnp.bfloat16)


def entry_step(place, dn_own, dn_got, h_own, dy_all, gains, weight):
    tok, width = h_own.shape
    rows = weight.shape[0]
    return pl.pallas_call(
        entry_kernel,
        in_specs=[SMEM] + [VM] * 6,
        out_specs=[VM] * 5,
        out_shape=[
            f32_like(tok, width),
            bf16_like(tok, width),
            bf16_like(rows // 2, tok),
            bf16_like(rows // 2, tok),
            f32_like(1, width),
        ],
        compiler_params=PARAMS,
        cost_estimate=cost(2 * tok * width * rows, 20e6),
        name="entry",
    )(place, dn_own, dn_got, h_own, dy_all, gains, weight)


def inputs_kernel(place, dq_ref, dk_ref, dv_ref, w_ref, own_ref, send_ref, d_ref):
    @pl.when(pl.program_id(0) == 0)
    def _():
        nq, nk = dq_ref.shape[0], dk_ref.shape[0]
        d_ref[:, :nq] = dq_ref[...].T
        d_ref[:, nq : nq + nk] = dk_ref[...].T
        d_ref[:, nq + nk :] = dv_ref[...].T

    field = mm(d_ref[...], w_ref[...], ((1,), (1,)))
    tok = own_ref.shape[0]

    @pl.when(place[0] == 0)
    def _():
        own_ref[...] = field[:tok]
        send_ref[...] = field[tok:].astype(jnp.bfloat16)

    @pl.when(place[0] == 1)
    def _():
        own_ref[...] = field[tok:]
        send_ref[...] = field[:tok].astype(jnp.bfloat16)


def inputs_step(place, dq_t, dk_t, dv_t, weight):
    width, cols = weight.shape
    tok = dq_t.shape[1] // 2
    out = pl.BlockSpec((tok, TILE), lambda n: (0, n))
    return pl.pallas_call(
        inputs_kernel,
        grid=(width // TILE,),
        in_specs=[SMEM] + [VM] * 3 + [pl.BlockSpec((TILE, cols), lambda n: (n, 0))],
        out_specs=[out, out, VM],
        out_shape=[f32_like(tok, width), bf16_like(tok, width), bf16_like(2 * tok, cols)],
        compiler_params=PARAMS,
        cost_estimate=cost(4 * tok * width * cols, 14e6),
        name="inputs",
    )(place, dq_t, dk_t, dv_t, weight)


def last_kernel(place, d1_own, d1_got, x_ref, dh_ref, gain, dx_ref, part_ref):
    part_ref[...] = jnp.zeros_like(part_ref)
    tok = dx_ref.shape[0]
    for part in range(tok // TILE):
        rows = slice(part * TILE, (part + 1) * TILE)
        field = fp32(x_ref[rows_at(place[0] * tok + part * TILE, TILE), :])
        scale = norm_scale(field)
        hat = field * scale
        grad = d1_own[rows, :] + fp32(d1_got[rows, :])
        part_ref[...] += jnp.sum(grad * hat, axis=0, keepdims=True)
        dx_ref[rows, :] = (dh_ref[rows, :] + rms_back(grad * gain[0:1, :], hat, scale)).astype(jnp.bfloat16)


def last_step(place, d1_own, d1_got, x_seq, dh_own, gains):
    tok, width = dh_own.shape
    return pl.pallas_call(
        last_kernel,
        in_specs=[SMEM] + [VM] * 5,
        out_specs=[VM] * 2,
        out_shape=[bf16_like(tok, width), f32_like(1, width)],
        compiler_params=PARAMS,
        cost_estimate=cost(0, 14e6),
        name="last",
    )(place, d1_own, d1_got, x_seq, dh_own, gains)


def chip_local(
    tokens,
    seq_lengths,
    dealing,
    first_gain,
    query_weight,
    key_matrix,
    value_matrix,
    out_weight,
    second_gain,
    gate_weight,
    up_weight,
    down_weight,
    cotangent,
):
    ctx = lax.axis_size("ctx")
    z = lax.axis_index("ctx")
    f = lax.axis_index("fsdp")
    g = lax.axis_index("grp")
    parity = z % 2
    parity_core = g == parity
    width = tokens.shape[2]
    tok = tokens.shape[1]
    seq = 2 * tok
    place = jnp.stack([g, parity]).astype(jnp.int32)

    def over_x(field):
        return lax.ppermute(field, "fsdp", [(i, i ^ 1) for i in range(4)])

    def over_y(field):
        return lax.ppermute(field, "fsdp", [(i, i ^ 2) for i in range(4)])

    def over_core(field):
        return lax.ppermute(field, "grp", [(0, 1), (1, 0)])

    swap_pairs = [(2 * i + (1 - i % 2), 2 * (i ^ 1) + i % 2) for i in range(ctx)]

    def swap(field):
        got = lax.ppermute(field, ("ctx", "grp"), swap_pairs)
        return jnp.where(parity_core, field, got)

    def along(field, pairs):
        return lax.ppermute(field, "ctx", pairs)

    def cut(field, start, size, axis):
        return lax.dynamic_slice_in_dim(field, start, size, axis)

    def in_order(mine, other, axis=0):
        first = jnp.where(g == 0, mine, other)
        second = jnp.where(g == 0, other, mine)
        return jnp.concatenate([first, second], axis=axis)

    heads_q = query_weight.shape[1] // 2
    heads_k = key_matrix.shape[1] // 2
    part_ff = down_weight.shape[0] // 2
    rows_in = gate_weight.shape[0]

    gain_own = jnp.pad(fp32(jnp.stack([first_gain, second_gain])), ((0, 6), (0, 0)))[None]
    qkv_w, out_w, pair_w, down_w, x_seq, dy_all, gain_all = gather_all(
        tokens, cotangent, query_weight, key_matrix, value_matrix, out_weight,
        gate_weight, up_weight, down_weight, gain_own,
    )
    gains = jnp.transpose(gain_all[:, :2], (1, 0, 2)).reshape(2, width)

    positions = jnp.arange(seq, dtype=jnp.int32)
    cosine, sine = rotation(positions, HEAD_SIZE // 2)
    cosine, sine = cosine.T, sine.T

    xn_one, qkv_t = project(x_seq, gains, qkv_w)
    attn_t, lse, q_t, k_t, v_t = attend_seq(qkv_t, cosine, sine)
    attn_keep = cut(attn_t, g * tok, tok, 1)
    attn_send = cut(attn_t, (1 - g) * tok, tok, 1)
    attn_got = over_core(attn_send)
    h_own, xn_own = residual(place, x_seq, attn_keep, attn_got, gains, out_w)
    xn_two = in_order(xn_own, over_core(xn_own))
    hidden, d_gate, d_up = hidden_step(xn_two, dy_all, pair_w, down_w)
    bf = jnp.bfloat16
    tokens_in = ((0,), (0,))
    down_grad = mm(hidden, dy_all, tokens_in, bf)
    gate_grad = mm(xn_two, d_gate, tokens_in, bf)
    up_grad = mm(xn_two, d_up, tokens_in, bf)
    dn_own, dn_send = back_step(place, d_gate, d_up, pair_w)
    dn_got = over_core(dn_send)
    res_own, res_send = result_step(place, hidden, h_own, down_w)
    layer_out = swap((res_own + fp32(over_core(res_send))).astype(bf))

    dh_own, da, dattn_keep, dattn_send, gain_two_part = entry_step(
        place, dn_own, dn_got, h_own, dy_all, gains, out_w
    )
    dattn_all = in_order(dattn_keep, over_core(dattn_send), axis=1)
    attn_mine = in_order(attn_keep, attn_got)
    dq_t, dk_t, dv_t = attend_seq_back(q_t, k_t, v_t, dattn_all, lse, cosine, sine)
    half_width = width // 2
    out_part = mm(attn_mine, da, ((1,), (0,)), bf)
    d1_own, d1_send, d_qkv = inputs_step(place, dq_t, dk_t, dv_t, qkv_w)
    qkv_grad = mm(xn_one, d_qkv, tokens_in, bf)
    dx, gain_one_part = last_step(place, d1_own, over_core(d1_send), x_seq, dh_own, gains)
    tokens_grad = swap(dx)

    def add(left, right):
        return (fp32(left) + fp32(right)).astype(bf)

    out_grad = add(
        cut(out_part, g * half_width, half_width, 1),
        over_core(cut(out_part, (1 - g) * half_width, half_width, 1)),
    )

    def scatter(grad):
        rows = grad.shape[0] // 4
        mid = rows // 2

        def block(j, low):
            return cut(grad, (f ^ j) * rows + low, mid, 0)

        got = over_x(jnp.concatenate([block(1, 0), block(3, 0)], axis=0))
        top = add(block(0, 0), got[:mid])
        top = add(top, over_y(add(block(2, 0), got[mid:])))
        got = over_y(jnp.concatenate([block(2, mid), block(3, mid)], axis=0))
        low = add(block(0, mid), got[:mid])
        low = add(low, over_x(add(block(1, mid), got[mid:])))
        both = jnp.concatenate([top, low], axis=0)
        both = add(both, along(both, [(0, 1), (3, 2)]))
        first, second = both[:mid], both[mid:]
        left = z == 1
        middle = [(1, 2), (2, 1)]
        got = along(jnp.where(left, second, first), middle)
        done = add(jnp.where(left, first, second), got)
        other = along(done, middle)
        total = jnp.concatenate(
            [jnp.where(left, done, other), jnp.where(left, other, done)], axis=0
        )
        got = along(total, [(1, 0), (2, 3)])
        return jnp.where((z == 1) | (z == 2), total, got)

    def widen(half, axis=1):
        return fp32(in_order(half, over_core(half), axis=axis))

    down_out = widen(scatter(down_grad), 0)

    def ff_out(grad):
        half = scatter(grad).reshape(rows_in, 4, 1, part_ff)
        return widen(half, 2).reshape(rows_in, 8 * part_ff)

    gate_out, up_out = ff_out(gate_grad), ff_out(up_grad)
    out_out = widen(scatter(out_grad))
    qkv_half = scatter(qkv_grad)
    query_out = widen(qkv_half[:, :heads_q])
    key_out = widen(qkv_half[:, heads_q : heads_q + heads_k])
    value_out = widen(qkv_half[:, heads_q + heads_k :])

    sums = jnp.concatenate([gain_one_part, gain_two_part])
    sums = sums + over_core(sums)
    sums = sums + over_x(sums)
    sums = sums + over_y(sums)
    sums = sums + along(sums, [(i, i ^ 1) for i in range(ctx)])
    sums = sums + along(sums, [(i, i ^ 2) for i in range(ctx)])
    sums = cut(sums, f * (width // 4), width // 4, 1)

    all_lse = lax.all_gather(lse.reshape(1, -1, seq), ("ctx", "grp"), axis=0, tiled=True)
    all_lse = all_lse.reshape(ctx // 2, 2, QUERY_HEADS, seq)
    pack_lse = lax.dynamic_index_in_dim(all_lse, g, 1, False)
    pack_lse = jnp.transpose(pack_lse, (1, 0, 2)).reshape(QUERY_HEADS, ctx, tok // BLK, BLK)
    mine = (dealing[0] == z).astype(jnp.float32)
    totals = jnp.sum(pack_lse * mine[None, :, :, None], axis=2).reshape(1, QUERY_HEADS, tok)

    return (
        layer_out[None],
        tokens_grad[None],
        totals,
        sums[0],
        query_out,
        key_out,
        value_out,
        out_out,
        sums[1],
        gate_out,
        up_out,
        down_out,
    )


def chip_holds_sequence(mesh, tokens, seq_lengths):
    sizes = dict(mesh.shape)
    packs, length, _ = tokens.shape
    count = seq_lengths.shape[1]
    return (
        sizes["fsdp"] == 4
        and sizes["grp"] == 2
        and sizes["ctx"] == 4
        and packs == sizes["fsdp"] * sizes["grp"]
        and length == count * MINLEN
        and 2 * length == sizes["ctx"] * MINLEN
    )


def solution(mesh):
    placed = (
        P(("fsdp", "grp"), "ctx", None),
        P(("fsdp", "grp"), None),
        P(("fsdp", "grp"), None, None),
        P("fsdp"),
        P("fsdp", None),
        P("fsdp", None),
        P("fsdp", None),
        P("fsdp", None),
        P("fsdp"),
        P("fsdp", None),
        P("fsdp", None),
        P("fsdp", None),
        P(("fsdp", "grp"), "ctx", None),
    )
    results = (
        P(("fsdp", "grp"), "ctx", None),
        P(("fsdp", "grp"), "ctx", None),
        P(("fsdp", "grp"), None, "ctx"),
        P("fsdp"),
        P("fsdp", None),
        P("fsdp", None),
        P("fsdp", None),
        P("fsdp", None),
        P("fsdp"),
        P("fsdp", None),
        P("fsdp", None),
        P("fsdp", None),
    )

    def program(*arrays):
        body = chip_local if chip_holds_sequence(mesh, arrays[0], arrays[1]) else local
        return jax.shard_map(
            body, mesh=mesh, in_specs=placed, out_specs=results, check_vma=False
        )(*arrays)

    return program
```

```python
import jax
import jax.numpy as jnp
from jax import lax
from jax.experimental import pallas as pl
from jax.experimental.pallas import tpu as pltpu
from jax.sharding import PartitionSpec as P

QUERY_HEADS = 16
KEY_VALUE_HEADS = 8
HEAD_SIZE = 96
BLK = 128


EPS = 1e-05
ROPE_BASE = 100000.0
MASKED = -1e30


def place_rows(positions, lengths):
    ends = jnp.cumsum(lengths, axis=-1)
    before = positions[..., :, None] >= ends[..., None, :]
    segment = jnp.sum(before.astype(jnp.int32), axis=-1)
    offset = jnp.sum(jnp.where(before, lengths[..., None, :], 0), axis=-1)
    return (segment, positions - offset)


def rotation(relative, half_size):
    frequency = ROPE_BASE ** (-(2.0 * jnp.arange(half_size, dtype=jnp.float32)) / (2 * half_size))
    angles = relative.astype(jnp.float32)[:, None] * frequency[None, :]
    return (jnp.cos(angles), jnp.sin(angles))


def rotate(field, cosine, sine_part):
    row_count = field.shape[0]
    half_size = cosine.shape[-1]
    split_heads = field.reshape(row_count, -1, 2 * half_size)
    front_half = split_heads[..., :half_size]
    back_half = split_heads[..., half_size:]
    cos_rows = cosine[:, None, :]
    sin_rows = sine_part[:, None, :]
    turned = jnp.concatenate(
        [
            front_half * cos_rows - back_half * sin_rows,
            back_half * cos_rows + front_half * sin_rows,
        ],
        axis=-1,
    )
    return turned.reshape(row_count, -1)


def rms_back(d_normed, normed, scale):
    return scale * (d_normed - normed * jnp.mean(d_normed * normed, axis=-1, keepdims=True))


def score_block(query_part, key_part, visible):
    scores = jnp.einsum(
        "rgd,kd->grk", query_part, key_part, preferred_element_type=jnp.float32
    ) * HEAD_SIZE ** (-0.5)
    return jnp.where(visible[None], scores, MASKED)


def attend_pack(query_pack, key_pack, value_pack, visible_list):
    token_count = query_pack.shape[0]
    rounds = len(visible_list)
    query_group_width = QUERY_HEADS // KEY_VALUE_HEADS
    context_count = key_pack.shape[0] // token_count

    def width_per_head(head_index, carry):
        out_buf, total_buf = carry
        query_head = lax.dynamic_slice_in_dim(
            query_pack, head_index * query_group_width * HEAD_SIZE, query_group_width * HEAD_SIZE, 1
        ).reshape(token_count, query_group_width, HEAD_SIZE)
        key_head = lax.dynamic_slice_in_dim(key_pack, head_index * HEAD_SIZE, HEAD_SIZE, 1).reshape(
            context_count, rounds, BLK, HEAD_SIZE
        )
        value_head = lax.dynamic_slice_in_dim(
            value_pack, head_index * HEAD_SIZE, HEAD_SIZE, 1
        ).reshape(context_count, rounds, BLK, HEAD_SIZE)
        running_top = jnp.full((query_group_width, token_count), MASKED, jnp.float32)
        running_sum = jnp.zeros((query_group_width, token_count), jnp.float32)
        for round_index in range(rounds):
            first_row = round_index * BLK
            scores = score_block(
                query_head[first_row:],
                key_head[:, round_index].reshape(-1, HEAD_SIZE),
                visible_list[round_index],
            )
            new_top = jnp.maximum(running_top[:, first_row:], jnp.max(scores, axis=-1))
            weights = jnp.where(
                visible_list[round_index][None], jnp.exp(scores - new_top[..., None]), 0.0
            )
            new_sum = running_sum[:, first_row:] * jnp.exp(
                running_top[:, first_row:] - new_top
            ) + jnp.sum(weights, axis=-1)
            running_top = running_top.at[:, first_row:].set(new_top)
            running_sum = running_sum.at[:, first_row:].set(new_sum)
        log_totals = running_top + jnp.log(running_sum)
        mixture = jnp.zeros((token_count, query_group_width, HEAD_SIZE), jnp.float32)
        for round_index in range(rounds):
            first_row = round_index * BLK
            scores = score_block(
                query_head[first_row:],
                key_head[:, round_index].reshape(-1, HEAD_SIZE),
                visible_list[round_index],
            )
            prob_bf = jnp.where(
                visible_list[round_index][None],
                jnp.exp(scores - log_totals[:, first_row:, None]),
                0.0,
            ).astype(jnp.bfloat16)
            mixture = mixture.at[first_row:].add(
                jnp.einsum(
                    "grk,kd->rgd",
                    prob_bf,
                    value_head[:, round_index].reshape(-1, HEAD_SIZE),
                    preferred_element_type=jnp.float32,
                )
            )
        out_buf = lax.dynamic_update_slice_in_dim(
            out_buf,
            mixture.astype(jnp.bfloat16).reshape(token_count, -1),
            head_index * query_group_width * HEAD_SIZE,
            1,
        )
        total_buf = lax.dynamic_update_slice_in_dim(
            total_buf, log_totals, head_index * query_group_width, 0
        )
        return (out_buf, total_buf)

    start_offsets = (
        jnp.zeros((token_count, QUERY_HEADS * HEAD_SIZE), jnp.bfloat16),
        jnp.zeros((QUERY_HEADS, token_count), jnp.float32),
    )
    return lax.fori_loop(0, KEY_VALUE_HEADS, width_per_head, start_offsets)


def attend_back(
    query_pack, key_pack, value_pack, grad_pack, attended_pack, total_pack, visible_list
):
    token_count = query_pack.shape[0]
    rounds = len(visible_list)
    query_group_width = QUERY_HEADS // KEY_VALUE_HEADS
    context_count = key_pack.shape[0] // token_count

    def width_per_head(head_index, carry):
        query_buf, key_buf, value_buf = carry
        query_head = lax.dynamic_slice_in_dim(
            query_pack, head_index * query_group_width * HEAD_SIZE, query_group_width * HEAD_SIZE, 1
        ).reshape(token_count, query_group_width, HEAD_SIZE)
        grad_head = lax.dynamic_slice_in_dim(
            grad_pack, head_index * query_group_width * HEAD_SIZE, query_group_width * HEAD_SIZE, 1
        ).reshape(token_count, query_group_width, HEAD_SIZE)
        output_head = lax.dynamic_slice_in_dim(
            attended_pack,
            head_index * query_group_width * HEAD_SIZE,
            query_group_width * HEAD_SIZE,
            1,
        ).reshape(token_count, query_group_width, HEAD_SIZE)
        key_head = lax.dynamic_slice_in_dim(key_pack, head_index * HEAD_SIZE, HEAD_SIZE, 1).reshape(
            context_count, rounds, BLK, HEAD_SIZE
        )
        value_head = lax.dynamic_slice_in_dim(
            value_pack, head_index * HEAD_SIZE, HEAD_SIZE, 1
        ).reshape(context_count, rounds, BLK, HEAD_SIZE)
        log_totals = lax.dynamic_slice_in_dim(
            total_pack, head_index * query_group_width, query_group_width, 0
        )
        delta = jnp.sum(grad_head.astype(jnp.float32) * output_head.astype(jnp.float32), axis=-1).T
        query_grad = jnp.zeros((token_count, query_group_width, HEAD_SIZE), jnp.float32)
        key_parts = []
        value_parts = []
        for round_index in range(rounds):
            first_row = round_index * BLK
            key_round = key_head[:, round_index].reshape(-1, HEAD_SIZE)
            value_round = value_head[:, round_index].reshape(-1, HEAD_SIZE)
            scores = score_block(query_head[first_row:], key_round, visible_list[round_index])
            probs_full = jnp.where(
                visible_list[round_index][None],
                jnp.exp(scores - log_totals[:, first_row:, None]),
                0.0,
            )
            d_probs = jnp.einsum(
                "rgd,kd->grk",
                grad_head[first_row:],
                value_round,
                preferred_element_type=jnp.float32,
            )
            d_scores = (
                HEAD_SIZE ** (-0.5) * probs_full * (d_probs - delta[:, first_row:, None])
            ).astype(jnp.bfloat16)
            value_parts.append(
                jnp.einsum(
                    "grk,rgd->kd",
                    probs_full.astype(jnp.bfloat16),
                    grad_head[first_row:],
                    preferred_element_type=jnp.float32,
                )
            )
            key_parts.append(
                jnp.einsum(
                    "grk,rgd->kd",
                    d_scores,
                    query_head[first_row:],
                    preferred_element_type=jnp.float32,
                )
            )
            query_grad = query_grad.at[first_row:].add(
                jnp.einsum("grk,kd->rgd", d_scores, key_round, preferred_element_type=jnp.float32)
            )
        key_block = jnp.stack(
            [part.reshape(context_count, BLK, HEAD_SIZE) for part in key_parts], axis=1
        ).reshape(-1, HEAD_SIZE)
        value_block = jnp.stack(
            [part.reshape(context_count, BLK, HEAD_SIZE) for part in value_parts], axis=1
        ).reshape(-1, HEAD_SIZE)
        query_buf = lax.dynamic_update_slice_in_dim(
            query_buf,
            query_grad.reshape(token_count, -1),
            head_index * query_group_width * HEAD_SIZE,
            1,
        )
        key_buf = lax.dynamic_update_slice_in_dim(key_buf, key_block, head_index * HEAD_SIZE, 1)
        value_buf = lax.dynamic_update_slice_in_dim(
            value_buf, value_block, head_index * HEAD_SIZE, 1
        )
        return (query_buf, key_buf, value_buf)

    start_offsets = (
        jnp.zeros((token_count, QUERY_HEADS * HEAD_SIZE), jnp.float32),
        jnp.zeros((context_count * token_count, KEY_VALUE_HEADS * HEAD_SIZE), jnp.float32),
        jnp.zeros((context_count * token_count, KEY_VALUE_HEADS * HEAD_SIZE), jnp.float32),
    )
    return lax.fori_loop(0, KEY_VALUE_HEADS, width_per_head, start_offsets)


def local(
    tokens,
    seq_lengths,
    dealing,
    first_gain,
    query_weight,
    key_matrix,
    value_matrix,
    out_weight,
    second_gain,
    gate_weight,
    up_weight,
    down_weight,
    cotangent,
):
    context_count = lax.axis_size("ctx")
    my_index = lax.axis_index("ctx")
    pack_count, token_count, model_dim = tokens.shape
    rounds = token_count // BLK
    spread = context_count // rounds
    ctx_range = jnp.arange(context_count, dtype=jnp.int32)
    matches = (dealing[..., None] == ctx_range).astype(jnp.int32)
    slot_of = jnp.sum(matches * ctx_range[:, None], axis=2)
    block_of = jnp.arange(rounds, dtype=jnp.int32)[None, :, None] * context_count + slot_of
    key_pos = (
        jnp.transpose(block_of, (0, 2, 1))[..., None] * BLK + jnp.arange(BLK, dtype=jnp.int32)
    ).reshape(pack_count, -1)
    key_seg = place_rows(key_pos, seq_lengths)[0]
    query_pos = lax.dynamic_slice_in_dim(key_pos, my_index * token_count, token_count, 1)
    query_seg, query_rel = place_rows(query_pos, seq_lengths)
    home_row = lax.dynamic_index_in_dim(dealing, my_index // spread, 1, False)
    targets = lax.dynamic_slice_in_dim(home_row, my_index % spread * rounds, rounds, 1)
    picker = (targets[:, None, :] == ctx_range[None, :, None]).astype(jnp.bfloat16)
    my_slots = lax.dynamic_index_in_dim(slot_of, my_index, 2, False)
    owner_index = (
        jnp.arange(rounds, dtype=jnp.int32)[None, :] * context_count + my_slots
    ) // rounds
    keep_slot = jnp.repeat(owner_index, spread, axis=1) == ctx_range[None, :]

    def spread_out(field):
        blocks = field.reshape(pack_count, rounds, BLK, model_dim)
        return jnp.einsum(
            "pkj,pjtd->pktd", picker, blocks, preferred_element_type=jnp.float32
        ).astype(jnp.bfloat16)

    def collect(received):
        grouped = received.reshape(pack_count, rounds, spread, BLK, model_dim)
        return (
            jnp.sum(grouped, axis=2, dtype=jnp.float32)
            .astype(jnp.bfloat16)
            .reshape(pack_count * token_count, model_dim)
        )

    def send_home(field):
        blocks = jnp.repeat(field.reshape(pack_count, rounds, BLK, model_dim), spread, axis=1)
        return jnp.where(keep_slot[:, :, None, None], blocks, jnp.zeros_like(blocks))

    def restore(returned):
        placed = jnp.einsum("pkj,pktd->pjtd", picker, returned, preferred_element_type=jnp.float32)
        return placed.astype(jnp.bfloat16).reshape(pack_count, token_count, model_dim)

    dealt_tokens, dealt_upstream = (
        lax.all_to_all(spread_out(tokens), "ctx", split_axis=1, concat_axis=1, tiled=True),
        lax.all_to_all(spread_out(cotangent), "ctx", split_axis=1, concat_axis=1, tiled=True),
    )
    inputs = collect(dealt_tokens)
    upstream = collect(dealt_upstream)
    gain_one, query_full, key_full, value_full, out_full = (
        lax.all_gather(first_gain, "fsdp", axis=0, tiled=True),
        lax.all_gather(query_weight, "fsdp", axis=0, tiled=True),
        lax.all_gather(key_matrix, "fsdp", axis=0, tiled=True),
        lax.all_gather(value_matrix, "fsdp", axis=0, tiled=True),
        lax.all_gather(out_weight, "fsdp", axis=0, tiled=True),
    )
    gain_two, gate_full, up_full, down_full = (
        lax.all_gather(second_gain, "fsdp", axis=0, tiled=True),
        lax.all_gather(gate_weight, "fsdp", axis=0, tiled=True),
        lax.all_gather(up_weight, "fsdp", axis=0, tiled=True),
        lax.all_gather(down_weight, "fsdp", axis=0, tiled=True),
    )
    gain_one32 = gain_one.astype(jnp.float32)
    gain_two32 = gain_two.astype(jnp.float32)
    cosine, sine_part = rotation(query_rel.reshape(-1), HEAD_SIZE // 2)
    inputs32 = inputs.astype(jnp.float32)
    scale_one = lax.rsqrt(jnp.mean(inputs32 * inputs32, axis=-1, keepdims=True) + EPS)
    normed_one = inputs32 * scale_one
    xn_one = (normed_one * gain_one32).astype(jnp.bfloat16)
    query_rot = rotate(
        jnp.dot(xn_one, query_full, preferred_element_type=jnp.float32), cosine, sine_part
    ).astype(jnp.bfloat16)
    key_rot = rotate(
        jnp.dot(xn_one, key_full, preferred_element_type=jnp.float32), cosine, sine_part
    ).astype(jnp.bfloat16)
    rows_of_values = jnp.dot(xn_one, value_full, preferred_element_type=jnp.float32).astype(
        jnp.bfloat16
    )
    key_local = key_rot.reshape(pack_count, token_count, -1)
    value_local = rows_of_values.reshape(pack_count, token_count, -1)
    gathered_keys, gathered_values = (
        lax.all_gather(key_local, "ctx", axis=1, tiled=True),
        lax.all_gather(value_local, "ctx", axis=1, tiled=True),
    )
    key_pos_rounds = key_pos.reshape(pack_count, context_count, rounds, BLK)
    key_seg_rounds = key_seg.reshape(pack_count, context_count, rounds, BLK)
    visible = []
    for round_index in range(rounds):
        first_row = round_index * BLK
        round_pos = key_pos_rounds[:, :, round_index].reshape(pack_count, -1)
        round_seg = key_seg_rounds[:, :, round_index].reshape(pack_count, -1)
        same_seq = query_seg[:, first_row:, None] == round_seg[:, None, :]
        earlier = round_pos[:, None, :] <= query_pos[:, first_row:, None]
        visible.append(same_seq & earlier)
    query_packs = query_rot.reshape(pack_count, token_count, -1)
    pack_index = 0
    pack_visible = [mask[pack_index] for mask in visible]
    attended_pack, total_pack = attend_pack(
        query_packs[pack_index],
        gathered_keys[pack_index],
        gathered_values[pack_index],
        pack_visible,
    )
    total_list = [total_pack]
    softmax_totals = jnp.stack(total_list, axis=0)
    hidden_in = inputs32 + jnp.dot(attended_pack, out_full, preferred_element_type=jnp.float32)
    scale_two = lax.rsqrt(jnp.mean(hidden_in * hidden_in, axis=-1, keepdims=True) + EPS)
    normed_two = hidden_in * scale_two
    xn_two = (normed_two * gain_two32).astype(jnp.bfloat16)
    gate_val = jnp.dot(xn_two, gate_full, preferred_element_type=jnp.float32)
    up_val = jnp.dot(xn_two, up_full, preferred_element_type=jnp.float32)
    activated = jax.nn.silu(gate_val)
    hidden = (activated * up_val).astype(jnp.bfloat16)
    result = (hidden_in + jnp.dot(hidden, down_full, preferred_element_type=jnp.float32)).astype(
        jnp.bfloat16
    )
    down_grad = jnp.dot(hidden.T, upstream, preferred_element_type=jnp.float32)
    d_hidden = jnp.dot(upstream, down_full.T, preferred_element_type=jnp.float32)
    sigmoid_gate = jax.nn.sigmoid(gate_val)
    d_gate = (d_hidden * up_val * sigmoid_gate * (1.0 + gate_val * (1.0 - sigmoid_gate))).astype(
        jnp.bfloat16
    )
    d_up = (d_hidden * activated).astype(jnp.bfloat16)
    gate_grad = jnp.dot(xn_two.T, d_gate, preferred_element_type=jnp.float32)
    up_grad = jnp.dot(xn_two.T, d_up, preferred_element_type=jnp.float32)
    d_norm_two = jnp.dot(d_gate, gate_full.T, preferred_element_type=jnp.float32) + jnp.dot(
        d_up, up_full.T, preferred_element_type=jnp.float32
    )
    gain_two_grad = jnp.sum(d_norm_two * normed_two, axis=0)
    d_hidden_in = upstream.astype(jnp.float32) + rms_back(
        d_norm_two * gain_two32, normed_two, scale_two
    )
    mlp_parts = (
        lax.psum_scatter(
            gain_two_grad.astype(jnp.bfloat16), "fsdp", scatter_dimension=0, tiled=True
        ).astype(jnp.float32),
        lax.psum_scatter(
            gate_grad.astype(jnp.bfloat16), "fsdp", scatter_dimension=0, tiled=True
        ).astype(jnp.float32),
        lax.psum_scatter(
            up_grad.astype(jnp.bfloat16), "fsdp", scatter_dimension=0, tiled=True
        ).astype(jnp.float32),
        lax.psum_scatter(
            down_grad.astype(jnp.bfloat16), "fsdp", scatter_dimension=0, tiled=True
        ).astype(jnp.float32),
    )
    d_branch = d_hidden_in.astype(jnp.bfloat16)
    out_grad = jnp.dot(attended_pack.T, d_branch, preferred_element_type=jnp.float32)
    d_attended = jnp.dot(d_branch, out_full.T, preferred_element_type=jnp.float32).astype(
        jnp.bfloat16
    )
    back_keys, back_values = (gathered_keys, gathered_values)
    grad_packs = d_attended.reshape(pack_count, token_count, -1)
    out_packs = attended_pack.reshape(pack_count, token_count, -1)
    pack_index = 0
    pack_visible = [mask[pack_index] for mask in visible]
    query_part, key_part, value_part = attend_back(
        query_packs[pack_index],
        back_keys[pack_index],
        back_values[pack_index],
        grad_packs[pack_index],
        out_packs[pack_index],
        softmax_totals[pack_index],
        pack_visible,
    )
    key_list = [key_part]
    value_list = [value_part]
    d_keys, d_values = (
        lax.psum_scatter(
            jnp.stack(key_list, axis=0).astype(jnp.bfloat16), "ctx", scatter_dimension=1, tiled=True
        ).astype(jnp.float32),
        lax.psum_scatter(
            jnp.stack(value_list, axis=0).astype(jnp.bfloat16),
            "ctx",
            scatter_dimension=1,
            tiled=True,
        ).astype(jnp.float32),
    )
    d_query = rotate(query_part, cosine, -sine_part).astype(jnp.bfloat16)
    d_key = rotate(d_keys.reshape(pack_count * token_count, -1), cosine, -sine_part).astype(
        jnp.bfloat16
    )
    d_value = d_values.reshape(pack_count * token_count, -1).astype(jnp.bfloat16)
    query_grad = jnp.dot(xn_one.T, d_query, preferred_element_type=jnp.float32)
    key_grad = jnp.dot(xn_one.T, d_key, preferred_element_type=jnp.float32)
    value_grad = jnp.dot(xn_one.T, d_value, preferred_element_type=jnp.float32)
    d_norm_one = (
        jnp.dot(d_query, query_full.T, preferred_element_type=jnp.float32)
        + jnp.dot(d_key, key_full.T, preferred_element_type=jnp.float32)
        + jnp.dot(d_value, value_full.T, preferred_element_type=jnp.float32)
    )
    gain_one_grad = jnp.sum(d_norm_one * normed_one, axis=0)
    d_inputs = d_hidden_in + rms_back(d_norm_one * gain_one32, normed_one, scale_one)
    attn_parts = (
        lax.psum_scatter(
            gain_one_grad.astype(jnp.bfloat16), "fsdp", scatter_dimension=0, tiled=True
        ).astype(jnp.float32),
        lax.psum_scatter(
            query_grad.astype(jnp.bfloat16), "fsdp", scatter_dimension=0, tiled=True
        ).astype(jnp.float32),
        lax.psum_scatter(
            key_grad.astype(jnp.bfloat16), "fsdp", scatter_dimension=0, tiled=True
        ).astype(jnp.float32),
        lax.psum_scatter(
            value_grad.astype(jnp.bfloat16), "fsdp", scatter_dimension=0, tiled=True
        ).astype(jnp.float32),
        lax.psum_scatter(
            out_grad.astype(jnp.bfloat16), "fsdp", scatter_dimension=0, tiled=True
        ).astype(jnp.float32),
    )
    finished = (
        lax.psum(attn_parts[0].astype(jnp.bfloat16), ("ctx", "grp")).astype(jnp.float32),
        lax.psum(attn_parts[1].astype(jnp.bfloat16), ("ctx", "grp")).astype(jnp.float32),
        lax.psum(attn_parts[2].astype(jnp.bfloat16), ("ctx", "grp")).astype(jnp.float32),
        lax.psum(attn_parts[3].astype(jnp.bfloat16), ("ctx", "grp")).astype(jnp.float32),
        lax.psum(attn_parts[4].astype(jnp.bfloat16), ("ctx", "grp")).astype(jnp.float32),
        lax.psum(mlp_parts[0].astype(jnp.bfloat16), ("ctx", "grp")).astype(jnp.float32),
        lax.psum(mlp_parts[1].astype(jnp.bfloat16), ("ctx", "grp")).astype(jnp.float32),
        lax.psum(mlp_parts[2].astype(jnp.bfloat16), ("ctx", "grp")).astype(jnp.float32),
        lax.psum(mlp_parts[3].astype(jnp.bfloat16), ("ctx", "grp")).astype(jnp.float32),
    )
    home_out, home_grad = (
        lax.all_to_all(send_home(result), "ctx", split_axis=1, concat_axis=1, tiled=True),
        lax.all_to_all(
            send_home(d_inputs.astype(jnp.bfloat16)), "ctx", split_axis=1, concat_axis=1, tiled=True
        ),
    )
    return (
        restore(home_out),
        restore(home_grad),
        softmax_totals,
        finished[0],
        finished[1],
        finished[2],
        finished[3],
        finished[4],
        finished[5],
        finished[6],
        finished[7],
        finished[8],
    )


MINLEN = 1024
QB = 256
VMEM_LIMIT = 56 * 1024 * 1024


def attend_kernel(q_ref, k_ref, v_ref, c_ref, s_ref, o_ref, lse_ref, qr_ref, kr_ref, vr_ref):
    cosine = c_ref[...]
    sine = s_ref[...]
    half = HEAD_SIZE // 2
    seq = cosine.shape[1]

    def turn(field):
        front, back = field[:half], field[half:]
        return jnp.concatenate(
            [front * cosine - back * sine, back * cosine + front * sine], axis=0
        )

    k_rot = turn(k_ref[...])
    kr_ref[...] = k_rot.astype(jnp.bfloat16)
    key = k_rot.T.astype(jnp.bfloat16)
    val_t = v_ref[...].astype(jnp.bfloat16)
    vr_ref[...] = val_t
    q0 = turn(q_ref[:HEAD_SIZE]).astype(jnp.bfloat16)
    q1 = turn(q_ref[HEAD_SIZE:]).astype(jnp.bfloat16)
    qr_ref[:HEAD_SIZE] = q0
    qr_ref[HEAD_SIZE:] = q1
    rows = lax.broadcasted_iota(jnp.int32, (QB, 2 * QB), 0)
    cols = lax.broadcasted_iota(jnp.int32, (QB, 2 * QB), 1)
    keep = rows <= jnp.where(cols >= QB, cols - QB, cols)
    for b in range(seq // QB):
        lo, n = b * QB, (b + 1) * QB
        q_t = jnp.concatenate([q0[:, lo:n], q1[:, lo:n]], axis=1)
        scores = jnp.dot(key[:n], q_t, preferred_element_type=jnp.float32) * HEAD_SIZE ** (-0.5)
        diag = jnp.where(keep, scores[lo:], MASKED)
        top = jnp.max(diag, axis=0, keepdims=True)
        if b > 0:
            top = jnp.maximum(top, jnp.max(scores[:lo], axis=0, keepdims=True))
        e_diag = jnp.exp(diag - top)
        total = jnp.sum(e_diag, axis=0, keepdims=True)
        out = jnp.dot(val_t[:, lo:n], e_diag.astype(jnp.bfloat16), preferred_element_type=jnp.float32)
        if b > 0:
            e_rest = jnp.exp(scores[:lo] - top)
            total = total + jnp.sum(e_rest, axis=0, keepdims=True)
            out = out + jnp.dot(
                val_t[:, :lo], e_rest.astype(jnp.bfloat16), preferred_element_type=jnp.float32
            )
        out = (out / total).astype(jnp.bfloat16)
        o_ref[:HEAD_SIZE, lo:n] = out[:, :QB]
        o_ref[HEAD_SIZE:, lo:n] = out[:, QB:]
        lse = top + jnp.log(total)
        lse_ref[0, 0:1, lo:n] = lse[:, :QB]
        lse_ref[0, 1:2, lo:n] = lse[:, QB:]


def attend_seq(qkv_t, cosine, sine):
    rows, seq = qkv_t.shape
    kv = rows // (4 * HEAD_SIZE)
    group = pl.BlockSpec((2 * HEAD_SIZE, seq), lambda j: (j, 0))

    def head(base):
        return pl.BlockSpec((HEAD_SIZE, seq), lambda j: (base + j, 0))

    table = pl.BlockSpec((HEAD_SIZE // 2, seq), lambda j: (0, 0))
    return pl.pallas_call(
        attend_kernel,
        grid=(kv,),
        in_specs=[group, head(2 * kv), head(3 * kv), table, table],
        out_specs=[
            group,
            pl.BlockSpec((1, 2, seq), lambda j: (j, 0, 0)),
            group,
            head(0),
            head(0),
        ],
        out_shape=[
            jax.ShapeDtypeStruct((2 * kv * HEAD_SIZE, seq), jnp.bfloat16),
            jax.ShapeDtypeStruct((kv, 2, seq), jnp.float32),
            jax.ShapeDtypeStruct((2 * kv * HEAD_SIZE, seq), jnp.bfloat16),
            jax.ShapeDtypeStruct((kv * HEAD_SIZE, seq), jnp.bfloat16),
            jax.ShapeDtypeStruct((kv * HEAD_SIZE, seq), jnp.bfloat16),
        ],
        compiler_params=pltpu.CompilerParams(vmem_limit_bytes=VMEM_LIMIT),
        cost_estimate=pl.CostEstimate(
            flops=4 * kv * 2 * seq * seq * HEAD_SIZE, bytes_accessed=10 * rows * seq, transcendentals=kv * seq * seq
        ),
        name="attend",
    )(qkv_t, qkv_t, qkv_t, cosine, sine)


def attend_back_kernel(
    q_ref, k_ref, v_ref, g_ref, lse_ref, c_ref, s_ref, dq_ref, dk_ref, dv_ref, dk_acc, dv_acc
):
    half = HEAD_SIZE // 2
    cosine = c_ref[...]
    sine = s_ref[...]
    seq = cosine.shape[1]

    def turn_back(field, cos, sin):
        front, back = field[:half], field[half:]
        return jnp.concatenate([front * cos + back * sin, back * cos - front * sin], axis=0)

    def flip(field):
        return field.astype(jnp.float32).T.astype(jnp.bfloat16)

    key_t = k_ref[...]
    key = flip(key_t)
    val = flip(v_ref[...])
    q0_t, q1_t = q_ref[:HEAD_SIZE], q_ref[HEAD_SIZE:]
    g0_t, g1_t = g_ref[:HEAD_SIZE], g_ref[HEAD_SIZE:]
    q0, q1, g0, g1 = flip(q0_t), flip(q1_t), flip(g0_t), flip(g1_t)
    dk_acc[...] = jnp.zeros_like(dk_acc)
    dv_acc[...] = jnp.zeros_like(dv_acc)
    rows = lax.broadcasted_iota(jnp.int32, (QB, 2 * QB), 0)
    cols = lax.broadcasted_iota(jnp.int32, (QB, 2 * QB), 1)
    keep = rows <= jnp.where(cols >= QB, cols - QB, cols)
    for b in range(seq // QB):
        lo, n = b * QB, (b + 1) * QB
        q_t = jnp.concatenate([q0_t[:, lo:n], q1_t[:, lo:n]], axis=1)
        g_t = jnp.concatenate([g0_t[:, lo:n], g1_t[:, lo:n]], axis=1)
        q_n = jnp.concatenate([q0[lo:n], q1[lo:n]], axis=0)
        g_n = jnp.concatenate([g0[lo:n], g1[lo:n]], axis=0)
        lse = jnp.concatenate([lse_ref[0, 0:1, lo:n], lse_ref[0, 1:2, lo:n]], axis=1)
        parts = []
        delta = None
        for start, stop in ([(0, lo)] if b > 0 else []) + [(lo, n)]:
            scores = jnp.dot(key[start:stop], q_t, preferred_element_type=jnp.float32) * HEAD_SIZE ** (-0.5)
            prob = jnp.exp(scores - lse)
            if start == lo:
                prob = jnp.where(keep, prob, 0.0)
            d_prob = jnp.dot(val[start:stop], g_t, preferred_element_type=jnp.float32)
            part = jnp.sum(prob * d_prob, axis=0, keepdims=True)
            delta = part if delta is None else delta + part
            dv_acc[start:stop] += jnp.dot(prob.astype(jnp.bfloat16), g_n, preferred_element_type=jnp.float32)
            parts.append((start, stop, prob, d_prob))
        dq_t = None
        for start, stop, prob, d_prob in parts:
            d_score = (prob * (d_prob - delta) * HEAD_SIZE ** (-0.5)).astype(jnp.bfloat16)
            dk_acc[start:stop] += jnp.dot(d_score, q_n, preferred_element_type=jnp.float32)
            part = jnp.dot(key_t[:, start:stop], d_score, preferred_element_type=jnp.float32)
            dq_t = part if dq_t is None else dq_t + part
        cos, sin = cosine[:, lo:n], sine[:, lo:n]
        dq_ref[:HEAD_SIZE, lo:n] = turn_back(dq_t[:, :QB], cos, sin).astype(jnp.bfloat16)
        dq_ref[HEAD_SIZE:, lo:n] = turn_back(dq_t[:, QB:], cos, sin).astype(jnp.bfloat16)
    dk_ref[...] = turn_back(dk_acc[...].T, cosine, sine).astype(jnp.bfloat16)
    dv_ref[...] = dv_acc[...].T.astype(jnp.bfloat16)


def attend_seq_back(q_t, k_t, v_t, g_t, lse, cosine, sine):
    rows, seq = k_t.shape
    kv = rows // HEAD_SIZE
    group = pl.BlockSpec((2 * HEAD_SIZE, seq), lambda j: (j, 0))
    head = pl.BlockSpec((HEAD_SIZE, seq), lambda j: (j, 0))
    table = pl.BlockSpec((HEAD_SIZE // 2, seq), lambda j: (0, 0))
    return pl.pallas_call(
        attend_back_kernel,
        grid=(kv,),
        in_specs=[group, head, head, group, pl.BlockSpec((1, 2, seq), lambda j: (j, 0, 0)), table, table],
        out_specs=[group, head, head],
        out_shape=[
            jax.ShapeDtypeStruct((2 * rows, seq), jnp.bfloat16),
            jax.ShapeDtypeStruct((rows, seq), jnp.bfloat16),
            jax.ShapeDtypeStruct((rows, seq), jnp.bfloat16),
        ],
        scratch_shapes=[
            pltpu.VMEM((seq, HEAD_SIZE), jnp.float32),
            pltpu.VMEM((seq, HEAD_SIZE), jnp.float32),
        ],
        compiler_params=pltpu.CompilerParams(vmem_limit_bytes=VMEM_LIMIT),
        cost_estimate=pl.CostEstimate(
            flops=10 * kv * 2 * seq * seq * HEAD_SIZE, bytes_accessed=20 * rows * seq, transcendentals=kv * seq * seq
        ),
        name="attend_back",
    )(q_t, k_t, v_t, g_t, lse, cosine, sine)


def fp32(field):
    return field.astype(jnp.float32)


def mm(left, right, dims=((1,), (0,)), out=jnp.float32):
    return lax.dot_general(left, right, (dims, ((), ())), preferred_element_type=out)


ANY = pl.BlockSpec(memory_space=pl.ANY)
SMEM = pl.BlockSpec(memory_space=pltpu.SMEM)
VM = pl.BlockSpec(memory_space=pltpu.VMEM)
PARAMS = pltpu.CompilerParams(vmem_limit_bytes=VMEM_LIMIT)
MESH = pl.DeviceIdType.MESH
TILE = 256


def bf16_like(*dims):
    return jax.ShapeDtypeStruct(dims, jnp.bfloat16)


def f32_like(*dims):
    return jax.ShapeDtypeStruct(dims, jnp.float32)


def cost(flops, moved):
    return pl.CostEstimate(flops=int(flops), bytes_accessed=int(moved), transcendentals=0)


class Spots:
    def __init__(self):
        z, f, g = lax.axis_index("ctx"), lax.axis_index("fsdp"), lax.axis_index("grp")
        self.z, self.f, self.g = z, f, g
        self.parity = z % 2
        self.fx = f + 1 - 2 * (f % 2)
        self.fy = f + 2 - 4 * (f // 2)
        self.fd = 3 - f
        across = z + 1 - 2 * self.parity
        self.x = (z, self.fx, g)
        self.y = (z, self.fy, g)
        self.diag = (z, self.fd, g)
        self.core = (z, f, 1 - g)
        self.across = (across, f, g)
        self.swap = (across, f, 1 - g)


def greet(*partners):
    barrier = pltpu.get_barrier_semaphore()
    for partner in partners:
        pl.semaphore_signal(barrier, inc=1, device_id=partner, device_id_type=MESH)
    pl.semaphore_wait(barrier, len(partners))


def rows_at(start, size):
    return pl.ds(pl.multiple_of(start, size), size)


def gather_kernel(
    tokens, cotangent, wq, wk, wv, wo, gate, up, down, gain,
    qkv_o, out_o, pair_o, down_o, x_o, dy_o, gain_o,
    send, recv, near, far, qkv_v, out_v, pair_v, down_v, tok_v, gain_v,
):
    at = Spots()
    g, f, parity = at.g, at.f, at.parity
    greet(at.x, at.y, at.diag, at.core, at.across, at.swap)
    taken = [0, 0]

    def remote(src, dst, device):
        i = taken[0]
        taken[0] += 1
        return pltpu.make_async_remote_copy(
            src_ref=src, dst_ref=dst, send_sem=send.at[i], recv_sem=recv.at[i],
            device_id=device, device_id_type=MESH,
        )

    class Bounce:
        def __init__(self, src, via, dst):
            i = taken[1]
            taken[1] += 1
            self.first = pltpu.make_async_copy(src, via, near.at[i])
            self.second = pltpu.make_async_copy(via, dst, far.at[i])

        def start(self):
            self.first.start()

        def turn(self):
            self.first.wait()
            self.second.start()

        def wait(self):
            self.second.wait()

    def start(copies):
        for copy in copies:
            copy.start()
        return copies

    def arrive(copies):
        for copy in copies:
            copy.wait_recv()

    tok = tokens.shape[1]
    feat = wq.shape[0]
    mid = feat // 2
    nq, nk, nv = (w.shape[1] // 2 for w in (wq, wk, wv))
    nf = down.shape[0] // 2
    wide = wo.shape[1] // 2
    count = 4
    top, low = slice(0, mid), slice(mid, feat)

    mine = rows_at(g * tok, tok)
    swaps = [
        remote(tokens.at[0], x_o.at[mine], at.swap),
        remote(cotangent.at[0], dy_o.at[mine], at.swap),
    ]
    keeps = [
        Bounce(tokens.at[0], tok_v.at[0], x_o.at[mine]),
        Bounce(cotangent.at[0], tok_v.at[1], dy_o.at[mine]),
    ]
    away = rows_at((1 - g) * tok, tok)
    swaps_out = [
        pltpu.make_async_remote_copy(
            src_ref=array.at[0], dst_ref=into.at[away], send_sem=send.at[i], recv_sem=recv.at[i],
            device_id=at.swap, device_id_type=MESH,
        )
        for i, (array, into) in enumerate(((tokens, x_o), (cotangent, dy_o)))
    ]
    shares = [remote(x_o.at[mine], x_o.at[mine], at.core), remote(dy_o.at[mine], dy_o.at[mine], at.core)]

    @pl.when(g != parity)
    def _():
        start(swaps_out)

    @pl.when(g == parity)
    def _():
        start(keeps)
        for copy in keeps:
            copy.turn()

    own_rows = f * feat

    def pair_sends(array, device, part):
        return [
            (
                array.at[part, rows_at((2 * k + g) * nf, nf)],
                pair_o.at[parity, rows_at(own_rows + part.start, mid), rows_at(k * nf, nf)],
                device,
            )
            for k in range(count)
        ]

    def pair_direct(part, device):
        first = taken[0]
        taken[0] += count

        def made(array):
            return [
                pltpu.make_async_remote_copy(
                    src_ref=src, dst_ref=dst, send_sem=send.at[first + k], recv_sem=recv.at[first + k],
                    device_id=to, device_id_type=MESH,
                )
                for k, (src, dst, to) in enumerate(pair_sends(array, device, part))
            ]

        @pl.when(parity == 0)
        def _():
            start(made(gate))

        @pl.when(parity == 1)
        def _():
            start(made(up))

        return made(gate)

    pair_xt = pair_direct(top, at.x)
    pair_yl = pair_direct(low, at.y)
    pair_xl = pair_direct(low, at.x)
    pair_yt = pair_direct(top, at.y)

    def qkv_direct(part, device):
        copies = []
        for array, width, column in ((wq, nq, 0), (wk, nk, nq), (wv, nv, nq + nk)):
            copies.append(
                remote(
                    array.at[part, rows_at(g * width, width)],
                    qkv_o.at[rows_at(own_rows + part.start, mid), column : column + width],
                    device,
                )
            )
        return start(copies)

    qkv_xt = qkv_direct(top, at.x)
    qkv_yl = qkv_direct(low, at.y)
    qkv_xl = qkv_direct(low, at.x)
    qkv_yt = qkv_direct(top, at.y)

    own = rows_at(own_rows, feat)
    locals_ = [
        Bounce(
            array.at[:, rows_at(g * width, width)],
            qkv_v.at[:, column : column + width],
            qkv_o.at[own, column : column + width],
        )
        for array, width, column in ((wq, nq, 0), (wk, nk, nq), (wv, nv, nq + nk))
    ]
    locals_.append(Bounce(wo, out_v, out_o.at[own]))
    locals_.append(Bounce(down.at[rows_at(g * nf, nf)], down_v, down_o.at[rows_at(f * nf, nf)]))
    for array, index in ((gate, 0), (up, 1)):
        for k in range(count):
            locals_.append(
                Bounce(
                    array.at[:, rows_at((2 * k + g) * nf, nf)],
                    pair_v.at[index, :, rows_at(k * nf, nf)],
                    pair_o.at[index, own, rows_at(k * nf, nf)],
                )
            )
    gain_place = gain_o.at[pl.ds(f, 1)]
    locals_.append(Bounce(gain, gain_v, gain_place))
    start(locals_)
    for copy in locals_:
        copy.turn()
    gains = start([remote(gain, gain_place, to) for to in (at.x, at.y, at.diag)])

    def forward(array_at, rows_x, rows_y):
        return remote(array_at(rows_x), array_at(rows_x), at.y), remote(
            array_at(rows_y), array_at(rows_y), at.x
        )

    x_top, y_low = rows_at(at.fx * feat, mid), rows_at(at.fy * feat + mid, mid)
    x_low, y_top = rows_at(at.fx * feat + mid, mid), rows_at(at.fy * feat, mid)
    d_top, d_low = rows_at(at.fd * feat, mid), rows_at(at.fd * feat + mid, mid)

    def pair_view(rows):
        return pair_o.at[parity, rows]

    def out_view(rows):
        return out_o.at[rows, rows_at(g * wide, wide)]

    pair_fy, pair_fx = forward(pair_view, x_top, y_low)
    sends = [pair_fy, pair_fx]

    def across(rows):
        copy = remote(pair_view(rows), pair_view(rows), at.across)
        copy.start()
        sends.append(copy)
        return copy

    arrive(pair_xt)
    pair_fy.start()
    z_copies = [across(x_top)]
    arrive(pair_yl)
    pair_fx.start()
    z_copies.append(across(y_low))

    def out_direct(part, device):
        copy = remote(
            wo.at[part, rows_at(g * wide, wide)],
            out_o.at[rows_at(own_rows + part.start, mid), rows_at(g * wide, wide)],
            device,
        )
        copy.start()
        return copy

    out_xt, out_yl = out_direct(top, at.x), out_direct(low, at.y)
    out_xl, out_yt = out_direct(low, at.x), out_direct(top, at.y)

    arrive(pair_xl)
    z_copies.append(across(x_low))
    arrive(pair_yt)
    z_copies.append(across(y_top))

    def qkv_view(rows):
        return qkv_o.at[rows]

    qkv_fy, qkv_fx = forward(qkv_view, x_top, y_low)
    arrive(qkv_xt)
    qkv_fy.start()
    arrive(qkv_yl)
    qkv_fx.start()

    dmid = nf // 2

    def down_direct(lower, device):
        copy = remote(
            down.at[rows_at(g * nf + lower, dmid)], down_o.at[rows_at(f * nf + lower, dmid)], device
        )
        copy.start()
        return copy

    down_xt, down_yl = down_direct(0, at.x), down_direct(dmid, at.y)
    down_xl, down_yt = down_direct(dmid, at.x), down_direct(0, at.y)

    pair_fy.wait_recv()
    z_copies.append(across(d_top))
    pair_fx.wait_recv()
    z_copies.append(across(d_low))

    for i in range(2):

        @pl.when(g != parity)
        def _():
            swaps[i].wait_recv()
            swaps_out[i].wait_send()

        @pl.when(g == parity)
        def _():
            keeps[i].wait()

        shares[i].start()

    out_fy, out_fx = forward(out_view, x_top, y_low)
    out_xt.wait_recv()
    out_fy.start()
    out_yl.wait_recv()
    out_fx.start()
    out_xl.wait_recv()
    out_yt.wait_recv()

    def share(rows):
        copy = remote(out_view(rows), out_view(rows), at.core)
        copy.start()
        return copy

    shared = [share(x_top), share(x_low), share(y_top), share(y_low)]

    def down_view(rows):
        return down_o.at[rows]

    down_fy, down_fx = forward(
        down_view, rows_at(at.fx * nf, dmid), rows_at(at.fy * nf + dmid, dmid)
    )
    down_xt.wait_recv()
    down_fy.start()
    down_yl.wait_recv()
    down_fx.start()

    out_fy.wait_recv()
    shared.append(share(d_top))
    out_fx.wait_recv()
    shared.append(share(d_low))

    arrive(qkv_xl)
    arrive(qkv_yt)
    arrive([qkv_fy, qkv_fx, down_xl, down_yt, down_fy, down_fx])
    arrive(gains)
    arrive(shares)
    arrive(shared)
    arrive(z_copies)
    for copy in locals_:
        copy.wait()
    for copy in (
        pair_xt + pair_yl + pair_xl + pair_yt + qkv_xt + qkv_yl + qkv_xl + qkv_yt + gains
        + sends + shares + shared
        + [out_xt, out_yl, out_xl, out_yt, out_fy, out_fx, qkv_fy, qkv_fx]
        + [down_xt, down_yl, down_xl, down_yt, down_fy, down_fx]
    ):
        copy.wait_send()


def gather_all(tokens, cotangent, wq, wk, wv, wo, gate, up, down, gain):
    tok, width = tokens.shape[1:]
    nf = down.shape[0] // 2
    cols = (wq.shape[1] + wk.shape[1] + wv.shape[1]) // 2
    return pl.pallas_call(
        gather_kernel,
        in_specs=[ANY] * 10,
        out_specs=[ANY] * 7,
        out_shape=[
            bf16_like(width, cols),
            bf16_like(4 * wo.shape[0], width),
            bf16_like(2, width, 4 * nf),
            bf16_like(4 * nf, width),
            bf16_like(2 * tok, width),
            bf16_like(2 * tok, width),
            jax.ShapeDtypeStruct((4,) + gain.shape[1:], gain.dtype),
        ],
        scratch_shapes=[
            pltpu.SemaphoreType.DMA((64,)),
            pltpu.SemaphoreType.DMA((64,)),
            pltpu.SemaphoreType.DMA((20,)),
            pltpu.SemaphoreType.DMA((20,)),
            pltpu.VMEM((width // 4, cols), jnp.bfloat16),
            pltpu.VMEM(wo.shape, jnp.bfloat16),
            pltpu.VMEM((2, width // 4, 4 * nf), jnp.bfloat16),
            pltpu.VMEM((nf, width), jnp.bfloat16),
            pltpu.VMEM((2, tok, width), jnp.bfloat16),
            pltpu.VMEM(gain.shape, gain.dtype),
        ],
        compiler_params=pltpu.CompilerParams(
            collective_id=0, has_side_effects=True, vmem_limit_bytes=VMEM_LIMIT
        ),
        cost_estimate=cost(0, 500e6),
        name="gather",
    )(tokens, cotangent, wq, wk, wv, wo, gate, up, down, gain)


def norm_scale(field):
    return lax.rsqrt(jnp.mean(field * field, axis=-1, keepdims=True) + EPS)


def project_kernel(x_ref, gain, w_ref, xn_ref, out_ref):
    seq = x_ref.shape[0]

    @pl.when(pl.program_id(0) == 0)
    def _():
        for part in range(seq // TILE):
            rows = slice(part * TILE, (part + 1) * TILE)
            field = fp32(x_ref[rows, :])
            xn_ref[rows, :] = (field * norm_scale(field) * gain[0:1, :]).astype(jnp.bfloat16)

    out_ref[...] = mm(w_ref[...].T, xn_ref[...], ((1,), (1,)))


def project(x_seq, gains, weight):
    seq, width = x_seq.shape
    cols = weight.shape[1]
    return pl.pallas_call(
        project_kernel,
        grid=(cols // TILE,),
        in_specs=[VM, VM, pl.BlockSpec((width, TILE), lambda n: (0, n))],
        out_specs=[VM, pl.BlockSpec((TILE, seq), lambda n: (n, 0))],
        out_shape=[bf16_like(seq, width), f32_like(cols, seq)],
        compiler_params=PARAMS,
        cost_estimate=cost(2 * seq * width * cols, 20e6),
        name="project",
    )(x_seq, gains, weight)


def residual_kernel(place, x_ref, attn_keep, attn_got, gain, w_ref, h_ref, xn_ref):
    core = place[0]
    heads = attn_keep.shape[0]
    keep_at, got_at = rows_at(core * heads, heads), rows_at((1 - core) * heads, heads)
    tok = h_ref.shape[0]
    field = mm(attn_keep[...].T, w_ref[keep_at, :])
    field = field + mm(attn_got[...].T, w_ref[got_at, :])
    h_ref[...] = field + fp32(x_ref[rows_at(core * tok, tok), :])
    for part in range(tok // TILE):
        rows = slice(part * TILE, (part + 1) * TILE)
        field = h_ref[rows, :]
        xn_ref[rows, :] = (field * norm_scale(field) * gain[1:2, :]).astype(jnp.bfloat16)


def residual(place, x_seq, attn_keep, attn_got, gains, weight):
    seq, width = x_seq.shape
    tok = seq // 2
    return pl.pallas_call(
        residual_kernel,
        in_specs=[SMEM] + [VM] * 5,
        out_specs=[VM, VM],
        out_shape=[f32_like(tok, width), bf16_like(tok, width)],
        compiler_params=PARAMS,
        cost_estimate=cost(2 * tok * width * weight.shape[0], 14e6),
        name="residual",
    )(place, x_seq, attn_keep, attn_got, gains, weight)


def hidden_kernel(xn_ref, dy_ref, gate_w, up_w, down_w, hid_ref, dgate_ref, dup_ref):
    gate = mm(xn_ref[...], gate_w[0])
    up = mm(xn_ref[...], up_w[0])
    d_hidden = mm(dy_ref[...], down_w[...], ((1,), (1,)))
    sig = 1.0 / (1.0 + jnp.exp(-gate))
    act = gate * sig
    hid_ref[...] = (act * up).astype(jnp.bfloat16)
    dgate_ref[...] = (d_hidden * up * (sig + act * (1.0 - sig))).astype(jnp.bfloat16)
    dup_ref[...] = (d_hidden * act).astype(jnp.bfloat16)


def hidden_step(xn, dy, pair, down):
    seq, width = xn.shape
    ff = down.shape[0]
    block = pl.BlockSpec((seq, TILE), lambda n: (0, n))
    return pl.pallas_call(
        hidden_kernel,
        grid=(ff // TILE,),
        in_specs=[
            VM,
            VM,
            pl.BlockSpec((1, width, TILE), lambda n: (0, 0, n)),
            pl.BlockSpec((1, width, TILE), lambda n: (1, 0, n)),
            pl.BlockSpec((TILE, width), lambda n: (n, 0)),
        ],
        out_specs=[block] * 3,
        out_shape=[bf16_like(seq, ff)] * 3,
        compiler_params=PARAMS,
        cost_estimate=cost(6 * seq * width * ff, 38e6),
        name="hidden",
    )(xn, dy, pair, pair, down)


def back_kernel(place, dgate_ref, dup_ref, gate_w, up_w, own_ref, send_ref):
    field = mm(dgate_ref[...], gate_w[0], ((1,), (1,)))
    field = field + mm(dup_ref[...], up_w[0], ((1,), (1,)))
    tok = own_ref.shape[0]

    @pl.when(place[0] == 0)
    def _():
        own_ref[...] = field[:tok]
        send_ref[...] = field[tok:].astype(jnp.bfloat16)

    @pl.when(place[0] == 1)
    def _():
        own_ref[...] = field[tok:]
        send_ref[...] = field[:tok].astype(jnp.bfloat16)


def back_step(place, d_gate, d_up, pair):
    seq, ff = d_gate.shape
    width = pair.shape[1]
    out = pl.BlockSpec((seq // 2, TILE), lambda n: (0, n))
    return pl.pallas_call(
        back_kernel,
        grid=(width // TILE,),
        in_specs=[
            SMEM,
            VM,
            VM,
            pl.BlockSpec((1, TILE, ff), lambda n: (0, n, 0)),
            pl.BlockSpec((1, TILE, ff), lambda n: (1, n, 0)),
        ],
        out_specs=[out, out],
        out_shape=[f32_like(seq // 2, width), bf16_like(seq // 2, width)],
        compiler_params=PARAMS,
        cost_estimate=cost(4 * seq * width * ff, 26e6),
        name="back",
    )(place, d_gate, d_up, pair, pair)


def result_kernel(place, hid_ref, h_ref, down_w, own_ref, send_ref):
    field = mm(hid_ref[...], down_w[...])
    tok = own_ref.shape[0]

    @pl.when(place[0] == 0)
    def _():
        own_ref[...] = field[:tok] + h_ref[...]
        send_ref[...] = field[tok:].astype(jnp.bfloat16)

    @pl.when(place[0] == 1)
    def _():
        own_ref[...] = field[tok:] + h_ref[...]
        send_ref[...] = field[:tok].astype(jnp.bfloat16)


def result_step(place, hidden, h_own, down):
    tok, width = h_own.shape
    ff = hidden.shape[1]
    out = pl.BlockSpec((tok, TILE), lambda n: (0, n))
    return pl.pallas_call(
        result_kernel,
        grid=(width // TILE,),
        in_specs=[SMEM, VM, out, pl.BlockSpec((ff, TILE), lambda n: (0, n))],
        out_specs=[out, out],
        out_shape=[f32_like(tok, width), bf16_like(tok, width)],
        compiler_params=PARAMS,
        cost_estimate=cost(4 * tok * width * ff, 20e6),
        name="result",
    )(place, hidden, h_own, down)


def entry_kernel(place, dn_own, dn_got, h_ref, dy_ref, gain, w_ref, dh_ref, da_ref, keep_ref, send_ref, part_ref):
    core = place[0]
    tok = dh_ref.shape[0]
    part_ref[...] = jnp.zeros_like(part_ref)
    for part in range(tok // TILE):
        rows = slice(part * TILE, (part + 1) * TILE)
        field = h_ref[rows, :]
        scale = norm_scale(field)
        hat = field * scale
        grad = dn_own[rows, :] + fp32(dn_got[rows, :])
        part_ref[...] += jnp.sum(grad * hat, axis=0, keepdims=True)
        dy = fp32(dy_ref[rows_at(core * tok + part * TILE, TILE), :])
        total = dy + rms_back(grad * gain[1:2, :], hat, scale)
        dh_ref[rows, :] = total
        da_ref[rows, :] = total.astype(jnp.bfloat16)
    heads = keep_ref.shape[0]
    for ref, at in ((send_ref, 1 - core), (keep_ref, core)):
        ref[...] = mm(w_ref[rows_at(at * heads, heads), :], da_ref[...], ((1,), (1,))).astype(jnp.bfloat16)


def entry_step(place, dn_own, dn_got, h_own, dy_all, gains, weight):
    tok, width = h_own.shape
    rows = weight.shape[0]
    return pl.pallas_call(
        entry_kernel,
        in_specs=[SMEM] + [VM] * 6,
        out_specs=[VM] * 5,
        out_shape=[
            f32_like(tok, width),
            bf16_like(tok, width),
            bf16_like(rows // 2, tok),
            bf16_like(rows // 2, tok),
            f32_like(1, width),
        ],
        compiler_params=PARAMS,
        cost_estimate=cost(2 * tok * width * rows, 20e6),
        name="entry",
    )(place, dn_own, dn_got, h_own, dy_all, gains, weight)


def inputs_kernel(place, dq_ref, dk_ref, dv_ref, w_ref, own_ref, send_ref, d_ref):
    @pl.when(pl.program_id(0) == 0)
    def _():
        nq, nk = dq_ref.shape[0], dk_ref.shape[0]
        d_ref[:, :nq] = dq_ref[...].T
        d_ref[:, nq : nq + nk] = dk_ref[...].T
        d_ref[:, nq + nk :] = dv_ref[...].T

    field = mm(d_ref[...], w_ref[...], ((1,), (1,)))
    tok = own_ref.shape[0]

    @pl.when(place[0] == 0)
    def _():
        own_ref[...] = field[:tok]
        send_ref[...] = field[tok:].astype(jnp.bfloat16)

    @pl.when(place[0] == 1)
    def _():
        own_ref[...] = field[tok:]
        send_ref[...] = field[:tok].astype(jnp.bfloat16)


def inputs_step(place, dq_t, dk_t, dv_t, weight):
    width, cols = weight.shape
    tok = dq_t.shape[1] // 2
    out = pl.BlockSpec((tok, TILE), lambda n: (0, n))
    return pl.pallas_call(
        inputs_kernel,
        grid=(width // TILE,),
        in_specs=[SMEM] + [VM] * 3 + [pl.BlockSpec((TILE, cols), lambda n: (n, 0))],
        out_specs=[out, out, VM],
        out_shape=[f32_like(tok, width), bf16_like(tok, width), bf16_like(2 * tok, cols)],
        compiler_params=PARAMS,
        cost_estimate=cost(4 * tok * width * cols, 14e6),
        name="inputs",
    )(place, dq_t, dk_t, dv_t, weight)


def last_kernel(place, d1_own, d1_got, x_ref, dh_ref, gain, dx_ref, part_ref):
    part_ref[...] = jnp.zeros_like(part_ref)
    tok = dx_ref.shape[0]
    for part in range(tok // TILE):
        rows = slice(part * TILE, (part + 1) * TILE)
        field = fp32(x_ref[rows_at(place[0] * tok + part * TILE, TILE), :])
        scale = norm_scale(field)
        hat = field * scale
        grad = d1_own[rows, :] + fp32(d1_got[rows, :])
        part_ref[...] += jnp.sum(grad * hat, axis=0, keepdims=True)
        dx_ref[rows, :] = (dh_ref[rows, :] + rms_back(grad * gain[0:1, :], hat, scale)).astype(jnp.bfloat16)


def last_step(place, d1_own, d1_got, x_seq, dh_own, gains):
    tok, width = dh_own.shape
    return pl.pallas_call(
        last_kernel,
        in_specs=[SMEM] + [VM] * 5,
        out_specs=[VM] * 2,
        out_shape=[bf16_like(tok, width), f32_like(1, width)],
        compiler_params=PARAMS,
        cost_estimate=cost(0, 14e6),
        name="last",
    )(place, d1_own, d1_got, x_seq, dh_own, gains)


class Group:
    def __init__(self, source, rows, refs, put):
        self.source, self.rows, self.put = source, rows, put
        self.acc, self.mid, self.got, self.late, self.outer, self.inner, self.done = refs


def add_rows(dst, left, right):
    rows = dst.shape[0]

    @pl.loop(0, rows // 64)
    def _(i):
        at = rows_at(i * 64, 64)
        dst[at] = (fp32(left[at]) + fp32(right[at])).astype(dst.dtype)


def collect_kernel(
    down, gate, up, qkv, out, sums,
    down_o, gate_o, up_o, query_o, key_o, value_o, out_o, sums_o,
    send, recv, near, out_mine, out_got, sums_got, *buffers,
):
    at = Spots()
    z, f, g = at.z, at.f, at.g
    is_inner = (z == 1) | (z == 2)
    is_outer = (z == 0) | (z == 3)
    toward = (1 + z // 2, f, g)
    outward = (3 * (z // 2), f, g)
    other = (3 - z, f, g)
    barrier = pltpu.get_barrier_semaphore()
    for partner in (at.x, at.y, at.core):
        pl.semaphore_signal(barrier, inc=1, device_id=partner, device_id_type=MESH)

    @pl.when(is_outer)
    def _():
        pl.semaphore_signal(barrier, inc=1, device_id=toward, device_id_type=MESH)
        pl.semaphore_wait(barrier, 4)

    @pl.when(is_inner)
    def _():
        pl.semaphore_signal(barrier, inc=1, device_id=outward, device_id_type=MESH)
        pl.semaphore_signal(barrier, inc=1, device_id=other, device_id_type=MESH)
        pl.semaphore_wait(barrier, 5)

    taken = [0, 0]

    def remote(src, dst, device):
        i = taken[0]
        taken[0] += 1
        return pltpu.make_async_remote_copy(
            src_ref=src, dst_ref=dst, send_sem=send.at[i], recv_sem=recv.at[i],
            device_id=device, device_id_type=MESH,
        )

    def local(src, dst):
        i = taken[1]
        taken[1] += 1
        return pltpu.make_async_copy(src, dst, near.at[i])

    nf = down.shape[0] // 4
    feat = gate.shape[0] // 4
    nq, nk = query_o.shape[1] // 2, key_o.shape[1] // 2
    wide = out_o.shape[1] // 2

    def put_down(group):
        return [(group.done, down_o.at[rows_at(g * nf, nf)])]

    def put_pair(into):
        def put(group):
            return [
                (group.done.at[:, rows_at(k * nf, nf)], into.at[:, rows_at((2 * k + g) * nf, nf)])
                for k in range(4)
            ]

        return put

    def put_qkv(group):
        return [
            (group.done.at[:, 0:nq], query_o.at[:, rows_at(g * nq, nq)]),
            (group.done.at[:, nq : nq + nk], key_o.at[:, rows_at(g * nk, nk)]),
            (group.done.at[:, nq + nk : nq + 2 * nk], value_o.at[:, rows_at(g * nk, nk)]),
        ]

    def put_out(group):
        return [(group.done, out_o.at[:, rows_at(g * wide, wide)])]

    groups = []
    for i, (source, rows, put) in enumerate(
        (
            (down, nf, put_down),
            (gate, feat, put_pair(gate_o)),
            (up, feat, put_pair(up_o)),
            (qkv, feat, put_qkv),
            (out_mine, feat, put_out),
        )
    ):
        groups.append(Group(source, rows, buffers[7 * i : 7 * i + 7], put))

    out_send = remote(out.at[:, rows_at((1 - g) * wide, wide)], out_got, at.core)
    out_keep = local(out.at[:, rows_at(g * wide, wide)], out_mine)
    sums_send = remote(sums, sums_got.at[0], at.core)
    out_send.start()
    out_keep.start()
    sums_send.start()

    for group in groups:
        rows, mid = group.rows, group.rows // 2
        src = group.source
        group.sends = [
            remote(src.at[rows_at(at.fd * rows, mid)], group.got.at[1], at.x),
            remote(src.at[rows_at(at.fd * rows + mid, mid)], group.got.at[3], at.y),
            remote(src.at[rows_at(at.fx * rows, mid)], group.got.at[0], at.x),
            remote(src.at[rows_at(at.fy * rows + mid, mid)], group.got.at[2], at.y),
        ]
        group.loads = [
            local(src.at[rows_at(at.fy * rows, mid)], group.mid.at[0]),
            local(src.at[rows_at(at.fx * rows + mid, mid)], group.mid.at[1]),
            local(src.at[rows_at(f * rows, rows)], group.acc),
        ]
        group.second = [
            remote(group.mid.at[0], group.late.at[0], at.y),
            remote(group.mid.at[1], group.late.at[1], at.x),
        ]
        group.in_z = remote(group.acc, group.outer, toward)
        top, low = pl.ds(0, mid), pl.ds(mid, mid)
        group.halves = (top, low)
        i = taken[0]
        taken[0] += 4

        def between(index, src_ref, dst_ref, device):
            return pltpu.make_async_remote_copy(
                src_ref=src_ref, dst_ref=dst_ref, send_sem=send.at[index], recv_sem=recv.at[index],
                device_id=device, device_id_type=MESH,
            )

        def crossing(keep, give, i=i, group=group):
            return (
                between(i, group.acc.at[give], group.inner, other),
                between(i + 1, group.done.at[keep], group.done.at[keep], other),
                between(i + 2, group.done.at[keep], group.done.at[keep], outward),
                between(i + 3, group.done.at[give], group.done.at[give], outward),
            )

        group.crossing = crossing
        pairs = group.put(group)
        group.shares = [remote(src_ref, dst_ref, at.core) for src_ref, dst_ref in pairs]
        group.stores = [local(src_ref, dst_ref) for src_ref, dst_ref in pairs]

    def begin(group):
        for copy in group.sends + group.loads:
            copy.start()

    def first(group):
        for i, which in ((0, 1), (1, 3)):
            group.sends[i].wait_recv()
            group.loads[i].wait()
            add_rows(group.mid.at[i], group.mid.at[i], group.got.at[which])
            group.second[i].start()
        group.loads[2].wait()
        for i, part, which in ((2, 0, 0), (3, 1, 2)):
            group.sends[i].wait_recv()
            half = group.acc.at[group.halves[part]]
            add_rows(half, half, group.got.at[which])

    def plane(group):
        for i in range(2):
            group.second[i].wait_recv()
            half = group.acc.at[group.halves[i]]
            add_rows(half, half, group.late.at[i])

        @pl.when(is_outer)
        def _():
            group.in_z.start()

    def by_side(group, step):
        top, low = group.halves

        @pl.when(z == 1)
        def _():
            step(top, low, group.crossing(top, low))

        @pl.when(z == 2)
        def _():
            step(low, top, group.crossing(low, top))

    def enter(group):
        def step(keep, give, copies):
            add_rows(group.acc.at[give], group.acc.at[give], group.outer.at[give])
            copies[0].start()
            add_rows(group.acc.at[keep], group.acc.at[keep], group.outer.at[keep])

        @pl.when(is_inner)
        def _():
            group.in_z.wait_recv()

        by_side(group, step)

    def settle(group):
        def step(keep, give, copies):
            copies[0].wait_recv()
            add_rows(group.done.at[keep], group.acc.at[keep], group.inner)
            copies[1].start()
            copies[2].start()

        by_side(group, step)

    def finish(group):
        def step(keep, give, copies):
            copies[1].wait_recv()
            copies[3].start()

        by_side(group, step)

    def deliver(group):
        top, low = group.halves

        @pl.when(is_outer)
        def _():
            copies = group.crossing(top, low)
            copies[2].wait_recv()
            copies[3].wait_recv()
            group.in_z.wait_send()

        def step(keep, give, copies):
            for copy in copies:
                copy.wait_send()

        by_side(group, step)
        for copy in group.shares + group.stores:
            copy.start()
        for copy in group.sends + group.second:
            copy.wait_send()

    begin(groups[0])
    begin(groups[1])
    out_send.wait_recv()
    out_keep.wait()

    @pl.loop(0, out_mine.shape[0] // 64)
    def _(i):
        rows = rows_at(i * 64, 64)
        out_mine[rows] = (fp32(out_mine[rows]) + fp32(out_got[rows])).astype(out_mine.dtype)

    sums_send.wait_recv()
    sums_o[...] = sums[...] + sums_got[0]
    hops = [sums_send]
    for i, device in ((1, at.x), (2, at.y)):
        hop = remote(sums_o, sums_got.at[i], device)
        hop.start()
        hop.wait()
        sums_o[...] += sums_got[i]
    inward = remote(sums_o, sums_got.at[3], toward)
    middle = remote(sums_o, sums_got.at[4], other)
    outgo = remote(sums_o, sums_got.at[5], outward)

    @pl.when(is_outer)
    def _():
        inward.start()

    @pl.when(is_inner)
    def _():
        inward.wait_recv()
        sums_o[...] += sums_got[3]
        middle.start()
        middle.wait()
        sums_o[...] += sums_got[4]
        outgo.start()

    stages = (first, plane, enter, settle, finish, deliver)
    count = len(groups)
    for step in range(count + len(stages) - 1):
        for behind, stage in enumerate(stages):
            i = step - behind
            if 0 <= i < count:
                stage(groups[i])
                if behind == 0 and i + 2 < count:
                    begin(groups[i + 2])

    @pl.when(is_outer)
    def _():
        inward.wait_send()
        outgo.wait_recv()
        sums_o[...] = sums_got[5]

    @pl.when(is_inner)
    def _():
        outgo.wait_send()

    sums_send.wait_send()
    out_send.wait_send()
    for group in groups:
        for copy in group.stores:
            copy.wait()
        for copy in group.shares:
            copy.wait_send()
            copy.wait_recv()


def collect(down, gate, up, qkv, out, sums, nq, nk):
    bf = jnp.bfloat16
    buffers = []
    shapes = []
    for grad, cols in ((down, down.shape[1]), (gate, gate.shape[1]), (up, up.shape[1]), (qkv, qkv.shape[1]), (out, out.shape[1] // 2)):
        rows = grad.shape[0] // 4
        mid = rows // 2
        shapes.append((rows, cols))
        buffers += [
            pltpu.VMEM((rows, cols), bf),
            pltpu.VMEM((2, mid, cols), bf),
            pltpu.VMEM((4, mid, cols), bf),
            pltpu.VMEM((2, mid, cols), bf),
            pltpu.VMEM((rows, cols), bf),
            pltpu.VMEM((mid, cols), bf),
            pltpu.VMEM((rows, cols), bf),
        ]
    feat = gate.shape[0] // 4
    return pl.pallas_call(
        collect_kernel,
        in_specs=[ANY] * 5 + [VM],
        out_specs=[ANY] * 7 + [VM],
        out_shape=[
            bf16_like(down.shape[0] // 2, down.shape[1]),
            bf16_like(feat, 2 * gate.shape[1]),
            bf16_like(feat, 2 * up.shape[1]),
            bf16_like(feat, 2 * nq),
            bf16_like(feat, 2 * nk),
            bf16_like(feat, 2 * nk),
            bf16_like(feat, out.shape[1]),
            f32_like(*sums.shape),
        ],
        scratch_shapes=[
            pltpu.SemaphoreType.DMA((96,)),
            pltpu.SemaphoreType.DMA((96,)),
            pltpu.SemaphoreType.DMA((32,)),
            pltpu.VMEM((out.shape[0], out.shape[1] // 2), bf),
            pltpu.VMEM((out.shape[0], out.shape[1] // 2), bf),
            pltpu.VMEM((6,) + sums.shape, jnp.float32),
        ]
        + buffers,
        compiler_params=pltpu.CompilerParams(
            collective_id=1, has_side_effects=True, vmem_limit_bytes=62 * 1024 * 1024
        ),
        cost_estimate=cost(0, 800e6),
        name="collect",
    )(down, gate, up, qkv, out, sums)


def chip_local(
    tokens,
    seq_lengths,
    dealing,
    first_gain,
    query_weight,
    key_matrix,
    value_matrix,
    out_weight,
    second_gain,
    gate_weight,
    up_weight,
    down_weight,
    cotangent,
):
    ctx = lax.axis_size("ctx")
    z = lax.axis_index("ctx")
    f = lax.axis_index("fsdp")
    g = lax.axis_index("grp")
    parity = z % 2
    parity_core = g == parity
    width = tokens.shape[2]
    tok = tokens.shape[1]
    seq = 2 * tok
    place = jnp.stack([g, parity]).astype(jnp.int32)

    def over_x(field):
        return lax.ppermute(field, "fsdp", [(i, i ^ 1) for i in range(4)])

    def over_y(field):
        return lax.ppermute(field, "fsdp", [(i, i ^ 2) for i in range(4)])

    def over_core(field):
        return lax.ppermute(field, "grp", [(0, 1), (1, 0)])

    swap_pairs = [(2 * i + (1 - i % 2), 2 * (i ^ 1) + i % 2) for i in range(ctx)]

    def swap(field):
        got = lax.ppermute(field, ("ctx", "grp"), swap_pairs)
        return jnp.where(parity_core, field, got)

    def along(field, pairs):
        return lax.ppermute(field, "ctx", pairs)

    def cut(field, start, size, axis):
        return lax.dynamic_slice_in_dim(field, start, size, axis)

    def in_order(mine, other, axis=0):
        first = jnp.where(g == 0, mine, other)
        second = jnp.where(g == 0, other, mine)
        return jnp.concatenate([first, second], axis=axis)

    heads_q = query_weight.shape[1] // 2
    heads_k = key_matrix.shape[1] // 2
    part_ff = down_weight.shape[0] // 2
    rows_in = gate_weight.shape[0]

    gain_own = jnp.pad(fp32(jnp.stack([first_gain, second_gain])), ((0, 6), (0, 0)))[None]
    qkv_w, out_w, pair_w, down_w, x_seq, dy_all, gain_all = gather_all(
        tokens, cotangent, query_weight, key_matrix, value_matrix, out_weight,
        gate_weight, up_weight, down_weight, gain_own,
    )
    gains = jnp.transpose(gain_all[:, :2], (1, 0, 2)).reshape(2, width)

    positions = jnp.arange(seq, dtype=jnp.int32)
    cosine, sine = rotation(positions, HEAD_SIZE // 2)
    cosine, sine = cosine.T, sine.T

    xn_one, qkv_t = project(x_seq, gains, qkv_w)
    attn_t, lse, q_t, k_t, v_t = attend_seq(qkv_t, cosine, sine)
    attn_keep = cut(attn_t, g * tok, tok, 1)
    attn_send = cut(attn_t, (1 - g) * tok, tok, 1)
    attn_got = over_core(attn_send)
    h_own, xn_own = residual(place, x_seq, attn_keep, attn_got, gains, out_w)
    xn_two = in_order(xn_own, over_core(xn_own))
    hidden, d_gate, d_up = hidden_step(xn_two, dy_all, pair_w, down_w)
    bf = jnp.bfloat16
    tokens_in = ((0,), (0,))
    down_grad = mm(hidden, dy_all, tokens_in, bf)
    gate_grad = mm(xn_two, d_gate, tokens_in, bf)
    up_grad = mm(xn_two, d_up, tokens_in, bf)
    dn_own, dn_send = back_step(place, d_gate, d_up, pair_w)
    dn_got = over_core(dn_send)
    res_own, res_send = result_step(place, hidden, h_own, down_w)
    layer_out = swap((res_own + fp32(over_core(res_send))).astype(bf))

    dh_own, da, dattn_keep, dattn_send, gain_two_part = entry_step(
        place, dn_own, dn_got, h_own, dy_all, gains, out_w
    )
    dattn_all = in_order(dattn_keep, over_core(dattn_send), axis=1)
    attn_mine = in_order(attn_keep, attn_got)
    dq_t, dk_t, dv_t = attend_seq_back(q_t, k_t, v_t, dattn_all, lse, cosine, sine)
    half_width = width // 2
    out_part = mm(attn_mine, da, ((1,), (0,)), bf)
    d1_own, d1_send, d_qkv = inputs_step(place, dq_t, dk_t, dv_t, qkv_w)
    qkv_grad = mm(xn_one, d_qkv, tokens_in, bf)
    dx, gain_one_part = last_step(place, d1_own, over_core(d1_send), x_seq, dh_own, gains)
    tokens_grad = swap(dx)

    parts = jnp.concatenate([gain_one_part, gain_two_part])
    down_sum, gate_sum, up_sum, query_sum, key_sum, value_sum, out_sum, sums = collect(
        down_grad, gate_grad, up_grad, qkv_grad, out_part,
        jnp.pad(parts, ((0, 6), (0, 0))), heads_q, heads_k,
    )
    sums = cut(sums, f * (width // 4), width // 4, 1)

    all_lse = lax.all_gather(lse.reshape(1, -1, seq), ("ctx", "grp"), axis=0, tiled=True)
    all_lse = all_lse.reshape(ctx // 2, 2, QUERY_HEADS, seq)
    pack_lse = lax.dynamic_index_in_dim(all_lse, g, 1, False)
    pack_lse = jnp.transpose(pack_lse, (1, 0, 2)).reshape(QUERY_HEADS, ctx, tok // BLK, BLK)
    mine = (dealing[0] == z).astype(jnp.float32)
    totals = jnp.sum(pack_lse * mine[None, :, :, None], axis=2).reshape(1, QUERY_HEADS, tok)

    return (
        layer_out[None],
        tokens_grad[None],
        totals,
        sums[0],
        fp32(query_sum),
        fp32(key_sum),
        fp32(value_sum),
        fp32(out_sum),
        sums[1],
        fp32(gate_sum),
        fp32(up_sum),
        fp32(down_sum),
    )


def chip_holds_sequence(mesh, tokens, seq_lengths):
    sizes = dict(mesh.shape)
    packs, length, _ = tokens.shape
    count = seq_lengths.shape[1]
    return (
        sizes["fsdp"] == 4
        and sizes["grp"] == 2
        and sizes["ctx"] == 4
        and packs == sizes["fsdp"] * sizes["grp"]
        and length == count * MINLEN
        and 2 * length == sizes["ctx"] * MINLEN
    )


def solution(mesh):
    placed = (
        P(("fsdp", "grp"), "ctx", None),
        P(("fsdp", "grp"), None),
        P(("fsdp", "grp"), None, None),
        P("fsdp"),
        P("fsdp", None),
        P("fsdp", None),
        P("fsdp", None),
        P("fsdp", None),
        P("fsdp"),
        P("fsdp", None),
        P("fsdp", None),
        P("fsdp", None),
        P(("fsdp", "grp"), "ctx", None),
    )
    results = (
        P(("fsdp", "grp"), "ctx", None),
        P(("fsdp", "grp"), "ctx", None),
        P(("fsdp", "grp"), None, "ctx"),
        P("fsdp"),
        P("fsdp", None),
        P("fsdp", None),
        P("fsdp", None),
        P("fsdp", None),
        P("fsdp"),
        P("fsdp", None),
        P("fsdp", None),
        P("fsdp", None),
    )

    def program(*arrays):
        body = chip_local if chip_holds_sequence(mesh, arrays[0], arrays[1]) else local
        return jax.shard_map(
            body, mesh=mesh, in_specs=placed, out_specs=results, check_vma=False
        )(*arrays)

    return program
```

```python
import jax
import jax.numpy as jnp
import numpy as np
from jax import lax
from jax.experimental import pallas as pl
from jax.experimental.pallas import tpu as pltpu
from jax.sharding import PartitionSpec as P

QUERY_HEADS = 16
KEY_VALUE_HEADS = 8
HEAD_SIZE = 96
BLK = 128


EPS = 1e-05
ROPE_BASE = 100000.0
MASKED = -1e30


def place_rows(positions, lengths):
    ends = jnp.cumsum(lengths, axis=-1)
    before = positions[..., :, None] >= ends[..., None, :]
    segment = jnp.sum(before.astype(jnp.int32), axis=-1)
    offset = jnp.sum(jnp.where(before, lengths[..., None, :], 0), axis=-1)
    return (segment, positions - offset)


def rotation(relative, half_size):
    frequency = ROPE_BASE ** (-(2.0 * jnp.arange(half_size, dtype=jnp.float32)) / (2 * half_size))
    angles = relative.astype(jnp.float32)[:, None] * frequency[None, :]
    return (jnp.cos(angles), jnp.sin(angles))


def rotate(field, cosine, sine_part):
    row_count = field.shape[0]
    half_size = cosine.shape[-1]
    split_heads = field.reshape(row_count, -1, 2 * half_size)
    front_half = split_heads[..., :half_size]
    back_half = split_heads[..., half_size:]
    cos_rows = cosine[:, None, :]
    sin_rows = sine_part[:, None, :]
    turned = jnp.concatenate(
        [
            front_half * cos_rows - back_half * sin_rows,
            back_half * cos_rows + front_half * sin_rows,
        ],
        axis=-1,
    )
    return turned.reshape(row_count, -1)


def rms_back(d_normed, normed, scale):
    return scale * (d_normed - normed * jnp.mean(d_normed * normed, axis=-1, keepdims=True))


def score_block(query_part, key_part, visible):
    scores = jnp.einsum(
        "rgd,kd->grk", query_part, key_part, preferred_element_type=jnp.float32
    ) * HEAD_SIZE ** (-0.5)
    return jnp.where(visible[None], scores, MASKED)


def attend_pack(query_pack, key_pack, value_pack, visible_list):
    token_count = query_pack.shape[0]
    rounds = len(visible_list)
    query_group_width = QUERY_HEADS // KEY_VALUE_HEADS
    context_count = key_pack.shape[0] // token_count

    def width_per_head(head_index, carry):
        out_buf, total_buf = carry
        query_head = lax.dynamic_slice_in_dim(
            query_pack, head_index * query_group_width * HEAD_SIZE, query_group_width * HEAD_SIZE, 1
        ).reshape(token_count, query_group_width, HEAD_SIZE)
        key_head = lax.dynamic_slice_in_dim(key_pack, head_index * HEAD_SIZE, HEAD_SIZE, 1).reshape(
            context_count, rounds, BLK, HEAD_SIZE
        )
        value_head = lax.dynamic_slice_in_dim(
            value_pack, head_index * HEAD_SIZE, HEAD_SIZE, 1
        ).reshape(context_count, rounds, BLK, HEAD_SIZE)
        running_top = jnp.full((query_group_width, token_count), MASKED, jnp.float32)
        running_sum = jnp.zeros((query_group_width, token_count), jnp.float32)
        for round_index in range(rounds):
            first_row = round_index * BLK
            scores = score_block(
                query_head[first_row:],
                key_head[:, round_index].reshape(-1, HEAD_SIZE),
                visible_list[round_index],
            )
            new_top = jnp.maximum(running_top[:, first_row:], jnp.max(scores, axis=-1))
            weights = jnp.where(
                visible_list[round_index][None], jnp.exp(scores - new_top[..., None]), 0.0
            )
            new_sum = running_sum[:, first_row:] * jnp.exp(
                running_top[:, first_row:] - new_top
            ) + jnp.sum(weights, axis=-1)
            running_top = running_top.at[:, first_row:].set(new_top)
            running_sum = running_sum.at[:, first_row:].set(new_sum)
        log_totals = running_top + jnp.log(running_sum)
        mixture = jnp.zeros((token_count, query_group_width, HEAD_SIZE), jnp.float32)
        for round_index in range(rounds):
            first_row = round_index * BLK
            scores = score_block(
                query_head[first_row:],
                key_head[:, round_index].reshape(-1, HEAD_SIZE),
                visible_list[round_index],
            )
            prob_bf = jnp.where(
                visible_list[round_index][None],
                jnp.exp(scores - log_totals[:, first_row:, None]),
                0.0,
            ).astype(jnp.bfloat16)
            mixture = mixture.at[first_row:].add(
                jnp.einsum(
                    "grk,kd->rgd",
                    prob_bf,
                    value_head[:, round_index].reshape(-1, HEAD_SIZE),
                    preferred_element_type=jnp.float32,
                )
            )
        out_buf = lax.dynamic_update_slice_in_dim(
            out_buf,
            mixture.astype(jnp.bfloat16).reshape(token_count, -1),
            head_index * query_group_width * HEAD_SIZE,
            1,
        )
        total_buf = lax.dynamic_update_slice_in_dim(
            total_buf, log_totals, head_index * query_group_width, 0
        )
        return (out_buf, total_buf)

    start_offsets = (
        jnp.zeros((token_count, QUERY_HEADS * HEAD_SIZE), jnp.bfloat16),
        jnp.zeros((QUERY_HEADS, token_count), jnp.float32),
    )
    return lax.fori_loop(0, KEY_VALUE_HEADS, width_per_head, start_offsets)


def attend_back(
    query_pack, key_pack, value_pack, grad_pack, attended_pack, total_pack, visible_list
):
    token_count = query_pack.shape[0]
    rounds = len(visible_list)
    query_group_width = QUERY_HEADS // KEY_VALUE_HEADS
    context_count = key_pack.shape[0] // token_count

    def width_per_head(head_index, carry):
        query_buf, key_buf, value_buf = carry
        query_head = lax.dynamic_slice_in_dim(
            query_pack, head_index * query_group_width * HEAD_SIZE, query_group_width * HEAD_SIZE, 1
        ).reshape(token_count, query_group_width, HEAD_SIZE)
        grad_head = lax.dynamic_slice_in_dim(
            grad_pack, head_index * query_group_width * HEAD_SIZE, query_group_width * HEAD_SIZE, 1
        ).reshape(token_count, query_group_width, HEAD_SIZE)
        output_head = lax.dynamic_slice_in_dim(
            attended_pack,
            head_index * query_group_width * HEAD_SIZE,
            query_group_width * HEAD_SIZE,
            1,
        ).reshape(token_count, query_group_width, HEAD_SIZE)
        key_head = lax.dynamic_slice_in_dim(key_pack, head_index * HEAD_SIZE, HEAD_SIZE, 1).reshape(
            context_count, rounds, BLK, HEAD_SIZE
        )
        value_head = lax.dynamic_slice_in_dim(
            value_pack, head_index * HEAD_SIZE, HEAD_SIZE, 1
        ).reshape(context_count, rounds, BLK, HEAD_SIZE)
        log_totals = lax.dynamic_slice_in_dim(
            total_pack, head_index * query_group_width, query_group_width, 0
        )
        delta = jnp.sum(grad_head.astype(jnp.float32) * output_head.astype(jnp.float32), axis=-1).T
        query_grad = jnp.zeros((token_count, query_group_width, HEAD_SIZE), jnp.float32)
        key_parts = []
        value_parts = []
        for round_index in range(rounds):
            first_row = round_index * BLK
            key_round = key_head[:, round_index].reshape(-1, HEAD_SIZE)
            value_round = value_head[:, round_index].reshape(-1, HEAD_SIZE)
            scores = score_block(query_head[first_row:], key_round, visible_list[round_index])
            probs_full = jnp.where(
                visible_list[round_index][None],
                jnp.exp(scores - log_totals[:, first_row:, None]),
                0.0,
            )
            d_probs = jnp.einsum(
                "rgd,kd->grk",
                grad_head[first_row:],
                value_round,
                preferred_element_type=jnp.float32,
            )
            d_scores = (
                HEAD_SIZE ** (-0.5) * probs_full * (d_probs - delta[:, first_row:, None])
            ).astype(jnp.bfloat16)
            value_parts.append(
                jnp.einsum(
                    "grk,rgd->kd",
                    probs_full.astype(jnp.bfloat16),
                    grad_head[first_row:],
                    preferred_element_type=jnp.float32,
                )
            )
            key_parts.append(
                jnp.einsum(
                    "grk,rgd->kd",
                    d_scores,
                    query_head[first_row:],
                    preferred_element_type=jnp.float32,
                )
            )
            query_grad = query_grad.at[first_row:].add(
                jnp.einsum("grk,kd->rgd", d_scores, key_round, preferred_element_type=jnp.float32)
            )
        key_block = jnp.stack(
            [part.reshape(context_count, BLK, HEAD_SIZE) for part in key_parts], axis=1
        ).reshape(-1, HEAD_SIZE)
        value_block = jnp.stack(
            [part.reshape(context_count, BLK, HEAD_SIZE) for part in value_parts], axis=1
        ).reshape(-1, HEAD_SIZE)
        query_buf = lax.dynamic_update_slice_in_dim(
            query_buf,
            query_grad.reshape(token_count, -1),
            head_index * query_group_width * HEAD_SIZE,
            1,
        )
        key_buf = lax.dynamic_update_slice_in_dim(key_buf, key_block, head_index * HEAD_SIZE, 1)
        value_buf = lax.dynamic_update_slice_in_dim(
            value_buf, value_block, head_index * HEAD_SIZE, 1
        )
        return (query_buf, key_buf, value_buf)

    start_offsets = (
        jnp.zeros((token_count, QUERY_HEADS * HEAD_SIZE), jnp.float32),
        jnp.zeros((context_count * token_count, KEY_VALUE_HEADS * HEAD_SIZE), jnp.float32),
        jnp.zeros((context_count * token_count, KEY_VALUE_HEADS * HEAD_SIZE), jnp.float32),
    )
    return lax.fori_loop(0, KEY_VALUE_HEADS, width_per_head, start_offsets)


def local(
    tokens,
    seq_lengths,
    dealing,
    first_gain,
    query_weight,
    key_matrix,
    value_matrix,
    out_weight,
    second_gain,
    gate_weight,
    up_weight,
    down_weight,
    cotangent,
):
    context_count = lax.axis_size("ctx")
    my_index = lax.axis_index("ctx")
    pack_count, token_count, model_dim = tokens.shape
    rounds = token_count // BLK
    spread = context_count // rounds
    ctx_range = jnp.arange(context_count, dtype=jnp.int32)
    matches = (dealing[..., None] == ctx_range).astype(jnp.int32)
    slot_of = jnp.sum(matches * ctx_range[:, None], axis=2)
    block_of = jnp.arange(rounds, dtype=jnp.int32)[None, :, None] * context_count + slot_of
    key_pos = (
        jnp.transpose(block_of, (0, 2, 1))[..., None] * BLK + jnp.arange(BLK, dtype=jnp.int32)
    ).reshape(pack_count, -1)
    key_seg = place_rows(key_pos, seq_lengths)[0]
    query_pos = lax.dynamic_slice_in_dim(key_pos, my_index * token_count, token_count, 1)
    query_seg, query_rel = place_rows(query_pos, seq_lengths)
    home_row = lax.dynamic_index_in_dim(dealing, my_index // spread, 1, False)
    targets = lax.dynamic_slice_in_dim(home_row, my_index % spread * rounds, rounds, 1)
    picker = (targets[:, None, :] == ctx_range[None, :, None]).astype(jnp.bfloat16)
    my_slots = lax.dynamic_index_in_dim(slot_of, my_index, 2, False)
    owner_index = (
        jnp.arange(rounds, dtype=jnp.int32)[None, :] * context_count + my_slots
    ) // rounds
    keep_slot = jnp.repeat(owner_index, spread, axis=1) == ctx_range[None, :]

    def spread_out(field):
        blocks = field.reshape(pack_count, rounds, BLK, model_dim)
        return jnp.einsum(
            "pkj,pjtd->pktd", picker, blocks, preferred_element_type=jnp.float32
        ).astype(jnp.bfloat16)

    def collect(received):
        grouped = received.reshape(pack_count, rounds, spread, BLK, model_dim)
        return (
            jnp.sum(grouped, axis=2, dtype=jnp.float32)
            .astype(jnp.bfloat16)
            .reshape(pack_count * token_count, model_dim)
        )

    def send_home(field):
        blocks = jnp.repeat(field.reshape(pack_count, rounds, BLK, model_dim), spread, axis=1)
        return jnp.where(keep_slot[:, :, None, None], blocks, jnp.zeros_like(blocks))

    def restore(returned):
        placed = jnp.einsum("pkj,pktd->pjtd", picker, returned, preferred_element_type=jnp.float32)
        return placed.astype(jnp.bfloat16).reshape(pack_count, token_count, model_dim)

    dealt_tokens, dealt_upstream = (
        lax.all_to_all(spread_out(tokens), "ctx", split_axis=1, concat_axis=1, tiled=True),
        lax.all_to_all(spread_out(cotangent), "ctx", split_axis=1, concat_axis=1, tiled=True),
    )
    inputs = collect(dealt_tokens)
    upstream = collect(dealt_upstream)
    gain_one, query_full, key_full, value_full, out_full = (
        lax.all_gather(first_gain, "fsdp", axis=0, tiled=True),
        lax.all_gather(query_weight, "fsdp", axis=0, tiled=True),
        lax.all_gather(key_matrix, "fsdp", axis=0, tiled=True),
        lax.all_gather(value_matrix, "fsdp", axis=0, tiled=True),
        lax.all_gather(out_weight, "fsdp", axis=0, tiled=True),
    )
    gain_two, gate_full, up_full, down_full = (
        lax.all_gather(second_gain, "fsdp", axis=0, tiled=True),
        lax.all_gather(gate_weight, "fsdp", axis=0, tiled=True),
        lax.all_gather(up_weight, "fsdp", axis=0, tiled=True),
        lax.all_gather(down_weight, "fsdp", axis=0, tiled=True),
    )
    gain_one32 = gain_one.astype(jnp.float32)
    gain_two32 = gain_two.astype(jnp.float32)
    cosine, sine_part = rotation(query_rel.reshape(-1), HEAD_SIZE // 2)
    inputs32 = inputs.astype(jnp.float32)
    scale_one = lax.rsqrt(jnp.mean(inputs32 * inputs32, axis=-1, keepdims=True) + EPS)
    normed_one = inputs32 * scale_one
    xn_one = (normed_one * gain_one32).astype(jnp.bfloat16)
    query_rot = rotate(
        jnp.dot(xn_one, query_full, preferred_element_type=jnp.float32), cosine, sine_part
    ).astype(jnp.bfloat16)
    key_rot = rotate(
        jnp.dot(xn_one, key_full, preferred_element_type=jnp.float32), cosine, sine_part
    ).astype(jnp.bfloat16)
    rows_of_values = jnp.dot(xn_one, value_full, preferred_element_type=jnp.float32).astype(
        jnp.bfloat16
    )
    key_local = key_rot.reshape(pack_count, token_count, -1)
    value_local = rows_of_values.reshape(pack_count, token_count, -1)
    gathered_keys, gathered_values = (
        lax.all_gather(key_local, "ctx", axis=1, tiled=True),
        lax.all_gather(value_local, "ctx", axis=1, tiled=True),
    )
    key_pos_rounds = key_pos.reshape(pack_count, context_count, rounds, BLK)
    key_seg_rounds = key_seg.reshape(pack_count, context_count, rounds, BLK)
    visible = []
    for round_index in range(rounds):
        first_row = round_index * BLK
        round_pos = key_pos_rounds[:, :, round_index].reshape(pack_count, -1)
        round_seg = key_seg_rounds[:, :, round_index].reshape(pack_count, -1)
        same_seq = query_seg[:, first_row:, None] == round_seg[:, None, :]
        earlier = round_pos[:, None, :] <= query_pos[:, first_row:, None]
        visible.append(same_seq & earlier)
    query_packs = query_rot.reshape(pack_count, token_count, -1)
    pack_index = 0
    pack_visible = [mask[pack_index] for mask in visible]
    attended_pack, total_pack = attend_pack(
        query_packs[pack_index],
        gathered_keys[pack_index],
        gathered_values[pack_index],
        pack_visible,
    )
    total_list = [total_pack]
    softmax_totals = jnp.stack(total_list, axis=0)
    hidden_in = inputs32 + jnp.dot(attended_pack, out_full, preferred_element_type=jnp.float32)
    scale_two = lax.rsqrt(jnp.mean(hidden_in * hidden_in, axis=-1, keepdims=True) + EPS)
    normed_two = hidden_in * scale_two
    xn_two = (normed_two * gain_two32).astype(jnp.bfloat16)
    gate_val = jnp.dot(xn_two, gate_full, preferred_element_type=jnp.float32)
    up_val = jnp.dot(xn_two, up_full, preferred_element_type=jnp.float32)
    activated = jax.nn.silu(gate_val)
    hidden = (activated * up_val).astype(jnp.bfloat16)
    result = (hidden_in + jnp.dot(hidden, down_full, preferred_element_type=jnp.float32)).astype(
        jnp.bfloat16
    )
    down_grad = jnp.dot(hidden.T, upstream, preferred_element_type=jnp.float32)
    d_hidden = jnp.dot(upstream, down_full.T, preferred_element_type=jnp.float32)
    sigmoid_gate = jax.nn.sigmoid(gate_val)
    d_gate = (d_hidden * up_val * sigmoid_gate * (1.0 + gate_val * (1.0 - sigmoid_gate))).astype(
        jnp.bfloat16
    )
    d_up = (d_hidden * activated).astype(jnp.bfloat16)
    gate_grad = jnp.dot(xn_two.T, d_gate, preferred_element_type=jnp.float32)
    up_grad = jnp.dot(xn_two.T, d_up, preferred_element_type=jnp.float32)
    d_norm_two = jnp.dot(d_gate, gate_full.T, preferred_element_type=jnp.float32) + jnp.dot(
        d_up, up_full.T, preferred_element_type=jnp.float32
    )
    gain_two_grad = jnp.sum(d_norm_two * normed_two, axis=0)
    d_hidden_in = upstream.astype(jnp.float32) + rms_back(
        d_norm_two * gain_two32, normed_two, scale_two
    )
    mlp_parts = (
        lax.psum_scatter(
            gain_two_grad.astype(jnp.bfloat16), "fsdp", scatter_dimension=0, tiled=True
        ).astype(jnp.float32),
        lax.psum_scatter(
            gate_grad.astype(jnp.bfloat16), "fsdp", scatter_dimension=0, tiled=True
        ).astype(jnp.float32),
        lax.psum_scatter(
            up_grad.astype(jnp.bfloat16), "fsdp", scatter_dimension=0, tiled=True
        ).astype(jnp.float32),
        lax.psum_scatter(
            down_grad.astype(jnp.bfloat16), "fsdp", scatter_dimension=0, tiled=True
        ).astype(jnp.float32),
    )
    d_branch = d_hidden_in.astype(jnp.bfloat16)
    out_grad = jnp.dot(attended_pack.T, d_branch, preferred_element_type=jnp.float32)
    d_attended = jnp.dot(d_branch, out_full.T, preferred_element_type=jnp.float32).astype(
        jnp.bfloat16
    )
    back_keys, back_values = (gathered_keys, gathered_values)
    grad_packs = d_attended.reshape(pack_count, token_count, -1)
    out_packs = attended_pack.reshape(pack_count, token_count, -1)
    pack_index = 0
    pack_visible = [mask[pack_index] for mask in visible]
    query_part, key_part, value_part = attend_back(
        query_packs[pack_index],
        back_keys[pack_index],
        back_values[pack_index],
        grad_packs[pack_index],
        out_packs[pack_index],
        softmax_totals[pack_index],
        pack_visible,
    )
    key_list = [key_part]
    value_list = [value_part]
    d_keys, d_values = (
        lax.psum_scatter(
            jnp.stack(key_list, axis=0).astype(jnp.bfloat16), "ctx", scatter_dimension=1, tiled=True
        ).astype(jnp.float32),
        lax.psum_scatter(
            jnp.stack(value_list, axis=0).astype(jnp.bfloat16),
            "ctx",
            scatter_dimension=1,
            tiled=True,
        ).astype(jnp.float32),
    )
    d_query = rotate(query_part, cosine, -sine_part).astype(jnp.bfloat16)
    d_key = rotate(d_keys.reshape(pack_count * token_count, -1), cosine, -sine_part).astype(
        jnp.bfloat16
    )
    d_value = d_values.reshape(pack_count * token_count, -1).astype(jnp.bfloat16)
    query_grad = jnp.dot(xn_one.T, d_query, preferred_element_type=jnp.float32)
    key_grad = jnp.dot(xn_one.T, d_key, preferred_element_type=jnp.float32)
    value_grad = jnp.dot(xn_one.T, d_value, preferred_element_type=jnp.float32)
    d_norm_one = (
        jnp.dot(d_query, query_full.T, preferred_element_type=jnp.float32)
        + jnp.dot(d_key, key_full.T, preferred_element_type=jnp.float32)
        + jnp.dot(d_value, value_full.T, preferred_element_type=jnp.float32)
    )
    gain_one_grad = jnp.sum(d_norm_one * normed_one, axis=0)
    d_inputs = d_hidden_in + rms_back(d_norm_one * gain_one32, normed_one, scale_one)
    attn_parts = (
        lax.psum_scatter(
            gain_one_grad.astype(jnp.bfloat16), "fsdp", scatter_dimension=0, tiled=True
        ).astype(jnp.float32),
        lax.psum_scatter(
            query_grad.astype(jnp.bfloat16), "fsdp", scatter_dimension=0, tiled=True
        ).astype(jnp.float32),
        lax.psum_scatter(
            key_grad.astype(jnp.bfloat16), "fsdp", scatter_dimension=0, tiled=True
        ).astype(jnp.float32),
        lax.psum_scatter(
            value_grad.astype(jnp.bfloat16), "fsdp", scatter_dimension=0, tiled=True
        ).astype(jnp.float32),
        lax.psum_scatter(
            out_grad.astype(jnp.bfloat16), "fsdp", scatter_dimension=0, tiled=True
        ).astype(jnp.float32),
    )
    finished = (
        lax.psum(attn_parts[0].astype(jnp.bfloat16), ("ctx", "grp")).astype(jnp.float32),
        lax.psum(attn_parts[1].astype(jnp.bfloat16), ("ctx", "grp")).astype(jnp.float32),
        lax.psum(attn_parts[2].astype(jnp.bfloat16), ("ctx", "grp")).astype(jnp.float32),
        lax.psum(attn_parts[3].astype(jnp.bfloat16), ("ctx", "grp")).astype(jnp.float32),
        lax.psum(attn_parts[4].astype(jnp.bfloat16), ("ctx", "grp")).astype(jnp.float32),
        lax.psum(mlp_parts[0].astype(jnp.bfloat16), ("ctx", "grp")).astype(jnp.float32),
        lax.psum(mlp_parts[1].astype(jnp.bfloat16), ("ctx", "grp")).astype(jnp.float32),
        lax.psum(mlp_parts[2].astype(jnp.bfloat16), ("ctx", "grp")).astype(jnp.float32),
        lax.psum(mlp_parts[3].astype(jnp.bfloat16), ("ctx", "grp")).astype(jnp.float32),
    )
    home_out, home_grad = (
        lax.all_to_all(send_home(result), "ctx", split_axis=1, concat_axis=1, tiled=True),
        lax.all_to_all(
            send_home(d_inputs.astype(jnp.bfloat16)), "ctx", split_axis=1, concat_axis=1, tiled=True
        ),
    )
    return (
        restore(home_out),
        restore(home_grad),
        softmax_totals,
        finished[0],
        finished[1],
        finished[2],
        finished[3],
        finished[4],
        finished[5],
        finished[6],
        finished[7],
        finished[8],
    )


MINLEN = 1024
QB = 256
VMEM_LIMIT = 56 * 1024 * 1024


def attend_kernel(
    place, q_ref, k_ref, v_ref, c_ref, s_ref, keep_ref, send_ref, lse_ref, qr_ref, kr_ref, vr_ref
):
    cosine = c_ref[...]
    sine = s_ref[...]
    half = HEAD_SIZE // 2
    seq = cosine.shape[1]

    def turn(field):
        front, back = field[:half], field[half:]
        return jnp.concatenate(
            [front * cosine - back * sine, back * cosine + front * sine], axis=0
        )

    k_rot = turn(k_ref[...])
    kr_ref[...] = k_rot.astype(jnp.bfloat16)
    key = k_rot.T.astype(jnp.bfloat16)
    val_t = v_ref[...].astype(jnp.bfloat16)
    vr_ref[...] = val_t
    q0 = turn(q_ref[:HEAD_SIZE]).astype(jnp.bfloat16)
    q1 = turn(q_ref[HEAD_SIZE:]).astype(jnp.bfloat16)
    qr_ref[:HEAD_SIZE] = q0
    qr_ref[HEAD_SIZE:] = q1
    rows = lax.broadcasted_iota(jnp.int32, (QB, 2 * QB), 0)
    cols = lax.broadcasted_iota(jnp.int32, (QB, 2 * QB), 1)
    keep = rows <= jnp.where(cols >= QB, cols - QB, cols)
    for b in range(seq // QB):
        lo, n = b * QB, (b + 1) * QB
        q_t = jnp.concatenate([q0[:, lo:n], q1[:, lo:n]], axis=1)
        scores = jnp.dot(key[:n], q_t, preferred_element_type=jnp.float32) * HEAD_SIZE ** (-0.5)
        diag = jnp.where(keep, scores[lo:], MASKED)
        top = jnp.max(diag, axis=0, keepdims=True)
        if b > 0:
            top = jnp.maximum(top, jnp.max(scores[:lo], axis=0, keepdims=True))
        e_diag = jnp.exp(diag - top)
        total = jnp.sum(e_diag, axis=0, keepdims=True)
        out = jnp.dot(val_t[:, lo:n], e_diag.astype(jnp.bfloat16), preferred_element_type=jnp.float32)
        if b > 0:
            e_rest = jnp.exp(scores[:lo] - top)
            total = total + jnp.sum(e_rest, axis=0, keepdims=True)
            out = out + jnp.dot(
                val_t[:, :lo], e_rest.astype(jnp.bfloat16), preferred_element_type=jnp.float32
            )
        out = (out / total).astype(jnp.bfloat16)
        tok = seq // 2
        col = slice(lo % tok, lo % tok + QB)

        def store(ref):
            ref[:HEAD_SIZE, col] = out[:, :QB]
            ref[HEAD_SIZE:, col] = out[:, QB:]

        @pl.when(place[0] == lo // tok)
        def _():
            store(keep_ref)

        @pl.when(place[0] != lo // tok)
        def _():
            store(send_ref)

        lse = top + jnp.log(total)
        lse_ref[0, 0:1, lo:n] = lse[:, :QB]
        lse_ref[0, 1:2, lo:n] = lse[:, QB:]


def attend_seq(place, qkv_t, cosine, sine):
    rows, seq = qkv_t.shape
    kv = rows // (4 * HEAD_SIZE)
    group = pl.BlockSpec((2 * HEAD_SIZE, seq), lambda j: (j, 0))

    def head(base):
        return pl.BlockSpec((HEAD_SIZE, seq), lambda j: (base + j, 0))

    table = pl.BlockSpec((HEAD_SIZE // 2, seq), lambda j: (0, 0))
    return pl.pallas_call(
        attend_kernel,
        grid=(kv,),
        in_specs=[pl.BlockSpec(memory_space=pltpu.SMEM), group, head(2 * kv), head(3 * kv), table, table],
        out_specs=[
            pl.BlockSpec((2 * HEAD_SIZE, seq // 2), lambda j: (j, 0)),
            pl.BlockSpec((2 * HEAD_SIZE, seq // 2), lambda j: (j, 0)),
            pl.BlockSpec((1, 2, seq), lambda j: (j, 0, 0)),
            group,
            head(0),
            head(0),
        ],
        out_shape=[
            jax.ShapeDtypeStruct((2 * kv * HEAD_SIZE, seq // 2), jnp.bfloat16),
            jax.ShapeDtypeStruct((2 * kv * HEAD_SIZE, seq // 2), jnp.bfloat16),
            jax.ShapeDtypeStruct((kv, 2, seq), jnp.float32),
            jax.ShapeDtypeStruct((2 * kv * HEAD_SIZE, seq), jnp.bfloat16),
            jax.ShapeDtypeStruct((kv * HEAD_SIZE, seq), jnp.bfloat16),
            jax.ShapeDtypeStruct((kv * HEAD_SIZE, seq), jnp.bfloat16),
        ],
        compiler_params=pltpu.CompilerParams(vmem_limit_bytes=VMEM_LIMIT),
        cost_estimate=pl.CostEstimate(
            flops=4 * kv * 2 * seq * seq * HEAD_SIZE, bytes_accessed=10 * rows * seq, transcendentals=kv * seq * seq
        ),
        name="attend",
    )(place, qkv_t, qkv_t, qkv_t, cosine, sine)


def attend_back_kernel(
    place, q_ref, k_ref, v_ref, keep_ref, got_ref, lse_ref, c_ref, s_ref,
    dq_ref, dk_ref, dv_ref, dk_acc, dv_acc,
):
    half = HEAD_SIZE // 2
    cosine = c_ref[...]
    sine = s_ref[...]
    seq = cosine.shape[1]

    def turn_back(field, cos, sin):
        front, back = field[:half], field[half:]
        return jnp.concatenate([front * cos + back * sin, back * cos - front * sin], axis=0)

    def flip(field):
        return field.astype(jnp.float32).T.astype(jnp.bfloat16)

    key_t = k_ref[...]
    key = flip(key_t)
    val = flip(v_ref[...])
    q0_t, q1_t = q_ref[:HEAD_SIZE], q_ref[HEAD_SIZE:]
    first_core = place[0] == 0
    early = jnp.where(first_core, keep_ref[...], got_ref[...])
    late = jnp.where(first_core, got_ref[...], keep_ref[...])
    grads = jnp.concatenate([early, late], axis=1)
    g0_t, g1_t = grads[:HEAD_SIZE], grads[HEAD_SIZE:]
    q0, q1, g0, g1 = flip(q0_t), flip(q1_t), flip(g0_t), flip(g1_t)
    dk_acc[...] = jnp.zeros_like(dk_acc)
    dv_acc[...] = jnp.zeros_like(dv_acc)
    rows = lax.broadcasted_iota(jnp.int32, (QB, 2 * QB), 0)
    cols = lax.broadcasted_iota(jnp.int32, (QB, 2 * QB), 1)
    keep = rows <= jnp.where(cols >= QB, cols - QB, cols)
    for b in range(seq // QB):
        lo, n = b * QB, (b + 1) * QB
        q_t = jnp.concatenate([q0_t[:, lo:n], q1_t[:, lo:n]], axis=1)
        g_t = jnp.concatenate([g0_t[:, lo:n], g1_t[:, lo:n]], axis=1)
        q_n = jnp.concatenate([q0[lo:n], q1[lo:n]], axis=0)
        g_n = jnp.concatenate([g0[lo:n], g1[lo:n]], axis=0)
        lse = jnp.concatenate([lse_ref[0, 0:1, lo:n], lse_ref[0, 1:2, lo:n]], axis=1)
        parts = []
        delta = None
        for start, stop in ([(0, lo)] if b > 0 else []) + [(lo, n)]:
            scores = jnp.dot(key[start:stop], q_t, preferred_element_type=jnp.float32) * HEAD_SIZE ** (-0.5)
            prob = jnp.exp(scores - lse)
            if start == lo:
                prob = jnp.where(keep, prob, 0.0)
            d_prob = jnp.dot(val[start:stop], g_t, preferred_element_type=jnp.float32)
            part = jnp.sum(prob * d_prob, axis=0, keepdims=True)
            delta = part if delta is None else delta + part
            dv_acc[start:stop] += jnp.dot(prob.astype(jnp.bfloat16), g_n, preferred_element_type=jnp.float32)
            parts.append((start, stop, prob, d_prob))
        dq_t = None
        for start, stop, prob, d_prob in parts:
            d_score = (prob * (d_prob - delta) * HEAD_SIZE ** (-0.5)).astype(jnp.bfloat16)
            dk_acc[start:stop] += jnp.dot(d_score, q_n, preferred_element_type=jnp.float32)
            part = jnp.dot(key_t[:, start:stop], d_score, preferred_element_type=jnp.float32)
            dq_t = part if dq_t is None else dq_t + part
        cos, sin = cosine[:, lo:n], sine[:, lo:n]
        dq_ref[:HEAD_SIZE, lo:n] = turn_back(dq_t[:, :QB], cos, sin).astype(jnp.bfloat16)
        dq_ref[HEAD_SIZE:, lo:n] = turn_back(dq_t[:, QB:], cos, sin).astype(jnp.bfloat16)
    dk_ref[...] = turn_back(dk_acc[...].T, cosine, sine).astype(jnp.bfloat16)
    dv_ref[...] = dv_acc[...].T.astype(jnp.bfloat16)


def attend_seq_back(place, q_t, k_t, v_t, g_keep, g_got, lse, cosine, sine):
    rows, seq = k_t.shape
    kv = rows // HEAD_SIZE
    group = pl.BlockSpec((2 * HEAD_SIZE, seq), lambda j: (j, 0))
    part = pl.BlockSpec((2 * HEAD_SIZE, seq // 2), lambda j: (j, 0))
    head = pl.BlockSpec((HEAD_SIZE, seq), lambda j: (j, 0))
    table = pl.BlockSpec((HEAD_SIZE // 2, seq), lambda j: (0, 0))
    return pl.pallas_call(
        attend_back_kernel,
        grid=(kv,),
        in_specs=[
            pl.BlockSpec(memory_space=pltpu.SMEM), group, head, head, part, part,
            pl.BlockSpec((1, 2, seq), lambda j: (j, 0, 0)), table, table,
        ],
        out_specs=[group, head, head],
        out_shape=[
            jax.ShapeDtypeStruct((2 * rows, seq), jnp.bfloat16),
            jax.ShapeDtypeStruct((rows, seq), jnp.bfloat16),
            jax.ShapeDtypeStruct((rows, seq), jnp.bfloat16),
        ],
        scratch_shapes=[
            pltpu.VMEM((seq, HEAD_SIZE), jnp.float32),
            pltpu.VMEM((seq, HEAD_SIZE), jnp.float32),
        ],
        compiler_params=pltpu.CompilerParams(vmem_limit_bytes=VMEM_LIMIT),
        cost_estimate=pl.CostEstimate(
            flops=10 * kv * 2 * seq * seq * HEAD_SIZE, bytes_accessed=20 * rows * seq, transcendentals=kv * seq * seq
        ),
        name="attend_back",
    )(place, q_t, k_t, v_t, g_keep, g_got, lse, cosine, sine)


def fp32(field):
    return field.astype(jnp.float32)


def mm(left, right, dims=((1,), (0,)), out=jnp.float32):
    return lax.dot_general(left, right, (dims, ((), ())), preferred_element_type=out)


ANY = pl.BlockSpec(memory_space=pl.ANY)
SMEM = pl.BlockSpec(memory_space=pltpu.SMEM)
VM = pl.BlockSpec(memory_space=pltpu.VMEM)
PARAMS = pltpu.CompilerParams(vmem_limit_bytes=VMEM_LIMIT)
MESH = pl.DeviceIdType.MESH
TILE = 256


def bf16_like(*dims):
    return jax.ShapeDtypeStruct(dims, jnp.bfloat16)


def f32_like(*dims):
    return jax.ShapeDtypeStruct(dims, jnp.float32)


def cost(flops, moved):
    return pl.CostEstimate(flops=int(flops), bytes_accessed=int(moved), transcendentals=0)


class Spots:
    def __init__(self):
        z, f, g = lax.axis_index("ctx"), lax.axis_index("fsdp"), lax.axis_index("grp")
        self.z, self.f, self.g = z, f, g
        self.parity = z % 2
        self.fx = f + 1 - 2 * (f % 2)
        self.fy = f + 2 - 4 * (f // 2)
        self.fd = 3 - f
        across = z + 1 - 2 * self.parity
        self.x = (z, self.fx, g)
        self.y = (z, self.fy, g)
        self.diag = (z, self.fd, g)
        self.core = (z, f, 1 - g)
        self.across = (across, f, g)
        self.swap = (across, f, 1 - g)


def greet(*partners):
    barrier = pltpu.get_barrier_semaphore()
    for partner in partners:
        pl.semaphore_signal(barrier, inc=1, device_id=partner, device_id_type=MESH)
    pl.semaphore_wait(barrier, len(partners))


def rows_at(start, size):
    return pl.ds(pl.multiple_of(start, size), size)


def gather_kernel(
    tokens, cotangent, wq, wk, wv, wo, gate, up, gain,
    qkv_o, out_o, pair_o, x_o, dy_o, gain_o,
    send, recv, near, far, qkv_v, out_v, pair_v, tok_v, gain_v,
):
    at = Spots()
    g, f, parity = at.g, at.f, at.parity
    greet(at.x, at.y, at.diag, at.core, at.across, at.swap)
    taken = [0, 0]

    def remote(src, dst, device):
        i = taken[0]
        taken[0] += 1
        return pltpu.make_async_remote_copy(
            src_ref=src, dst_ref=dst, send_sem=send.at[i], recv_sem=recv.at[i],
            device_id=device, device_id_type=MESH,
        )

    class Bounce:
        def __init__(self, src, via, dst):
            i = taken[1]
            taken[1] += 1
            self.first = pltpu.make_async_copy(src, via, near.at[i])
            self.second = pltpu.make_async_copy(via, dst, far.at[i])

        def start(self):
            self.first.start()

        def turn(self):
            self.first.wait()
            self.second.start()

        def wait(self):
            self.second.wait()

    def start(copies):
        for copy in copies:
            copy.start()
        return copies

    def arrive(copies):
        for copy in copies:
            copy.wait_recv()

    tok = tokens.shape[1]
    feat = wq.shape[0]
    mid = feat // 2
    nq, nk, nv = (w.shape[1] // 2 for w in (wq, wk, wv))
    nf = gate.shape[1] // 8
    wide = wo.shape[1] // 2
    count = 4
    top, low = slice(0, mid), slice(mid, feat)

    mine = rows_at(g * tok, tok)
    swaps = [
        remote(tokens.at[0], x_o.at[mine], at.swap),
        remote(cotangent.at[0], dy_o.at[mine], at.swap),
    ]
    keeps = [
        Bounce(tokens.at[0], tok_v.at[0], x_o.at[mine]),
        Bounce(cotangent.at[0], tok_v.at[1], dy_o.at[mine]),
    ]
    away = rows_at((1 - g) * tok, tok)
    swaps_out = [
        pltpu.make_async_remote_copy(
            src_ref=array.at[0], dst_ref=into.at[away], send_sem=send.at[i], recv_sem=recv.at[i],
            device_id=at.swap, device_id_type=MESH,
        )
        for i, (array, into) in enumerate(((tokens, x_o), (cotangent, dy_o)))
    ]
    shares = [remote(x_o.at[mine], x_o.at[mine], at.core), remote(dy_o.at[mine], dy_o.at[mine], at.core)]

    @pl.when(g != parity)
    def _():
        start(swaps_out)

    @pl.when(g == parity)
    def _():
        start(keeps)
        for copy in keeps:
            copy.turn()

    own_rows = f * feat
    shared_cols = (count - 1) * nf

    def pair_direct(part, device):
        first = taken[0]
        taken[0] += count + 1
        rows = rows_at(own_rows + part.start, mid)

        def made(array, index, k, i):
            return pltpu.make_async_remote_copy(
                src_ref=array.at[part, rows_at((2 * k + g) * nf, nf)],
                dst_ref=pair_o.at[index, rows, rows_at(k * nf, nf)],
                send_sem=send.at[first + i], recv_sem=recv.at[first + i],
                device_id=device, device_id_type=MESH,
            )

        def some(array):
            return [made(array, parity, k, k) for k in range(count - 1)]

        @pl.when(parity == 0)
        def _():
            start(some(gate))

        @pl.when(parity == 1)
        def _():
            start(some(up))

        last = start([made(gate, 0, count - 1, count - 1), made(up, 1, count - 1, count)])
        return some(gate), last

    pair_xt, last_xt = pair_direct(top, at.x)
    pair_yl, last_yl = pair_direct(low, at.y)
    pair_xl, last_xl = pair_direct(low, at.x)
    pair_yt, last_yt = pair_direct(top, at.y)

    def qkv_direct(part, device):
        copies = []
        for array, width, column in ((wq, nq, 0), (wk, nk, nq), (wv, nv, nq + nk)):
            copies.append(
                remote(
                    array.at[part, rows_at(g * width, width)],
                    qkv_o.at[rows_at(own_rows + part.start, mid), column : column + width],
                    device,
                )
            )
        return start(copies)

    qkv_xt = qkv_direct(top, at.x)
    qkv_yl = qkv_direct(low, at.y)
    qkv_xl = qkv_direct(low, at.x)
    qkv_yt = qkv_direct(top, at.y)

    own = rows_at(own_rows, feat)
    locals_ = [
        Bounce(
            array.at[:, rows_at(g * width, width)],
            qkv_v.at[:, column : column + width],
            qkv_o.at[own, column : column + width],
        )
        for array, width, column in ((wq, nq, 0), (wk, nk, nq), (wv, nv, nq + nk))
    ]
    locals_.append(Bounce(wo, out_v, out_o.at[own]))
    for array, index in ((gate, 0), (up, 1)):
        for k in range(count):
            locals_.append(
                Bounce(
                    array.at[:, rows_at((2 * k + g) * nf, nf)],
                    pair_v.at[index, :, rows_at(k * nf, nf)],
                    pair_o.at[index, own, rows_at(k * nf, nf)],
                )
            )
    gain_place = gain_o.at[pl.ds(f, 1)]
    locals_.append(Bounce(gain, gain_v, gain_place))
    start(locals_)
    for copy in locals_:
        copy.turn()
    gains = start([remote(gain, gain_place, to) for to in (at.x, at.y, at.diag)])

    def forward(array_at, rows_x, rows_y):
        return remote(array_at(rows_x), array_at(rows_x), at.y), remote(
            array_at(rows_y), array_at(rows_y), at.x
        )

    x_top, y_low = rows_at(at.fx * feat, mid), rows_at(at.fy * feat + mid, mid)
    x_low, y_top = rows_at(at.fx * feat + mid, mid), rows_at(at.fy * feat, mid)
    d_top, d_low = rows_at(at.fd * feat, mid), rows_at(at.fd * feat + mid, mid)

    def pair_view(rows):
        return pair_o.at[parity, rows, 0:shared_cols]

    def last_view(rows):
        return pair_o.at[:, rows, shared_cols : shared_cols + nf]

    def out_view(rows):
        return out_o.at[rows, rows_at(g * wide, wide)]

    pair_fy, pair_fx = forward(pair_view, x_top, y_low)
    last_fy, last_fx = forward(last_view, x_top, y_low)
    sends = [pair_fy, pair_fx, last_fy, last_fx]

    def across(rows):
        copy = remote(pair_view(rows), pair_view(rows), at.across)
        copy.start()
        sends.append(copy)
        return copy

    arrive(pair_xt)
    pair_fy.start()
    z_copies = [across(x_top)]
    arrive(pair_yl)
    pair_fx.start()
    z_copies.append(across(y_low))

    def out_direct(part, device):
        copy = remote(
            wo.at[part, rows_at(g * wide, wide)],
            out_o.at[rows_at(own_rows + part.start, mid), rows_at(g * wide, wide)],
            device,
        )
        copy.start()
        return copy

    out_xt, out_yl = out_direct(top, at.x), out_direct(low, at.y)
    out_xl, out_yt = out_direct(low, at.x), out_direct(top, at.y)

    arrive(pair_xl)
    z_copies.append(across(x_low))
    arrive(pair_yt)
    z_copies.append(across(y_top))

    def qkv_view(rows):
        return qkv_o.at[rows]

    qkv_fy, qkv_fx = forward(qkv_view, x_top, y_low)
    arrive(qkv_xt)
    qkv_fy.start()
    arrive(qkv_yl)
    qkv_fx.start()
    arrive(last_xt)
    last_fy.start()
    arrive(last_yl)
    last_fx.start()

    pair_fy.wait_recv()
    z_copies.append(across(d_top))
    pair_fx.wait_recv()
    z_copies.append(across(d_low))

    for i in range(2):

        @pl.when(g != parity)
        def _():
            swaps[i].wait_recv()
            swaps_out[i].wait_send()

        @pl.when(g == parity)
        def _():
            keeps[i].wait()

        shares[i].start()

    out_fy, out_fx = forward(out_view, x_top, y_low)
    out_xt.wait_recv()
    out_fy.start()
    out_yl.wait_recv()
    out_fx.start()
    out_xl.wait_recv()
    out_yt.wait_recv()

    def share(rows):
        copy = remote(out_view(rows), out_view(rows), at.core)
        copy.start()
        return copy

    shared = [share(x_top), share(x_low), share(y_top), share(y_low)]

    out_fy.wait_recv()
    shared.append(share(d_top))
    out_fx.wait_recv()
    shared.append(share(d_low))

    arrive(qkv_xl)
    arrive(qkv_yt)
    arrive([qkv_fy, qkv_fx, last_fy, last_fx])
    arrive(last_xl + last_yt)
    arrive(gains)
    arrive(shares)
    arrive(shared)
    arrive(z_copies)
    for copy in locals_:
        copy.wait()
    for copy in (
        pair_xt + pair_yl + pair_xl + pair_yt + qkv_xt + qkv_yl + qkv_xl + qkv_yt + gains
        + sends + shares + shared
        + [out_xt, out_yl, out_xl, out_yt, out_fy, out_fx, qkv_fy, qkv_fx]
        + last_xt + last_yl + last_xl + last_yt
    ):
        copy.wait_send()


def gather_all(tokens, cotangent, wq, wk, wv, wo, gate, up, gain):
    tok, width = tokens.shape[1:]
    nf = gate.shape[1] // 8
    cols = (wq.shape[1] + wk.shape[1] + wv.shape[1]) // 2
    return pl.pallas_call(
        gather_kernel,
        in_specs=[ANY] * 9,
        out_specs=[ANY] * 6,
        out_shape=[
            bf16_like(width, cols),
            bf16_like(4 * wo.shape[0], width),
            bf16_like(2, width, 4 * nf),
            bf16_like(2 * tok, width),
            bf16_like(2 * tok, width),
            jax.ShapeDtypeStruct((4,) + gain.shape[1:], gain.dtype),
        ],
        scratch_shapes=[
            pltpu.SemaphoreType.DMA((72,)),
            pltpu.SemaphoreType.DMA((72,)),
            pltpu.SemaphoreType.DMA((20,)),
            pltpu.SemaphoreType.DMA((20,)),
            pltpu.VMEM((width // 4, cols), jnp.bfloat16),
            pltpu.VMEM(wo.shape, jnp.bfloat16),
            pltpu.VMEM((2, width // 4, 4 * nf), jnp.bfloat16),
            pltpu.VMEM((2, tok, width), jnp.bfloat16),
            pltpu.VMEM(gain.shape, gain.dtype),
        ],
        compiler_params=pltpu.CompilerParams(
            collective_id=0, has_side_effects=True, vmem_limit_bytes=VMEM_LIMIT
        ),
        cost_estimate=cost(0, 500e6),
        name="gather",
    )(tokens, cotangent, wq, wk, wv, wo, gate, up, gain)


def norm_scale(field):
    return lax.rsqrt(jnp.mean(field * field, axis=-1, keepdims=True) + EPS)


def project_kernel(x_ref, gain, w_ref, xn_ref, out_ref):
    seq = x_ref.shape[0]

    @pl.when(pl.program_id(0) == 0)
    def _():
        for part in range(seq // TILE):
            rows = slice(part * TILE, (part + 1) * TILE)
            field = fp32(x_ref[rows, :])
            xn_ref[rows, :] = (field * norm_scale(field) * gain[0:1, :]).astype(jnp.bfloat16)

    out_ref[...] = mm(w_ref[...].T, xn_ref[...], ((1,), (1,)))


def project(x_seq, gains, weight):
    seq, width = x_seq.shape
    cols = weight.shape[1]
    return pl.pallas_call(
        project_kernel,
        grid=(cols // TILE,),
        in_specs=[VM, VM, pl.BlockSpec((width, TILE), lambda n: (0, n))],
        out_specs=[VM, pl.BlockSpec((TILE, seq), lambda n: (n, 0))],
        out_shape=[bf16_like(seq, width), f32_like(cols, seq)],
        compiler_params=PARAMS,
        cost_estimate=cost(2 * seq * width * cols, 20e6),
        name="project",
    )(x_seq, gains, weight)


def residual_kernel(place, x_ref, attn_keep, attn_got, gain, w_ref, h_ref, xn_ref, attn_ref):
    core = place[0]
    heads = attn_keep.shape[0]
    keep_at, got_at = rows_at(core * heads, heads), rows_at((1 - core) * heads, heads)
    tok = h_ref.shape[0]
    attn_ref[keep_at, :] = attn_keep[...]
    attn_ref[got_at, :] = attn_got[...]
    field = mm(attn_keep[...].T, w_ref[keep_at, :])
    field = field + mm(attn_got[...].T, w_ref[got_at, :])
    h_ref[...] = field + fp32(x_ref[rows_at(core * tok, tok), :])
    for part in range(tok // TILE):
        rows = slice(part * TILE, (part + 1) * TILE)
        field = h_ref[rows, :]
        xn_ref[rows, :] = (field * norm_scale(field) * gain[1:2, :]).astype(jnp.bfloat16)


def residual(place, x_seq, attn_keep, attn_got, gains, weight):
    seq, width = x_seq.shape
    tok = seq // 2
    return pl.pallas_call(
        residual_kernel,
        in_specs=[SMEM] + [VM] * 5,
        out_specs=[VM, VM, VM],
        out_shape=[f32_like(tok, width), bf16_like(tok, width), bf16_like(weight.shape[0], tok)],
        compiler_params=PARAMS,
        cost_estimate=cost(2 * tok * width * weight.shape[0], 14e6),
        name="residual",
    )(place, x_seq, attn_keep, attn_got, gains, weight)


def hidden_kernel(place, xn_own, xn_got, gate_w, up_w, hid_ref, for_gate_ref, act_ref, xn_ref):
    @pl.when(pl.program_id(0) == 0)
    def _():
        tok = xn_own.shape[0]
        xn_ref[rows_at(place[0] * tok, tok), :] = xn_own[...]
        xn_ref[rows_at((1 - place[0]) * tok, tok), :] = xn_got[...]

    gate = mm(xn_ref[...], gate_w[0])
    up = mm(xn_ref[...], up_w[0])
    sig = 1.0 / (1.0 + jnp.exp(-gate))
    act = gate * sig
    hid_ref[...] = (act * up).astype(jnp.bfloat16)
    for_gate_ref[...] = (up * (sig + act * (1.0 - sig))).astype(jnp.bfloat16)
    act_ref[...] = act.astype(jnp.bfloat16)


def hidden_step(place, xn_own, xn_got, pair):
    seq, width = 2 * xn_own.shape[0], xn_own.shape[1]
    ff = pair.shape[2]
    block = pl.BlockSpec((seq, TILE), lambda n: (0, n))
    return pl.pallas_call(
        hidden_kernel,
        grid=(ff // TILE,),
        in_specs=[
            SMEM,
            VM,
            VM,
            pl.BlockSpec((1, width, TILE), lambda n: (0, 0, n)),
            pl.BlockSpec((1, width, TILE), lambda n: (1, 0, n)),
        ],
        out_specs=[block] * 3 + [VM],
        out_shape=[bf16_like(seq, ff)] * 3 + [bf16_like(seq, width)],
        compiler_params=PARAMS,
        cost_estimate=cost(4 * seq * width * ff, 30e6),
        name="hidden",
    )(place, xn_own, xn_got, pair, pair)


def hidden_back_kernel(dy_ref, down_w, for_gate_ref, act_ref, dgate_ref, dup_ref):
    d_hidden = mm(dy_ref[...], down_w[...], ((1,), (1,)))
    dgate_ref[...] = (d_hidden * fp32(for_gate_ref[...])).astype(jnp.bfloat16)
    dup_ref[...] = (d_hidden * fp32(act_ref[...])).astype(jnp.bfloat16)


def hidden_back(dy, down, for_gate, act):
    seq, width = dy.shape
    ff = down.shape[0]
    block = pl.BlockSpec((seq, TILE), lambda n: (0, n))
    return pl.pallas_call(
        hidden_back_kernel,
        grid=(ff // TILE,),
        in_specs=[VM, pl.BlockSpec((TILE, width), lambda n: (n, 0)), block, block],
        out_specs=[block] * 2,
        out_shape=[bf16_like(seq, ff)] * 2,
        compiler_params=PARAMS,
        cost_estimate=cost(2 * seq * width * ff, 26e6),
        name="hidden_back",
    )(dy, down, for_gate, act)


def back_kernel(place, dgate_ref, dup_ref, gate_w, up_w, own_ref, send_ref):
    field = mm(dgate_ref[...], gate_w[0], ((1,), (1,)))
    field = field + mm(dup_ref[...], up_w[0], ((1,), (1,)))
    tok = own_ref.shape[0]

    @pl.when(place[0] == 0)
    def _():
        own_ref[...] = field[:tok]
        send_ref[...] = field[tok:].astype(jnp.bfloat16)

    @pl.when(place[0] == 1)
    def _():
        own_ref[...] = field[tok:]
        send_ref[...] = field[:tok].astype(jnp.bfloat16)


def back_step(place, d_gate, d_up, pair):
    seq, ff = d_gate.shape
    width = pair.shape[1]
    out = pl.BlockSpec((seq // 2, TILE), lambda n: (0, n))
    return pl.pallas_call(
        back_kernel,
        grid=(width // TILE,),
        in_specs=[
            SMEM,
            VM,
            VM,
            pl.BlockSpec((1, TILE, ff), lambda n: (0, n, 0)),
            pl.BlockSpec((1, TILE, ff), lambda n: (1, n, 0)),
        ],
        out_specs=[out, out],
        out_shape=[f32_like(seq // 2, width), bf16_like(seq // 2, width)],
        compiler_params=PARAMS,
        cost_estimate=cost(4 * seq * width * ff, 26e6),
        name="back",
    )(place, d_gate, d_up, pair, pair)


def result_kernel(place, hid_ref, h_ref, down_w, own_ref, send_ref):
    field = mm(hid_ref[...], down_w[...])
    tok = own_ref.shape[0]

    @pl.when(place[0] == 0)
    def _():
        own_ref[...] = field[:tok] + h_ref[...]
        send_ref[...] = field[tok:].astype(jnp.bfloat16)

    @pl.when(place[0] == 1)
    def _():
        own_ref[...] = field[tok:] + h_ref[...]
        send_ref[...] = field[:tok].astype(jnp.bfloat16)


def result_step(place, hidden, h_own, down):
    tok, width = h_own.shape
    ff = hidden.shape[1]
    out = pl.BlockSpec((tok, TILE), lambda n: (0, n))
    return pl.pallas_call(
        result_kernel,
        grid=(width // TILE,),
        in_specs=[SMEM, VM, out, pl.BlockSpec((ff, TILE), lambda n: (0, n))],
        out_specs=[out, out],
        out_shape=[f32_like(tok, width), bf16_like(tok, width)],
        compiler_params=PARAMS,
        cost_estimate=cost(4 * tok * width * ff, 20e6),
        name="result",
    )(place, hidden, h_own, down)


def entry_kernel(place, dn_own, dn_got, h_ref, dy_ref, gain, w_ref, dh_ref, da_ref, keep_ref, send_ref, part_ref):
    core = place[0]
    tok = dh_ref.shape[0]
    part_ref[...] = jnp.zeros_like(part_ref)
    for part in range(tok // TILE):
        rows = slice(part * TILE, (part + 1) * TILE)
        field = h_ref[rows, :]
        scale = norm_scale(field)
        hat = field * scale
        grad = dn_own[rows, :] + fp32(dn_got[rows, :])
        part_ref[...] += jnp.sum(grad * hat, axis=0, keepdims=True)
        dy = fp32(dy_ref[rows_at(core * tok + part * TILE, TILE), :])
        total = dy + rms_back(grad * gain[1:2, :], hat, scale)
        dh_ref[rows, :] = total
        da_ref[rows, :] = total.astype(jnp.bfloat16)
    heads = keep_ref.shape[0]
    for ref, at in ((send_ref, 1 - core), (keep_ref, core)):
        ref[...] = mm(w_ref[rows_at(at * heads, heads), :], da_ref[...], ((1,), (1,))).astype(jnp.bfloat16)


def entry_step(place, dn_own, dn_got, h_own, dy_all, gains, weight):
    tok, width = h_own.shape
    rows = weight.shape[0]
    return pl.pallas_call(
        entry_kernel,
        in_specs=[SMEM] + [VM] * 6,
        out_specs=[VM] * 5,
        out_shape=[
            f32_like(tok, width),
            bf16_like(tok, width),
            bf16_like(rows // 2, tok),
            bf16_like(rows // 2, tok),
            f32_like(1, width),
        ],
        compiler_params=PARAMS,
        cost_estimate=cost(2 * tok * width * rows, 20e6),
        name="entry",
    )(place, dn_own, dn_got, h_own, dy_all, gains, weight)


def inputs_kernel(place, dq_ref, dk_ref, dv_ref, w_ref, own_ref, send_ref, d_ref):
    @pl.when(pl.program_id(0) == 0)
    def _():
        nq, nk = dq_ref.shape[0], dk_ref.shape[0]
        d_ref[:, :nq] = dq_ref[...].T
        d_ref[:, nq : nq + nk] = dk_ref[...].T
        d_ref[:, nq + nk :] = dv_ref[...].T

    field = mm(d_ref[...], w_ref[...], ((1,), (1,)))
    tok = own_ref.shape[0]

    @pl.when(place[0] == 0)
    def _():
        own_ref[...] = field[:tok]
        send_ref[...] = field[tok:].astype(jnp.bfloat16)

    @pl.when(place[0] == 1)
    def _():
        own_ref[...] = field[tok:]
        send_ref[...] = field[:tok].astype(jnp.bfloat16)


def inputs_step(place, dq_t, dk_t, dv_t, weight):
    width, cols = weight.shape
    tok = dq_t.shape[1] // 2
    out = pl.BlockSpec((tok, TILE), lambda n: (0, n))
    return pl.pallas_call(
        inputs_kernel,
        grid=(width // TILE,),
        in_specs=[SMEM] + [VM] * 3 + [pl.BlockSpec((TILE, cols), lambda n: (n, 0))],
        out_specs=[out, out, VM],
        out_shape=[f32_like(tok, width), bf16_like(tok, width), bf16_like(2 * tok, cols)],
        compiler_params=PARAMS,
        cost_estimate=cost(4 * tok * width * cols, 14e6),
        name="inputs",
    )(place, dq_t, dk_t, dv_t, weight)


def last_kernel(place, d1_own, d1_got, x_ref, dh_ref, gain, dx_ref, part_ref):
    part_ref[...] = jnp.zeros_like(part_ref)
    tok = dx_ref.shape[0]
    for part in range(tok // TILE):
        rows = slice(part * TILE, (part + 1) * TILE)
        field = fp32(x_ref[rows_at(place[0] * tok + part * TILE, TILE), :])
        scale = norm_scale(field)
        hat = field * scale
        grad = d1_own[rows, :] + fp32(d1_got[rows, :])
        part_ref[...] += jnp.sum(grad * hat, axis=0, keepdims=True)
        dx_ref[rows, :] = (dh_ref[rows, :] + rms_back(grad * gain[0:1, :], hat, scale)).astype(jnp.bfloat16)


def last_step(place, d1_own, d1_got, x_seq, dh_own, gains):
    tok, width = dh_own.shape
    return pl.pallas_call(
        last_kernel,
        in_specs=[SMEM] + [VM] * 5,
        out_specs=[VM] * 2,
        out_shape=[bf16_like(tok, width), f32_like(1, width)],
        compiler_params=PARAMS,
        cost_estimate=cost(0, 14e6),
        name="last",
    )(place, d1_own, d1_got, x_seq, dh_own, gains)


class Group:
    def __init__(self, source, rows, put):
        self.source, self.rows, self.put = source, rows, put
        mid = rows // 2
        self.top, self.low = pl.ds(0, mid), pl.ds(mid, mid)


def add_rows(dst, left, right):
    rows = dst.shape[0]

    @pl.loop(0, rows // 64)
    def _(i):
        at = rows_at(i * 64, 64)
        dst[at] = (fp32(left[at]) + fp32(right[at])).astype(dst.dtype)


ORDER_START = (
    "gie", "b1u", "end",
)
ORDER = (
    "gwe", "b0u", "jod", "sed", "kee", "zad", "h1u", "ene", "fid", "wad", "h0u", "joe", "zbd",
    "see", "zae", "b1o", "plu", "b1q", "giu", "b0o", "fie", "enu", "h1o", "wae", "gwu", "zbe",
    "b0q", "kwe", "keu", "jou", "seu", "zau", "h1q", "h0o", "plo", "dee", "gio", "h0q", "wau",
    "gwo", "fiu", "zbu", "eno", "keo", "joo", "plq", "seo", "zao", "giq", "kwo", "kwu", "ded",
    "enq", "gwq", "keq", "fio", "wao", "zbo", "joq", "kwq", "seq", "zaq", "waq", "fiq", "zbq",
    "deu", "deo", "deq",
)


def collect_kernel(
    down, down_in, gate, up, qkv, out, sums, lse,
    down_o, gate_o, up_o, query_o, key_o, value_o, out_o, sums_o, lse_o,
    send, recv, near, lse_send, lse_recv, lse_near, out_mine, out_got, sums_got, *buffers,
):
    at = Spots()
    z, f, g, parity = at.z, at.f, at.g, at.parity
    is_inner = (z == 1) | (z == 2)
    is_outer = (z == 0) | (z == 3)
    toward = (1 + z // 2, f, g)
    outward = (3 * (z // 2), f, g)
    other = (3 - z, f, g)
    chips = 4
    barrier = pltpu.get_barrier_semaphore()
    for partner in (at.x, at.y):
        pl.semaphore_signal(barrier, inc=1, device_id=partner, device_id_type=MESH)
    for level in range(chips):
        for core in range(2):

            @pl.when((z != level) | (g != core))
            def _():
                pl.semaphore_signal(barrier, inc=1, device_id=(level, f, core), device_id_type=MESH)

    pl.semaphore_wait(barrier, 2 * chips + 1)

    taken = [0, 0]

    def between(index, src, dst, device):
        return pltpu.make_async_remote_copy(
            src_ref=src, dst_ref=dst, send_sem=send.at[index], recv_sem=recv.at[index],
            device_id=device, device_id_type=MESH,
        )

    def remote(src, dst, device):
        taken[0] += 1
        return between(taken[0] - 1, src, dst, device)

    def local(src, dst):
        i = taken[1]
        taken[1] += 1
        return pltpu.make_async_copy(src, dst, near.at[i])

    nf = down.shape[0]
    feat = gate.shape[0]
    nq, nk = query_o.shape[1] // 2, key_o.shape[1] // 2
    wide = out_o.shape[1] // 2

    def put_down(done):
        return [(done, down_o.at[rows_at(g * nf, nf)])]

    def put_pair(into):
        def put(done):
            return [
                (done.at[:, rows_at(k * nf, nf)], into.at[:, rows_at((2 * k + g) * nf, nf)])
                for k in range(4)
            ]

        return put

    def put_qkv(done):
        return [
            (done.at[:, 0:nq], query_o.at[:, rows_at(g * nq, nq)]),
            (done.at[:, nq : nq + nk], key_o.at[:, rows_at(g * nk, nk)]),
            (done.at[:, nq + nk : nq + 2 * nk], value_o.at[:, rows_at(g * nk, nk)]),
        ]

    def put_out(done):
        return [(done, out_o.at[:, rows_at(g * wide, wide)])]

    lse_place = lse_o.at[2 * (z // 2) + g]
    for level in range(chips):
        copy = pltpu.make_async_remote_copy(
            src_ref=lse, dst_ref=lse_place, send_sem=lse_send.at[level],
            recv_sem=lse_recv.at[2 * (z // 2) + g],
            device_id=(level, f, parity), device_id_type=MESH,
        )

        @pl.when((z != level) | (g != parity))
        def _():
            copy.start()

    lse_keep = pltpu.make_async_copy(lse, lse_place, lse_near)

    @pl.when(g == parity)
    def _():
        lse_keep.start()

    out_send = remote(out.at[:, rows_at((1 - g) * wide, wide)], out_got, at.core)
    out_keep = local(out.at[:, rows_at(g * wide, wide)], out_mine)
    sums_send = remote(sums, sums_got.at[0], at.core)

    groups = []
    used = 0
    for source, rows, put, ready in (
        (down, nf, put_down, True),
        (gate, feat, put_pair(gate_o), True),
        (up, feat, put_pair(up_o), False),
        (qkv, feat, put_qkv, False),
        (out_mine, feat, put_out, False),
    ):
        group = Group(source, rows, put)
        groups.append(group)
        mid = rows // 2
        group.acc, group.outer, group.inner, group.done = buffers[used : used + 4]
        used += 4
        if ready:
            group.load = local(source, group.acc)
            if source is down:
                group.load_in = local(down_in, group.outer)
        else:
            group.mid, group.got, group.late = buffers[used : used + 3]
            used += 3
            group.sends = [
                remote(source.at[rows_at(at.fd * rows, mid)], group.got.at[1], at.x),
                remote(source.at[rows_at(at.fd * rows + mid, mid)], group.got.at[3], at.y),
                remote(source.at[rows_at(at.fx * rows, mid)], group.got.at[0], at.x),
                remote(source.at[rows_at(at.fy * rows + mid, mid)], group.got.at[2], at.y),
            ]
            group.loads = [
                local(source.at[rows_at(at.fy * rows, mid)], group.mid.at[0]),
                local(source.at[rows_at(at.fx * rows + mid, mid)], group.mid.at[1]),
                local(source.at[rows_at(f * rows, rows)], group.acc),
            ]
            group.second = [
                remote(group.mid.at[0], group.late.at[0], at.y),
                remote(group.mid.at[1], group.late.at[1], at.x),
            ]
        i = taken[0]
        taken[0] += 6
        group.first = i

        def inward(part, slot, group=group, i=i):
            return between(i + slot, group.acc.at[part], group.outer.at[part], toward)

        group.inward = inward

        def crossing(keep, give, i=i, group=group):
            return (
                between(i + 2, group.acc.at[give], group.inner, other),
                between(i + 3, group.done.at[keep], group.done.at[keep], other),
                between(i + 4, group.done.at[keep], group.done.at[keep], outward),
                between(i + 5, group.done.at[give], group.done.at[give], outward),
            )

        group.crossing = crossing
        pairs = group.put(group.done)
        group.shares = [remote(src_ref, dst_ref, at.core) for src_ref, dst_ref in pairs]
        group.stores = [local(src_ref, dst_ref) for src_ref, dst_ref in pairs]

    def by_end(group, step):
        @pl.when(z == 0)
        def _():
            step(group.low, group.top)

        @pl.when(z == 3)
        def _():
            step(group.top, group.low)

    def by_side(group, step):
        @pl.when(z == 1)
        def _():
            step(group.top, group.low, group.crossing(group.top, group.low))

        @pl.when(z == 2)
        def _():
            step(group.low, group.top, group.crossing(group.low, group.top))

    def b1(group):
        for copy in group.sends[:2] + group.loads:
            copy.start()

    def b0(group):
        for copy in group.sends[2:]:
            copy.start()

    def h1(group):
        for i, which in ((0, 1), (1, 3)):
            group.sends[i].wait_recv()
            group.loads[i].wait()
            add_rows(group.mid.at[i], group.mid.at[i], group.got.at[which])
            group.second[i].start()

    def h0(group):
        group.loads[2].wait()
        for i, part, which in ((2, group.top, 0), (3, group.low, 2)):
            group.sends[i].wait_recv()
            add_rows(group.acc.at[part], group.acc.at[part], group.got.at[which])

    def pl_(group):
        for i, part in ((0, group.top), (1, group.low)):
            group.second[i].wait_recv()
            add_rows(group.acc.at[part], group.acc.at[part], group.late.at[i])

    def gi(group):
        by_end(group, lambda give, keep: group.inward(give, 0).start())

    def gw(group):
        by_end(group, lambda give, keep: group.inward(give, 0).wait_send())

    def ke(group):
        by_end(group, lambda give, keep: group.inward(keep, 1).start())

    def kw(group):
        by_end(group, lambda give, keep: group.inward(keep, 1).wait_send())

    def en(group):
        def step(keep, give, copies):
            if group is not d:
                group.inward(give, 0).wait_recv()
            add_rows(group.acc.at[give], group.acc.at[give], group.outer.at[give])
            copies[0].start()

        by_side(group, step)

    def jo(group):
        def step(keep, give, copies):
            if group is not d:
                group.inward(keep, 1).wait_recv()
            add_rows(group.acc.at[keep], group.acc.at[keep], group.outer.at[keep])

        by_side(group, step)

    def se(group):
        def step(keep, give, copies):
            copies[0].wait_recv()
            add_rows(group.done.at[keep], group.acc.at[keep], group.inner)
            copies[1].start()

        by_side(group, step)

    def za(group):
        by_side(group, lambda keep, give, copies: copies[2].start())

    def fi(group):
        by_side(group, lambda keep, give, copies: copies[1].wait_recv())

    def wa(group):
        by_side(group, lambda keep, give, copies: copies[2].wait_send())

    def zb(group):
        by_side(group, lambda keep, give, copies: copies[3].start())

    def de(group):
        def end(give, keep):
            copies = group.crossing(keep, give)
            copies[2].wait_recv()
            copies[3].wait_recv()

        by_end(group, end)

        def step(keep, give, copies):
            for i in (0, 1, 3):
                copies[i].wait_send()

        by_side(group, step)
        for copy in group.shares + group.stores:
            copy.start()

    d, e, u, q, o = groups
    for copy in (e.load, d.load, d.load_in, out_keep, out_send, sums_send):
        copy.start()
    steps = {
        "b1": b1, "b0": b0, "h1": h1, "h0": h0, "pl": pl_, "gi": gi, "gw": gw, "ke": ke, "kw": kw,
        "en": en, "jo": jo, "se": se, "za": za, "fi": fi, "wa": wa, "zb": zb, "de": de,
    }
    named = {"d": d, "e": e, "u": u, "q": q, "o": o}

    def play(order):
        for name in order:
            steps[name[:2]](named[name[2]])

    e.load.wait()
    play(ORDER_START[:2])
    d.load.wait()
    d.load_in.wait()
    play(ORDER_START[2:])

    sums_send.wait_recv()
    sums_o[...] = sums[...] + sums_got[0]
    for i, device in ((1, at.x), (2, at.y)):
        small = remote(sums_o, sums_got.at[i], device)
        small.start()
        small.wait()
        sums_o[...] += sums_got[i]
    sums_in = remote(sums_o, sums_got.at[3], toward)
    sums_mid = remote(sums_o, sums_got.at[4], other)
    sums_out = remote(sums_o, sums_got.at[5], outward)

    @pl.when(is_outer)
    def _():
        sums_in.start()

    out_send.wait_recv()
    out_keep.wait()
    add_rows(out_mine, out_mine, out_got)

    play(ORDER)

    @pl.when(is_inner)
    def _():
        sums_in.wait_recv()
        sums_o[...] += sums_got[3]
        sums_mid.start()
        sums_mid.wait()
        sums_o[...] += sums_got[4]
        sums_out.start()

    @pl.when(is_outer)
    def _():
        sums_in.wait_send()
        sums_out.wait_recv()
        sums_o[...] = sums_got[5]

    @pl.when(is_inner)
    def _():
        sums_out.wait_send()

    sums_send.wait_send()
    out_send.wait_send()
    for group in (u, q, o):
        for copy in group.sends + group.second:
            copy.wait_send()
    for group in groups:
        for copy in group.stores:
            copy.wait()
        for copy in group.shares:
            copy.wait_send()
            copy.wait_recv()
    for level in range(chips):
        copy = pltpu.make_async_remote_copy(
            src_ref=lse, dst_ref=lse_place, send_sem=lse_send.at[level], recv_sem=lse_recv.at[level],
            device_id=(level, f, parity), device_id_type=MESH,
        )

        @pl.when((z != level) | (g != parity))
        def _():
            copy.wait_send()

        @pl.when((z != 2 * (level // 2) + g) | (g != level % 2))
        def _():
            copy.wait_recv()

    @pl.when(g == parity)
    def _():
        lse_keep.wait()


def collect(down, down_in, gate, up, qkv, out, sums, lse, nq, nk):
    bf = jnp.bfloat16
    buffers = []
    wide = out.shape[1] // 2
    for rows, cols, ready in (
        (down.shape[0], down.shape[1], True),
        (gate.shape[0], gate.shape[1], True),
        (up.shape[0] // 4, up.shape[1], False),
        (qkv.shape[0] // 4, qkv.shape[1], False),
        (out.shape[0] // 4, wide, False),
    ):
        mid = rows // 2
        buffers += [
            pltpu.VMEM((rows, cols), bf),
            pltpu.VMEM((rows, cols), bf),
            pltpu.VMEM((mid, cols), bf),
            pltpu.VMEM((rows, cols), bf),
        ]
        if not ready:
            buffers += [
                pltpu.VMEM((2, mid, cols), bf),
                pltpu.VMEM((4, mid, cols), bf),
                pltpu.VMEM((2, mid, cols), bf),
            ]
    feat = gate.shape[0]
    return pl.pallas_call(
        collect_kernel,
        in_specs=[ANY] * 6 + [VM, VM],
        out_specs=[ANY] * 7 + [VM, VM],
        out_shape=[
            bf16_like(2 * down.shape[0], down.shape[1]),
            bf16_like(feat, 2 * gate.shape[1]),
            bf16_like(feat, 2 * up.shape[1]),
            bf16_like(feat, 2 * nq),
            bf16_like(feat, 2 * nk),
            bf16_like(feat, 2 * nk),
            bf16_like(feat, out.shape[1]),
            f32_like(*sums.shape),
            f32_like(4, *lse.shape),
        ],
        scratch_shapes=[
            pltpu.SemaphoreType.DMA((96,)),
            pltpu.SemaphoreType.DMA((96,)),
            pltpu.SemaphoreType.DMA((32,)),
            pltpu.SemaphoreType.DMA((4,)),
            pltpu.SemaphoreType.DMA((4,)),
            pltpu.SemaphoreType.DMA,
            pltpu.VMEM((out.shape[0], wide), bf),
            pltpu.VMEM((out.shape[0], wide), bf),
            pltpu.VMEM((6,) + sums.shape, jnp.float32),
        ]
        + buffers,
        compiler_params=pltpu.CompilerParams(
            collective_id=1, has_side_effects=True, vmem_limit_bytes=58 * 1024 * 1024
        ),
        cost_estimate=cost(0, 500e6),
        name="collect",
    )(down, down_in, gate, up, qkv, out, sums, lse)


def widen_kernel(*refs):
    half = len(refs) // 2
    for narrow, wide in zip(refs[:half], refs[half:]):
        wide[...] = fp32(narrow[...])


def widen(arrays, steps=8):
    specs = [pl.BlockSpec((a.shape[0] // steps, a.shape[1]), lambda n: (n, 0)) for a in arrays]
    return pl.pallas_call(
        widen_kernel,
        grid=(steps,),
        in_specs=specs,
        out_specs=specs,
        out_shape=[f32_like(*a.shape) for a in arrays],
        compiler_params=PARAMS,
        cost_estimate=cost(0, 40e6),
        name="widen",
    )(*arrays)


def turning_tables(seq):
    half = HEAD_SIZE // 2
    places = np.arange(half, dtype=np.float32)
    frequency = np.float32(ROPE_BASE) ** (-(np.float32(2.0) * places) / np.float32(2 * half))
    angles = frequency[:, None] * np.arange(seq, dtype=np.float32)[None, :]
    return np.cos(angles).astype(np.float32), np.sin(angles).astype(np.float32)


def chip_local(
    tokens,
    seq_lengths,
    dealing,
    first_gain,
    query_weight,
    key_matrix,
    value_matrix,
    out_weight,
    second_gain,
    gate_weight,
    up_weight,
    down_weight,
    cotangent,
):
    ctx = lax.axis_size("ctx")
    z = lax.axis_index("ctx")
    f = lax.axis_index("fsdp")
    g = lax.axis_index("grp")
    parity = z % 2
    parity_core = g == parity
    width = tokens.shape[2]
    tok = tokens.shape[1]
    seq = 2 * tok
    place = jnp.stack([g, parity]).astype(jnp.int32)

    def over_x(field):
        return lax.ppermute(field, "fsdp", [(i, i ^ 1) for i in range(4)])

    def over_y(field):
        return lax.ppermute(field, "fsdp", [(i, i ^ 2) for i in range(4)])

    def over_core(field):
        return lax.ppermute(field, "grp", [(0, 1), (1, 0)])

    swap_pairs = [(2 * i + (1 - i % 2), 2 * (i ^ 1) + i % 2) for i in range(ctx)]

    def swap(field):
        got = lax.ppermute(field, ("ctx", "grp"), swap_pairs)
        return jnp.where(parity_core, field, got)

    def along(field, pairs):
        return lax.ppermute(field, "ctx", pairs)

    def cut(field, start, size, axis):
        return lax.dynamic_slice_in_dim(field, start, size, axis)

    def in_order(mine, other, axis=0):
        first = jnp.where(g == 0, mine, other)
        second = jnp.where(g == 0, other, mine)
        return jnp.concatenate([first, second], axis=axis)

    heads_q = query_weight.shape[1] // 2
    heads_k = key_matrix.shape[1] // 2
    part_ff = down_weight.shape[0] // 2
    rows_in = gate_weight.shape[0]

    gain_own = jnp.pad(fp32(jnp.stack([first_gain, second_gain])), ((0, 6), (0, 0)))[None]
    qkv_w, out_w, pair_w, x_seq, dy_all, gain_all = gather_all(
        tokens, cotangent, query_weight, key_matrix, value_matrix, out_weight,
        gate_weight, up_weight, gain_own,
    )
    down_own, x_seq = lax.optimization_barrier((cut(down_weight, g * part_ff, part_ff, 0), x_seq))
    down_w = lax.all_gather(down_own, "fsdp", axis=0, tiled=True)
    gains = jnp.transpose(gain_all[:, :2], (1, 0, 2)).reshape(2, width)

    cosine, sine = turning_tables(seq)

    xn_one, qkv_t = project(x_seq, gains, qkv_w)
    attn_keep, attn_send, lse, q_t, k_t, v_t = attend_seq(place, qkv_t, cosine, sine)
    attn_got = over_core(attn_send)
    h_own, xn_own, attn_mine = residual(place, x_seq, attn_keep, attn_got, gains, out_w)
    hidden, for_gate, act, xn_two = hidden_step(place, xn_own, over_core(xn_own), pair_w)
    d_gate, d_up = hidden_back(dy_all, down_w, for_gate, act)
    bf = jnp.bfloat16
    tokens_in = ((0,), (0,))
    down_grad = mm(hidden, dy_all, tokens_in, bf)
    gate_grad = mm(xn_two, d_gate, tokens_in, bf)
    down_plane = lax.psum_scatter(down_grad, "fsdp", scatter_dimension=0, tiled=True)
    down_in = along(down_plane, [(0, 1), (3, 2)])
    gate_plane = lax.psum_scatter(gate_grad, "fsdp", scatter_dimension=0, tiled=True)
    d_gate, d_up, hidden, _, _ = lax.optimization_barrier((d_gate, d_up, hidden, down_grad, gate_grad))
    dn_own, dn_send = back_step(place, d_gate, d_up, pair_w)
    dn_got = over_core(dn_send)
    res_own, res_send = result_step(place, hidden, h_own, down_w)
    up_grad = mm(xn_two, d_up, tokens_in, bf)
    layer_out = swap((res_own + fp32(over_core(res_send))).astype(bf))

    dh_own, da, dattn_keep, dattn_send, gain_two_part = entry_step(
        place, dn_own, dn_got, h_own, dy_all, gains, out_w
    )
    dattn_got = over_core(dattn_send)
    q_t, _ = lax.optimization_barrier((q_t, down_plane))
    dq_t, dk_t, dv_t = attend_seq_back(
        place, q_t, k_t, v_t, dattn_keep, dattn_got, lse, cosine, sine
    )
    half_width = width // 2
    out_part = mm(attn_mine, da, ((1,), (0,)), bf)
    d1_own, d1_send, d_qkv = inputs_step(place, dq_t, dk_t, dv_t, qkv_w)
    d_qkv, down_in = lax.optimization_barrier((d_qkv, down_in))
    qkv_grad = mm(xn_one, d_qkv, tokens_in, bf)
    dx, gain_one_part = last_step(place, d1_own, over_core(d1_send), x_seq, dh_own, gains)
    tokens_grad = swap(dx)

    parts = jnp.concatenate([gain_one_part, gain_two_part])
    down_sum, gate_sum, up_sum, query_sum, key_sum, value_sum, out_sum, sums, all_lse = collect(
        down_plane, down_in, gate_plane, up_grad, qkv_grad, out_part,
        jnp.pad(parts, ((0, 6), (0, 0))), lse.reshape(-1, seq), heads_q, heads_k,
    )
    sums = cut(sums, f * (width // 4), width // 4, 1)
    query_out, key_out, value_out, out_out, gate_out, up_out, down_out = widen(
        (query_sum, key_sum, value_sum, out_sum, gate_sum, up_sum, down_sum)
    )

    pack_lse = all_lse.reshape(ctx // 2, QUERY_HEADS, seq)
    pack_lse = jnp.transpose(pack_lse, (1, 0, 2)).reshape(QUERY_HEADS, ctx, tok // BLK, BLK)
    mine = (dealing[0] == z).astype(jnp.float32)
    totals = jnp.sum(pack_lse * mine[None, :, :, None], axis=2).reshape(1, QUERY_HEADS, tok)

    return (
        layer_out[None],
        tokens_grad[None],
        totals,
        sums[0],
        query_out,
        key_out,
        value_out,
        out_out,
        sums[1],
        gate_out,
        up_out,
        down_out,
    )


def chip_holds_sequence(mesh, tokens, seq_lengths):
    sizes = dict(mesh.shape)
    packs, length, _ = tokens.shape
    count = seq_lengths.shape[1]
    return (
        sizes["fsdp"] == 4
        and sizes["grp"] == 2
        and sizes["ctx"] == 4
        and packs == sizes["fsdp"] * sizes["grp"]
        and length == count * MINLEN
        and 2 * length == sizes["ctx"] * MINLEN
    )


def solution(mesh):
    placed = (
        P(("fsdp", "grp"), "ctx", None),
        P(("fsdp", "grp"), None),
        P(("fsdp", "grp"), None, None),
        P("fsdp"),
        P("fsdp", None),
        P("fsdp", None),
        P("fsdp", None),
        P("fsdp", None),
        P("fsdp"),
        P("fsdp", None),
        P("fsdp", None),
        P("fsdp", None),
        P(("fsdp", "grp"), "ctx", None),
    )
    results = (
        P(("fsdp", "grp"), "ctx", None),
        P(("fsdp", "grp"), "ctx", None),
        P(("fsdp", "grp"), None, "ctx"),
        P("fsdp"),
        P("fsdp", None),
        P("fsdp", None),
        P("fsdp", None),
        P("fsdp", None),
        P("fsdp"),
        P("fsdp", None),
        P("fsdp", None),
        P("fsdp", None),
    )

    def program(*arrays):
        body = chip_local if chip_holds_sequence(mesh, arrays[0], arrays[1]) else local
        return jax.shard_map(
            body, mesh=mesh, in_specs=placed, out_specs=results, check_vma=False
        )(*arrays)

    return program
```

```python
import jax
import jax.numpy as jnp
import numpy as np
from jax import lax
from jax.experimental import pallas as pl
from jax.experimental.pallas import tpu as pltpu
from jax.sharding import PartitionSpec as P

QUERY_HEADS = 16
KEY_VALUE_HEADS = 8
HEAD_SIZE = 96
BLK = 128


EPS = 1e-05
ROPE_BASE = 100000.0
MASKED = -1e30


def place_rows(positions, lengths):
    ends = jnp.cumsum(lengths, axis=-1)
    before = positions[..., :, None] >= ends[..., None, :]
    segment = jnp.sum(before.astype(jnp.int32), axis=-1)
    offset = jnp.sum(jnp.where(before, lengths[..., None, :], 0), axis=-1)
    return (segment, positions - offset)


def rotation(relative, half_size):
    frequency = ROPE_BASE ** (-(2.0 * jnp.arange(half_size, dtype=jnp.float32)) / (2 * half_size))
    angles = relative.astype(jnp.float32)[:, None] * frequency[None, :]
    return (jnp.cos(angles), jnp.sin(angles))


def rotate(field, cosine, sine_part):
    row_count = field.shape[0]
    half_size = cosine.shape[-1]
    split_heads = field.reshape(row_count, -1, 2 * half_size)
    front_half = split_heads[..., :half_size]
    back_half = split_heads[..., half_size:]
    cos_rows = cosine[:, None, :]
    sin_rows = sine_part[:, None, :]
    turned = jnp.concatenate(
        [
            front_half * cos_rows - back_half * sin_rows,
            back_half * cos_rows + front_half * sin_rows,
        ],
        axis=-1,
    )
    return turned.reshape(row_count, -1)


def rms_back(d_normed, normed, scale):
    return scale * (d_normed - normed * jnp.mean(d_normed * normed, axis=-1, keepdims=True))


def score_block(query_part, key_part, visible):
    scores = jnp.einsum(
        "rgd,kd->grk", query_part, key_part, preferred_element_type=jnp.float32
    ) * HEAD_SIZE ** (-0.5)
    return jnp.where(visible[None], scores, MASKED)


def attend_pack(query_pack, key_pack, value_pack, visible_list):
    token_count = query_pack.shape[0]
    rounds = len(visible_list)
    query_group_width = QUERY_HEADS // KEY_VALUE_HEADS
    context_count = key_pack.shape[0] // token_count

    def width_per_head(head_index, carry):
        out_buf, total_buf = carry
        query_head = lax.dynamic_slice_in_dim(
            query_pack, head_index * query_group_width * HEAD_SIZE, query_group_width * HEAD_SIZE, 1
        ).reshape(token_count, query_group_width, HEAD_SIZE)
        key_head = lax.dynamic_slice_in_dim(key_pack, head_index * HEAD_SIZE, HEAD_SIZE, 1).reshape(
            context_count, rounds, BLK, HEAD_SIZE
        )
        value_head = lax.dynamic_slice_in_dim(
            value_pack, head_index * HEAD_SIZE, HEAD_SIZE, 1
        ).reshape(context_count, rounds, BLK, HEAD_SIZE)
        running_top = jnp.full((query_group_width, token_count), MASKED, jnp.float32)
        running_sum = jnp.zeros((query_group_width, token_count), jnp.float32)
        for round_index in range(rounds):
            first_row = round_index * BLK
            scores = score_block(
                query_head[first_row:],
                key_head[:, round_index].reshape(-1, HEAD_SIZE),
                visible_list[round_index],
            )
            new_top = jnp.maximum(running_top[:, first_row:], jnp.max(scores, axis=-1))
            weights = jnp.where(
                visible_list[round_index][None], jnp.exp(scores - new_top[..., None]), 0.0
            )
            new_sum = running_sum[:, first_row:] * jnp.exp(
                running_top[:, first_row:] - new_top
            ) + jnp.sum(weights, axis=-1)
            running_top = running_top.at[:, first_row:].set(new_top)
            running_sum = running_sum.at[:, first_row:].set(new_sum)
        log_totals = running_top + jnp.log(running_sum)
        mixture = jnp.zeros((token_count, query_group_width, HEAD_SIZE), jnp.float32)
        for round_index in range(rounds):
            first_row = round_index * BLK
            scores = score_block(
                query_head[first_row:],
                key_head[:, round_index].reshape(-1, HEAD_SIZE),
                visible_list[round_index],
            )
            prob_bf = jnp.where(
                visible_list[round_index][None],
                jnp.exp(scores - log_totals[:, first_row:, None]),
                0.0,
            ).astype(jnp.bfloat16)
            mixture = mixture.at[first_row:].add(
                jnp.einsum(
                    "grk,kd->rgd",
                    prob_bf,
                    value_head[:, round_index].reshape(-1, HEAD_SIZE),
                    preferred_element_type=jnp.float32,
                )
            )
        out_buf = lax.dynamic_update_slice_in_dim(
            out_buf,
            mixture.astype(jnp.bfloat16).reshape(token_count, -1),
            head_index * query_group_width * HEAD_SIZE,
            1,
        )
        total_buf = lax.dynamic_update_slice_in_dim(
            total_buf, log_totals, head_index * query_group_width, 0
        )
        return (out_buf, total_buf)

    start_offsets = (
        jnp.zeros((token_count, QUERY_HEADS * HEAD_SIZE), jnp.bfloat16),
        jnp.zeros((QUERY_HEADS, token_count), jnp.float32),
    )
    return lax.fori_loop(0, KEY_VALUE_HEADS, width_per_head, start_offsets)


def attend_back(
    query_pack, key_pack, value_pack, grad_pack, attended_pack, total_pack, visible_list
):
    token_count = query_pack.shape[0]
    rounds = len(visible_list)
    query_group_width = QUERY_HEADS // KEY_VALUE_HEADS
    context_count = key_pack.shape[0] // token_count

    def width_per_head(head_index, carry):
        query_buf, key_buf, value_buf = carry
        query_head = lax.dynamic_slice_in_dim(
            query_pack, head_index * query_group_width * HEAD_SIZE, query_group_width * HEAD_SIZE, 1
        ).reshape(token_count, query_group_width, HEAD_SIZE)
        grad_head = lax.dynamic_slice_in_dim(
            grad_pack, head_index * query_group_width * HEAD_SIZE, query_group_width * HEAD_SIZE, 1
        ).reshape(token_count, query_group_width, HEAD_SIZE)
        output_head = lax.dynamic_slice_in_dim(
            attended_pack,
            head_index * query_group_width * HEAD_SIZE,
            query_group_width * HEAD_SIZE,
            1,
        ).reshape(token_count, query_group_width, HEAD_SIZE)
        key_head = lax.dynamic_slice_in_dim(key_pack, head_index * HEAD_SIZE, HEAD_SIZE, 1).reshape(
            context_count, rounds, BLK, HEAD_SIZE
        )
        value_head = lax.dynamic_slice_in_dim(
            value_pack, head_index * HEAD_SIZE, HEAD_SIZE, 1
        ).reshape(context_count, rounds, BLK, HEAD_SIZE)
        log_totals = lax.dynamic_slice_in_dim(
            total_pack, head_index * query_group_width, query_group_width, 0
        )
        delta = jnp.sum(grad_head.astype(jnp.float32) * output_head.astype(jnp.float32), axis=-1).T
        query_grad = jnp.zeros((token_count, query_group_width, HEAD_SIZE), jnp.float32)
        key_parts = []
        value_parts = []
        for round_index in range(rounds):
            first_row = round_index * BLK
            key_round = key_head[:, round_index].reshape(-1, HEAD_SIZE)
            value_round = value_head[:, round_index].reshape(-1, HEAD_SIZE)
            scores = score_block(query_head[first_row:], key_round, visible_list[round_index])
            probs_full = jnp.where(
                visible_list[round_index][None],
                jnp.exp(scores - log_totals[:, first_row:, None]),
                0.0,
            )
            d_probs = jnp.einsum(
                "rgd,kd->grk",
                grad_head[first_row:],
                value_round,
                preferred_element_type=jnp.float32,
            )
            d_scores = (
                HEAD_SIZE ** (-0.5) * probs_full * (d_probs - delta[:, first_row:, None])
            ).astype(jnp.bfloat16)
            value_parts.append(
                jnp.einsum(
                    "grk,rgd->kd",
                    probs_full.astype(jnp.bfloat16),
                    grad_head[first_row:],
                    preferred_element_type=jnp.float32,
                )
            )
            key_parts.append(
                jnp.einsum(
                    "grk,rgd->kd",
                    d_scores,
                    query_head[first_row:],
                    preferred_element_type=jnp.float32,
                )
            )
            query_grad = query_grad.at[first_row:].add(
                jnp.einsum("grk,kd->rgd", d_scores, key_round, preferred_element_type=jnp.float32)
            )
        key_block = jnp.stack(
            [part.reshape(context_count, BLK, HEAD_SIZE) for part in key_parts], axis=1
        ).reshape(-1, HEAD_SIZE)
        value_block = jnp.stack(
            [part.reshape(context_count, BLK, HEAD_SIZE) for part in value_parts], axis=1
        ).reshape(-1, HEAD_SIZE)
        query_buf = lax.dynamic_update_slice_in_dim(
            query_buf,
            query_grad.reshape(token_count, -1),
            head_index * query_group_width * HEAD_SIZE,
            1,
        )
        key_buf = lax.dynamic_update_slice_in_dim(key_buf, key_block, head_index * HEAD_SIZE, 1)
        value_buf = lax.dynamic_update_slice_in_dim(
            value_buf, value_block, head_index * HEAD_SIZE, 1
        )
        return (query_buf, key_buf, value_buf)

    start_offsets = (
        jnp.zeros((token_count, QUERY_HEADS * HEAD_SIZE), jnp.float32),
        jnp.zeros((context_count * token_count, KEY_VALUE_HEADS * HEAD_SIZE), jnp.float32),
        jnp.zeros((context_count * token_count, KEY_VALUE_HEADS * HEAD_SIZE), jnp.float32),
    )
    return lax.fori_loop(0, KEY_VALUE_HEADS, width_per_head, start_offsets)


def local(
    tokens,
    seq_lengths,
    dealing,
    first_gain,
    query_weight,
    key_matrix,
    value_matrix,
    out_weight,
    second_gain,
    gate_weight,
    up_weight,
    down_weight,
    cotangent,
):
    context_count = lax.axis_size("ctx")
    my_index = lax.axis_index("ctx")
    pack_count, token_count, model_dim = tokens.shape
    rounds = token_count // BLK
    spread = context_count // rounds
    ctx_range = jnp.arange(context_count, dtype=jnp.int32)
    matches = (dealing[..., None] == ctx_range).astype(jnp.int32)
    slot_of = jnp.sum(matches * ctx_range[:, None], axis=2)
    block_of = jnp.arange(rounds, dtype=jnp.int32)[None, :, None] * context_count + slot_of
    key_pos = (
        jnp.transpose(block_of, (0, 2, 1))[..., None] * BLK + jnp.arange(BLK, dtype=jnp.int32)
    ).reshape(pack_count, -1)
    key_seg = place_rows(key_pos, seq_lengths)[0]
    query_pos = lax.dynamic_slice_in_dim(key_pos, my_index * token_count, token_count, 1)
    query_seg, query_rel = place_rows(query_pos, seq_lengths)
    home_row = lax.dynamic_index_in_dim(dealing, my_index // spread, 1, False)
    targets = lax.dynamic_slice_in_dim(home_row, my_index % spread * rounds, rounds, 1)
    picker = (targets[:, None, :] == ctx_range[None, :, None]).astype(jnp.bfloat16)
    my_slots = lax.dynamic_index_in_dim(slot_of, my_index, 2, False)
    owner_index = (
        jnp.arange(rounds, dtype=jnp.int32)[None, :] * context_count + my_slots
    ) // rounds
    keep_slot = jnp.repeat(owner_index, spread, axis=1) == ctx_range[None, :]

    def spread_out(field):
        blocks = field.reshape(pack_count, rounds, BLK, model_dim)
        return jnp.einsum(
            "pkj,pjtd->pktd", picker, blocks, preferred_element_type=jnp.float32
        ).astype(jnp.bfloat16)

    def collect(received):
        grouped = received.reshape(pack_count, rounds, spread, BLK, model_dim)
        return (
            jnp.sum(grouped, axis=2, dtype=jnp.float32)
            .astype(jnp.bfloat16)
            .reshape(pack_count * token_count, model_dim)
        )

    def send_home(field):
        blocks = jnp.repeat(field.reshape(pack_count, rounds, BLK, model_dim), spread, axis=1)
        return jnp.where(keep_slot[:, :, None, None], blocks, jnp.zeros_like(blocks))

    def restore(returned):
        placed = jnp.einsum("pkj,pktd->pjtd", picker, returned, preferred_element_type=jnp.float32)
        return placed.astype(jnp.bfloat16).reshape(pack_count, token_count, model_dim)

    dealt_tokens, dealt_upstream = (
        lax.all_to_all(spread_out(tokens), "ctx", split_axis=1, concat_axis=1, tiled=True),
        lax.all_to_all(spread_out(cotangent), "ctx", split_axis=1, concat_axis=1, tiled=True),
    )
    inputs = collect(dealt_tokens)
    upstream = collect(dealt_upstream)
    gain_one, query_full, key_full, value_full, out_full = (
        lax.all_gather(first_gain, "fsdp", axis=0, tiled=True),
        lax.all_gather(query_weight, "fsdp", axis=0, tiled=True),
        lax.all_gather(key_matrix, "fsdp", axis=0, tiled=True),
        lax.all_gather(value_matrix, "fsdp", axis=0, tiled=True),
        lax.all_gather(out_weight, "fsdp", axis=0, tiled=True),
    )
    gain_two, gate_full, up_full, down_full = (
        lax.all_gather(second_gain, "fsdp", axis=0, tiled=True),
        lax.all_gather(gate_weight, "fsdp", axis=0, tiled=True),
        lax.all_gather(up_weight, "fsdp", axis=0, tiled=True),
        lax.all_gather(down_weight, "fsdp", axis=0, tiled=True),
    )
    gain_one32 = gain_one.astype(jnp.float32)
    gain_two32 = gain_two.astype(jnp.float32)
    cosine, sine_part = rotation(query_rel.reshape(-1), HEAD_SIZE // 2)
    inputs32 = inputs.astype(jnp.float32)
    scale_one = lax.rsqrt(jnp.mean(inputs32 * inputs32, axis=-1, keepdims=True) + EPS)
    normed_one = inputs32 * scale_one
    xn_one = (normed_one * gain_one32).astype(jnp.bfloat16)
    query_rot = rotate(
        jnp.dot(xn_one, query_full, preferred_element_type=jnp.float32), cosine, sine_part
    ).astype(jnp.bfloat16)
    key_rot = rotate(
        jnp.dot(xn_one, key_full, preferred_element_type=jnp.float32), cosine, sine_part
    ).astype(jnp.bfloat16)
    rows_of_values = jnp.dot(xn_one, value_full, preferred_element_type=jnp.float32).astype(
        jnp.bfloat16
    )
    key_local = key_rot.reshape(pack_count, token_count, -1)
    value_local = rows_of_values.reshape(pack_count, token_count, -1)
    gathered_keys, gathered_values = (
        lax.all_gather(key_local, "ctx", axis=1, tiled=True),
        lax.all_gather(value_local, "ctx", axis=1, tiled=True),
    )
    key_pos_rounds = key_pos.reshape(pack_count, context_count, rounds, BLK)
    key_seg_rounds = key_seg.reshape(pack_count, context_count, rounds, BLK)
    visible = []
    for round_index in range(rounds):
        first_row = round_index * BLK
        round_pos = key_pos_rounds[:, :, round_index].reshape(pack_count, -1)
        round_seg = key_seg_rounds[:, :, round_index].reshape(pack_count, -1)
        same_seq = query_seg[:, first_row:, None] == round_seg[:, None, :]
        earlier = round_pos[:, None, :] <= query_pos[:, first_row:, None]
        visible.append(same_seq & earlier)
    query_packs = query_rot.reshape(pack_count, token_count, -1)
    pack_index = 0
    pack_visible = [mask[pack_index] for mask in visible]
    attended_pack, total_pack = attend_pack(
        query_packs[pack_index],
        gathered_keys[pack_index],
        gathered_values[pack_index],
        pack_visible,
    )
    total_list = [total_pack]
    softmax_totals = jnp.stack(total_list, axis=0)
    hidden_in = inputs32 + jnp.dot(attended_pack, out_full, preferred_element_type=jnp.float32)
    scale_two = lax.rsqrt(jnp.mean(hidden_in * hidden_in, axis=-1, keepdims=True) + EPS)
    normed_two = hidden_in * scale_two
    xn_two = (normed_two * gain_two32).astype(jnp.bfloat16)
    gate_val = jnp.dot(xn_two, gate_full, preferred_element_type=jnp.float32)
    up_val = jnp.dot(xn_two, up_full, preferred_element_type=jnp.float32)
    activated = jax.nn.silu(gate_val)
    hidden = (activated * up_val).astype(jnp.bfloat16)
    result = (hidden_in + jnp.dot(hidden, down_full, preferred_element_type=jnp.float32)).astype(
        jnp.bfloat16
    )
    down_grad = jnp.dot(hidden.T, upstream, preferred_element_type=jnp.float32)
    d_hidden = jnp.dot(upstream, down_full.T, preferred_element_type=jnp.float32)
    sigmoid_gate = jax.nn.sigmoid(gate_val)
    d_gate = (d_hidden * up_val * sigmoid_gate * (1.0 + gate_val * (1.0 - sigmoid_gate))).astype(
        jnp.bfloat16
    )
    d_up = (d_hidden * activated).astype(jnp.bfloat16)
    gate_grad = jnp.dot(xn_two.T, d_gate, preferred_element_type=jnp.float32)
    up_grad = jnp.dot(xn_two.T, d_up, preferred_element_type=jnp.float32)
    d_norm_two = jnp.dot(d_gate, gate_full.T, preferred_element_type=jnp.float32) + jnp.dot(
        d_up, up_full.T, preferred_element_type=jnp.float32
    )
    gain_two_grad = jnp.sum(d_norm_two * normed_two, axis=0)
    d_hidden_in = upstream.astype(jnp.float32) + rms_back(
        d_norm_two * gain_two32, normed_two, scale_two
    )
    mlp_parts = (
        lax.psum_scatter(
            gain_two_grad.astype(jnp.bfloat16), "fsdp", scatter_dimension=0, tiled=True
        ).astype(jnp.float32),
        lax.psum_scatter(
            gate_grad.astype(jnp.bfloat16), "fsdp", scatter_dimension=0, tiled=True
        ).astype(jnp.float32),
        lax.psum_scatter(
            up_grad.astype(jnp.bfloat16), "fsdp", scatter_dimension=0, tiled=True
        ).astype(jnp.float32),
        lax.psum_scatter(
            down_grad.astype(jnp.bfloat16), "fsdp", scatter_dimension=0, tiled=True
        ).astype(jnp.float32),
    )
    d_branch = d_hidden_in.astype(jnp.bfloat16)
    out_grad = jnp.dot(attended_pack.T, d_branch, preferred_element_type=jnp.float32)
    d_attended = jnp.dot(d_branch, out_full.T, preferred_element_type=jnp.float32).astype(
        jnp.bfloat16
    )
    back_keys, back_values = (gathered_keys, gathered_values)
    grad_packs = d_attended.reshape(pack_count, token_count, -1)
    out_packs = attended_pack.reshape(pack_count, token_count, -1)
    pack_index = 0
    pack_visible = [mask[pack_index] for mask in visible]
    query_part, key_part, value_part = attend_back(
        query_packs[pack_index],
        back_keys[pack_index],
        back_values[pack_index],
        grad_packs[pack_index],
        out_packs[pack_index],
        softmax_totals[pack_index],
        pack_visible,
    )
    key_list = [key_part]
    value_list = [value_part]
    d_keys, d_values = (
        lax.psum_scatter(
            jnp.stack(key_list, axis=0).astype(jnp.bfloat16), "ctx", scatter_dimension=1, tiled=True
        ).astype(jnp.float32),
        lax.psum_scatter(
            jnp.stack(value_list, axis=0).astype(jnp.bfloat16),
            "ctx",
            scatter_dimension=1,
            tiled=True,
        ).astype(jnp.float32),
    )
    d_query = rotate(query_part, cosine, -sine_part).astype(jnp.bfloat16)
    d_key = rotate(d_keys.reshape(pack_count * token_count, -1), cosine, -sine_part).astype(
        jnp.bfloat16
    )
    d_value = d_values.reshape(pack_count * token_count, -1).astype(jnp.bfloat16)
    query_grad = jnp.dot(xn_one.T, d_query, preferred_element_type=jnp.float32)
    key_grad = jnp.dot(xn_one.T, d_key, preferred_element_type=jnp.float32)
    value_grad = jnp.dot(xn_one.T, d_value, preferred_element_type=jnp.float32)
    d_norm_one = (
        jnp.dot(d_query, query_full.T, preferred_element_type=jnp.float32)
        + jnp.dot(d_key, key_full.T, preferred_element_type=jnp.float32)
        + jnp.dot(d_value, value_full.T, preferred_element_type=jnp.float32)
    )
    gain_one_grad = jnp.sum(d_norm_one * normed_one, axis=0)
    d_inputs = d_hidden_in + rms_back(d_norm_one * gain_one32, normed_one, scale_one)
    attn_parts = (
        lax.psum_scatter(
            gain_one_grad.astype(jnp.bfloat16), "fsdp", scatter_dimension=0, tiled=True
        ).astype(jnp.float32),
        lax.psum_scatter(
            query_grad.astype(jnp.bfloat16), "fsdp", scatter_dimension=0, tiled=True
        ).astype(jnp.float32),
        lax.psum_scatter(
            key_grad.astype(jnp.bfloat16), "fsdp", scatter_dimension=0, tiled=True
        ).astype(jnp.float32),
        lax.psum_scatter(
            value_grad.astype(jnp.bfloat16), "fsdp", scatter_dimension=0, tiled=True
        ).astype(jnp.float32),
        lax.psum_scatter(
            out_grad.astype(jnp.bfloat16), "fsdp", scatter_dimension=0, tiled=True
        ).astype(jnp.float32),
    )
    finished = (
        lax.psum(attn_parts[0].astype(jnp.bfloat16), ("ctx", "grp")).astype(jnp.float32),
        lax.psum(attn_parts[1].astype(jnp.bfloat16), ("ctx", "grp")).astype(jnp.float32),
        lax.psum(attn_parts[2].astype(jnp.bfloat16), ("ctx", "grp")).astype(jnp.float32),
        lax.psum(attn_parts[3].astype(jnp.bfloat16), ("ctx", "grp")).astype(jnp.float32),
        lax.psum(attn_parts[4].astype(jnp.bfloat16), ("ctx", "grp")).astype(jnp.float32),
        lax.psum(mlp_parts[0].astype(jnp.bfloat16), ("ctx", "grp")).astype(jnp.float32),
        lax.psum(mlp_parts[1].astype(jnp.bfloat16), ("ctx", "grp")).astype(jnp.float32),
        lax.psum(mlp_parts[2].astype(jnp.bfloat16), ("ctx", "grp")).astype(jnp.float32),
        lax.psum(mlp_parts[3].astype(jnp.bfloat16), ("ctx", "grp")).astype(jnp.float32),
    )
    home_out, home_grad = (
        lax.all_to_all(send_home(result), "ctx", split_axis=1, concat_axis=1, tiled=True),
        lax.all_to_all(
            send_home(d_inputs.astype(jnp.bfloat16)), "ctx", split_axis=1, concat_axis=1, tiled=True
        ),
    )
    return (
        restore(home_out),
        restore(home_grad),
        softmax_totals,
        finished[0],
        finished[1],
        finished[2],
        finished[3],
        finished[4],
        finished[5],
        finished[6],
        finished[7],
        finished[8],
    )


MINLEN = 1024
QB = 256
VMEM_LIMIT = 56 * 1024 * 1024


def attend_kernel(
    place, q_ref, k_ref, v_ref, c_ref, s_ref,
    keep_ref, send_ref, lse_ref, qr_ref, kr_ref, vr_ref, held,
):
    cosine = c_ref[...]
    sine = s_ref[...]
    half = HEAD_SIZE // 2
    seq = cosine.shape[1]

    def turn(field):
        front, back = field[:half], field[half:]
        return jnp.concatenate(
            [front * cosine - back * sine, back * cosine + front * sine], axis=0
        )

    k_rot = turn(k_ref[...])
    kr_ref[...] = k_rot.astype(jnp.bfloat16)
    key = k_rot.T.astype(jnp.bfloat16)
    val_t = v_ref[...].astype(jnp.bfloat16)
    vr_ref[...] = val_t
    q0 = turn(q_ref[:HEAD_SIZE]).astype(jnp.bfloat16)
    q1 = turn(q_ref[HEAD_SIZE:]).astype(jnp.bfloat16)
    qr_ref[:HEAD_SIZE] = q0
    qr_ref[HEAD_SIZE:] = q1
    rows = lax.broadcasted_iota(jnp.int32, (QB, 2 * QB), 0)
    cols = lax.broadcasted_iota(jnp.int32, (QB, 2 * QB), 1)
    keep = rows <= jnp.where(cols >= QB, cols - QB, cols)
    for b in range(seq // QB):
        lo, n = b * QB, (b + 1) * QB
        q_t = jnp.concatenate([q0[:, lo:n], q1[:, lo:n]], axis=1)
        scores = jnp.dot(key[:n], q_t, preferred_element_type=jnp.float32) * HEAD_SIZE ** (-0.5)
        diag = jnp.where(keep, scores[lo:], MASKED)
        top = jnp.max(diag, axis=0, keepdims=True)
        if b > 0:
            top = jnp.maximum(top, jnp.max(scores[:lo], axis=0, keepdims=True))
        e_diag = jnp.exp(diag - top)
        total = jnp.sum(e_diag, axis=0, keepdims=True)
        out = jnp.dot(val_t[:, lo:n], e_diag.astype(jnp.bfloat16), preferred_element_type=jnp.float32)
        if b > 0:
            e_rest = jnp.exp(scores[:lo] - top)
            total = total + jnp.sum(e_rest, axis=0, keepdims=True)
            out = out + jnp.dot(
                val_t[:, :lo], e_rest.astype(jnp.bfloat16), preferred_element_type=jnp.float32
            )
        out = (out / total).astype(jnp.bfloat16)
        held[:HEAD_SIZE, lo:n] = out[:, :QB]
        held[HEAD_SIZE:, lo:n] = out[:, QB:]
        lse = top + jnp.log(total)
        lse_ref[0, 0:1, lo:n] = lse[:, :QB]
        lse_ref[0, 1:2, lo:n] = lse[:, QB:]
    tok = seq // 2
    for core in range(2):

        @pl.when(place[0] == core)
        def _():
            keep_ref[...] = held[:, core * tok : (core + 1) * tok]
            send_ref[...] = held[:, (1 - core) * tok : (2 - core) * tok]


def attend_seq(place, qkv_t, cosine, sine):
    rows, seq = qkv_t.shape
    kv = rows // (4 * HEAD_SIZE)
    group = pl.BlockSpec((2 * HEAD_SIZE, seq), lambda j: (j, 0))

    def head(base):
        return pl.BlockSpec((HEAD_SIZE, seq), lambda j: (base + j, 0))

    table = pl.BlockSpec((HEAD_SIZE // 2, seq), lambda j: (0, 0))
    return pl.pallas_call(
        attend_kernel,
        grid=(kv,),
        in_specs=[pl.BlockSpec(memory_space=pltpu.SMEM), group, head(2 * kv), head(3 * kv), table, table],
        out_specs=[
            pl.BlockSpec((2 * HEAD_SIZE, seq // 2), lambda j: (j, 0)),
            pl.BlockSpec((2 * HEAD_SIZE, seq // 2), lambda j: (j, 0)),
            pl.BlockSpec((1, 2, seq), lambda j: (j, 0, 0)),
            group,
            head(0),
            head(0),
        ],
        out_shape=[
            jax.ShapeDtypeStruct((2 * kv * HEAD_SIZE, seq // 2), jnp.bfloat16),
            jax.ShapeDtypeStruct((2 * kv * HEAD_SIZE, seq // 2), jnp.bfloat16),
            jax.ShapeDtypeStruct((kv, 2, seq), jnp.float32),
            jax.ShapeDtypeStruct((2 * kv * HEAD_SIZE, seq), jnp.bfloat16),
            jax.ShapeDtypeStruct((kv * HEAD_SIZE, seq), jnp.bfloat16),
            jax.ShapeDtypeStruct((kv * HEAD_SIZE, seq), jnp.bfloat16),
        ],
        scratch_shapes=[pltpu.VMEM((2 * HEAD_SIZE, seq), jnp.bfloat16)],
        compiler_params=pltpu.CompilerParams(vmem_limit_bytes=VMEM_LIMIT),
        cost_estimate=pl.CostEstimate(
            flops=4 * kv * 2 * seq * seq * HEAD_SIZE, bytes_accessed=10 * rows * seq, transcendentals=kv * seq * seq
        ),
        name="attend",
    )(place, qkv_t, qkv_t, qkv_t, cosine, sine)


def attend_back_kernel(
    place, q_ref, k_ref, v_ref, keep_ref, got_ref, lse_ref, c_ref, s_ref,
    dq_ref, dk_ref, dv_ref, dk_acc, dv_acc,
):
    half = HEAD_SIZE // 2
    cosine = c_ref[...]
    sine = s_ref[...]
    seq = cosine.shape[1]

    def turn_back(field, cos, sin):
        front, back = field[:half], field[half:]
        return jnp.concatenate([front * cos + back * sin, back * cos - front * sin], axis=0)

    def flip(field):
        return field.astype(jnp.float32).T.astype(jnp.bfloat16)

    key_t = k_ref[...]
    key = flip(key_t)
    val = flip(v_ref[...])
    q0_t, q1_t = q_ref[:HEAD_SIZE], q_ref[HEAD_SIZE:]
    first_core = place[0] == 0
    early = jnp.where(first_core, keep_ref[...], got_ref[...])
    late = jnp.where(first_core, got_ref[...], keep_ref[...])
    grads = jnp.concatenate([early, late], axis=1)
    g0_t, g1_t = grads[:HEAD_SIZE], grads[HEAD_SIZE:]
    q0, q1, g0, g1 = flip(q0_t), flip(q1_t), flip(g0_t), flip(g1_t)
    dk_acc[...] = jnp.zeros_like(dk_acc)
    dv_acc[...] = jnp.zeros_like(dv_acc)
    rows = lax.broadcasted_iota(jnp.int32, (QB, 2 * QB), 0)
    cols = lax.broadcasted_iota(jnp.int32, (QB, 2 * QB), 1)
    keep = rows <= jnp.where(cols >= QB, cols - QB, cols)
    for b in range(seq // QB):
        lo, n = b * QB, (b + 1) * QB
        q_t = jnp.concatenate([q0_t[:, lo:n], q1_t[:, lo:n]], axis=1)
        g_t = jnp.concatenate([g0_t[:, lo:n], g1_t[:, lo:n]], axis=1)
        q_n = jnp.concatenate([q0[lo:n], q1[lo:n]], axis=0)
        g_n = jnp.concatenate([g0[lo:n], g1[lo:n]], axis=0)
        lse = jnp.concatenate([lse_ref[0, 0:1, lo:n], lse_ref[0, 1:2, lo:n]], axis=1)
        parts = []
        delta = None
        for start, stop in ([(0, lo)] if b > 0 else []) + [(lo, n)]:
            scores = jnp.dot(key[start:stop], q_t, preferred_element_type=jnp.float32) * HEAD_SIZE ** (-0.5)
            prob = jnp.exp(scores - lse)
            if start == lo:
                prob = jnp.where(keep, prob, 0.0)
            d_prob = jnp.dot(val[start:stop], g_t, preferred_element_type=jnp.float32)
            part = jnp.sum(prob * d_prob, axis=0, keepdims=True)
            delta = part if delta is None else delta + part
            dv_acc[start:stop] += jnp.dot(prob.astype(jnp.bfloat16), g_n, preferred_element_type=jnp.float32)
            parts.append((start, stop, prob, d_prob))
        dq_t = None
        for start, stop, prob, d_prob in parts:
            d_score = (prob * (d_prob - delta) * HEAD_SIZE ** (-0.5)).astype(jnp.bfloat16)
            dk_acc[start:stop] += jnp.dot(d_score, q_n, preferred_element_type=jnp.float32)
            part = jnp.dot(key_t[:, start:stop], d_score, preferred_element_type=jnp.float32)
            dq_t = part if dq_t is None else dq_t + part
        cos, sin = cosine[:, lo:n], sine[:, lo:n]
        dq_ref[:HEAD_SIZE, lo:n] = turn_back(dq_t[:, :QB], cos, sin).astype(jnp.bfloat16)
        dq_ref[HEAD_SIZE:, lo:n] = turn_back(dq_t[:, QB:], cos, sin).astype(jnp.bfloat16)
    dk_ref[...] = turn_back(dk_acc[...].T, cosine, sine).astype(jnp.bfloat16)
    dv_ref[...] = dv_acc[...].T.astype(jnp.bfloat16)


def attend_seq_back(place, q_t, k_t, v_t, g_keep, g_got, lse, cosine, sine):
    rows, seq = k_t.shape
    kv = rows // HEAD_SIZE
    group = pl.BlockSpec((2 * HEAD_SIZE, seq), lambda j: (j, 0))
    part = pl.BlockSpec((2 * HEAD_SIZE, seq // 2), lambda j: (j, 0))
    head = pl.BlockSpec((HEAD_SIZE, seq), lambda j: (j, 0))
    table = pl.BlockSpec((HEAD_SIZE // 2, seq), lambda j: (0, 0))
    return pl.pallas_call(
        attend_back_kernel,
        grid=(kv,),
        in_specs=[
            pl.BlockSpec(memory_space=pltpu.SMEM), group, head, head, part, part,
            pl.BlockSpec((1, 2, seq), lambda j: (j, 0, 0)), table, table,
        ],
        out_specs=[group, head, head],
        out_shape=[
            jax.ShapeDtypeStruct((2 * rows, seq), jnp.bfloat16),
            jax.ShapeDtypeStruct((rows, seq), jnp.bfloat16),
            jax.ShapeDtypeStruct((rows, seq), jnp.bfloat16),
        ],
        scratch_shapes=[
            pltpu.VMEM((seq, HEAD_SIZE), jnp.float32),
            pltpu.VMEM((seq, HEAD_SIZE), jnp.float32),
        ],
        compiler_params=pltpu.CompilerParams(vmem_limit_bytes=VMEM_LIMIT),
        cost_estimate=pl.CostEstimate(
            flops=10 * kv * 2 * seq * seq * HEAD_SIZE, bytes_accessed=20 * rows * seq, transcendentals=kv * seq * seq
        ),
        name="attend_back",
    )(place, q_t, k_t, v_t, g_keep, g_got, lse, cosine, sine)


def fp32(field):
    return field.astype(jnp.float32)


def mm(left, right, dims=((1,), (0,)), out=jnp.float32):
    return lax.dot_general(left, right, (dims, ((), ())), preferred_element_type=out)


ANY = pl.BlockSpec(memory_space=pl.ANY)
SMEM = pl.BlockSpec(memory_space=pltpu.SMEM)
VM = pl.BlockSpec(memory_space=pltpu.VMEM)
PARAMS = pltpu.CompilerParams(vmem_limit_bytes=VMEM_LIMIT)
MESH = pl.DeviceIdType.MESH
TILE = 256


def bf16_like(*dims):
    return jax.ShapeDtypeStruct(dims, jnp.bfloat16)


def f32_like(*dims):
    return jax.ShapeDtypeStruct(dims, jnp.float32)


def cost(flops, moved):
    return pl.CostEstimate(flops=int(flops), bytes_accessed=int(moved), transcendentals=0)


class Spots:
    def __init__(self):
        z, f, g = lax.axis_index("ctx"), lax.axis_index("fsdp"), lax.axis_index("grp")
        self.z, self.f, self.g = z, f, g
        self.parity = z % 2
        self.fx = f + 1 - 2 * (f % 2)
        self.fy = f + 2 - 4 * (f // 2)
        self.fd = 3 - f
        across = z + 1 - 2 * self.parity
        self.x = (z, self.fx, g)
        self.y = (z, self.fy, g)
        self.diag = (z, self.fd, g)
        self.core = (z, f, 1 - g)
        self.across = (across, f, g)
        self.swap = (across, f, 1 - g)


def greet(*partners):
    barrier = pltpu.get_barrier_semaphore()
    for partner in partners:
        pl.semaphore_signal(barrier, inc=1, device_id=partner, device_id_type=MESH)
    pl.semaphore_wait(barrier, len(partners))


def rows_at(start, size):
    return pl.ds(pl.multiple_of(start, size), size)


def gather_kernel(
    tokens, cotangent, wq, wk, wv, wo, gate, up, down, gain,
    qkv_o, out_o, pair_o, down_o, x_o, dy_o, gain_o,
    send, recv, near, far, qkv_v, out_v, pair_v, down_v, tok_v, gain_v,
):
    at = Spots()
    g, f, parity = at.g, at.f, at.parity
    greet(at.x, at.y, at.diag, at.core, at.across, at.swap)
    taken = [0, 0]

    def remote(src, dst, device):
        i = taken[0]
        taken[0] += 1
        return pltpu.make_async_remote_copy(
            src_ref=src, dst_ref=dst, send_sem=send.at[i], recv_sem=recv.at[i],
            device_id=device, device_id_type=MESH,
        )

    class Bounce:
        def __init__(self, src, via, dst):
            i = taken[1]
            taken[1] += 1
            self.first = pltpu.make_async_copy(src, via, near.at[i])
            self.second = pltpu.make_async_copy(via, dst, far.at[i])

        def start(self):
            self.first.start()

        def turn(self):
            self.first.wait()
            self.second.start()

        def wait(self):
            self.second.wait()

    def start(copies):
        for copy in copies:
            copy.start()
        return copies

    def arrive(copies):
        for copy in copies:
            copy.wait_recv()

    tok = tokens.shape[1]
    feat = wq.shape[0]
    mid = feat // 2
    nq, nk, nv = (w.shape[1] // 2 for w in (wq, wk, wv))
    nf = gate.shape[1] // 8
    wide = wo.shape[1] // 2
    count = 4
    top, low = slice(0, mid), slice(mid, feat)

    mine = rows_at(g * tok, tok)
    swaps = [
        remote(tokens.at[0], x_o.at[mine], at.swap),
        remote(cotangent.at[0], dy_o.at[mine], at.swap),
    ]
    keeps = [
        Bounce(tokens.at[0], tok_v.at[0], x_o.at[mine]),
        Bounce(cotangent.at[0], tok_v.at[1], dy_o.at[mine]),
    ]
    away = rows_at((1 - g) * tok, tok)
    swaps_out = [
        pltpu.make_async_remote_copy(
            src_ref=array.at[0], dst_ref=into.at[away], send_sem=send.at[i], recv_sem=recv.at[i],
            device_id=at.swap, device_id_type=MESH,
        )
        for i, (array, into) in enumerate(((tokens, x_o), (cotangent, dy_o)))
    ]
    shares = [remote(x_o.at[mine], x_o.at[mine], at.core), remote(dy_o.at[mine], dy_o.at[mine], at.core)]

    @pl.when(g != parity)
    def _():
        start(swaps_out)

    @pl.when(g == parity)
    def _():
        start(keeps)
        for copy in keeps:
            copy.turn()

    own_rows = f * feat
    shared_cols = (count - 1) * nf

    def pair_direct(part, device):
        first = taken[0]
        taken[0] += count + 1
        rows = rows_at(own_rows + part.start, mid)

        def made(array, index, k, i):
            return pltpu.make_async_remote_copy(
                src_ref=array.at[part, rows_at((2 * k + g) * nf, nf)],
                dst_ref=pair_o.at[index, rows, rows_at(k * nf, nf)],
                send_sem=send.at[first + i], recv_sem=recv.at[first + i],
                device_id=device, device_id_type=MESH,
            )

        def some(array):
            return [made(array, parity, k, k) for k in range(count - 1)]

        @pl.when(parity == 0)
        def _():
            start(some(gate))

        @pl.when(parity == 1)
        def _():
            start(some(up))

        last = start([made(gate, 0, count - 1, count - 1), made(up, 1, count - 1, count)])
        return some(gate), last

    pair_xt, last_xt = pair_direct(top, at.x)
    pair_yl, last_yl = pair_direct(low, at.y)
    pair_xl, last_xl = pair_direct(low, at.x)
    pair_yt, last_yt = pair_direct(top, at.y)

    def qkv_direct(part, device):
        copies = []
        for array, width, column in ((wq, nq, 0), (wk, nk, nq), (wv, nv, nq + nk)):
            copies.append(
                remote(
                    array.at[part, rows_at(g * width, width)],
                    qkv_o.at[rows_at(own_rows + part.start, mid), column : column + width],
                    device,
                )
            )
        return start(copies)

    qkv_xt = qkv_direct(top, at.x)
    qkv_yl = qkv_direct(low, at.y)
    qkv_xl = qkv_direct(low, at.x)
    qkv_yt = qkv_direct(top, at.y)

    own = rows_at(own_rows, feat)
    locals_ = [
        Bounce(
            array.at[:, rows_at(g * width, width)],
            qkv_v.at[:, column : column + width],
            qkv_o.at[own, column : column + width],
        )
        for array, width, column in ((wq, nq, 0), (wk, nk, nq), (wv, nv, nq + nk))
    ]
    locals_.append(Bounce(wo, out_v, out_o.at[own]))
    locals_.append(Bounce(down.at[rows_at(g * nf, nf)], down_v, down_o))
    for array, index in ((gate, 0), (up, 1)):
        for k in range(count):
            locals_.append(
                Bounce(
                    array.at[:, rows_at((2 * k + g) * nf, nf)],
                    pair_v.at[index, :, rows_at(k * nf, nf)],
                    pair_o.at[index, own, rows_at(k * nf, nf)],
                )
            )
    gain_place = gain_o.at[pl.ds(f, 1)]
    locals_.append(Bounce(gain, gain_v, gain_place))
    start(locals_)
    for copy in locals_:
        copy.turn()
    gains = start([remote(gain, gain_place, to) for to in (at.x, at.y, at.diag)])

    def forward(array_at, rows_x, rows_y):
        return remote(array_at(rows_x), array_at(rows_x), at.y), remote(
            array_at(rows_y), array_at(rows_y), at.x
        )

    x_top, y_low = rows_at(at.fx * feat, mid), rows_at(at.fy * feat + mid, mid)
    x_low, y_top = rows_at(at.fx * feat + mid, mid), rows_at(at.fy * feat, mid)
    d_top, d_low = rows_at(at.fd * feat, mid), rows_at(at.fd * feat + mid, mid)

    def pair_view(rows):
        return pair_o.at[parity, rows, 0:shared_cols]

    def last_view(rows):
        return pair_o.at[:, rows, shared_cols : shared_cols + nf]

    def out_view(rows):
        return out_o.at[rows, rows_at(g * wide, wide)]

    pair_fy, pair_fx = forward(pair_view, x_top, y_low)
    last_fy, last_fx = forward(last_view, x_top, y_low)
    sends = [pair_fy, pair_fx, last_fy, last_fx]

    def across(rows):
        copy = remote(pair_view(rows), pair_view(rows), at.across)
        copy.start()
        sends.append(copy)
        return copy

    arrive(pair_xt)
    pair_fy.start()
    z_copies = [across(x_top)]
    arrive(pair_yl)
    pair_fx.start()
    z_copies.append(across(y_low))

    def out_direct(part, device):
        copy = remote(
            wo.at[part, rows_at(g * wide, wide)],
            out_o.at[rows_at(own_rows + part.start, mid), rows_at(g * wide, wide)],
            device,
        )
        copy.start()
        return copy

    out_xt, out_yl = out_direct(top, at.x), out_direct(low, at.y)
    out_xl, out_yt = out_direct(low, at.x), out_direct(top, at.y)

    arrive(pair_xl)
    z_copies.append(across(x_low))
    arrive(pair_yt)
    z_copies.append(across(y_top))

    def qkv_view(rows):
        return qkv_o.at[rows]

    qkv_fy, qkv_fx = forward(qkv_view, x_top, y_low)
    arrive(qkv_xt)
    qkv_fy.start()
    arrive(qkv_yl)
    qkv_fx.start()
    arrive(last_xt)
    last_fy.start()
    arrive(last_yl)
    last_fx.start()

    pair_fy.wait_recv()
    z_copies.append(across(d_top))
    pair_fx.wait_recv()
    z_copies.append(across(d_low))

    for i in range(2):

        @pl.when(g != parity)
        def _():
            swaps[i].wait_recv()
            swaps_out[i].wait_send()

        @pl.when(g == parity)
        def _():
            keeps[i].wait()

        shares[i].start()

    out_fy, out_fx = forward(out_view, x_top, y_low)
    out_xt.wait_recv()
    out_fy.start()
    out_yl.wait_recv()
    out_fx.start()
    out_xl.wait_recv()
    out_yt.wait_recv()

    def share(rows):
        copy = remote(out_view(rows), out_view(rows), at.core)
        copy.start()
        return copy

    shared = [share(x_top), share(x_low), share(y_top), share(y_low)]

    out_fy.wait_recv()
    shared.append(share(d_top))
    out_fx.wait_recv()
    shared.append(share(d_low))

    arrive(qkv_xl)
    arrive(qkv_yt)
    arrive([qkv_fy, qkv_fx, last_fy, last_fx])
    arrive(last_xl + last_yt)
    arrive(gains)
    arrive(shares)
    arrive(shared)
    arrive(z_copies)
    for copy in locals_:
        copy.wait()
    for copy in (
        pair_xt + pair_yl + pair_xl + pair_yt + qkv_xt + qkv_yl + qkv_xl + qkv_yt + gains
        + sends + shares + shared
        + [out_xt, out_yl, out_xl, out_yt, out_fy, out_fx, qkv_fy, qkv_fx]
        + last_xt + last_yl + last_xl + last_yt
    ):
        copy.wait_send()


def gather_all(tokens, cotangent, wq, wk, wv, wo, gate, up, down, gain):
    tok, width = tokens.shape[1:]
    nf = gate.shape[1] // 8
    cols = (wq.shape[1] + wk.shape[1] + wv.shape[1]) // 2
    return pl.pallas_call(
        gather_kernel,
        in_specs=[ANY] * 10,
        out_specs=[ANY] * 7,
        out_shape=[
            bf16_like(width, cols),
            bf16_like(4 * wo.shape[0], width),
            bf16_like(2, width, 4 * nf),
            bf16_like(nf, width),
            bf16_like(2 * tok, width),
            bf16_like(2 * tok, width),
            jax.ShapeDtypeStruct((4,) + gain.shape[1:], gain.dtype),
        ],
        scratch_shapes=[
            pltpu.SemaphoreType.DMA((72,)),
            pltpu.SemaphoreType.DMA((72,)),
            pltpu.SemaphoreType.DMA((20,)),
            pltpu.SemaphoreType.DMA((20,)),
            pltpu.VMEM((width // 4, cols), jnp.bfloat16),
            pltpu.VMEM(wo.shape, jnp.bfloat16),
            pltpu.VMEM((2, width // 4, 4 * nf), jnp.bfloat16),
            pltpu.VMEM((nf, width), jnp.bfloat16),
            pltpu.VMEM((2, tok, width), jnp.bfloat16),
            pltpu.VMEM(gain.shape, gain.dtype),
        ],
        compiler_params=pltpu.CompilerParams(
            collective_id=0, has_side_effects=True, vmem_limit_bytes=VMEM_LIMIT
        ),
        cost_estimate=cost(0, 500e6),
        name="gather",
    )(tokens, cotangent, wq, wk, wv, wo, gate, up, down, gain)


def norm_scale(field):
    return lax.rsqrt(jnp.mean(field * field, axis=-1, keepdims=True) + EPS)


def project_kernel(x_ref, gain, w_ref, xn_ref, out_ref):
    seq = x_ref.shape[0]

    @pl.when(pl.program_id(0) == 0)
    def _():
        for part in range(seq // TILE):
            rows = slice(part * TILE, (part + 1) * TILE)
            field = fp32(x_ref[rows, :])
            xn_ref[rows, :] = (field * norm_scale(field) * gain[0:1, :]).astype(jnp.bfloat16)

    out_ref[...] = mm(w_ref[...].T, xn_ref[...], ((1,), (1,)))


def project(x_seq, gains, weight):
    seq, width = x_seq.shape
    cols = weight.shape[1]
    return pl.pallas_call(
        project_kernel,
        grid=(cols // TILE,),
        in_specs=[VM, VM, pl.BlockSpec((width, TILE), lambda n: (0, n))],
        out_specs=[VM, pl.BlockSpec((TILE, seq), lambda n: (n, 0))],
        out_shape=[bf16_like(seq, width), f32_like(cols, seq)],
        compiler_params=PARAMS,
        cost_estimate=cost(2 * seq * width * cols, 20e6),
        name="project",
    )(x_seq, gains, weight)


def residual_kernel(place, x_ref, attn_keep, attn_got, gain, w_ref, h_ref, xn_ref, attn_ref):
    core = place[0]
    heads = attn_keep.shape[0]
    keep_at, got_at = rows_at(core * heads, heads), rows_at((1 - core) * heads, heads)
    attn_ref[keep_at, :] = attn_keep[...]
    attn_ref[got_at, :] = attn_got[...]
    field = fp32(x_ref[...]) + mm(attn_ref[...].T, w_ref[...])
    h_ref[...] = field
    xn_ref[...] = (field * norm_scale(field) * gain[1:2, :]).astype(jnp.bfloat16)


def residual(place, x_seq, attn_keep, attn_got, gains, weight):
    seq, width = x_seq.shape
    tok = seq // 2
    heads = attn_keep.shape[0]
    steps = tok // TILE
    rows = pl.BlockSpec((TILE, width), lambda i, place: (i, 0))
    return pl.pallas_call(
        residual_kernel,
        grid_spec=pltpu.PrefetchScalarGridSpec(
            num_scalar_prefetch=1,
            grid=(steps,),
            in_specs=[
                pl.BlockSpec((TILE, width), lambda i, place: (steps * place[0] + i, 0)),
                pl.BlockSpec((heads, TILE), lambda i, place: (0, i)),
                pl.BlockSpec((heads, TILE), lambda i, place: (0, i)),
                VM,
                VM,
            ],
            out_specs=[rows, rows, pl.BlockSpec((2 * heads, TILE), lambda i, place: (0, i))],
        ),
        out_shape=[f32_like(tok, width), bf16_like(tok, width), bf16_like(2 * heads, tok)],
        compiler_params=PARAMS,
        cost_estimate=cost(2 * tok * width * weight.shape[0], 14e6),
        name="residual",
    )(place, x_seq, attn_keep, attn_got, gains, weight)


def hidden_kernel(place, xn_own, xn_got, gate_w, up_w, hid_ref, for_gate_ref, act_ref, xn_ref):
    @pl.when(pl.program_id(0) == 0)
    def _():
        tok = xn_own.shape[0]
        xn_ref[rows_at(place[0] * tok, tok), :] = xn_own[...]
        xn_ref[rows_at((1 - place[0]) * tok, tok), :] = xn_got[...]

    gate = mm(xn_ref[...], gate_w[0])
    up = mm(xn_ref[...], up_w[0])
    sig = 1.0 / (1.0 + jnp.exp(-gate))
    act = gate * sig
    hid_ref[...] = (act * up).astype(jnp.bfloat16)
    for_gate_ref[...] = (up * (sig + act * (1.0 - sig))).astype(jnp.bfloat16)
    act_ref[...] = act.astype(jnp.bfloat16)


def hidden_step(place, xn_own, xn_got, pair):
    seq, width = 2 * xn_own.shape[0], xn_own.shape[1]
    ff = pair.shape[2]
    block = pl.BlockSpec((seq, TILE), lambda n: (0, n))
    return pl.pallas_call(
        hidden_kernel,
        grid=(ff // TILE,),
        in_specs=[
            SMEM,
            VM,
            VM,
            pl.BlockSpec((1, width, TILE), lambda n: (0, 0, n)),
            pl.BlockSpec((1, width, TILE), lambda n: (1, 0, n)),
        ],
        out_specs=[block] * 3 + [VM],
        out_shape=[bf16_like(seq, ff)] * 3 + [bf16_like(seq, width)],
        compiler_params=PARAMS,
        cost_estimate=cost(4 * seq * width * ff, 30e6),
        name="hidden",
    )(place, xn_own, xn_got, pair, pair)


def hidden_back_kernel(dy_ref, down_w, for_gate_ref, act_ref, dgate_ref, dup_ref):
    d_hidden = mm(dy_ref[...], down_w[...], ((1,), (1,)))
    dgate_ref[...] = (d_hidden * fp32(for_gate_ref[...])).astype(jnp.bfloat16)
    dup_ref[...] = (d_hidden * fp32(act_ref[...])).astype(jnp.bfloat16)


def hidden_back(dy, down, for_gate, act):
    seq, width = dy.shape
    ff = down.shape[0]
    block = pl.BlockSpec((seq, TILE), lambda n: (0, n))
    return pl.pallas_call(
        hidden_back_kernel,
        grid=(ff // TILE,),
        in_specs=[VM, pl.BlockSpec((TILE, width), lambda n: (n, 0)), block, block],
        out_specs=[block] * 2,
        out_shape=[bf16_like(seq, ff)] * 2,
        compiler_params=PARAMS,
        cost_estimate=cost(2 * seq * width * ff, 26e6),
        name="hidden_back",
    )(dy, down, for_gate, act)


def back_kernel(place, dgate_ref, dup_ref, gate_w, up_w, own_ref, send_ref):
    field = mm(dgate_ref[...], gate_w[0], ((1,), (1,)))
    field = field + mm(dup_ref[...], up_w[0], ((1,), (1,)))
    tok = own_ref.shape[0]

    @pl.when(place[0] == 0)
    def _():
        own_ref[...] = field[:tok]
        send_ref[...] = field[tok:].astype(jnp.bfloat16)

    @pl.when(place[0] == 1)
    def _():
        own_ref[...] = field[tok:]
        send_ref[...] = field[:tok].astype(jnp.bfloat16)


def back_step(place, d_gate, d_up, pair):
    seq, ff = d_gate.shape
    width = pair.shape[1]
    out = pl.BlockSpec((seq // 2, TILE), lambda n: (0, n))
    return pl.pallas_call(
        back_kernel,
        grid=(width // TILE,),
        in_specs=[
            SMEM,
            VM,
            VM,
            pl.BlockSpec((1, TILE, ff), lambda n: (0, n, 0)),
            pl.BlockSpec((1, TILE, ff), lambda n: (1, n, 0)),
        ],
        out_specs=[out, out],
        out_shape=[f32_like(seq // 2, width), bf16_like(seq // 2, width)],
        compiler_params=PARAMS,
        cost_estimate=cost(4 * seq * width * ff, 26e6),
        name="back",
    )(place, d_gate, d_up, pair, pair)


def result_kernel(place, hid_ref, h_ref, down_w, own_ref, send_ref):
    field = mm(hid_ref[...], down_w[...])
    tok = own_ref.shape[0]

    @pl.when(place[0] == 0)
    def _():
        own_ref[...] = field[:tok] + h_ref[...]
        send_ref[...] = field[tok:].astype(jnp.bfloat16)

    @pl.when(place[0] == 1)
    def _():
        own_ref[...] = field[tok:] + h_ref[...]
        send_ref[...] = field[:tok].astype(jnp.bfloat16)


def result_step(place, hidden, h_own, down):
    tok, width = h_own.shape
    ff = hidden.shape[1]
    out = pl.BlockSpec((tok, TILE), lambda n: (0, n))
    return pl.pallas_call(
        result_kernel,
        grid=(width // TILE,),
        in_specs=[SMEM, VM, out, pl.BlockSpec((ff, TILE), lambda n: (0, n))],
        out_specs=[out, out],
        out_shape=[f32_like(tok, width), bf16_like(tok, width)],
        compiler_params=PARAMS,
        cost_estimate=cost(4 * tok * width * ff, 20e6),
        name="result",
    )(place, hidden, h_own, down)


def entry_kernel(place, dn_own, dn_got, h_ref, dy_ref, gain, w_ref, dh_ref, da_ref, keep_ref, send_ref, part_ref):
    core = place[0]

    @pl.when(pl.program_id(0) == 0)
    def _():
        part_ref[...] = jnp.zeros_like(part_ref)

    field = h_ref[...]
    scale = norm_scale(field)
    hat = field * scale
    grad = dn_own[...] + fp32(dn_got[...])
    part_ref[...] += jnp.sum(grad * hat, axis=0, keepdims=True)
    total = fp32(dy_ref[...]) + rms_back(grad * gain[1:2, :], hat, scale)
    dh_ref[...] = total
    da_ref[...] = total.astype(jnp.bfloat16)
    heads = keep_ref.shape[0]
    for ref, at in ((send_ref, 1 - core), (keep_ref, core)):
        ref[...] = mm(w_ref[rows_at(at * heads, heads), :], da_ref[...], ((1,), (1,))).astype(jnp.bfloat16)


def entry_step(place, dn_own, dn_got, h_own, dy_all, gains, weight):
    tok, width = h_own.shape
    heads = weight.shape[0] // 2
    steps = tok // TILE
    rows = pl.BlockSpec((TILE, width), lambda i, place: (i, 0))
    cols = pl.BlockSpec((heads, TILE), lambda i, place: (0, i))
    return pl.pallas_call(
        entry_kernel,
        grid_spec=pltpu.PrefetchScalarGridSpec(
            num_scalar_prefetch=1,
            grid=(steps,),
            in_specs=[
                rows,
                rows,
                rows,
                pl.BlockSpec((TILE, width), lambda i, place: (steps * place[0] + i, 0)),
                VM,
                VM,
            ],
            out_specs=[rows, rows, cols, cols, VM],
        ),
        out_shape=[
            f32_like(tok, width),
            bf16_like(tok, width),
            bf16_like(heads, tok),
            bf16_like(heads, tok),
            f32_like(1, width),
        ],
        compiler_params=PARAMS,
        cost_estimate=cost(2 * tok * width * weight.shape[0], 20e6),
        name="entry",
    )(place, dn_own, dn_got, h_own, dy_all, gains, weight)


def inputs_kernel(place, dq_ref, dk_ref, dv_ref, w_ref, own_ref, send_ref, d_ref):
    @pl.when(pl.program_id(0) == 0)
    def _():
        nq, nk = dq_ref.shape[0], dk_ref.shape[0]
        d_ref[:, :nq] = dq_ref[...].T
        d_ref[:, nq : nq + nk] = dk_ref[...].T
        d_ref[:, nq + nk :] = dv_ref[...].T

    field = mm(d_ref[...], w_ref[...], ((1,), (1,)))
    tok = own_ref.shape[0]

    @pl.when(place[0] == 0)
    def _():
        own_ref[...] = field[:tok]
        send_ref[...] = field[tok:].astype(jnp.bfloat16)

    @pl.when(place[0] == 1)
    def _():
        own_ref[...] = field[tok:]
        send_ref[...] = field[:tok].astype(jnp.bfloat16)


def inputs_step(place, dq_t, dk_t, dv_t, weight):
    width, cols = weight.shape
    tok = dq_t.shape[1] // 2
    out = pl.BlockSpec((tok, TILE), lambda n: (0, n))
    return pl.pallas_call(
        inputs_kernel,
        grid=(width // TILE,),
        in_specs=[SMEM] + [VM] * 3 + [pl.BlockSpec((TILE, cols), lambda n: (n, 0))],
        out_specs=[out, out, VM],
        out_shape=[f32_like(tok, width), bf16_like(tok, width), bf16_like(2 * tok, cols)],
        compiler_params=PARAMS,
        cost_estimate=cost(4 * tok * width * cols, 14e6),
        name="inputs",
    )(place, dq_t, dk_t, dv_t, weight)


def last_kernel(place, d1_own, d1_got, x_ref, dh_ref, gain, dx_ref, part_ref):
    @pl.when(pl.program_id(0) == 0)
    def _():
        part_ref[...] = jnp.zeros_like(part_ref)

    field = fp32(x_ref[...])
    scale = norm_scale(field)
    hat = field * scale
    grad = d1_own[...] + fp32(d1_got[...])
    part_ref[...] += jnp.sum(grad * hat, axis=0, keepdims=True)
    dx_ref[...] = (dh_ref[...] + rms_back(grad * gain[0:1, :], hat, scale)).astype(jnp.bfloat16)


def last_step(place, d1_own, d1_got, x_seq, dh_own, gains):
    tok, width = dh_own.shape
    tile = TILE // 2
    steps = tok // tile
    rows = pl.BlockSpec((tile, width), lambda i, place: (i, 0))
    return pl.pallas_call(
        last_kernel,
        grid_spec=pltpu.PrefetchScalarGridSpec(
            num_scalar_prefetch=1,
            grid=(steps,),
            in_specs=[
                rows,
                rows,
                pl.BlockSpec((tile, width), lambda i, place: (steps * place[0] + i, 0)),
                rows,
                VM,
            ],
            out_specs=[rows, VM],
        ),
        out_shape=[bf16_like(tok, width), f32_like(1, width)],
        compiler_params=PARAMS,
        cost_estimate=cost(0, 14e6),
        name="last",
    )(place, d1_own, d1_got, x_seq, dh_own, gains)


class Group:
    def __init__(self, source, rows, put):
        self.source, self.rows, self.put = source, rows, put
        mid = rows // 2
        self.top, self.low = pl.ds(0, mid), pl.ds(mid, mid)


def add_rows(dst, left, right):
    rows = dst.shape[0]

    @pl.loop(0, rows // 64)
    def _(i):
        at = rows_at(i * 64, 64)
        dst[at] = (fp32(left[at]) + fp32(right[at])).astype(dst.dtype)


ORDER = (
    "b1u", "gie", "s1", "b0u", "end", "jod", "go", "gq", "ene", "gwe", "sed", "kee", "zad",
    "joe", "see", "zae", "h1u", "b1q", "wad", "fid", "b0q", "h0u", "s2", "kwe", "zbd", "plu",
    "giu", "wae", "fie", "enu", "gwu", "keu", "ded", "zbe", "h1q", "h0q", "s3", "ao", "jou",
    "seu", "zau", "plq", "giq", "b1o", "b0o", "h1o", "wau", "gwq", "fiu", "keq", "zbu", "enq",
    "h0o", "dee", "plo", "s4", "gio", "kwu", "joq", "eno", "gwo", "seq", "keo", "zaq", "joo",
    "seo", "s5", "zao", "kwo", "fiq", "waq", "zbq", "wao", "deu", "fio", "kwq", "zbo", "deq",
    "deo",
)


def collect_kernel(
    down, down_in, gate, up, xn, d_qkv, attn, da, sums, lse,
    down_o, gate_o, up_o, query_o, key_o, value_o, out_o, sums_o, lse_o,
    send, recv, near, lse_send, lse_recv, lse_near, out_mine, out_got, sums_got,
    out_away, qkv, xn_v, d_qkv_v, attn_v, da_v, *buffers,
):
    at = Spots()
    z, f, g, parity = at.z, at.f, at.g, at.parity
    is_inner = (z == 1) | (z == 2)
    is_outer = (z == 0) | (z == 3)
    toward = (1 + z // 2, f, g)
    outward = (3 * (z // 2), f, g)
    other = (3 - z, f, g)
    chips = 4
    barrier = pltpu.get_barrier_semaphore()
    for partner in (at.x, at.y):
        pl.semaphore_signal(barrier, inc=1, device_id=partner, device_id_type=MESH)
    for level in range(chips):
        for core in range(2):

            @pl.when((z != level) | (g != core))
            def _():
                pl.semaphore_signal(barrier, inc=1, device_id=(level, f, core), device_id_type=MESH)

    pl.semaphore_wait(barrier, 2 * chips + 1)

    taken = [0, 0]

    def between(index, src, dst, device):
        return pltpu.make_async_remote_copy(
            src_ref=src, dst_ref=dst, send_sem=send.at[index], recv_sem=recv.at[index],
            device_id=device, device_id_type=MESH,
        )

    def remote(src, dst, device):
        taken[0] += 1
        return between(taken[0] - 1, src, dst, device)

    def local(src, dst):
        i = taken[1]
        taken[1] += 1
        return pltpu.make_async_copy(src, dst, near.at[i])

    nf = down.shape[0]
    feat = gate.shape[0]
    nq, nk = query_o.shape[1] // 2, key_o.shape[1] // 2
    wide = out_o.shape[1] // 2

    def put_down(done):
        return [(done, down_o.at[rows_at(g * nf, nf)])]

    def put_pair(into):
        def put(done):
            return [
                (done.at[:, rows_at(k * nf, nf)], into.at[:, rows_at((2 * k + g) * nf, nf)])
                for k in range(4)
            ]

        return put

    def put_qkv(done):
        return [
            (done.at[:, 0:nq], query_o.at[:, rows_at(g * nq, nq)]),
            (done.at[:, nq : nq + nk], key_o.at[:, rows_at(g * nk, nk)]),
            (done.at[:, nq + nk : nq + 2 * nk], value_o.at[:, rows_at(g * nk, nk)]),
        ]

    def put_out(done):
        return [(done, out_o.at[:, rows_at(g * wide, wide)])]

    lse_place = lse_o.at[2 * (z // 2) + g]
    for level in range(chips):
        copy = pltpu.make_async_remote_copy(
            src_ref=lse, dst_ref=lse_place, send_sem=lse_send.at[level],
            recv_sem=lse_recv.at[2 * (z // 2) + g],
            device_id=(level, f, parity), device_id_type=MESH,
        )

        @pl.when((z != level) | (g != parity))
        def _():
            copy.start()

    lse_keep = pltpu.make_async_copy(lse, lse_place, lse_near)

    @pl.when(g == parity)
    def _():
        lse_keep.start()

    out_send = remote(out_away, out_got, at.core)
    operands = [local(xn, xn_v), local(d_qkv, d_qkv_v), local(attn, attn_v), local(da, da_v)]
    sums_send = remote(sums, sums_got.at[0], at.core)

    groups = []
    used = 0
    for source, rows, put, ready in (
        (down, nf, put_down, True),
        (gate, feat, put_pair(gate_o), True),
        (up, feat, put_pair(up_o), False),
        (qkv, feat, put_qkv, False),
        (out_mine, feat, put_out, False),
    ):
        group = Group(source, rows, put)
        groups.append(group)
        mid = rows // 2
        group.acc, group.outer, group.inner, group.done = buffers[used : used + 4]
        used += 4
        if ready:
            group.load = local(source, group.acc)
            if source is down:
                group.load_in = local(down_in, group.outer)
        else:
            group.mid, group.got, group.late = buffers[used : used + 3]
            used += 3
            group.sends = [
                remote(source.at[rows_at(at.fd * rows, mid)], group.got.at[1], at.x),
                remote(source.at[rows_at(at.fd * rows + mid, mid)], group.got.at[3], at.y),
                remote(source.at[rows_at(at.fx * rows, mid)], group.got.at[0], at.x),
                remote(source.at[rows_at(at.fy * rows + mid, mid)], group.got.at[2], at.y),
            ]
            group.loads = [
                local(source.at[rows_at(at.fy * rows, mid)], group.mid.at[0]),
                local(source.at[rows_at(at.fx * rows + mid, mid)], group.mid.at[1]),
                local(source.at[rows_at(f * rows, rows)], group.acc),
            ]
            group.second = [
                remote(group.mid.at[0], group.late.at[0], at.y),
                remote(group.mid.at[1], group.late.at[1], at.x),
            ]
        i = taken[0]
        taken[0] += 6
        group.first = i

        def inward(part, slot, group=group, i=i):
            return between(i + slot, group.acc.at[part], group.outer.at[part], toward)

        group.inward = inward

        def crossing(keep, give, i=i, group=group):
            return (
                between(i + 2, group.acc.at[give], group.inner, other),
                between(i + 3, group.done.at[keep], group.done.at[keep], other),
                between(i + 4, group.done.at[keep], group.done.at[keep], outward),
                between(i + 5, group.done.at[give], group.done.at[give], outward),
            )

        group.crossing = crossing
        pairs = group.put(group.done)
        group.shares = [remote(src_ref, dst_ref, at.core) for src_ref, dst_ref in pairs]
        group.stores = [local(src_ref, dst_ref) for src_ref, dst_ref in pairs]

    def by_end(group, step):
        @pl.when(z == 0)
        def _():
            step(group.low, group.top)

        @pl.when(z == 3)
        def _():
            step(group.top, group.low)

    def by_side(group, step):
        @pl.when(z == 1)
        def _():
            step(group.top, group.low, group.crossing(group.top, group.low))

        @pl.when(z == 2)
        def _():
            step(group.low, group.top, group.crossing(group.low, group.top))

    def b1(group):
        for copy in group.sends[:2] + group.loads:
            copy.start()

    def b0(group):
        for copy in group.sends[2:]:
            copy.start()

    def h1(group):
        for i, which in ((0, 1), (1, 3)):
            group.sends[i].wait_recv()
            group.loads[i].wait()
            add_rows(group.mid.at[i], group.mid.at[i], group.got.at[which])
            group.second[i].start()

    def h0(group):
        group.loads[2].wait()
        for i, part, which in ((2, group.top, 0), (3, group.low, 2)):
            group.sends[i].wait_recv()
            add_rows(group.acc.at[part], group.acc.at[part], group.got.at[which])

    def pl_(group):
        for i, part in ((0, group.top), (1, group.low)):
            group.second[i].wait_recv()
            add_rows(group.acc.at[part], group.acc.at[part], group.late.at[i])

    def gi(group):
        if group is e:
            e.load.wait()
        by_end(group, lambda give, keep: group.inward(give, 0).start())

    def gw(group):
        by_end(group, lambda give, keep: group.inward(give, 0).wait_send())

    def ke(group):
        by_end(group, lambda give, keep: group.inward(keep, 1).start())

    def kw(group):
        by_end(group, lambda give, keep: group.inward(keep, 1).wait_send())

    def en(group):
        if group is d:
            d.load.wait()
            d.load_in.wait()

        def step(keep, give, copies):
            if group is not d:
                group.inward(give, 0).wait_recv()
            add_rows(group.acc.at[give], group.acc.at[give], group.outer.at[give])
            copies[0].start()

        by_side(group, step)

    def jo(group):
        def step(keep, give, copies):
            if group is not d:
                group.inward(keep, 1).wait_recv()
            add_rows(group.acc.at[keep], group.acc.at[keep], group.outer.at[keep])

        by_side(group, step)

    def se(group):
        def step(keep, give, copies):
            copies[0].wait_recv()
            add_rows(group.done.at[keep], group.acc.at[keep], group.inner)
            copies[1].start()

        by_side(group, step)

    def za(group):
        by_side(group, lambda keep, give, copies: copies[2].start())

    def fi(group):
        by_side(group, lambda keep, give, copies: copies[1].wait_recv())

    def wa(group):
        by_side(group, lambda keep, give, copies: copies[2].wait_send())

    def zb(group):
        by_side(group, lambda keep, give, copies: copies[3].start())

    def de(group):
        def end(give, keep):
            copies = group.crossing(keep, give)
            copies[2].wait_recv()
            copies[3].wait_recv()

        by_end(group, end)

        def step(keep, give, copies):
            for i in (0, 1, 3):
                copies[i].wait_send()

        by_side(group, step)
        for copy in group.shares + group.stores:
            copy.start()

    d, e, u, q, o = groups
    for copy in [e.load, d.load, d.load_in, sums_send] + operands:
        copy.start()
    steps = {
        "b1": b1, "b0": b0, "h1": h1, "h0": h0, "pl": pl_, "gi": gi, "gw": gw, "ke": ke, "kw": kw,
        "en": en, "jo": jo, "se": se, "za": za, "fi": fi, "wa": wa, "zb": zb, "de": de,
    }
    named = {"d": d, "e": e, "u": u, "q": q, "o": o}

    over_x = remote(sums_o, sums_got.at[1], at.x)
    over_y = remote(sums_o, sums_got.at[2], at.y)
    sums_in = remote(sums_o, sums_got.at[3], toward)
    sums_mid = remote(sums_o, sums_got.at[4], other)
    sums_out = remote(sums_o, sums_got.at[5], outward)

    def sums_1():
        sums_send.wait_recv()
        sums_o[...] = sums[...] + sums_got[0]
        over_x.start()

    def sums_2():
        over_x.wait()
        sums_o[...] += sums_got[1]
        over_y.start()

    def sums_3():
        over_y.wait()
        sums_o[...] += sums_got[2]

        @pl.when(is_outer)
        def _():
            sums_in.start()

    def sums_4():
        @pl.when(is_inner)
        def _():
            sums_in.wait_recv()
            sums_o[...] += sums_got[3]
            sums_mid.start()

    def sums_5():
        @pl.when(is_inner)
        def _():
            sums_mid.wait()
            sums_o[...] += sums_got[4]
            sums_out.start()

    def out_gradient():
        for copy in operands[2:]:
            copy.wait()
        tile = wide // 2
        for ref, core in ((out_away, 1 - g), (out_mine, g)):
            for n in range(2):
                cols = rows_at(core * wide + n * tile, tile)
                ref[:, n * tile : (n + 1) * tile] = mm(attn_v[...], da_v[:, cols]).astype(ref.dtype)
            if ref is out_away:
                out_send.start()

    def qkv_gradient():
        for copy in operands[:2]:
            copy.wait()
        tile = 2 * TILE
        for n in range(qkv.shape[1] // tile):
            cols = slice(n * tile, (n + 1) * tile)
            qkv[:, cols] = mm(xn_v[...], d_qkv_v[:, cols], ((0,), (0,))).astype(qkv.dtype)

    def out_sum():
        out_send.wait_recv()
        add_rows(out_mine, out_mine, out_got)

    single = {
        "s1": sums_1, "s2": sums_2, "s3": sums_3, "s4": sums_4, "s5": sums_5,
        "go": out_gradient, "gq": qkv_gradient, "ao": out_sum,
    }
    for name in ORDER:
        if len(name) == 2:
            single[name]()
        else:
            steps[name[:2]](named[name[2]])

    @pl.when(is_outer)
    def _():
        sums_in.wait_send()
        sums_out.wait_recv()
        sums_o[...] = sums_got[5]

    @pl.when(is_inner)
    def _():
        sums_out.wait_send()

    sums_send.wait_send()
    out_send.wait_send()
    for group in (u, q, o):
        for copy in group.sends + group.second:
            copy.wait_send()
    for group in groups:
        for copy in group.stores:
            copy.wait()
        for copy in group.shares:
            copy.wait_send()
            copy.wait_recv()
    for level in range(chips):
        copy = pltpu.make_async_remote_copy(
            src_ref=lse, dst_ref=lse_place, send_sem=lse_send.at[level], recv_sem=lse_recv.at[level],
            device_id=(level, f, parity), device_id_type=MESH,
        )

        @pl.when((z != level) | (g != parity))
        def _():
            copy.wait_send()

        @pl.when((z != 2 * (level // 2) + g) | (g != level % 2))
        def _():
            copy.wait_recv()

    @pl.when(g == parity)
    def _():
        lse_keep.wait()


def collect(down, down_in, gate, up, xn, d_qkv, attn, da, sums, lse, nq, nk):
    bf = jnp.bfloat16
    buffers = []
    wide = da.shape[1] // 2
    feat = gate.shape[0]
    for rows, cols, ready in (
        (down.shape[0], down.shape[1], True),
        (gate.shape[0], gate.shape[1], True),
        (up.shape[0] // 4, up.shape[1], False),
        (feat, d_qkv.shape[1], False),
        (attn.shape[0] // 4, wide, False),
    ):
        mid = rows // 2
        buffers += [
            pltpu.VMEM((rows, cols), bf),
            pltpu.VMEM((rows, cols), bf),
            pltpu.VMEM((mid, cols), bf),
            pltpu.VMEM((rows, cols), bf),
        ]
        if not ready:
            buffers += [
                pltpu.VMEM((2, mid, cols), bf),
                pltpu.VMEM((4, mid, cols), bf),
                pltpu.VMEM((2, mid, cols), bf),
            ]
    return pl.pallas_call(
        collect_kernel,
        in_specs=[ANY] * 8 + [VM, VM],
        out_specs=[ANY] * 7 + [VM, VM],
        out_shape=[
            bf16_like(2 * down.shape[0], down.shape[1]),
            bf16_like(feat, 2 * gate.shape[1]),
            bf16_like(feat, 2 * up.shape[1]),
            bf16_like(feat, 2 * nq),
            bf16_like(feat, 2 * nk),
            bf16_like(feat, 2 * nk),
            bf16_like(feat, da.shape[1]),
            f32_like(*sums.shape),
            f32_like(4, *lse.shape),
        ],
        scratch_shapes=[
            pltpu.SemaphoreType.DMA((96,)),
            pltpu.SemaphoreType.DMA((96,)),
            pltpu.SemaphoreType.DMA((32,)),
            pltpu.SemaphoreType.DMA((4,)),
            pltpu.SemaphoreType.DMA((4,)),
            pltpu.SemaphoreType.DMA,
            pltpu.VMEM((attn.shape[0], wide), bf),
            pltpu.VMEM((attn.shape[0], wide), bf),
            pltpu.VMEM((6,) + sums.shape, jnp.float32),
            pltpu.VMEM((attn.shape[0], wide), bf),
            pltpu.VMEM((xn.shape[1], d_qkv.shape[1]), bf),
            pltpu.VMEM(xn.shape, bf),
            pltpu.VMEM(d_qkv.shape, bf),
            pltpu.VMEM(attn.shape, bf),
            pltpu.VMEM(da.shape, bf),
        ]
        + buffers,
        compiler_params=pltpu.CompilerParams(
            collective_id=1, has_side_effects=True, vmem_limit_bytes=62 * 1024 * 1024
        ),
        cost_estimate=cost(0, 500e6),
        name="collect",
    )(down, down_in, gate, up, xn, d_qkv, attn, da, sums, lse)


def widen_kernel(*refs):
    half = len(refs) // 2
    for narrow, wide in zip(refs[:half], refs[half:]):
        wide[...] = fp32(narrow[...])


def widen(arrays, steps=8):
    specs = [pl.BlockSpec((a.shape[0] // steps, a.shape[1]), lambda n: (n, 0)) for a in arrays]
    return pl.pallas_call(
        widen_kernel,
        grid=(steps,),
        in_specs=specs,
        out_specs=specs,
        out_shape=[f32_like(*a.shape) for a in arrays],
        compiler_params=PARAMS,
        cost_estimate=cost(0, 40e6),
        name="widen",
    )(*arrays)


def turning_tables(seq):
    half = HEAD_SIZE // 2
    places = np.arange(half, dtype=np.float32)
    frequency = np.float32(ROPE_BASE) ** (-(np.float32(2.0) * places) / np.float32(2 * half))
    angles = frequency[:, None] * np.arange(seq, dtype=np.float32)[None, :]
    return np.cos(angles).astype(np.float32), np.sin(angles).astype(np.float32)


def chip_local(
    tokens,
    seq_lengths,
    dealing,
    first_gain,
    query_weight,
    key_matrix,
    value_matrix,
    out_weight,
    second_gain,
    gate_weight,
    up_weight,
    down_weight,
    cotangent,
):
    ctx = lax.axis_size("ctx")
    z = lax.axis_index("ctx")
    f = lax.axis_index("fsdp")
    g = lax.axis_index("grp")
    parity = z % 2
    parity_core = g == parity
    width = tokens.shape[2]
    tok = tokens.shape[1]
    seq = 2 * tok
    place = jnp.stack([g, parity]).astype(jnp.int32)

    def over_x(field):
        return lax.ppermute(field, "fsdp", [(i, i ^ 1) for i in range(4)])

    def over_y(field):
        return lax.ppermute(field, "fsdp", [(i, i ^ 2) for i in range(4)])

    def over_core(field):
        return lax.ppermute(field, "grp", [(0, 1), (1, 0)])

    swap_pairs = [(2 * i + (1 - i % 2), 2 * (i ^ 1) + i % 2) for i in range(ctx)]

    def swap(field):
        got = lax.ppermute(field, ("ctx", "grp"), swap_pairs)
        return jnp.where(parity_core, field, got)

    def along(field, pairs):
        return lax.ppermute(field, "ctx", pairs)

    def cut(field, start, size, axis):
        return lax.dynamic_slice_in_dim(field, start, size, axis)

    def in_order(mine, other, axis=0):
        first = jnp.where(g == 0, mine, other)
        second = jnp.where(g == 0, other, mine)
        return jnp.concatenate([first, second], axis=axis)

    heads_q = query_weight.shape[1] // 2
    heads_k = key_matrix.shape[1] // 2
    part_ff = down_weight.shape[0] // 2
    rows_in = gate_weight.shape[0]

    gain_own = jnp.pad(fp32(jnp.stack([first_gain, second_gain])), ((0, 6), (0, 0)))[None]
    qkv_w, out_w, pair_w, down_own, x_seq, dy_all, gain_all = gather_all(
        tokens, cotangent, query_weight, key_matrix, value_matrix, out_weight,
        gate_weight, up_weight, down_weight, gain_own,
    )
    down_w = lax.all_gather(down_own, "fsdp", axis=0, tiled=True)
    gains = jnp.transpose(gain_all[:, :2], (1, 0, 2)).reshape(2, width)

    cosine, sine = turning_tables(seq)

    xn_one, qkv_t = project(x_seq, gains, qkv_w)
    attn_keep, attn_send, lse, q_t, k_t, v_t = attend_seq(place, qkv_t, cosine, sine)
    attn_got = over_core(attn_send)
    h_own, xn_own, attn_mine = residual(place, x_seq, attn_keep, attn_got, gains, out_w)
    hidden, for_gate, act, xn_two = hidden_step(place, xn_own, over_core(xn_own), pair_w)
    d_gate, d_up = hidden_back(dy_all, down_w, for_gate, act)
    bf = jnp.bfloat16
    tokens_in = ((0,), (0,))
    down_grad = mm(hidden, dy_all, tokens_in, bf)
    gate_grad = mm(xn_two, d_gate, tokens_in, bf)
    down_plane = lax.psum_scatter(down_grad, "fsdp", scatter_dimension=0, tiled=True)
    down_in = along(down_plane, [(0, 1), (3, 2)])
    gate_plane = lax.psum_scatter(gate_grad, "fsdp", scatter_dimension=0, tiled=True)
    d_gate, d_up, hidden, _, _ = lax.optimization_barrier((d_gate, d_up, hidden, down_grad, gate_grad))
    dn_own, dn_send = back_step(place, d_gate, d_up, pair_w)
    dn_got = over_core(dn_send)
    res_own, res_send = result_step(place, hidden, h_own, down_w)
    up_grad = mm(xn_two, d_up, tokens_in, bf)
    layer_out = swap((res_own + fp32(over_core(res_send))).astype(bf))

    dh_own, da, dattn_keep, dattn_send, gain_two_part = entry_step(
        place, dn_own, dn_got, h_own, dy_all, gains, out_w
    )
    dattn_got = over_core(dattn_send)
    q_t, _ = lax.optimization_barrier((q_t, down_plane))
    dq_t, dk_t, dv_t = attend_seq_back(
        place, q_t, k_t, v_t, dattn_keep, dattn_got, lse, cosine, sine
    )
    half_width = width // 2
    d1_own, d1_send, d_qkv = inputs_step(place, dq_t, dk_t, dv_t, qkv_w)
    dh_own, down_in = lax.optimization_barrier((dh_own, down_in))
    dx, gain_one_part = last_step(place, d1_own, over_core(d1_send), x_seq, dh_own, gains)
    tokens_grad = swap(dx)

    parts = jnp.concatenate([gain_one_part, gain_two_part])
    down_sum, gate_sum, up_sum, query_sum, key_sum, value_sum, out_sum, sums, all_lse = collect(
        down_plane, down_in, gate_plane, up_grad, xn_one, d_qkv, attn_mine, da,
        jnp.pad(parts, ((0, 6), (0, 0))), lse.reshape(-1, seq), heads_q, heads_k,
    )
    sums = cut(sums, f * (width // 4), width // 4, 1)
    query_out, key_out, value_out, out_out, gate_out, up_out, down_out = widen(
        (query_sum, key_sum, value_sum, out_sum, gate_sum, up_sum, down_sum)
    )

    pack_lse = all_lse.reshape(ctx // 2, QUERY_HEADS, seq)
    pack_lse = jnp.transpose(pack_lse, (1, 0, 2)).reshape(QUERY_HEADS, ctx, tok // BLK, BLK)
    mine = (dealing[0] == z).astype(jnp.float32)
    totals = jnp.sum(pack_lse * mine[None, :, :, None], axis=2).reshape(1, QUERY_HEADS, tok)

    return (
        layer_out[None],
        tokens_grad[None],
        totals,
        sums[0],
        query_out,
        key_out,
        value_out,
        out_out,
        sums[1],
        gate_out,
        up_out,
        down_out,
    )


def chip_holds_sequence(mesh, tokens, seq_lengths):
    sizes = dict(mesh.shape)
    packs, length, _ = tokens.shape
    count = seq_lengths.shape[1]
    return (
        sizes["fsdp"] == 4
        and sizes["grp"] == 2
        and sizes["ctx"] == 4
        and packs == sizes["fsdp"] * sizes["grp"]
        and length == count * MINLEN
        and 2 * length == sizes["ctx"] * MINLEN
    )


def solution(mesh):
    placed = (
        P(("fsdp", "grp"), "ctx", None),
        P(("fsdp", "grp"), None),
        P(("fsdp", "grp"), None, None),
        P("fsdp"),
        P("fsdp", None),
        P("fsdp", None),
        P("fsdp", None),
        P("fsdp", None),
        P("fsdp"),
        P("fsdp", None),
        P("fsdp", None),
        P("fsdp", None),
        P(("fsdp", "grp"), "ctx", None),
    )
    results = (
        P(("fsdp", "grp"), "ctx", None),
        P(("fsdp", "grp"), "ctx", None),
        P(("fsdp", "grp"), None, "ctx"),
        P("fsdp"),
        P("fsdp", None),
        P("fsdp", None),
        P("fsdp", None),
        P("fsdp", None),
        P("fsdp"),
        P("fsdp", None),
        P("fsdp", None),
        P("fsdp", None),
    )

    def program(*arrays):
        body = chip_local if chip_holds_sequence(mesh, arrays[0], arrays[1]) else local
        return jax.shard_map(
            body, mesh=mesh, in_specs=placed, out_specs=results, check_vma=False
        )(*arrays)

    return program
```

```python
import jax
import jax.numpy as jnp
import numpy as np
from jax import lax
from jax.experimental import pallas as pl
from jax.experimental.pallas import tpu as pltpu
from jax.sharding import PartitionSpec as P

QUERY_HEADS = 16
KEY_VALUE_HEADS = 8
HEAD_SIZE = 96
BLK = 128


EPS = 1e-05
ROPE_BASE = 100000.0
MASKED = -1e30


def place_rows(positions, lengths):
    ends = jnp.cumsum(lengths, axis=-1)
    before = positions[..., :, None] >= ends[..., None, :]
    segment = jnp.sum(before.astype(jnp.int32), axis=-1)
    offset = jnp.sum(jnp.where(before, lengths[..., None, :], 0), axis=-1)
    return (segment, positions - offset)


def rotation(relative, half_size):
    frequency = ROPE_BASE ** (-(2.0 * jnp.arange(half_size, dtype=jnp.float32)) / (2 * half_size))
    angles = relative.astype(jnp.float32)[:, None] * frequency[None, :]
    return (jnp.cos(angles), jnp.sin(angles))


def rotate(field, cosine, sine_part):
    row_count = field.shape[0]
    half_size = cosine.shape[-1]
    split_heads = field.reshape(row_count, -1, 2 * half_size)
    front_half = split_heads[..., :half_size]
    back_half = split_heads[..., half_size:]
    cos_rows = cosine[:, None, :]
    sin_rows = sine_part[:, None, :]
    turned = jnp.concatenate(
        [
            front_half * cos_rows - back_half * sin_rows,
            back_half * cos_rows + front_half * sin_rows,
        ],
        axis=-1,
    )
    return turned.reshape(row_count, -1)


def rms_back(d_normed, normed, scale):
    return scale * (d_normed - normed * jnp.mean(d_normed * normed, axis=-1, keepdims=True))


def score_block(query_part, key_part, visible):
    scores = jnp.einsum(
        "rgd,kd->grk", query_part, key_part, preferred_element_type=jnp.float32
    ) * HEAD_SIZE ** (-0.5)
    return jnp.where(visible[None], scores, MASKED)


def attend_pack(query_pack, key_pack, value_pack, visible_list):
    token_count = query_pack.shape[0]
    rounds = len(visible_list)
    query_group_width = QUERY_HEADS // KEY_VALUE_HEADS
    context_count = key_pack.shape[0] // token_count

    def width_per_head(head_index, carry):
        out_buf, total_buf = carry
        query_head = lax.dynamic_slice_in_dim(
            query_pack, head_index * query_group_width * HEAD_SIZE, query_group_width * HEAD_SIZE, 1
        ).reshape(token_count, query_group_width, HEAD_SIZE)
        key_head = lax.dynamic_slice_in_dim(key_pack, head_index * HEAD_SIZE, HEAD_SIZE, 1).reshape(
            context_count, rounds, BLK, HEAD_SIZE
        )
        value_head = lax.dynamic_slice_in_dim(
            value_pack, head_index * HEAD_SIZE, HEAD_SIZE, 1
        ).reshape(context_count, rounds, BLK, HEAD_SIZE)
        running_top = jnp.full((query_group_width, token_count), MASKED, jnp.float32)
        running_sum = jnp.zeros((query_group_width, token_count), jnp.float32)
        for round_index in range(rounds):
            first_row = round_index * BLK
            scores = score_block(
                query_head[first_row:],
                key_head[:, round_index].reshape(-1, HEAD_SIZE),
                visible_list[round_index],
            )
            new_top = jnp.maximum(running_top[:, first_row:], jnp.max(scores, axis=-1))
            weights = jnp.where(
                visible_list[round_index][None], jnp.exp(scores - new_top[..., None]), 0.0
            )
            new_sum = running_sum[:, first_row:] * jnp.exp(
                running_top[:, first_row:] - new_top
            ) + jnp.sum(weights, axis=-1)
            running_top = running_top.at[:, first_row:].set(new_top)
            running_sum = running_sum.at[:, first_row:].set(new_sum)
        log_totals = running_top + jnp.log(running_sum)
        mixture = jnp.zeros((token_count, query_group_width, HEAD_SIZE), jnp.float32)
        for round_index in range(rounds):
            first_row = round_index * BLK
            scores = score_block(
                query_head[first_row:],
                key_head[:, round_index].reshape(-1, HEAD_SIZE),
                visible_list[round_index],
            )
            prob_bf = jnp.where(
                visible_list[round_index][None],
                jnp.exp(scores - log_totals[:, first_row:, None]),
                0.0,
            ).astype(jnp.bfloat16)
            mixture = mixture.at[first_row:].add(
                jnp.einsum(
                    "grk,kd->rgd",
                    prob_bf,
                    value_head[:, round_index].reshape(-1, HEAD_SIZE),
                    preferred_element_type=jnp.float32,
                )
            )
        out_buf = lax.dynamic_update_slice_in_dim(
            out_buf,
            mixture.astype(jnp.bfloat16).reshape(token_count, -1),
            head_index * query_group_width * HEAD_SIZE,
            1,
        )
        total_buf = lax.dynamic_update_slice_in_dim(
            total_buf, log_totals, head_index * query_group_width, 0
        )
        return (out_buf, total_buf)

    start_offsets = (
        jnp.zeros((token_count, QUERY_HEADS * HEAD_SIZE), jnp.bfloat16),
        jnp.zeros((QUERY_HEADS, token_count), jnp.float32),
    )
    return lax.fori_loop(0, KEY_VALUE_HEADS, width_per_head, start_offsets)


def attend_back(
    query_pack, key_pack, value_pack, grad_pack, attended_pack, total_pack, visible_list
):
    token_count = query_pack.shape[0]
    rounds = len(visible_list)
    query_group_width = QUERY_HEADS // KEY_VALUE_HEADS
    context_count = key_pack.shape[0] // token_count

    def width_per_head(head_index, carry):
        query_buf, key_buf, value_buf = carry
        query_head = lax.dynamic_slice_in_dim(
            query_pack, head_index * query_group_width * HEAD_SIZE, query_group_width * HEAD_SIZE, 1
        ).reshape(token_count, query_group_width, HEAD_SIZE)
        grad_head = lax.dynamic_slice_in_dim(
            grad_pack, head_index * query_group_width * HEAD_SIZE, query_group_width * HEAD_SIZE, 1
        ).reshape(token_count, query_group_width, HEAD_SIZE)
        output_head = lax.dynamic_slice_in_dim(
            attended_pack,
            head_index * query_group_width * HEAD_SIZE,
            query_group_width * HEAD_SIZE,
            1,
        ).reshape(token_count, query_group_width, HEAD_SIZE)
        key_head = lax.dynamic_slice_in_dim(key_pack, head_index * HEAD_SIZE, HEAD_SIZE, 1).reshape(
            context_count, rounds, BLK, HEAD_SIZE
        )
        value_head = lax.dynamic_slice_in_dim(
            value_pack, head_index * HEAD_SIZE, HEAD_SIZE, 1
        ).reshape(context_count, rounds, BLK, HEAD_SIZE)
        log_totals = lax.dynamic_slice_in_dim(
            total_pack, head_index * query_group_width, query_group_width, 0
        )
        delta = jnp.sum(grad_head.astype(jnp.float32) * output_head.astype(jnp.float32), axis=-1).T
        query_grad = jnp.zeros((token_count, query_group_width, HEAD_SIZE), jnp.float32)
        key_parts = []
        value_parts = []
        for round_index in range(rounds):
            first_row = round_index * BLK
            key_round = key_head[:, round_index].reshape(-1, HEAD_SIZE)
            value_round = value_head[:, round_index].reshape(-1, HEAD_SIZE)
            scores = score_block(query_head[first_row:], key_round, visible_list[round_index])
            probs_full = jnp.where(
                visible_list[round_index][None],
                jnp.exp(scores - log_totals[:, first_row:, None]),
                0.0,
            )
            d_probs = jnp.einsum(
                "rgd,kd->grk",
                grad_head[first_row:],
                value_round,
                preferred_element_type=jnp.float32,
            )
            d_scores = (
                HEAD_SIZE ** (-0.5) * probs_full * (d_probs - delta[:, first_row:, None])
            ).astype(jnp.bfloat16)
            value_parts.append(
                jnp.einsum(
                    "grk,rgd->kd",
                    probs_full.astype(jnp.bfloat16),
                    grad_head[first_row:],
                    preferred_element_type=jnp.float32,
                )
            )
            key_parts.append(
                jnp.einsum(
                    "grk,rgd->kd",
                    d_scores,
                    query_head[first_row:],
                    preferred_element_type=jnp.float32,
                )
            )
            query_grad = query_grad.at[first_row:].add(
                jnp.einsum("grk,kd->rgd", d_scores, key_round, preferred_element_type=jnp.float32)
            )
        key_block = jnp.stack(
            [part.reshape(context_count, BLK, HEAD_SIZE) for part in key_parts], axis=1
        ).reshape(-1, HEAD_SIZE)
        value_block = jnp.stack(
            [part.reshape(context_count, BLK, HEAD_SIZE) for part in value_parts], axis=1
        ).reshape(-1, HEAD_SIZE)
        query_buf = lax.dynamic_update_slice_in_dim(
            query_buf,
            query_grad.reshape(token_count, -1),
            head_index * query_group_width * HEAD_SIZE,
            1,
        )
        key_buf = lax.dynamic_update_slice_in_dim(key_buf, key_block, head_index * HEAD_SIZE, 1)
        value_buf = lax.dynamic_update_slice_in_dim(
            value_buf, value_block, head_index * HEAD_SIZE, 1
        )
        return (query_buf, key_buf, value_buf)

    start_offsets = (
        jnp.zeros((token_count, QUERY_HEADS * HEAD_SIZE), jnp.float32),
        jnp.zeros((context_count * token_count, KEY_VALUE_HEADS * HEAD_SIZE), jnp.float32),
        jnp.zeros((context_count * token_count, KEY_VALUE_HEADS * HEAD_SIZE), jnp.float32),
    )
    return lax.fori_loop(0, KEY_VALUE_HEADS, width_per_head, start_offsets)


def local(
    tokens,
    seq_lengths,
    dealing,
    first_gain,
    query_weight,
    key_matrix,
    value_matrix,
    out_weight,
    second_gain,
    gate_weight,
    up_weight,
    down_weight,
    cotangent,
):
    context_count = lax.axis_size("ctx")
    my_index = lax.axis_index("ctx")
    pack_count, token_count, model_dim = tokens.shape
    rounds = token_count // BLK
    spread = context_count // rounds
    ctx_range = jnp.arange(context_count, dtype=jnp.int32)
    matches = (dealing[..., None] == ctx_range).astype(jnp.int32)
    slot_of = jnp.sum(matches * ctx_range[:, None], axis=2)
    block_of = jnp.arange(rounds, dtype=jnp.int32)[None, :, None] * context_count + slot_of
    key_pos = (
        jnp.transpose(block_of, (0, 2, 1))[..., None] * BLK + jnp.arange(BLK, dtype=jnp.int32)
    ).reshape(pack_count, -1)
    key_seg = place_rows(key_pos, seq_lengths)[0]
    query_pos = lax.dynamic_slice_in_dim(key_pos, my_index * token_count, token_count, 1)
    query_seg, query_rel = place_rows(query_pos, seq_lengths)
    home_row = lax.dynamic_index_in_dim(dealing, my_index // spread, 1, False)
    targets = lax.dynamic_slice_in_dim(home_row, my_index % spread * rounds, rounds, 1)
    picker = (targets[:, None, :] == ctx_range[None, :, None]).astype(jnp.bfloat16)
    my_slots = lax.dynamic_index_in_dim(slot_of, my_index, 2, False)
    owner_index = (
        jnp.arange(rounds, dtype=jnp.int32)[None, :] * context_count + my_slots
    ) // rounds
    keep_slot = jnp.repeat(owner_index, spread, axis=1) == ctx_range[None, :]

    def spread_out(field):
        blocks = field.reshape(pack_count, rounds, BLK, model_dim)
        return jnp.einsum(
            "pkj,pjtd->pktd", picker, blocks, preferred_element_type=jnp.float32
        ).astype(jnp.bfloat16)

    def collect(received):
        grouped = received.reshape(pack_count, rounds, spread, BLK, model_dim)
        return (
            jnp.sum(grouped, axis=2, dtype=jnp.float32)
            .astype(jnp.bfloat16)
            .reshape(pack_count * token_count, model_dim)
        )

    def send_home(field):
        blocks = jnp.repeat(field.reshape(pack_count, rounds, BLK, model_dim), spread, axis=1)
        return jnp.where(keep_slot[:, :, None, None], blocks, jnp.zeros_like(blocks))

    def restore(returned):
        placed = jnp.einsum("pkj,pktd->pjtd", picker, returned, preferred_element_type=jnp.float32)
        return placed.astype(jnp.bfloat16).reshape(pack_count, token_count, model_dim)

    dealt_tokens, dealt_upstream = (
        lax.all_to_all(spread_out(tokens), "ctx", split_axis=1, concat_axis=1, tiled=True),
        lax.all_to_all(spread_out(cotangent), "ctx", split_axis=1, concat_axis=1, tiled=True),
    )
    inputs = collect(dealt_tokens)
    upstream = collect(dealt_upstream)
    gain_one, query_full, key_full, value_full, out_full = (
        lax.all_gather(first_gain, "fsdp", axis=0, tiled=True),
        lax.all_gather(query_weight, "fsdp", axis=0, tiled=True),
        lax.all_gather(key_matrix, "fsdp", axis=0, tiled=True),
        lax.all_gather(value_matrix, "fsdp", axis=0, tiled=True),
        lax.all_gather(out_weight, "fsdp", axis=0, tiled=True),
    )
    gain_two, gate_full, up_full, down_full = (
        lax.all_gather(second_gain, "fsdp", axis=0, tiled=True),
        lax.all_gather(gate_weight, "fsdp", axis=0, tiled=True),
        lax.all_gather(up_weight, "fsdp", axis=0, tiled=True),
        lax.all_gather(down_weight, "fsdp", axis=0, tiled=True),
    )
    gain_one32 = gain_one.astype(jnp.float32)
    gain_two32 = gain_two.astype(jnp.float32)
    cosine, sine_part = rotation(query_rel.reshape(-1), HEAD_SIZE // 2)
    inputs32 = inputs.astype(jnp.float32)
    scale_one = lax.rsqrt(jnp.mean(inputs32 * inputs32, axis=-1, keepdims=True) + EPS)
    normed_one = inputs32 * scale_one
    xn_one = (normed_one * gain_one32).astype(jnp.bfloat16)
    query_rot = rotate(
        jnp.dot(xn_one, query_full, preferred_element_type=jnp.float32), cosine, sine_part
    ).astype(jnp.bfloat16)
    key_rot = rotate(
        jnp.dot(xn_one, key_full, preferred_element_type=jnp.float32), cosine, sine_part
    ).astype(jnp.bfloat16)
    rows_of_values = jnp.dot(xn_one, value_full, preferred_element_type=jnp.float32).astype(
        jnp.bfloat16
    )
    key_local = key_rot.reshape(pack_count, token_count, -1)
    value_local = rows_of_values.reshape(pack_count, token_count, -1)
    gathered_keys, gathered_values = (
        lax.all_gather(key_local, "ctx", axis=1, tiled=True),
        lax.all_gather(value_local, "ctx", axis=1, tiled=True),
    )
    key_pos_rounds = key_pos.reshape(pack_count, context_count, rounds, BLK)
    key_seg_rounds = key_seg.reshape(pack_count, context_count, rounds, BLK)
    visible = []
    for round_index in range(rounds):
        first_row = round_index * BLK
        round_pos = key_pos_rounds[:, :, round_index].reshape(pack_count, -1)
        round_seg = key_seg_rounds[:, :, round_index].reshape(pack_count, -1)
        same_seq = query_seg[:, first_row:, None] == round_seg[:, None, :]
        earlier = round_pos[:, None, :] <= query_pos[:, first_row:, None]
        visible.append(same_seq & earlier)
    query_packs = query_rot.reshape(pack_count, token_count, -1)
    pack_index = 0
    pack_visible = [mask[pack_index] for mask in visible]
    attended_pack, total_pack = attend_pack(
        query_packs[pack_index],
        gathered_keys[pack_index],
        gathered_values[pack_index],
        pack_visible,
    )
    total_list = [total_pack]
    softmax_totals = jnp.stack(total_list, axis=0)
    hidden_in = inputs32 + jnp.dot(attended_pack, out_full, preferred_element_type=jnp.float32)
    scale_two = lax.rsqrt(jnp.mean(hidden_in * hidden_in, axis=-1, keepdims=True) + EPS)
    normed_two = hidden_in * scale_two
    xn_two = (normed_two * gain_two32).astype(jnp.bfloat16)
    gate_val = jnp.dot(xn_two, gate_full, preferred_element_type=jnp.float32)
    up_val = jnp.dot(xn_two, up_full, preferred_element_type=jnp.float32)
    activated = jax.nn.silu(gate_val)
    hidden = (activated * up_val).astype(jnp.bfloat16)
    result = (hidden_in + jnp.dot(hidden, down_full, preferred_element_type=jnp.float32)).astype(
        jnp.bfloat16
    )
    down_grad = jnp.dot(hidden.T, upstream, preferred_element_type=jnp.float32)
    d_hidden = jnp.dot(upstream, down_full.T, preferred_element_type=jnp.float32)
    sigmoid_gate = jax.nn.sigmoid(gate_val)
    d_gate = (d_hidden * up_val * sigmoid_gate * (1.0 + gate_val * (1.0 - sigmoid_gate))).astype(
        jnp.bfloat16
    )
    d_up = (d_hidden * activated).astype(jnp.bfloat16)
    gate_grad = jnp.dot(xn_two.T, d_gate, preferred_element_type=jnp.float32)
    up_grad = jnp.dot(xn_two.T, d_up, preferred_element_type=jnp.float32)
    d_norm_two = jnp.dot(d_gate, gate_full.T, preferred_element_type=jnp.float32) + jnp.dot(
        d_up, up_full.T, preferred_element_type=jnp.float32
    )
    gain_two_grad = jnp.sum(d_norm_two * normed_two, axis=0)
    d_hidden_in = upstream.astype(jnp.float32) + rms_back(
        d_norm_two * gain_two32, normed_two, scale_two
    )
    mlp_parts = (
        lax.psum_scatter(
            gain_two_grad.astype(jnp.bfloat16), "fsdp", scatter_dimension=0, tiled=True
        ).astype(jnp.float32),
        lax.psum_scatter(
            gate_grad.astype(jnp.bfloat16), "fsdp", scatter_dimension=0, tiled=True
        ).astype(jnp.float32),
        lax.psum_scatter(
            up_grad.astype(jnp.bfloat16), "fsdp", scatter_dimension=0, tiled=True
        ).astype(jnp.float32),
        lax.psum_scatter(
            down_grad.astype(jnp.bfloat16), "fsdp", scatter_dimension=0, tiled=True
        ).astype(jnp.float32),
    )
    d_branch = d_hidden_in.astype(jnp.bfloat16)
    out_grad = jnp.dot(attended_pack.T, d_branch, preferred_element_type=jnp.float32)
    d_attended = jnp.dot(d_branch, out_full.T, preferred_element_type=jnp.float32).astype(
        jnp.bfloat16
    )
    back_keys, back_values = (gathered_keys, gathered_values)
    grad_packs = d_attended.reshape(pack_count, token_count, -1)
    out_packs = attended_pack.reshape(pack_count, token_count, -1)
    pack_index = 0
    pack_visible = [mask[pack_index] for mask in visible]
    query_part, key_part, value_part = attend_back(
        query_packs[pack_index],
        back_keys[pack_index],
        back_values[pack_index],
        grad_packs[pack_index],
        out_packs[pack_index],
        softmax_totals[pack_index],
        pack_visible,
    )
    key_list = [key_part]
    value_list = [value_part]
    d_keys, d_values = (
        lax.psum_scatter(
            jnp.stack(key_list, axis=0).astype(jnp.bfloat16), "ctx", scatter_dimension=1, tiled=True
        ).astype(jnp.float32),
        lax.psum_scatter(
            jnp.stack(value_list, axis=0).astype(jnp.bfloat16),
            "ctx",
            scatter_dimension=1,
            tiled=True,
        ).astype(jnp.float32),
    )
    d_query = rotate(query_part, cosine, -sine_part).astype(jnp.bfloat16)
    d_key = rotate(d_keys.reshape(pack_count * token_count, -1), cosine, -sine_part).astype(
        jnp.bfloat16
    )
    d_value = d_values.reshape(pack_count * token_count, -1).astype(jnp.bfloat16)
    query_grad = jnp.dot(xn_one.T, d_query, preferred_element_type=jnp.float32)
    key_grad = jnp.dot(xn_one.T, d_key, preferred_element_type=jnp.float32)
    value_grad = jnp.dot(xn_one.T, d_value, preferred_element_type=jnp.float32)
    d_norm_one = (
        jnp.dot(d_query, query_full.T, preferred_element_type=jnp.float32)
        + jnp.dot(d_key, key_full.T, preferred_element_type=jnp.float32)
        + jnp.dot(d_value, value_full.T, preferred_element_type=jnp.float32)
    )
    gain_one_grad = jnp.sum(d_norm_one * normed_one, axis=0)
    d_inputs = d_hidden_in + rms_back(d_norm_one * gain_one32, normed_one, scale_one)
    attn_parts = (
        lax.psum_scatter(
            gain_one_grad.astype(jnp.bfloat16), "fsdp", scatter_dimension=0, tiled=True
        ).astype(jnp.float32),
        lax.psum_scatter(
            query_grad.astype(jnp.bfloat16), "fsdp", scatter_dimension=0, tiled=True
        ).astype(jnp.float32),
        lax.psum_scatter(
            key_grad.astype(jnp.bfloat16), "fsdp", scatter_dimension=0, tiled=True
        ).astype(jnp.float32),
        lax.psum_scatter(
            value_grad.astype(jnp.bfloat16), "fsdp", scatter_dimension=0, tiled=True
        ).astype(jnp.float32),
        lax.psum_scatter(
            out_grad.astype(jnp.bfloat16), "fsdp", scatter_dimension=0, tiled=True
        ).astype(jnp.float32),
    )
    finished = (
        lax.psum(attn_parts[0].astype(jnp.bfloat16), ("ctx", "grp")).astype(jnp.float32),
        lax.psum(attn_parts[1].astype(jnp.bfloat16), ("ctx", "grp")).astype(jnp.float32),
        lax.psum(attn_parts[2].astype(jnp.bfloat16), ("ctx", "grp")).astype(jnp.float32),
        lax.psum(attn_parts[3].astype(jnp.bfloat16), ("ctx", "grp")).astype(jnp.float32),
        lax.psum(attn_parts[4].astype(jnp.bfloat16), ("ctx", "grp")).astype(jnp.float32),
        lax.psum(mlp_parts[0].astype(jnp.bfloat16), ("ctx", "grp")).astype(jnp.float32),
        lax.psum(mlp_parts[1].astype(jnp.bfloat16), ("ctx", "grp")).astype(jnp.float32),
        lax.psum(mlp_parts[2].astype(jnp.bfloat16), ("ctx", "grp")).astype(jnp.float32),
        lax.psum(mlp_parts[3].astype(jnp.bfloat16), ("ctx", "grp")).astype(jnp.float32),
    )
    home_out, home_grad = (
        lax.all_to_all(send_home(result), "ctx", split_axis=1, concat_axis=1, tiled=True),
        lax.all_to_all(
            send_home(d_inputs.astype(jnp.bfloat16)), "ctx", split_axis=1, concat_axis=1, tiled=True
        ),
    )
    return (
        restore(home_out),
        restore(home_grad),
        softmax_totals,
        finished[0],
        finished[1],
        finished[2],
        finished[3],
        finished[4],
        finished[5],
        finished[6],
        finished[7],
        finished[8],
    )


MINLEN = 1024
QB = 256
VMEM_LIMIT = 56 * 1024 * 1024


def fill_tables(cl_ref, sl_ref, ch_ref, sh_ref, c_ref, s_ref):
    @pl.when(pl.program_id(0) == 0)
    def _():
        cos_low, sin_low = cl_ref[...], sl_ref[...]
        for i in range(c_ref.shape[1] // BLK):
            at = slice(i * BLK, (i + 1) * BLK)
            cos_high, sin_high = ch_ref[:, i : i + 1], sh_ref[:, i : i + 1]
            c_ref[:, at] = cos_high * cos_low - sin_high * sin_low
            s_ref[:, at] = sin_high * cos_low + cos_high * sin_low


def attend_kernel(
    place, q_ref, k_ref, v_ref, cl_ref, sl_ref, ch_ref, sh_ref,
    keep_ref, send_ref, lse_ref, qr_ref, kr_ref, vr_ref, held, c_ref, s_ref,
):
    fill_tables(cl_ref, sl_ref, ch_ref, sh_ref, c_ref, s_ref)
    cosine = c_ref[...]
    sine = s_ref[...]
    half = HEAD_SIZE // 2
    seq = cosine.shape[1]

    def turn(field):
        front, back = field[:half], field[half:]
        return jnp.concatenate(
            [front * cosine - back * sine, back * cosine + front * sine], axis=0
        )

    k_rot = turn(k_ref[...])
    kr_ref[...] = k_rot.astype(jnp.bfloat16)
    key = k_rot.T.astype(jnp.bfloat16)
    val_t = v_ref[...].astype(jnp.bfloat16)
    vr_ref[...] = val_t
    q0 = turn(q_ref[:HEAD_SIZE]).astype(jnp.bfloat16)
    q1 = turn(q_ref[HEAD_SIZE:]).astype(jnp.bfloat16)
    qr_ref[:HEAD_SIZE] = q0
    qr_ref[HEAD_SIZE:] = q1
    rows = lax.broadcasted_iota(jnp.int32, (QB, 2 * QB), 0)
    cols = lax.broadcasted_iota(jnp.int32, (QB, 2 * QB), 1)
    keep = rows <= jnp.where(cols >= QB, cols - QB, cols)
    for b in range(seq // QB):
        lo, n = b * QB, (b + 1) * QB
        q_t = jnp.concatenate([q0[:, lo:n], q1[:, lo:n]], axis=1)
        scores = jnp.dot(key[:n], q_t, preferred_element_type=jnp.float32) * HEAD_SIZE ** (-0.5)
        diag = jnp.where(keep, scores[lo:], MASKED)
        top = jnp.max(diag, axis=0, keepdims=True)
        if b > 0:
            top = jnp.maximum(top, jnp.max(scores[:lo], axis=0, keepdims=True))
        e_diag = jnp.exp(diag - top)
        total = jnp.sum(e_diag, axis=0, keepdims=True)
        out = jnp.dot(val_t[:, lo:n], e_diag.astype(jnp.bfloat16), preferred_element_type=jnp.float32)
        if b > 0:
            e_rest = jnp.exp(scores[:lo] - top)
            total = total + jnp.sum(e_rest, axis=0, keepdims=True)
            out = out + jnp.dot(
                val_t[:, :lo], e_rest.astype(jnp.bfloat16), preferred_element_type=jnp.float32
            )
        out = (out / total).astype(jnp.bfloat16)
        held[:HEAD_SIZE, lo:n] = out[:, :QB]
        held[HEAD_SIZE:, lo:n] = out[:, QB:]
        lse = top + jnp.log(total)
        lse_ref[0, 0:1, lo:n] = lse[:, :QB]
        lse_ref[0, 1:2, lo:n] = lse[:, QB:]
    tok = seq // 2
    for core in range(2):

        @pl.when(place[0] == core)
        def _():
            keep_ref[...] = held[:, core * tok : (core + 1) * tok]
            send_ref[...] = held[:, (1 - core) * tok : (2 - core) * tok]


def attend_seq(place, qkv_t, tables):
    rows, seq = qkv_t.shape
    kv = rows // (4 * HEAD_SIZE)
    group = pl.BlockSpec((2 * HEAD_SIZE, seq), lambda j: (j, 0))

    def head(base):
        return pl.BlockSpec((HEAD_SIZE, seq), lambda j: (base + j, 0))

    table = pl.BlockSpec(memory_space=pltpu.VMEM)
    return pl.pallas_call(
        attend_kernel,
        grid=(kv,),
        in_specs=[pl.BlockSpec(memory_space=pltpu.SMEM), group, head(2 * kv), head(3 * kv), table, table, table, table],
        out_specs=[
            pl.BlockSpec((2 * HEAD_SIZE, seq // 2), lambda j: (j, 0)),
            pl.BlockSpec((2 * HEAD_SIZE, seq // 2), lambda j: (j, 0)),
            pl.BlockSpec((1, 2, seq), lambda j: (j, 0, 0)),
            group,
            head(0),
            head(0),
        ],
        out_shape=[
            jax.ShapeDtypeStruct((2 * kv * HEAD_SIZE, seq // 2), jnp.bfloat16),
            jax.ShapeDtypeStruct((2 * kv * HEAD_SIZE, seq // 2), jnp.bfloat16),
            jax.ShapeDtypeStruct((kv, 2, seq), jnp.float32),
            jax.ShapeDtypeStruct((2 * kv * HEAD_SIZE, seq), jnp.bfloat16),
            jax.ShapeDtypeStruct((kv * HEAD_SIZE, seq), jnp.bfloat16),
            jax.ShapeDtypeStruct((kv * HEAD_SIZE, seq), jnp.bfloat16),
        ],
        scratch_shapes=[
            pltpu.VMEM((2 * HEAD_SIZE, seq), jnp.bfloat16),
            pltpu.VMEM((HEAD_SIZE // 2, seq), jnp.float32),
            pltpu.VMEM((HEAD_SIZE // 2, seq), jnp.float32),
        ],
        compiler_params=pltpu.CompilerParams(vmem_limit_bytes=VMEM_LIMIT),
        cost_estimate=pl.CostEstimate(
            flops=4 * kv * 2 * seq * seq * HEAD_SIZE, bytes_accessed=10 * rows * seq, transcendentals=kv * seq * seq
        ),
        name="attend",
    )(place, qkv_t, qkv_t, qkv_t, *tables)


def attend_back_kernel(
    place, q_ref, k_ref, v_ref, keep_ref, got_ref, lse_ref, cl_ref, sl_ref, ch_ref, sh_ref,
    dq_ref, dk_ref, dv_ref, dk_acc, dv_acc, c_ref, s_ref,
):
    fill_tables(cl_ref, sl_ref, ch_ref, sh_ref, c_ref, s_ref)
    half = HEAD_SIZE // 2
    cosine = c_ref[...]
    sine = s_ref[...]
    seq = cosine.shape[1]

    def turn_back(field, cos, sin):
        front, back = field[:half], field[half:]
        return jnp.concatenate([front * cos + back * sin, back * cos - front * sin], axis=0)

    def flip(field):
        return field.astype(jnp.float32).T.astype(jnp.bfloat16)

    key_t = k_ref[...]
    key = flip(key_t)
    val = flip(v_ref[...])
    q0_t, q1_t = q_ref[:HEAD_SIZE], q_ref[HEAD_SIZE:]
    first_core = place[0] == 0
    early = jnp.where(first_core, keep_ref[...], got_ref[...])
    late = jnp.where(first_core, got_ref[...], keep_ref[...])
    grads = jnp.concatenate([early, late], axis=1)
    g0_t, g1_t = grads[:HEAD_SIZE], grads[HEAD_SIZE:]
    q0, q1, g0, g1 = flip(q0_t), flip(q1_t), flip(g0_t), flip(g1_t)
    dk_acc[...] = jnp.zeros_like(dk_acc)
    dv_acc[...] = jnp.zeros_like(dv_acc)
    rows = lax.broadcasted_iota(jnp.int32, (QB, 2 * QB), 0)
    cols = lax.broadcasted_iota(jnp.int32, (QB, 2 * QB), 1)
    keep = rows <= jnp.where(cols >= QB, cols - QB, cols)
    for b in range(seq // QB):
        lo, n = b * QB, (b + 1) * QB
        q_t = jnp.concatenate([q0_t[:, lo:n], q1_t[:, lo:n]], axis=1)
        g_t = jnp.concatenate([g0_t[:, lo:n], g1_t[:, lo:n]], axis=1)
        q_n = jnp.concatenate([q0[lo:n], q1[lo:n]], axis=0)
        g_n = jnp.concatenate([g0[lo:n], g1[lo:n]], axis=0)
        lse = jnp.concatenate([lse_ref[0, 0:1, lo:n], lse_ref[0, 1:2, lo:n]], axis=1)
        parts = []
        delta = None
        for start, stop in ([(0, lo)] if b > 0 else []) + [(lo, n)]:
            scores = jnp.dot(key[start:stop], q_t, preferred_element_type=jnp.float32) * HEAD_SIZE ** (-0.5)
            prob = jnp.exp(scores - lse)
            if start == lo:
                prob = jnp.where(keep, prob, 0.0)
            d_prob = jnp.dot(val[start:stop], g_t, preferred_element_type=jnp.float32)
            part = jnp.sum(prob * d_prob, axis=0, keepdims=True)
            delta = part if delta is None else delta + part
            dv_acc[start:stop] += jnp.dot(prob.astype(jnp.bfloat16), g_n, preferred_element_type=jnp.float32)
            parts.append((start, stop, prob, d_prob))
        dq_t = None
        for start, stop, prob, d_prob in parts:
            d_score = (prob * (d_prob - delta) * HEAD_SIZE ** (-0.5)).astype(jnp.bfloat16)
            dk_acc[start:stop] += jnp.dot(d_score, q_n, preferred_element_type=jnp.float32)
            part = jnp.dot(key_t[:, start:stop], d_score, preferred_element_type=jnp.float32)
            dq_t = part if dq_t is None else dq_t + part
        cos, sin = cosine[:, lo:n], sine[:, lo:n]
        dq_ref[:HEAD_SIZE, lo:n] = turn_back(dq_t[:, :QB], cos, sin).astype(jnp.bfloat16)
        dq_ref[HEAD_SIZE:, lo:n] = turn_back(dq_t[:, QB:], cos, sin).astype(jnp.bfloat16)
    dk_ref[...] = turn_back(dk_acc[...].T, cosine, sine).astype(jnp.bfloat16)
    dv_ref[...] = dv_acc[...].T.astype(jnp.bfloat16)


def attend_seq_back(place, q_t, k_t, v_t, g_keep, g_got, lse, tables):
    rows, seq = k_t.shape
    kv = rows // HEAD_SIZE
    group = pl.BlockSpec((2 * HEAD_SIZE, seq), lambda j: (j, 0))
    part = pl.BlockSpec((2 * HEAD_SIZE, seq // 2), lambda j: (j, 0))
    head = pl.BlockSpec((HEAD_SIZE, seq), lambda j: (j, 0))
    table = pl.BlockSpec(memory_space=pltpu.VMEM)
    return pl.pallas_call(
        attend_back_kernel,
        grid=(kv,),
        in_specs=[
            pl.BlockSpec(memory_space=pltpu.SMEM), group, head, head, part, part,
            pl.BlockSpec((1, 2, seq), lambda j: (j, 0, 0)), table, table, table, table,
        ],
        out_specs=[group, head, head],
        out_shape=[
            jax.ShapeDtypeStruct((2 * rows, seq), jnp.bfloat16),
            jax.ShapeDtypeStruct((rows, seq), jnp.bfloat16),
            jax.ShapeDtypeStruct((rows, seq), jnp.bfloat16),
        ],
        scratch_shapes=[
            pltpu.VMEM((seq, HEAD_SIZE), jnp.float32),
            pltpu.VMEM((seq, HEAD_SIZE), jnp.float32),
            pltpu.VMEM((HEAD_SIZE // 2, seq), jnp.float32),
            pltpu.VMEM((HEAD_SIZE // 2, seq), jnp.float32),
        ],
        compiler_params=pltpu.CompilerParams(vmem_limit_bytes=VMEM_LIMIT),
        cost_estimate=pl.CostEstimate(
            flops=10 * kv * 2 * seq * seq * HEAD_SIZE, bytes_accessed=20 * rows * seq, transcendentals=kv * seq * seq
        ),
        name="attend_back",
    )(place, q_t, k_t, v_t, g_keep, g_got, lse, *tables)


def fp32(field):
    return field.astype(jnp.float32)


def mm(left, right, dims=((1,), (0,)), out=jnp.float32):
    return lax.dot_general(left, right, (dims, ((), ())), preferred_element_type=out)


ANY = pl.BlockSpec(memory_space=pl.ANY)
SMEM = pl.BlockSpec(memory_space=pltpu.SMEM)
VM = pl.BlockSpec(memory_space=pltpu.VMEM)
PARAMS = pltpu.CompilerParams(vmem_limit_bytes=VMEM_LIMIT)
MESH = pl.DeviceIdType.MESH
TILE = 256


def bf16_like(*dims):
    return jax.ShapeDtypeStruct(dims, jnp.bfloat16)


def f32_like(*dims):
    return jax.ShapeDtypeStruct(dims, jnp.float32)


def cost(flops, moved):
    return pl.CostEstimate(flops=int(flops), bytes_accessed=int(moved), transcendentals=0)


class Spots:
    def __init__(self):
        z, f, g = lax.axis_index("ctx"), lax.axis_index("fsdp"), lax.axis_index("grp")
        self.z, self.f, self.g = z, f, g
        self.parity = z % 2
        self.fx = f + 1 - 2 * (f % 2)
        self.fy = f + 2 - 4 * (f // 2)
        self.fd = 3 - f
        across = z + 1 - 2 * self.parity
        self.x = (z, self.fx, g)
        self.y = (z, self.fy, g)
        self.diag = (z, self.fd, g)
        self.core = (z, f, 1 - g)
        self.across = (across, f, g)
        self.swap = (across, f, 1 - g)


def greet(*partners):
    barrier = pltpu.get_barrier_semaphore()
    for partner in partners:
        pl.semaphore_signal(barrier, inc=1, device_id=partner, device_id_type=MESH)
    pl.semaphore_wait(barrier, len(partners))


def rows_at(start, size):
    return pl.ds(pl.multiple_of(start, size), size)


def gather_kernel(
    tokens, cotangent, wq, wk, wv, wo, gate, up, down, gain,
    qkv_o, out_o, pair_o, down_o, x_o, dy_o, gain_o, xn_o, turned_o,
    send, recv, near, far, qkv_v, out_v, pair_v, down_v, tok_v, gain_v,
    extra, x_v, w_v, gains_v, xn_v, turned_v,
):
    at = Spots()
    g, f, parity = at.g, at.f, at.parity
    greet(at.x, at.y, at.diag, at.core, at.across, at.swap)
    taken = [0, 0]

    def remote(src, dst, device):
        i = taken[0]
        taken[0] += 1
        return pltpu.make_async_remote_copy(
            src_ref=src, dst_ref=dst, send_sem=send.at[i], recv_sem=recv.at[i],
            device_id=device, device_id_type=MESH,
        )

    class Bounce:
        def __init__(self, src, via, dst):
            i = taken[1]
            taken[1] += 1
            self.first = pltpu.make_async_copy(src, via, near.at[i])
            self.second = pltpu.make_async_copy(via, dst, far.at[i])

        def start(self):
            self.first.start()

        def turn(self):
            self.first.wait()
            self.second.start()

        def wait(self):
            self.second.wait()

    def start(copies):
        for copy in copies:
            copy.start()
        return copies

    def arrive(copies):
        for copy in copies:
            copy.wait_recv()

    tok = tokens.shape[1]
    feat = wq.shape[0]
    mid = feat // 2
    nq, nk, nv = (w.shape[1] // 2 for w in (wq, wk, wv))
    nf = gate.shape[1] // 8
    wide = wo.shape[1] // 2
    count = 4
    top, low = slice(0, mid), slice(mid, feat)

    mine = rows_at(g * tok, tok)
    swaps = [
        remote(tokens.at[0], x_o.at[mine], at.swap),
        remote(cotangent.at[0], dy_o.at[mine], at.swap),
    ]
    keeps = [
        Bounce(tokens.at[0], tok_v.at[0], x_o.at[mine]),
        Bounce(cotangent.at[0], tok_v.at[1], dy_o.at[mine]),
    ]
    away = rows_at((1 - g) * tok, tok)
    swaps_out = [
        pltpu.make_async_remote_copy(
            src_ref=array.at[0], dst_ref=into.at[away], send_sem=send.at[i], recv_sem=recv.at[i],
            device_id=at.swap, device_id_type=MESH,
        )
        for i, (array, into) in enumerate(((tokens, x_o), (cotangent, dy_o)))
    ]
    shares = [remote(x_o.at[mine], x_o.at[mine], at.core), remote(dy_o.at[mine], dy_o.at[mine], at.core)]

    @pl.when(g != parity)
    def _():
        start(swaps_out)

    @pl.when(g == parity)
    def _():
        start(keeps)
        for copy in keeps:
            copy.turn()

    own_rows = f * feat
    shared_cols = (count - 1) * nf

    def pair_direct(part, device):
        first = taken[0]
        taken[0] += count + 1
        rows = rows_at(own_rows + part.start, mid)

        def made(array, index, k, i):
            return pltpu.make_async_remote_copy(
                src_ref=array.at[part, rows_at((2 * k + g) * nf, nf)],
                dst_ref=pair_o.at[index, rows, rows_at(k * nf, nf)],
                send_sem=send.at[first + i], recv_sem=recv.at[first + i],
                device_id=device, device_id_type=MESH,
            )

        def some(array):
            return [made(array, parity, k, k) for k in range(count - 1)]

        @pl.when(parity == 0)
        def _():
            start(some(gate))

        @pl.when(parity == 1)
        def _():
            start(some(up))

        last = start([made(gate, 0, count - 1, count - 1), made(up, 1, count - 1, count)])
        return some(gate), last

    pair_xt, last_xt = pair_direct(top, at.x)
    pair_yl, last_yl = pair_direct(low, at.y)
    pair_xl, last_xl = pair_direct(low, at.x)
    pair_yt, last_yt = pair_direct(top, at.y)

    def qkv_direct(part, device):
        copies = []
        for array, width, column in ((wq, nq, 0), (wk, nk, nq), (wv, nv, nq + nk)):
            copies.append(
                remote(
                    array.at[part, rows_at(g * width, width)],
                    qkv_o.at[rows_at(own_rows + part.start, mid), column : column + width],
                    device,
                )
            )
        return start(copies)

    qkv_xt = qkv_direct(top, at.x)
    qkv_yl = qkv_direct(low, at.y)
    qkv_xl = qkv_direct(low, at.x)
    qkv_yt = qkv_direct(top, at.y)

    own = rows_at(own_rows, feat)
    locals_ = [
        Bounce(
            array.at[:, rows_at(g * width, width)],
            qkv_v.at[:, column : column + width],
            qkv_o.at[own, column : column + width],
        )
        for array, width, column in ((wq, nq, 0), (wk, nk, nq), (wv, nv, nq + nk))
    ]
    locals_.append(Bounce(wo, out_v, out_o.at[own]))
    locals_.append(Bounce(down.at[rows_at(g * nf, nf)], down_v, down_o))
    for array, index in ((gate, 0), (up, 1)):
        for k in range(count):
            locals_.append(
                Bounce(
                    array.at[:, rows_at((2 * k + g) * nf, nf)],
                    pair_v.at[index, :, rows_at(k * nf, nf)],
                    pair_o.at[index, own, rows_at(k * nf, nf)],
                )
            )
    gain_place = gain_o.at[pl.ds(f, 1)]
    locals_.append(Bounce(gain, gain_v, gain_place))
    start(locals_)
    for copy in locals_:
        copy.turn()
    gains = start([remote(gain, gain_place, to) for to in (at.x, at.y, at.diag)])

    def forward(array_at, rows_x, rows_y):
        return remote(array_at(rows_x), array_at(rows_x), at.y), remote(
            array_at(rows_y), array_at(rows_y), at.x
        )

    x_top, y_low = rows_at(at.fx * feat, mid), rows_at(at.fy * feat + mid, mid)
    x_low, y_top = rows_at(at.fx * feat + mid, mid), rows_at(at.fy * feat, mid)
    d_top, d_low = rows_at(at.fd * feat, mid), rows_at(at.fd * feat + mid, mid)

    def pair_view(rows):
        return pair_o.at[parity, rows, 0:shared_cols]

    def last_view(rows):
        return pair_o.at[:, rows, shared_cols : shared_cols + nf]

    def out_view(rows):
        return out_o.at[rows, rows_at(g * wide, wide)]

    pair_fy, pair_fx = forward(pair_view, x_top, y_low)
    last_fy, last_fx = forward(last_view, x_top, y_low)
    sends = [pair_fy, pair_fx, last_fy, last_fx]

    def across(rows):
        copy = remote(pair_view(rows), pair_view(rows), at.across)
        copy.start()
        sends.append(copy)
        return copy

    arrive(pair_xt)
    pair_fy.start()
    z_copies = [across(x_top)]
    arrive(pair_yl)
    pair_fx.start()
    z_copies.append(across(y_low))

    def out_direct(part, device):
        copy = remote(
            wo.at[part, rows_at(g * wide, wide)],
            out_o.at[rows_at(own_rows + part.start, mid), rows_at(g * wide, wide)],
            device,
        )
        copy.start()
        return copy

    out_xt, out_yl = out_direct(top, at.x), out_direct(low, at.y)
    out_xl, out_yt = out_direct(low, at.x), out_direct(top, at.y)

    arrive(pair_xl)
    z_copies.append(across(x_low))
    arrive(pair_yt)
    z_copies.append(across(y_top))

    def qkv_view(rows):
        return qkv_o.at[rows]

    qkv_fy, qkv_fx = forward(qkv_view, x_top, y_low)
    arrive(qkv_xt)
    qkv_fy.start()
    arrive(qkv_yl)
    qkv_fx.start()
    arrive(last_xt)
    last_fy.start()
    arrive(last_yl)
    last_fx.start()

    pair_fy.wait_recv()
    z_copies.append(across(d_top))
    pair_fx.wait_recv()
    z_copies.append(across(d_low))

    for i in range(2):

        @pl.when(g != parity)
        def _():
            swaps[i].wait_recv()
            swaps_out[i].wait_send()

        @pl.when(g == parity)
        def _():
            keeps[i].wait()

        shares[i].start()

    out_fy, out_fx = forward(out_view, x_top, y_low)
    out_xt.wait_recv()
    out_fy.start()
    out_yl.wait_recv()
    out_fx.start()
    out_xl.wait_recv()
    out_yt.wait_recv()

    def share(rows):
        copy = remote(out_view(rows), out_view(rows), at.core)
        copy.start()
        return copy

    shared = [share(x_top), share(x_low), share(y_top), share(y_low)]

    arrive(qkv_xl + qkv_yt + [qkv_fy, qkv_fx] + gains + shares[:1])
    for copy in locals_[:3] + locals_[-1:]:
        copy.wait()
    loads = [
        pltpu.make_async_copy(src, dst, extra.at[i])
        for i, (src, dst) in enumerate(((x_o, x_v), (gain_o, gains_v), (qkv_o, w_v)))
    ]
    start(loads)
    for copy in loads:
        copy.wait()
    row = gain_row(gains_v, 0)

    @pl.loop(0, x_v.shape[0] // TILE)
    def _(n):
        part = rows_at(n * TILE, TILE)
        field = fp32(x_v[part, :])
        xn_v[part, :] = (field * norm_scale(field) * row).astype(jnp.bfloat16)

    @pl.loop(0, w_v.shape[1] // TILE)
    def _(n):
        part = rows_at(n * TILE, TILE)
        turned_v[part, :] = mm(w_v[:, part].T, xn_v[...], ((1,), (1,)))

    results = start(
        [pltpu.make_async_copy(xn_v, xn_o, extra.at[3]), pltpu.make_async_copy(turned_v, turned_o, extra.at[4])]
    )

    out_fy.wait_recv()
    shared.append(share(d_top))
    out_fx.wait_recv()
    shared.append(share(d_low))

    arrive([last_fy, last_fx])
    arrive(last_xl + last_yt)
    arrive(shares[1:])
    arrive(shared)
    arrive(z_copies)
    for copy in locals_[3:-1] + results:
        copy.wait()
    for copy in (
        pair_xt + pair_yl + pair_xl + pair_yt + qkv_xt + qkv_yl + qkv_xl + qkv_yt + gains
        + sends + shares + shared
        + [out_xt, out_yl, out_xl, out_yt, out_fy, out_fx, qkv_fy, qkv_fx]
        + last_xt + last_yl + last_xl + last_yt
    ):
        copy.wait_send()


def gather_all(tokens, cotangent, wq, wk, wv, wo, gate, up, down, gain):
    tok, width = tokens.shape[1:]
    nf = gate.shape[1] // 8
    cols = (wq.shape[1] + wk.shape[1] + wv.shape[1]) // 2
    return pl.pallas_call(
        gather_kernel,
        in_specs=[ANY] * 10,
        out_specs=[ANY] * 9,
        out_shape=[
            bf16_like(width, cols),
            bf16_like(4 * wo.shape[0], width),
            bf16_like(2, width, 4 * nf),
            bf16_like(nf, width),
            bf16_like(2 * tok, width),
            bf16_like(2 * tok, width),
            jax.ShapeDtypeStruct((4,) + gain.shape[1:], gain.dtype),
            bf16_like(2 * tok, width),
            f32_like(cols, 2 * tok),
        ],
        scratch_shapes=[
            pltpu.SemaphoreType.DMA((72,)),
            pltpu.SemaphoreType.DMA((72,)),
            pltpu.SemaphoreType.DMA((20,)),
            pltpu.SemaphoreType.DMA((20,)),
            pltpu.VMEM((width // 4, cols), jnp.bfloat16),
            pltpu.VMEM(wo.shape, jnp.bfloat16),
            pltpu.VMEM((2, width // 4, 4 * nf), jnp.bfloat16),
            pltpu.VMEM((nf, width), jnp.bfloat16),
            pltpu.VMEM((2, tok, width), jnp.bfloat16),
            pltpu.VMEM(gain.shape, gain.dtype),
            pltpu.SemaphoreType.DMA((5,)),
            pltpu.VMEM((2 * tok, width), jnp.bfloat16),
            pltpu.VMEM((width, cols), jnp.bfloat16),
            pltpu.VMEM((4,) + gain.shape[1:], gain.dtype),
            pltpu.VMEM((2 * tok, width), jnp.bfloat16),
            pltpu.VMEM((cols, 2 * tok), jnp.float32),
        ],
        compiler_params=pltpu.CompilerParams(
            collective_id=0, has_side_effects=True, vmem_limit_bytes=VMEM_LIMIT
        ),
        cost_estimate=cost(0, 500e6),
        name="gather",
    )(tokens, cotangent, wq, wk, wv, wo, gate, up, down, gain)


def gain_row(gain, which):
    return jnp.concatenate([gain[k, which : which + 1, :] for k in range(gain.shape[0])], axis=1)


def norm_scale(field):
    return lax.rsqrt(jnp.mean(field * field, axis=-1, keepdims=True) + EPS)


def residual_kernel(place, x_ref, attn_keep, attn_got, gain, w_ref, h_ref, xn_ref, attn_ref):
    core = place[0]
    heads = attn_keep.shape[0]
    keep_at, got_at = rows_at(core * heads, heads), rows_at((1 - core) * heads, heads)
    attn_ref[keep_at, :] = attn_keep[...]
    attn_ref[got_at, :] = attn_got[...]
    field = fp32(x_ref[...]) + mm(attn_ref[...].T, w_ref[...])
    h_ref[...] = field
    xn_ref[...] = (field * norm_scale(field) * gain_row(gain, 1)).astype(jnp.bfloat16)


def residual(place, x_seq, attn_keep, attn_got, gains, weight):
    seq, width = x_seq.shape
    tok = seq // 2
    heads = attn_keep.shape[0]
    steps = tok // TILE
    rows = pl.BlockSpec((TILE, width), lambda i, place: (i, 0))
    return pl.pallas_call(
        residual_kernel,
        grid_spec=pltpu.PrefetchScalarGridSpec(
            num_scalar_prefetch=1,
            grid=(steps,),
            in_specs=[
                pl.BlockSpec((TILE, width), lambda i, place: (steps * place[0] + i, 0)),
                pl.BlockSpec((heads, TILE), lambda i, place: (0, i)),
                pl.BlockSpec((heads, TILE), lambda i, place: (0, i)),
                VM,
                VM,
            ],
            out_specs=[rows, rows, pl.BlockSpec((2 * heads, TILE), lambda i, place: (0, i))],
        ),
        out_shape=[f32_like(tok, width), bf16_like(tok, width), bf16_like(2 * heads, tok)],
        compiler_params=PARAMS,
        cost_estimate=cost(2 * tok * width * weight.shape[0], 14e6),
        name="residual",
    )(place, x_seq, attn_keep, attn_got, gains, weight)


def hidden_kernel(place, xn_own, xn_got, gate_w, up_w, hid_ref, for_gate_ref, act_ref, xn_ref):
    @pl.when(pl.program_id(0) == 0)
    def _():
        tok = xn_own.shape[0]
        xn_ref[rows_at(place[0] * tok, tok), :] = xn_own[...]
        xn_ref[rows_at((1 - place[0]) * tok, tok), :] = xn_got[...]

    gate = mm(xn_ref[...], gate_w[0])
    up = mm(xn_ref[...], up_w[0])
    sig = 1.0 / (1.0 + jnp.exp(-gate))
    act = gate * sig
    hid_ref[...] = (act * up).astype(jnp.bfloat16)
    for_gate_ref[...] = (up * (sig + act * (1.0 - sig))).astype(jnp.bfloat16)
    act_ref[...] = act.astype(jnp.bfloat16)


def hidden_step(place, xn_own, xn_got, pair):
    seq, width = 2 * xn_own.shape[0], xn_own.shape[1]
    ff = pair.shape[2]
    block = pl.BlockSpec((seq, TILE), lambda n: (0, n))
    return pl.pallas_call(
        hidden_kernel,
        grid=(ff // TILE,),
        in_specs=[
            SMEM,
            VM,
            VM,
            pl.BlockSpec((1, width, TILE), lambda n: (0, 0, n)),
            pl.BlockSpec((1, width, TILE), lambda n: (1, 0, n)),
        ],
        out_specs=[block] * 3 + [VM],
        out_shape=[bf16_like(seq, ff)] * 3 + [bf16_like(seq, width)],
        compiler_params=PARAMS,
        cost_estimate=cost(4 * seq * width * ff, 30e6),
        name="hidden",
    )(place, xn_own, xn_got, pair, pair)


def hidden_back_kernel(dy_ref, down_w, for_gate_ref, act_ref, dgate_ref, dup_ref):
    d_hidden = mm(dy_ref[...], down_w[...], ((1,), (1,)))
    dgate_ref[...] = (d_hidden * fp32(for_gate_ref[...])).astype(jnp.bfloat16)
    dup_ref[...] = (d_hidden * fp32(act_ref[...])).astype(jnp.bfloat16)


def hidden_back(dy, down, for_gate, act):
    seq, width = dy.shape
    ff = down.shape[0]
    block = pl.BlockSpec((seq, TILE), lambda n: (0, n))
    return pl.pallas_call(
        hidden_back_kernel,
        grid=(ff // TILE,),
        in_specs=[VM, pl.BlockSpec((TILE, width), lambda n: (n, 0)), block, block],
        out_specs=[block] * 2,
        out_shape=[bf16_like(seq, ff)] * 2,
        compiler_params=PARAMS,
        cost_estimate=cost(2 * seq * width * ff, 26e6),
        name="hidden_back",
    )(dy, down, for_gate, act)


def back_kernel(place, dgate_ref, dup_ref, gate_w, up_w, own_ref, send_ref):
    field = mm(dgate_ref[...], gate_w[0], ((1,), (1,)))
    field = field + mm(dup_ref[...], up_w[0], ((1,), (1,)))
    tok = own_ref.shape[0]

    @pl.when(place[0] == 0)
    def _():
        own_ref[...] = field[:tok]
        send_ref[...] = field[tok:].astype(jnp.bfloat16)

    @pl.when(place[0] == 1)
    def _():
        own_ref[...] = field[tok:]
        send_ref[...] = field[:tok].astype(jnp.bfloat16)


def back_step(place, d_gate, d_up, pair):
    seq, ff = d_gate.shape
    width = pair.shape[1]
    out = pl.BlockSpec((seq // 2, TILE), lambda n: (0, n))
    return pl.pallas_call(
        back_kernel,
        grid=(width // TILE,),
        in_specs=[
            SMEM,
            VM,
            VM,
            pl.BlockSpec((1, TILE, ff), lambda n: (0, n, 0)),
            pl.BlockSpec((1, TILE, ff), lambda n: (1, n, 0)),
        ],
        out_specs=[out, out],
        out_shape=[f32_like(seq // 2, width), bf16_like(seq // 2, width)],
        compiler_params=PARAMS,
        cost_estimate=cost(4 * seq * width * ff, 26e6),
        name="back",
    )(place, d_gate, d_up, pair, pair)


def result_kernel(place, hid_ref, h_ref, down_w, own_ref, send_ref):
    field = mm(hid_ref[...], down_w[...])
    tok = own_ref.shape[0]

    @pl.when(place[0] == 0)
    def _():
        own_ref[...] = field[:tok] + h_ref[...]
        send_ref[...] = field[tok:].astype(jnp.bfloat16)

    @pl.when(place[0] == 1)
    def _():
        own_ref[...] = field[tok:] + h_ref[...]
        send_ref[...] = field[:tok].astype(jnp.bfloat16)


def result_step(place, hidden, h_own, down):
    tok, width = h_own.shape
    ff = hidden.shape[1]
    out = pl.BlockSpec((tok, TILE), lambda n: (0, n))
    return pl.pallas_call(
        result_kernel,
        grid=(width // TILE,),
        in_specs=[SMEM, VM, out, pl.BlockSpec((ff, TILE), lambda n: (0, n))],
        out_specs=[out, out],
        out_shape=[f32_like(tok, width), bf16_like(tok, width)],
        compiler_params=PARAMS,
        cost_estimate=cost(4 * tok * width * ff, 20e6),
        name="result",
    )(place, hidden, h_own, down)


def entry_kernel(place, dn_own, dn_got, h_ref, dy_ref, gain, w_ref, dh_ref, da_ref, keep_ref, send_ref, part_ref):
    core = place[0]

    @pl.when(pl.program_id(0) == 0)
    def _():
        part_ref[...] = jnp.zeros_like(part_ref)

    field = h_ref[...]
    scale = norm_scale(field)
    hat = field * scale
    grad = dn_own[...] + fp32(dn_got[...])
    part_ref[...] += jnp.sum(grad * hat, axis=0, keepdims=True)
    total = fp32(dy_ref[...]) + rms_back(grad * gain_row(gain, 1), hat, scale)
    dh_ref[...] = total
    da_ref[...] = total.astype(jnp.bfloat16)
    heads = keep_ref.shape[0]
    for ref, at in ((send_ref, 1 - core), (keep_ref, core)):
        ref[...] = mm(w_ref[rows_at(at * heads, heads), :], da_ref[...], ((1,), (1,))).astype(jnp.bfloat16)


def entry_step(place, dn_own, dn_got, h_own, dy_all, gains, weight):
    tok, width = h_own.shape
    heads = weight.shape[0] // 2
    steps = tok // TILE
    rows = pl.BlockSpec((TILE, width), lambda i, place: (i, 0))
    cols = pl.BlockSpec((heads, TILE), lambda i, place: (0, i))
    return pl.pallas_call(
        entry_kernel,
        grid_spec=pltpu.PrefetchScalarGridSpec(
            num_scalar_prefetch=1,
            grid=(steps,),
            in_specs=[
                rows,
                rows,
                rows,
                pl.BlockSpec((TILE, width), lambda i, place: (steps * place[0] + i, 0)),
                VM,
                VM,
            ],
            out_specs=[rows, rows, cols, cols, VM],
        ),
        out_shape=[
            f32_like(tok, width),
            bf16_like(tok, width),
            bf16_like(heads, tok),
            bf16_like(heads, tok),
            f32_like(1, width),
        ],
        compiler_params=PARAMS,
        cost_estimate=cost(2 * tok * width * weight.shape[0], 20e6),
        name="entry",
    )(place, dn_own, dn_got, h_own, dy_all, gains, weight)


def inputs_kernel(place, dq_ref, dk_ref, dv_ref, w_ref, own_ref, send_ref, d_ref):
    @pl.when(pl.program_id(0) == 0)
    def _():
        nq, nk = dq_ref.shape[0], dk_ref.shape[0]
        d_ref[:, :nq] = dq_ref[...].T
        d_ref[:, nq : nq + nk] = dk_ref[...].T
        d_ref[:, nq + nk :] = dv_ref[...].T

    field = mm(d_ref[...], w_ref[...], ((1,), (1,)))
    tok = own_ref.shape[0]

    @pl.when(place[0] == 0)
    def _():
        own_ref[...] = field[:tok]
        send_ref[...] = field[tok:].astype(jnp.bfloat16)

    @pl.when(place[0] == 1)
    def _():
        own_ref[...] = field[tok:]
        send_ref[...] = field[:tok].astype(jnp.bfloat16)


def inputs_step(place, dq_t, dk_t, dv_t, weight):
    width, cols = weight.shape
    tok = dq_t.shape[1] // 2
    out = pl.BlockSpec((tok, TILE), lambda n: (0, n))
    return pl.pallas_call(
        inputs_kernel,
        grid=(width // TILE,),
        in_specs=[SMEM] + [VM] * 3 + [pl.BlockSpec((TILE, cols), lambda n: (n, 0))],
        out_specs=[out, out, VM],
        out_shape=[f32_like(tok, width), bf16_like(tok, width), bf16_like(2 * tok, cols)],
        compiler_params=PARAMS,
        cost_estimate=cost(4 * tok * width * cols, 14e6),
        name="inputs",
    )(place, dq_t, dk_t, dv_t, weight)


def last_kernel(place, d1_own, d1_got, x_ref, dh_ref, gain, dx_ref, part_ref):
    @pl.when(pl.program_id(0) == 0)
    def _():
        part_ref[...] = jnp.zeros_like(part_ref)

    field = fp32(x_ref[...])
    scale = norm_scale(field)
    hat = field * scale
    grad = d1_own[...] + fp32(d1_got[...])
    part_ref[...] += jnp.sum(grad * hat, axis=0, keepdims=True)
    dx_ref[...] = (dh_ref[...] + rms_back(grad * gain_row(gain, 0), hat, scale)).astype(jnp.bfloat16)


def last_step(place, d1_own, d1_got, x_seq, dh_own, gains):
    tok, width = dh_own.shape
    tile = TILE // 2
    steps = tok // tile
    rows = pl.BlockSpec((tile, width), lambda i, place: (i, 0))
    return pl.pallas_call(
        last_kernel,
        grid_spec=pltpu.PrefetchScalarGridSpec(
            num_scalar_prefetch=1,
            grid=(steps,),
            in_specs=[
                rows,
                rows,
                pl.BlockSpec((tile, width), lambda i, place: (steps * place[0] + i, 0)),
                rows,
                VM,
            ],
            out_specs=[rows, VM],
        ),
        out_shape=[bf16_like(tok, width), f32_like(1, width)],
        compiler_params=PARAMS,
        cost_estimate=cost(0, 14e6),
        name="last",
    )(place, d1_own, d1_got, x_seq, dh_own, gains)


class Group:
    def __init__(self, source, rows, put):
        self.source, self.rows, self.put = source, rows, put
        mid = rows // 2
        self.top, self.low = pl.ds(0, mid), pl.ds(mid, mid)


def add_rows(dst, left, right):
    rows = dst.shape[0]

    @pl.loop(0, rows // 64)
    def _(i):
        at = rows_at(i * 64, 64)
        dst[at] = (fp32(left[at]) + fp32(right[at])).astype(dst.dtype)


ORDER = (
    "end", "b1u", "jod", "gie", "s1", "gq", "b0u", "gwe", "sed", "h1u", "zad", "go", "ene",
    "b1q", "wad", "fid", "zbd", "kee", "joe", "b0q", "h0u", "s2", "plu", "see", "zae", "giu",
    "enu", "gwu", "wae", "fie", "zbe", "keu", "h1q", "ao", "b1o", "h0q", "b0o", "s3", "jou",
    "seu", "zau", "plq", "giq", "h1o", "kwe", "h0o", "enq", "gwq", "fiu", "wau", "keq", "kwu",
    "zbu", "plo", "ded", "joq", "gio", "s4", "gwo", "eno", "keo", "kwo", "kwq", "seq", "zaq",
    "joo", "seo", "zao", "waq", "fiq", "s5", "zbq", "fio", "wao", "dee", "deu", "zbo", "deq",
    "deo",
)


def collect_kernel(
    down, down_in, gate, up, xn, d_qkv, attn, da, sums, lse,
    down_o, gate_o, up_o, query_o, key_o, value_o, out_o, sums_o, lse_o,
    send, recv, near, lse_send, lse_recv, lse_near, out_mine, out_got, sums_got,
    out_away, qkv, xn_v, d_qkv_v, attn_v, da_v, *buffers,
):
    at = Spots()
    z, f, g, parity = at.z, at.f, at.g, at.parity
    is_inner = (z == 1) | (z == 2)
    is_outer = (z == 0) | (z == 3)
    toward = (1 + z // 2, f, g)
    outward = (3 * (z // 2), f, g)
    other = (3 - z, f, g)
    chips = 4
    barrier = pltpu.get_barrier_semaphore()
    for partner in (at.x, at.y):
        pl.semaphore_signal(barrier, inc=1, device_id=partner, device_id_type=MESH)
    for level in range(chips):
        for core in range(2):

            @pl.when((z != level) | (g != core))
            def _():
                pl.semaphore_signal(barrier, inc=1, device_id=(level, f, core), device_id_type=MESH)

    pl.semaphore_wait(barrier, 2 * chips + 1)

    taken = [0, 0]

    def between(index, src, dst, device):
        return pltpu.make_async_remote_copy(
            src_ref=src, dst_ref=dst, send_sem=send.at[index], recv_sem=recv.at[index],
            device_id=device, device_id_type=MESH,
        )

    def remote(src, dst, device):
        taken[0] += 1
        return between(taken[0] - 1, src, dst, device)

    def local(src, dst):
        i = taken[1]
        taken[1] += 1
        return pltpu.make_async_copy(src, dst, near.at[i])

    nf = down.shape[0]
    feat = gate.shape[0]
    nq, nk = query_o.shape[1] // 2, key_o.shape[1] // 2
    wide = out_o.shape[1] // 2

    def put_down(done):
        return [(done, down_o.at[rows_at(g * nf, nf)])]

    def put_pair(into):
        def put(done):
            return [
                (done.at[:, rows_at(k * nf, nf)], into.at[:, rows_at((2 * k + g) * nf, nf)])
                for k in range(4)
            ]

        return put

    def put_qkv(done):
        return [
            (done.at[:, 0:nq], query_o.at[:, rows_at(g * nq, nq)]),
            (done.at[:, nq : nq + nk], key_o.at[:, rows_at(g * nk, nk)]),
            (done.at[:, nq + nk : nq + 2 * nk], value_o.at[:, rows_at(g * nk, nk)]),
        ]

    def put_out(done):
        return [(done, out_o.at[:, rows_at(g * wide, wide)])]

    lse_place = lse_o.at[2 * (z // 2) + g]
    for level in range(chips):
        copy = pltpu.make_async_remote_copy(
            src_ref=lse, dst_ref=lse_place, send_sem=lse_send.at[level],
            recv_sem=lse_recv.at[2 * (z // 2) + g],
            device_id=(level, f, parity), device_id_type=MESH,
        )

        @pl.when((z != level) | (g != parity))
        def _():
            copy.start()

    lse_keep = pltpu.make_async_copy(lse, lse_place, lse_near)

    @pl.when(g == parity)
    def _():
        lse_keep.start()

    out_send = remote(out_away, out_got, at.core)
    operands = [local(xn, xn_v), local(d_qkv, d_qkv_v), local(attn, attn_v), local(da, da_v)]
    sums_send = remote(sums, sums_got.at[0], at.core)

    groups = []
    used = 0
    for source, rows, put, ready in (
        (down, nf, put_down, True),
        (gate, feat, put_pair(gate_o), True),
        (up, feat, put_pair(up_o), False),
        (qkv, feat, put_qkv, False),
        (out_mine, feat, put_out, False),
    ):
        group = Group(source, rows, put)
        groups.append(group)
        mid = rows // 2
        group.acc, group.outer, group.inner, group.done = buffers[used : used + 4]
        used += 4
        if ready:
            group.load = local(source, group.acc)
            if source is down:
                group.load_in = local(down_in, group.outer)
        else:
            group.mid, group.got, group.late = buffers[used : used + 3]
            used += 3
            group.sends = [
                remote(source.at[rows_at(at.fd * rows, mid)], group.got.at[1], at.x),
                remote(source.at[rows_at(at.fd * rows + mid, mid)], group.got.at[3], at.y),
                remote(source.at[rows_at(at.fx * rows, mid)], group.got.at[0], at.x),
                remote(source.at[rows_at(at.fy * rows + mid, mid)], group.got.at[2], at.y),
            ]
            group.loads = [
                local(source.at[rows_at(at.fy * rows, mid)], group.mid.at[0]),
                local(source.at[rows_at(at.fx * rows + mid, mid)], group.mid.at[1]),
                local(source.at[rows_at(f * rows, rows)], group.acc),
            ]
            group.second = [
                remote(group.mid.at[0], group.late.at[0], at.y),
                remote(group.mid.at[1], group.late.at[1], at.x),
            ]
        i = taken[0]
        taken[0] += 6
        group.first = i

        def inward(part, slot, group=group, i=i):
            return between(i + slot, group.acc.at[part], group.outer.at[part], toward)

        group.inward = inward

        def crossing(keep, give, i=i, group=group):
            return (
                between(i + 2, group.acc.at[give], group.inner, other),
                between(i + 3, group.done.at[keep], group.done.at[keep], other),
                between(i + 4, group.done.at[keep], group.done.at[keep], outward),
                between(i + 5, group.done.at[give], group.done.at[give], outward),
            )

        group.crossing = crossing
        pairs = group.put(group.done)
        group.shares = [remote(src_ref, dst_ref, at.core) for src_ref, dst_ref in pairs]
        group.stores = [local(src_ref, dst_ref) for src_ref, dst_ref in pairs]

    def by_end(group, step):
        @pl.when(z == 0)
        def _():
            step(group.low, group.top)

        @pl.when(z == 3)
        def _():
            step(group.top, group.low)

    def by_side(group, step):
        @pl.when(z == 1)
        def _():
            step(group.top, group.low, group.crossing(group.top, group.low))

        @pl.when(z == 2)
        def _():
            step(group.low, group.top, group.crossing(group.low, group.top))

    def b1(group):
        for copy in group.sends[:2] + group.loads:
            copy.start()

    def b0(group):
        for copy in group.sends[2:]:
            copy.start()

    def h1(group):
        for i, which in ((0, 1), (1, 3)):
            group.sends[i].wait_recv()
            group.loads[i].wait()
            add_rows(group.mid.at[i], group.mid.at[i], group.got.at[which])
            group.second[i].start()

    def h0(group):
        group.loads[2].wait()
        for i, part, which in ((2, group.top, 0), (3, group.low, 2)):
            group.sends[i].wait_recv()
            add_rows(group.acc.at[part], group.acc.at[part], group.got.at[which])

    def pl_(group):
        for i, part in ((0, group.top), (1, group.low)):
            group.second[i].wait_recv()
            add_rows(group.acc.at[part], group.acc.at[part], group.late.at[i])

    def gi(group):
        if group is e:
            e.load.wait()
        by_end(group, lambda give, keep: group.inward(give, 0).start())

    def gw(group):
        by_end(group, lambda give, keep: group.inward(give, 0).wait_send())

    def ke(group):
        by_end(group, lambda give, keep: group.inward(keep, 1).start())

    def kw(group):
        by_end(group, lambda give, keep: group.inward(keep, 1).wait_send())

    def en(group):
        if group is d:
            d.load.wait()
            d.load_in.wait()

        def step(keep, give, copies):
            if group is not d:
                group.inward(give, 0).wait_recv()
            add_rows(group.acc.at[give], group.acc.at[give], group.outer.at[give])
            copies[0].start()

        by_side(group, step)

    def jo(group):
        def step(keep, give, copies):
            if group is not d:
                group.inward(keep, 1).wait_recv()
            add_rows(group.acc.at[keep], group.acc.at[keep], group.outer.at[keep])

        by_side(group, step)

    def se(group):
        def step(keep, give, copies):
            copies[0].wait_recv()
            add_rows(group.done.at[keep], group.acc.at[keep], group.inner)
            copies[1].start()

        by_side(group, step)

    def za(group):
        by_side(group, lambda keep, give, copies: copies[2].start())

    def fi(group):
        by_side(group, lambda keep, give, copies: copies[1].wait_recv())

    def wa(group):
        by_side(group, lambda keep, give, copies: copies[2].wait_send())

    def zb(group):
        by_side(group, lambda keep, give, copies: copies[3].start())

    def de(group):
        def end(give, keep):
            copies = group.crossing(keep, give)
            copies[2].wait_recv()
            copies[3].wait_recv()

        by_end(group, end)

        def step(keep, give, copies):
            for i in (0, 1, 3):
                copies[i].wait_send()

        by_side(group, step)
        for copy in group.shares + group.stores:
            copy.start()

    d, e, u, q, o = groups
    for copy in [e.load, d.load, d.load_in, sums_send] + operands:
        copy.start()
    steps = {
        "b1": b1, "b0": b0, "h1": h1, "h0": h0, "pl": pl_, "gi": gi, "gw": gw, "ke": ke, "kw": kw,
        "en": en, "jo": jo, "se": se, "za": za, "fi": fi, "wa": wa, "zb": zb, "de": de,
    }
    named = {"d": d, "e": e, "u": u, "q": q, "o": o}

    over_x = remote(sums_o, sums_got.at[1], at.x)
    over_y = remote(sums_o, sums_got.at[2], at.y)
    sums_in = remote(sums_o, sums_got.at[3], toward)
    sums_mid = remote(sums_o, sums_got.at[4], other)
    sums_out = remote(sums_o, sums_got.at[5], outward)

    def sums_1():
        sums_send.wait_recv()
        sums_o[...] = sums[...] + sums_got[0]
        over_x.start()

    def sums_2():
        over_x.wait()
        sums_o[...] += sums_got[1]
        over_y.start()

    def sums_3():
        over_y.wait()
        sums_o[...] += sums_got[2]

        @pl.when(is_outer)
        def _():
            sums_in.start()

    def sums_4():
        @pl.when(is_inner)
        def _():
            sums_in.wait_recv()
            sums_o[...] += sums_got[3]
            sums_mid.start()

    def sums_5():
        @pl.when(is_inner)
        def _():
            sums_mid.wait()
            sums_o[...] += sums_got[4]
            sums_out.start()

    def out_gradient():
        for copy in operands[2:]:
            copy.wait()
        tile = wide // 2
        for ref, core in ((out_away, 1 - g), (out_mine, g)):


            @pl.loop(0, 2)
            def _(n):
                cols = rows_at(core * wide + n * tile, tile)
                ref[:, rows_at(n * tile, tile)] = mm(attn_v[...], da_v[:, cols]).astype(ref.dtype)

            if ref is out_away:
                out_send.start()

    def qkv_gradient():
        for copy in operands[:2]:
            copy.wait()
        tile = 2 * TILE

        @pl.loop(0, qkv.shape[1] // tile)
        def _(n):
            cols = rows_at(n * tile, tile)
            qkv[:, cols] = mm(xn_v[...], d_qkv_v[:, cols], ((0,), (0,))).astype(qkv.dtype)

    def out_sum():
        out_send.wait_recv()
        add_rows(out_mine, out_mine, out_got)

    single = {
        "s1": sums_1, "s2": sums_2, "s3": sums_3, "s4": sums_4, "s5": sums_5,
        "go": out_gradient, "gq": qkv_gradient, "ao": out_sum,
    }
    for name in ORDER:
        if len(name) == 2:
            single[name]()
        else:
            steps[name[:2]](named[name[2]])

    @pl.when(is_outer)
    def _():
        sums_in.wait_send()
        sums_out.wait_recv()
        sums_o[...] = sums_got[5]

    @pl.when(is_inner)
    def _():
        sums_out.wait_send()

    sums_send.wait_send()
    out_send.wait_send()
    for group in (u, q, o):
        for copy in group.sends + group.second:
            copy.wait_send()
    for group in groups:
        for copy in group.stores:
            copy.wait()
        for copy in group.shares:
            copy.wait_send()
            copy.wait_recv()
    for level in range(chips):
        copy = pltpu.make_async_remote_copy(
            src_ref=lse, dst_ref=lse_place, send_sem=lse_send.at[level], recv_sem=lse_recv.at[level],
            device_id=(level, f, parity), device_id_type=MESH,
        )

        @pl.when((z != level) | (g != parity))
        def _():
            copy.wait_send()

        @pl.when((z != 2 * (level // 2) + g) | (g != level % 2))
        def _():
            copy.wait_recv()

    @pl.when(g == parity)
    def _():
        lse_keep.wait()


def collect(down, down_in, gate, up, xn, d_qkv, attn, da, sums, lse, nq, nk):
    bf = jnp.bfloat16
    buffers = []
    wide = da.shape[1] // 2
    feat = gate.shape[0]
    for rows, cols, ready in (
        (down.shape[0], down.shape[1], True),
        (gate.shape[0], gate.shape[1], True),
        (up.shape[0] // 4, up.shape[1], False),
        (feat, d_qkv.shape[1], False),
        (attn.shape[0] // 4, wide, False),
    ):
        mid = rows // 2
        buffers += [
            pltpu.VMEM((rows, cols), bf),
            pltpu.VMEM((rows, cols), bf),
            pltpu.VMEM((mid, cols), bf),
            pltpu.VMEM((rows, cols), bf),
        ]
        if not ready:
            buffers += [
                pltpu.VMEM((2, mid, cols), bf),
                pltpu.VMEM((4, mid, cols), bf),
                pltpu.VMEM((2, mid, cols), bf),
            ]
    return pl.pallas_call(
        collect_kernel,
        in_specs=[ANY] * 8 + [VM, VM],
        out_specs=[ANY] * 7 + [VM, VM],
        out_shape=[
            bf16_like(2 * down.shape[0], down.shape[1]),
            bf16_like(feat, 2 * gate.shape[1]),
            bf16_like(feat, 2 * up.shape[1]),
            bf16_like(feat, 2 * nq),
            bf16_like(feat, 2 * nk),
            bf16_like(feat, 2 * nk),
            bf16_like(feat, da.shape[1]),
            f32_like(*sums.shape),
            f32_like(4, *lse.shape),
        ],
        scratch_shapes=[
            pltpu.SemaphoreType.DMA((96,)),
            pltpu.SemaphoreType.DMA((96,)),
            pltpu.SemaphoreType.DMA((32,)),
            pltpu.SemaphoreType.DMA((4,)),
            pltpu.SemaphoreType.DMA((4,)),
            pltpu.SemaphoreType.DMA,
            pltpu.VMEM((attn.shape[0], wide), bf),
            pltpu.VMEM((attn.shape[0], wide), bf),
            pltpu.VMEM((6,) + sums.shape, jnp.float32),
            pltpu.VMEM((attn.shape[0], wide), bf),
            pltpu.VMEM((xn.shape[1], d_qkv.shape[1]), bf),
            pltpu.VMEM(xn.shape, bf),
            pltpu.VMEM(d_qkv.shape, bf),
            pltpu.VMEM(attn.shape, bf),
            pltpu.VMEM(da.shape, bf),
        ]
        + buffers,
        compiler_params=pltpu.CompilerParams(
            collective_id=1, has_side_effects=True, vmem_limit_bytes=62 * 1024 * 1024
        ),
        cost_estimate=cost(0, 500e6),
        name="collect",
    )(down, down_in, gate, up, xn, d_qkv, attn, da, sums, lse)


def widen_kernel(spot, dealing, lse, sums, *refs):
    totals, first, second = refs[-3:]
    half = (len(refs) - 3) // 2
    for narrow, wide in zip(refs[:half], refs[half:-3]):
        wide[...] = fp32(narrow[...])

    @pl.when(pl.program_id(0) == 0)
    def _():
        shard = rows_at(spot[1] * first.shape[0], first.shape[0])
        first[...] = sums[0, shard]
        second[...] = sums[1, shard]
        heads = lse.shape[1]
        for r in range(4):
            for i in range(4):

                @pl.when(dealing[r, i] == spot[0])
                def _():
                    col = (4 * r + i) % 8 * BLK
                    for core in range(2):
                        totals[core * heads : (core + 1) * heads, r * BLK : (r + 1) * BLK] = lse[
                            2 * (r // 2) + core, :, col : col + BLK
                        ]


def widen(spot, dealing, lse, sums, arrays, steps=8):
    specs = [pl.BlockSpec((a.shape[0] // steps, a.shape[1]), lambda n: (n, 0)) for a in arrays]
    shard = sums.shape[1] // 4
    return pl.pallas_call(
        widen_kernel,
        grid=(steps,),
        in_specs=[SMEM, SMEM, VM, VM] + specs,
        out_specs=specs + [VM] * 3,
        out_shape=[f32_like(*a.shape) for a in arrays]
        + [f32_like(2 * lse.shape[1], 4 * BLK), f32_like(shard), f32_like(shard)],
        compiler_params=PARAMS,
        cost_estimate=cost(0, 40e6),
        name="widen",
    )(spot, dealing, lse, sums, *arrays)


def turning_tables(seq):
    half = HEAD_SIZE // 2
    frequency = ROPE_BASE ** (-2.0 * np.arange(half) / (2 * half))
    low = frequency[:, None] * np.arange(BLK)[None, :]
    high = frequency[:, None] * (BLK * np.arange(seq // BLK))[None, :]
    return tuple(part.astype(np.float32) for part in (np.cos(low), np.sin(low), np.cos(high), np.sin(high)))


def chip_local(
    tokens,
    seq_lengths,
    dealing,
    first_gain,
    query_weight,
    key_matrix,
    value_matrix,
    out_weight,
    second_gain,
    gate_weight,
    up_weight,
    down_weight,
    cotangent,
):
    ctx = lax.axis_size("ctx")
    z = lax.axis_index("ctx")
    f = lax.axis_index("fsdp")
    g = lax.axis_index("grp")
    parity = z % 2
    parity_core = g == parity
    width = tokens.shape[2]
    tok = tokens.shape[1]
    seq = 2 * tok
    place = jnp.stack([g, parity]).astype(jnp.int32)

    def over_x(field):
        return lax.ppermute(field, "fsdp", [(i, i ^ 1) for i in range(4)])

    def over_y(field):
        return lax.ppermute(field, "fsdp", [(i, i ^ 2) for i in range(4)])

    def over_core(field):
        return lax.ppermute(field, "grp", [(0, 1), (1, 0)])

    swap_pairs = [(2 * i + (1 - i % 2), 2 * (i ^ 1) + i % 2) for i in range(ctx)]

    def swap(field):
        got = lax.ppermute(field, ("ctx", "grp"), swap_pairs)
        return jnp.where(parity_core, field, got)

    def along(field, pairs):
        return lax.ppermute(field, "ctx", pairs)

    def cut(field, start, size, axis):
        return lax.dynamic_slice_in_dim(field, start, size, axis)

    def in_order(mine, other, axis=0):
        first = jnp.where(g == 0, mine, other)
        second = jnp.where(g == 0, other, mine)
        return jnp.concatenate([first, second], axis=axis)

    heads_q = query_weight.shape[1] // 2
    heads_k = key_matrix.shape[1] // 2
    part_ff = down_weight.shape[0] // 2
    rows_in = gate_weight.shape[0]

    row = lax.broadcasted_iota(jnp.int32, (1, 8, first_gain.shape[0]), 1)
    gain_own = jnp.where(row == 0, fp32(first_gain), jnp.where(row == 1, fp32(second_gain), 0.0))
    qkv_w, out_w, pair_w, down_own, x_seq, dy_all, gain_all, xn_one, qkv_t = gather_all(
        tokens, cotangent, query_weight, key_matrix, value_matrix, out_weight,
        gate_weight, up_weight, down_weight, gain_own,
    )
    down_w = lax.all_gather(down_own, "fsdp", axis=0, tiled=True)

    tables = turning_tables(seq)

    attn_keep, attn_send, lse, q_t, k_t, v_t = attend_seq(place, qkv_t, tables)
    attn_got = over_core(attn_send)
    h_own, xn_own, attn_mine = residual(place, x_seq, attn_keep, attn_got, gain_all, out_w)
    hidden, for_gate, act, xn_two = hidden_step(place, xn_own, over_core(xn_own), pair_w)
    d_gate, d_up = hidden_back(dy_all, down_w, for_gate, act)
    bf = jnp.bfloat16
    tokens_in = ((0,), (0,))
    down_grad = mm(hidden, dy_all, tokens_in, bf)
    gate_grad = mm(xn_two, d_gate, tokens_in, bf)
    down_plane = lax.psum_scatter(down_grad, "fsdp", scatter_dimension=0, tiled=True)
    down_in = along(down_plane, [(0, 1), (3, 2)])
    gate_plane = lax.psum_scatter(gate_grad, "fsdp", scatter_dimension=0, tiled=True)
    d_gate, d_up, hidden, _, _ = lax.optimization_barrier((d_gate, d_up, hidden, down_grad, gate_grad))
    dn_own, dn_send = back_step(place, d_gate, d_up, pair_w)
    dn_got = over_core(dn_send)
    res_own, res_send = result_step(place, hidden, h_own, down_w)
    up_grad = mm(xn_two, d_up, tokens_in, bf)
    layer_out = swap((res_own + fp32(over_core(res_send))).astype(bf))

    dh_own, da, dattn_keep, dattn_send, gain_two_part = entry_step(
        place, dn_own, dn_got, h_own, dy_all, gain_all, out_w
    )
    dattn_got = over_core(dattn_send)
    q_t, _ = lax.optimization_barrier((q_t, down_plane))
    dq_t, dk_t, dv_t = attend_seq_back(
        place, q_t, k_t, v_t, dattn_keep, dattn_got, lse, tables
    )
    half_width = width // 2
    d1_own, d1_send, d_qkv = inputs_step(place, dq_t, dk_t, dv_t, qkv_w)
    dh_own, down_in = lax.optimization_barrier((dh_own, down_in))
    dx, gain_one_part = last_step(place, d1_own, over_core(d1_send), x_seq, dh_own, gain_all)
    tokens_grad = swap(dx)

    parts = jnp.concatenate([gain_one_part, gain_two_part])
    down_sum, gate_sum, up_sum, query_sum, key_sum, value_sum, out_sum, sums, all_lse = collect(
        down_plane, down_in, gate_plane, up_grad, xn_one, d_qkv, attn_mine, da,
        jnp.pad(parts, ((0, 6), (0, 0))), lse.reshape(-1, seq), heads_q, heads_k,
    )
    query_out, key_out, value_out, out_out, gate_out, up_out, down_out, totals, gain_one, gain_two = widen(
        jnp.stack([z, f]).astype(jnp.int32), dealing[0], all_lse, sums,
        (query_sum, key_sum, value_sum, out_sum, gate_sum, up_sum, down_sum),
    )

    return (
        layer_out[None],
        tokens_grad[None],
        totals[None],
        gain_one,
        query_out,
        key_out,
        value_out,
        out_out,
        gain_two,
        gate_out,
        up_out,
        down_out,
    )


def chip_holds_sequence(mesh, tokens, seq_lengths):
    sizes = dict(mesh.shape)
    packs, length, _ = tokens.shape
    count = seq_lengths.shape[1]
    return (
        sizes["fsdp"] == 4
        and sizes["grp"] == 2
        and sizes["ctx"] == 4
        and packs == sizes["fsdp"] * sizes["grp"]
        and length == count * MINLEN
        and 2 * length == sizes["ctx"] * MINLEN
    )


def solution(mesh):
    placed = (
        P(("fsdp", "grp"), "ctx", None),
        P(("fsdp", "grp"), None),
        P(("fsdp", "grp"), None, None),
        P("fsdp"),
        P("fsdp", None),
        P("fsdp", None),
        P("fsdp", None),
        P("fsdp", None),
        P("fsdp"),
        P("fsdp", None),
        P("fsdp", None),
        P("fsdp", None),
        P(("fsdp", "grp"), "ctx", None),
    )
    results = (
        P(("fsdp", "grp"), "ctx", None),
        P(("fsdp", "grp"), "ctx", None),
        P(("fsdp", "grp"), None, "ctx"),
        P("fsdp"),
        P("fsdp", None),
        P("fsdp", None),
        P("fsdp", None),
        P("fsdp", None),
        P("fsdp"),
        P("fsdp", None),
        P("fsdp", None),
        P("fsdp", None),
    )

    def program(*arrays):
        body = chip_local if chip_holds_sequence(mesh, arrays[0], arrays[1]) else local
        return jax.shard_map(
            body, mesh=mesh, in_specs=placed, out_specs=results, check_vma=False
        )(*arrays)

    return program
```

```python
import jax
import jax.numpy as jnp
import numpy as np
from jax import lax
from jax.experimental import pallas as pl
from jax.experimental.pallas import tpu as pltpu
from jax.sharding import PartitionSpec as P

QUERY_HEADS = 16
KEY_VALUE_HEADS = 8
HEAD_SIZE = 96
BLK = 128


EPS = 1e-05
ROPE_BASE = 100000.0
MASKED = -1e30


def place_rows(positions, lengths):
    ends = jnp.cumsum(lengths, axis=-1)
    before = positions[..., :, None] >= ends[..., None, :]
    segment = jnp.sum(before.astype(jnp.int32), axis=-1)
    offset = jnp.sum(jnp.where(before, lengths[..., None, :], 0), axis=-1)
    return (segment, positions - offset)


def rotation(relative, half_size):
    frequency = ROPE_BASE ** (-(2.0 * jnp.arange(half_size, dtype=jnp.float32)) / (2 * half_size))
    angles = relative.astype(jnp.float32)[:, None] * frequency[None, :]
    return (jnp.cos(angles), jnp.sin(angles))


def rotate(field, cosine, sine_part):
    row_count = field.shape[0]
    half_size = cosine.shape[-1]
    split_heads = field.reshape(row_count, -1, 2 * half_size)
    front_half = split_heads[..., :half_size]
    back_half = split_heads[..., half_size:]
    cos_rows = cosine[:, None, :]
    sin_rows = sine_part[:, None, :]
    turned = jnp.concatenate(
        [
            front_half * cos_rows - back_half * sin_rows,
            back_half * cos_rows + front_half * sin_rows,
        ],
        axis=-1,
    )
    return turned.reshape(row_count, -1)


def rms_back(d_normed, normed, scale):
    return scale * (d_normed - normed * jnp.mean(d_normed * normed, axis=-1, keepdims=True))


def score_block(query_part, key_part, visible):
    scores = jnp.einsum(
        "rgd,kd->grk", query_part, key_part, preferred_element_type=jnp.float32
    ) * HEAD_SIZE ** (-0.5)
    return jnp.where(visible[None], scores, MASKED)


def attend_pack(query_pack, key_pack, value_pack, visible_list):
    token_count = query_pack.shape[0]
    rounds = len(visible_list)
    query_group_width = QUERY_HEADS // KEY_VALUE_HEADS
    context_count = key_pack.shape[0] // token_count

    def width_per_head(head_index, carry):
        out_buf, total_buf = carry
        query_head = lax.dynamic_slice_in_dim(
            query_pack, head_index * query_group_width * HEAD_SIZE, query_group_width * HEAD_SIZE, 1
        ).reshape(token_count, query_group_width, HEAD_SIZE)
        key_head = lax.dynamic_slice_in_dim(key_pack, head_index * HEAD_SIZE, HEAD_SIZE, 1).reshape(
            context_count, rounds, BLK, HEAD_SIZE
        )
        value_head = lax.dynamic_slice_in_dim(
            value_pack, head_index * HEAD_SIZE, HEAD_SIZE, 1
        ).reshape(context_count, rounds, BLK, HEAD_SIZE)
        running_top = jnp.full((query_group_width, token_count), MASKED, jnp.float32)
        running_sum = jnp.zeros((query_group_width, token_count), jnp.float32)
        for round_index in range(rounds):
            first_row = round_index * BLK
            scores = score_block(
                query_head[first_row:],
                key_head[:, round_index].reshape(-1, HEAD_SIZE),
                visible_list[round_index],
            )
            new_top = jnp.maximum(running_top[:, first_row:], jnp.max(scores, axis=-1))
            weights = jnp.where(
                visible_list[round_index][None], jnp.exp(scores - new_top[..., None]), 0.0
            )
            new_sum = running_sum[:, first_row:] * jnp.exp(
                running_top[:, first_row:] - new_top
            ) + jnp.sum(weights, axis=-1)
            running_top = running_top.at[:, first_row:].set(new_top)
            running_sum = running_sum.at[:, first_row:].set(new_sum)
        log_totals = running_top + jnp.log(running_sum)
        mixture = jnp.zeros((token_count, query_group_width, HEAD_SIZE), jnp.float32)
        for round_index in range(rounds):
            first_row = round_index * BLK
            scores = score_block(
                query_head[first_row:],
                key_head[:, round_index].reshape(-1, HEAD_SIZE),
                visible_list[round_index],
            )
            prob_bf = jnp.where(
                visible_list[round_index][None],
                jnp.exp(scores - log_totals[:, first_row:, None]),
                0.0,
            ).astype(jnp.bfloat16)
            mixture = mixture.at[first_row:].add(
                jnp.einsum(
                    "grk,kd->rgd",
                    prob_bf,
                    value_head[:, round_index].reshape(-1, HEAD_SIZE),
                    preferred_element_type=jnp.float32,
                )
            )
        out_buf = lax.dynamic_update_slice_in_dim(
            out_buf,
            mixture.astype(jnp.bfloat16).reshape(token_count, -1),
            head_index * query_group_width * HEAD_SIZE,
            1,
        )
        total_buf = lax.dynamic_update_slice_in_dim(
            total_buf, log_totals, head_index * query_group_width, 0
        )
        return (out_buf, total_buf)

    start_offsets = (
        jnp.zeros((token_count, QUERY_HEADS * HEAD_SIZE), jnp.bfloat16),
        jnp.zeros((QUERY_HEADS, token_count), jnp.float32),
    )
    return lax.fori_loop(0, KEY_VALUE_HEADS, width_per_head, start_offsets)


def attend_back(
    query_pack, key_pack, value_pack, grad_pack, attended_pack, total_pack, visible_list
):
    token_count = query_pack.shape[0]
    rounds = len(visible_list)
    query_group_width = QUERY_HEADS // KEY_VALUE_HEADS
    context_count = key_pack.shape[0] // token_count

    def width_per_head(head_index, carry):
        query_buf, key_buf, value_buf = carry
        query_head = lax.dynamic_slice_in_dim(
            query_pack, head_index * query_group_width * HEAD_SIZE, query_group_width * HEAD_SIZE, 1
        ).reshape(token_count, query_group_width, HEAD_SIZE)
        grad_head = lax.dynamic_slice_in_dim(
            grad_pack, head_index * query_group_width * HEAD_SIZE, query_group_width * HEAD_SIZE, 1
        ).reshape(token_count, query_group_width, HEAD_SIZE)
        output_head = lax.dynamic_slice_in_dim(
            attended_pack,
            head_index * query_group_width * HEAD_SIZE,
            query_group_width * HEAD_SIZE,
            1,
        ).reshape(token_count, query_group_width, HEAD_SIZE)
        key_head = lax.dynamic_slice_in_dim(key_pack, head_index * HEAD_SIZE, HEAD_SIZE, 1).reshape(
            context_count, rounds, BLK, HEAD_SIZE
        )
        value_head = lax.dynamic_slice_in_dim(
            value_pack, head_index * HEAD_SIZE, HEAD_SIZE, 1
        ).reshape(context_count, rounds, BLK, HEAD_SIZE)
        log_totals = lax.dynamic_slice_in_dim(
            total_pack, head_index * query_group_width, query_group_width, 0
        )
        delta = jnp.sum(grad_head.astype(jnp.float32) * output_head.astype(jnp.float32), axis=-1).T
        query_grad = jnp.zeros((token_count, query_group_width, HEAD_SIZE), jnp.float32)
        key_parts = []
        value_parts = []
        for round_index in range(rounds):
            first_row = round_index * BLK
            key_round = key_head[:, round_index].reshape(-1, HEAD_SIZE)
            value_round = value_head[:, round_index].reshape(-1, HEAD_SIZE)
            scores = score_block(query_head[first_row:], key_round, visible_list[round_index])
            probs_full = jnp.where(
                visible_list[round_index][None],
                jnp.exp(scores - log_totals[:, first_row:, None]),
                0.0,
            )
            d_probs = jnp.einsum(
                "rgd,kd->grk",
                grad_head[first_row:],
                value_round,
                preferred_element_type=jnp.float32,
            )
            d_scores = (
                HEAD_SIZE ** (-0.5) * probs_full * (d_probs - delta[:, first_row:, None])
            ).astype(jnp.bfloat16)
            value_parts.append(
                jnp.einsum(
                    "grk,rgd->kd",
                    probs_full.astype(jnp.bfloat16),
                    grad_head[first_row:],
                    preferred_element_type=jnp.float32,
                )
            )
            key_parts.append(
                jnp.einsum(
                    "grk,rgd->kd",
                    d_scores,
                    query_head[first_row:],
                    preferred_element_type=jnp.float32,
                )
            )
            query_grad = query_grad.at[first_row:].add(
                jnp.einsum("grk,kd->rgd", d_scores, key_round, preferred_element_type=jnp.float32)
            )
        key_block = jnp.stack(
            [part.reshape(context_count, BLK, HEAD_SIZE) for part in key_parts], axis=1
        ).reshape(-1, HEAD_SIZE)
        value_block = jnp.stack(
            [part.reshape(context_count, BLK, HEAD_SIZE) for part in value_parts], axis=1
        ).reshape(-1, HEAD_SIZE)
        query_buf = lax.dynamic_update_slice_in_dim(
            query_buf,
            query_grad.reshape(token_count, -1),
            head_index * query_group_width * HEAD_SIZE,
            1,
        )
        key_buf = lax.dynamic_update_slice_in_dim(key_buf, key_block, head_index * HEAD_SIZE, 1)
        value_buf = lax.dynamic_update_slice_in_dim(
            value_buf, value_block, head_index * HEAD_SIZE, 1
        )
        return (query_buf, key_buf, value_buf)

    start_offsets = (
        jnp.zeros((token_count, QUERY_HEADS * HEAD_SIZE), jnp.float32),
        jnp.zeros((context_count * token_count, KEY_VALUE_HEADS * HEAD_SIZE), jnp.float32),
        jnp.zeros((context_count * token_count, KEY_VALUE_HEADS * HEAD_SIZE), jnp.float32),
    )
    return lax.fori_loop(0, KEY_VALUE_HEADS, width_per_head, start_offsets)


def local(
    tokens,
    seq_lengths,
    dealing,
    first_gain,
    query_weight,
    key_matrix,
    value_matrix,
    out_weight,
    second_gain,
    gate_weight,
    up_weight,
    down_weight,
    cotangent,
):
    context_count = lax.axis_size("ctx")
    my_index = lax.axis_index("ctx")
    pack_count, token_count, model_dim = tokens.shape
    rounds = token_count // BLK
    spread = context_count // rounds
    ctx_range = jnp.arange(context_count, dtype=jnp.int32)
    matches = (dealing[..., None] == ctx_range).astype(jnp.int32)
    slot_of = jnp.sum(matches * ctx_range[:, None], axis=2)
    block_of = jnp.arange(rounds, dtype=jnp.int32)[None, :, None] * context_count + slot_of
    key_pos = (
        jnp.transpose(block_of, (0, 2, 1))[..., None] * BLK + jnp.arange(BLK, dtype=jnp.int32)
    ).reshape(pack_count, -1)
    key_seg = place_rows(key_pos, seq_lengths)[0]
    query_pos = lax.dynamic_slice_in_dim(key_pos, my_index * token_count, token_count, 1)
    query_seg, query_rel = place_rows(query_pos, seq_lengths)
    home_row = lax.dynamic_index_in_dim(dealing, my_index // spread, 1, False)
    targets = lax.dynamic_slice_in_dim(home_row, my_index % spread * rounds, rounds, 1)
    picker = (targets[:, None, :] == ctx_range[None, :, None]).astype(jnp.bfloat16)
    my_slots = lax.dynamic_index_in_dim(slot_of, my_index, 2, False)
    owner_index = (
        jnp.arange(rounds, dtype=jnp.int32)[None, :] * context_count + my_slots
    ) // rounds
    keep_slot = jnp.repeat(owner_index, spread, axis=1) == ctx_range[None, :]

    def spread_out(field):
        blocks = field.reshape(pack_count, rounds, BLK, model_dim)
        return jnp.einsum(
            "pkj,pjtd->pktd", picker, blocks, preferred_element_type=jnp.float32
        ).astype(jnp.bfloat16)

    def collect(received):
        grouped = received.reshape(pack_count, rounds, spread, BLK, model_dim)
        return (
            jnp.sum(grouped, axis=2, dtype=jnp.float32)
            .astype(jnp.bfloat16)
            .reshape(pack_count * token_count, model_dim)
        )

    def send_home(field):
        blocks = jnp.repeat(field.reshape(pack_count, rounds, BLK, model_dim), spread, axis=1)
        return jnp.where(keep_slot[:, :, None, None], blocks, jnp.zeros_like(blocks))

    def restore(returned):
        placed = jnp.einsum("pkj,pktd->pjtd", picker, returned, preferred_element_type=jnp.float32)
        return placed.astype(jnp.bfloat16).reshape(pack_count, token_count, model_dim)

    dealt_tokens, dealt_upstream = (
        lax.all_to_all(spread_out(tokens), "ctx", split_axis=1, concat_axis=1, tiled=True),
        lax.all_to_all(spread_out(cotangent), "ctx", split_axis=1, concat_axis=1, tiled=True),
    )
    inputs = collect(dealt_tokens)
    upstream = collect(dealt_upstream)
    gain_one, query_full, key_full, value_full, out_full = (
        lax.all_gather(first_gain, "fsdp", axis=0, tiled=True),
        lax.all_gather(query_weight, "fsdp", axis=0, tiled=True),
        lax.all_gather(key_matrix, "fsdp", axis=0, tiled=True),
        lax.all_gather(value_matrix, "fsdp", axis=0, tiled=True),
        lax.all_gather(out_weight, "fsdp", axis=0, tiled=True),
    )
    gain_two, gate_full, up_full, down_full = (
        lax.all_gather(second_gain, "fsdp", axis=0, tiled=True),
        lax.all_gather(gate_weight, "fsdp", axis=0, tiled=True),
        lax.all_gather(up_weight, "fsdp", axis=0, tiled=True),
        lax.all_gather(down_weight, "fsdp", axis=0, tiled=True),
    )
    gain_one32 = gain_one.astype(jnp.float32)
    gain_two32 = gain_two.astype(jnp.float32)
    cosine, sine_part = rotation(query_rel.reshape(-1), HEAD_SIZE // 2)
    inputs32 = inputs.astype(jnp.float32)
    scale_one = lax.rsqrt(jnp.mean(inputs32 * inputs32, axis=-1, keepdims=True) + EPS)
    normed_one = inputs32 * scale_one
    xn_one = (normed_one * gain_one32).astype(jnp.bfloat16)
    query_rot = rotate(
        jnp.dot(xn_one, query_full, preferred_element_type=jnp.float32), cosine, sine_part
    ).astype(jnp.bfloat16)
    key_rot = rotate(
        jnp.dot(xn_one, key_full, preferred_element_type=jnp.float32), cosine, sine_part
    ).astype(jnp.bfloat16)
    rows_of_values = jnp.dot(xn_one, value_full, preferred_element_type=jnp.float32).astype(
        jnp.bfloat16
    )
    key_local = key_rot.reshape(pack_count, token_count, -1)
    value_local = rows_of_values.reshape(pack_count, token_count, -1)
    gathered_keys, gathered_values = (
        lax.all_gather(key_local, "ctx", axis=1, tiled=True),
        lax.all_gather(value_local, "ctx", axis=1, tiled=True),
    )
    key_pos_rounds = key_pos.reshape(pack_count, context_count, rounds, BLK)
    key_seg_rounds = key_seg.reshape(pack_count, context_count, rounds, BLK)
    visible = []
    for round_index in range(rounds):
        first_row = round_index * BLK
        round_pos = key_pos_rounds[:, :, round_index].reshape(pack_count, -1)
        round_seg = key_seg_rounds[:, :, round_index].reshape(pack_count, -1)
        same_seq = query_seg[:, first_row:, None] == round_seg[:, None, :]
        earlier = round_pos[:, None, :] <= query_pos[:, first_row:, None]
        visible.append(same_seq & earlier)
    query_packs = query_rot.reshape(pack_count, token_count, -1)
    pack_index = 0
    pack_visible = [mask[pack_index] for mask in visible]
    attended_pack, total_pack = attend_pack(
        query_packs[pack_index],
        gathered_keys[pack_index],
        gathered_values[pack_index],
        pack_visible,
    )
    total_list = [total_pack]
    softmax_totals = jnp.stack(total_list, axis=0)
    hidden_in = inputs32 + jnp.dot(attended_pack, out_full, preferred_element_type=jnp.float32)
    scale_two = lax.rsqrt(jnp.mean(hidden_in * hidden_in, axis=-1, keepdims=True) + EPS)
    normed_two = hidden_in * scale_two
    xn_two = (normed_two * gain_two32).astype(jnp.bfloat16)
    gate_val = jnp.dot(xn_two, gate_full, preferred_element_type=jnp.float32)
    up_val = jnp.dot(xn_two, up_full, preferred_element_type=jnp.float32)
    activated = jax.nn.silu(gate_val)
    hidden = (activated * up_val).astype(jnp.bfloat16)
    result = (hidden_in + jnp.dot(hidden, down_full, preferred_element_type=jnp.float32)).astype(
        jnp.bfloat16
    )
    down_grad = jnp.dot(hidden.T, upstream, preferred_element_type=jnp.float32)
    d_hidden = jnp.dot(upstream, down_full.T, preferred_element_type=jnp.float32)
    sigmoid_gate = jax.nn.sigmoid(gate_val)
    d_gate = (d_hidden * up_val * sigmoid_gate * (1.0 + gate_val * (1.0 - sigmoid_gate))).astype(
        jnp.bfloat16
    )
    d_up = (d_hidden * activated).astype(jnp.bfloat16)
    gate_grad = jnp.dot(xn_two.T, d_gate, preferred_element_type=jnp.float32)
    up_grad = jnp.dot(xn_two.T, d_up, preferred_element_type=jnp.float32)
    d_norm_two = jnp.dot(d_gate, gate_full.T, preferred_element_type=jnp.float32) + jnp.dot(
        d_up, up_full.T, preferred_element_type=jnp.float32
    )
    gain_two_grad = jnp.sum(d_norm_two * normed_two, axis=0)
    d_hidden_in = upstream.astype(jnp.float32) + rms_back(
        d_norm_two * gain_two32, normed_two, scale_two
    )
    mlp_parts = (
        lax.psum_scatter(
            gain_two_grad.astype(jnp.bfloat16), "fsdp", scatter_dimension=0, tiled=True
        ).astype(jnp.float32),
        lax.psum_scatter(
            gate_grad.astype(jnp.bfloat16), "fsdp", scatter_dimension=0, tiled=True
        ).astype(jnp.float32),
        lax.psum_scatter(
            up_grad.astype(jnp.bfloat16), "fsdp", scatter_dimension=0, tiled=True
        ).astype(jnp.float32),
        lax.psum_scatter(
            down_grad.astype(jnp.bfloat16), "fsdp", scatter_dimension=0, tiled=True
        ).astype(jnp.float32),
    )
    d_branch = d_hidden_in.astype(jnp.bfloat16)
    out_grad = jnp.dot(attended_pack.T, d_branch, preferred_element_type=jnp.float32)
    d_attended = jnp.dot(d_branch, out_full.T, preferred_element_type=jnp.float32).astype(
        jnp.bfloat16
    )
    back_keys, back_values = (gathered_keys, gathered_values)
    grad_packs = d_attended.reshape(pack_count, token_count, -1)
    out_packs = attended_pack.reshape(pack_count, token_count, -1)
    pack_index = 0
    pack_visible = [mask[pack_index] for mask in visible]
    query_part, key_part, value_part = attend_back(
        query_packs[pack_index],
        back_keys[pack_index],
        back_values[pack_index],
        grad_packs[pack_index],
        out_packs[pack_index],
        softmax_totals[pack_index],
        pack_visible,
    )
    key_list = [key_part]
    value_list = [value_part]
    d_keys, d_values = (
        lax.psum_scatter(
            jnp.stack(key_list, axis=0).astype(jnp.bfloat16), "ctx", scatter_dimension=1, tiled=True
        ).astype(jnp.float32),
        lax.psum_scatter(
            jnp.stack(value_list, axis=0).astype(jnp.bfloat16),
            "ctx",
            scatter_dimension=1,
            tiled=True,
        ).astype(jnp.float32),
    )
    d_query = rotate(query_part, cosine, -sine_part).astype(jnp.bfloat16)
    d_key = rotate(d_keys.reshape(pack_count * token_count, -1), cosine, -sine_part).astype(
        jnp.bfloat16
    )
    d_value = d_values.reshape(pack_count * token_count, -1).astype(jnp.bfloat16)
    query_grad = jnp.dot(xn_one.T, d_query, preferred_element_type=jnp.float32)
    key_grad = jnp.dot(xn_one.T, d_key, preferred_element_type=jnp.float32)
    value_grad = jnp.dot(xn_one.T, d_value, preferred_element_type=jnp.float32)
    d_norm_one = (
        jnp.dot(d_query, query_full.T, preferred_element_type=jnp.float32)
        + jnp.dot(d_key, key_full.T, preferred_element_type=jnp.float32)
        + jnp.dot(d_value, value_full.T, preferred_element_type=jnp.float32)
    )
    gain_one_grad = jnp.sum(d_norm_one * normed_one, axis=0)
    d_inputs = d_hidden_in + rms_back(d_norm_one * gain_one32, normed_one, scale_one)
    attn_parts = (
        lax.psum_scatter(
            gain_one_grad.astype(jnp.bfloat16), "fsdp", scatter_dimension=0, tiled=True
        ).astype(jnp.float32),
        lax.psum_scatter(
            query_grad.astype(jnp.bfloat16), "fsdp", scatter_dimension=0, tiled=True
        ).astype(jnp.float32),
        lax.psum_scatter(
            key_grad.astype(jnp.bfloat16), "fsdp", scatter_dimension=0, tiled=True
        ).astype(jnp.float32),
        lax.psum_scatter(
            value_grad.astype(jnp.bfloat16), "fsdp", scatter_dimension=0, tiled=True
        ).astype(jnp.float32),
        lax.psum_scatter(
            out_grad.astype(jnp.bfloat16), "fsdp", scatter_dimension=0, tiled=True
        ).astype(jnp.float32),
    )
    finished = (
        lax.psum(attn_parts[0].astype(jnp.bfloat16), ("ctx", "grp")).astype(jnp.float32),
        lax.psum(attn_parts[1].astype(jnp.bfloat16), ("ctx", "grp")).astype(jnp.float32),
        lax.psum(attn_parts[2].astype(jnp.bfloat16), ("ctx", "grp")).astype(jnp.float32),
        lax.psum(attn_parts[3].astype(jnp.bfloat16), ("ctx", "grp")).astype(jnp.float32),
        lax.psum(attn_parts[4].astype(jnp.bfloat16), ("ctx", "grp")).astype(jnp.float32),
        lax.psum(mlp_parts[0].astype(jnp.bfloat16), ("ctx", "grp")).astype(jnp.float32),
        lax.psum(mlp_parts[1].astype(jnp.bfloat16), ("ctx", "grp")).astype(jnp.float32),
        lax.psum(mlp_parts[2].astype(jnp.bfloat16), ("ctx", "grp")).astype(jnp.float32),
        lax.psum(mlp_parts[3].astype(jnp.bfloat16), ("ctx", "grp")).astype(jnp.float32),
    )
    home_out, home_grad = (
        lax.all_to_all(send_home(result), "ctx", split_axis=1, concat_axis=1, tiled=True),
        lax.all_to_all(
            send_home(d_inputs.astype(jnp.bfloat16)), "ctx", split_axis=1, concat_axis=1, tiled=True
        ),
    )
    return (
        restore(home_out),
        restore(home_grad),
        softmax_totals,
        finished[0],
        finished[1],
        finished[2],
        finished[3],
        finished[4],
        finished[5],
        finished[6],
        finished[7],
        finished[8],
    )


MINLEN = 1024
QB = 256
VMEM_LIMIT = 56 * 1024 * 1024


def fill_tables(cl_ref, sl_ref, ch_ref, sh_ref, c_ref, s_ref):
    @pl.when(pl.program_id(0) == 0)
    def _():
        cos_low, sin_low = cl_ref[...], sl_ref[...]
        for i in range(c_ref.shape[1] // BLK):
            at = slice(i * BLK, (i + 1) * BLK)
            cos_high, sin_high = ch_ref[:, i : i + 1], sh_ref[:, i : i + 1]
            c_ref[:, at] = cos_high * cos_low - sin_high * sin_low
            s_ref[:, at] = sin_high * cos_low + cos_high * sin_low


def attend_kernel(
    place, q_ref, k_ref, v_ref, cl_ref, sl_ref, ch_ref, sh_ref,
    keep_ref, send_ref, lse_ref, qr_ref, kr_ref, vr_ref, held, c_ref, s_ref,
):
    fill_tables(cl_ref, sl_ref, ch_ref, sh_ref, c_ref, s_ref)
    cosine = c_ref[...]
    sine = s_ref[...]
    half = HEAD_SIZE // 2
    seq = cosine.shape[1]

    def turn(field):
        front, back = field[:half], field[half:]
        return jnp.concatenate(
            [front * cosine - back * sine, back * cosine + front * sine], axis=0
        )

    k_rot = turn(k_ref[...])
    kr_ref[...] = k_rot.astype(jnp.bfloat16)
    key = k_rot.T.astype(jnp.bfloat16)
    val_t = v_ref[...].astype(jnp.bfloat16)
    vr_ref[...] = val_t
    q0 = turn(q_ref[:HEAD_SIZE]).astype(jnp.bfloat16)
    q1 = turn(q_ref[HEAD_SIZE:]).astype(jnp.bfloat16)
    qr_ref[:HEAD_SIZE] = q0
    qr_ref[HEAD_SIZE:] = q1
    rows = lax.broadcasted_iota(jnp.int32, (QB, 2 * QB), 0)
    cols = lax.broadcasted_iota(jnp.int32, (QB, 2 * QB), 1)
    keep = rows <= jnp.where(cols >= QB, cols - QB, cols)
    for b in range(seq // QB):
        lo, n = b * QB, (b + 1) * QB
        q_t = jnp.concatenate([q0[:, lo:n], q1[:, lo:n]], axis=1)
        scores = jnp.dot(key[:n], q_t, preferred_element_type=jnp.float32) * HEAD_SIZE ** (-0.5)
        diag = jnp.where(keep, scores[lo:], MASKED)
        top = jnp.max(diag, axis=0, keepdims=True)
        if b > 0:
            top = jnp.maximum(top, jnp.max(scores[:lo], axis=0, keepdims=True))
        e_diag = jnp.exp(diag - top)
        total = jnp.sum(e_diag, axis=0, keepdims=True)
        out = jnp.dot(val_t[:, lo:n], e_diag.astype(jnp.bfloat16), preferred_element_type=jnp.float32)
        if b > 0:
            e_rest = jnp.exp(scores[:lo] - top)
            total = total + jnp.sum(e_rest, axis=0, keepdims=True)
            out = out + jnp.dot(
                val_t[:, :lo], e_rest.astype(jnp.bfloat16), preferred_element_type=jnp.float32
            )
        out = (out / total).astype(jnp.bfloat16)
        held[:HEAD_SIZE, lo:n] = out[:, :QB]
        held[HEAD_SIZE:, lo:n] = out[:, QB:]
        lse = top + jnp.log(total)
        lse_ref[0, 0:1, lo:n] = lse[:, :QB]
        lse_ref[0, 1:2, lo:n] = lse[:, QB:]
    tok = seq // 2
    for core in range(2):

        @pl.when(place[0] == core)
        def _():
            keep_ref[...] = held[:, core * tok : (core + 1) * tok]
            send_ref[...] = held[:, (1 - core) * tok : (2 - core) * tok]


def attend_seq(place, qkv_t, tables):
    rows, seq = qkv_t.shape
    kv = rows // (4 * HEAD_SIZE)
    group = pl.BlockSpec((2 * HEAD_SIZE, seq), lambda j: (j, 0))

    def head(base):
        return pl.BlockSpec((HEAD_SIZE, seq), lambda j: (base + j, 0))

    table = pl.BlockSpec(memory_space=pltpu.VMEM)
    return pl.pallas_call(
        attend_kernel,
        grid=(kv,),
        in_specs=[pl.BlockSpec(memory_space=pltpu.SMEM), group, head(2 * kv), head(3 * kv), table, table, table, table],
        out_specs=[
            pl.BlockSpec((2 * HEAD_SIZE, seq // 2), lambda j: (j, 0)),
            pl.BlockSpec((2 * HEAD_SIZE, seq // 2), lambda j: (j, 0)),
            pl.BlockSpec((1, 2, seq), lambda j: (j, 0, 0)),
            group,
            head(0),
            head(0),
        ],
        out_shape=[
            jax.ShapeDtypeStruct((2 * kv * HEAD_SIZE, seq // 2), jnp.bfloat16),
            jax.ShapeDtypeStruct((2 * kv * HEAD_SIZE, seq // 2), jnp.bfloat16),
            jax.ShapeDtypeStruct((kv, 2, seq), jnp.float32),
            jax.ShapeDtypeStruct((2 * kv * HEAD_SIZE, seq), jnp.bfloat16),
            jax.ShapeDtypeStruct((kv * HEAD_SIZE, seq), jnp.bfloat16),
            jax.ShapeDtypeStruct((kv * HEAD_SIZE, seq), jnp.bfloat16),
        ],
        scratch_shapes=[
            pltpu.VMEM((2 * HEAD_SIZE, seq), jnp.bfloat16),
            pltpu.VMEM((HEAD_SIZE // 2, seq), jnp.float32),
            pltpu.VMEM((HEAD_SIZE // 2, seq), jnp.float32),
        ],
        compiler_params=pltpu.CompilerParams(vmem_limit_bytes=VMEM_LIMIT),
        cost_estimate=pl.CostEstimate(
            flops=4 * kv * 2 * seq * seq * HEAD_SIZE, bytes_accessed=10 * rows * seq, transcendentals=kv * seq * seq
        ),
        name="attend",
    )(place, qkv_t, qkv_t, qkv_t, *tables)


def attend_back_kernel(
    place, q_ref, k_ref, v_ref, keep_ref, got_ref, lse_ref, cl_ref, sl_ref, ch_ref, sh_ref,
    dq_ref, dk_ref, dv_ref, dk_acc, dv_acc, c_ref, s_ref,
):
    fill_tables(cl_ref, sl_ref, ch_ref, sh_ref, c_ref, s_ref)
    half = HEAD_SIZE // 2
    cosine = c_ref[...]
    sine = s_ref[...]
    seq = cosine.shape[1]

    def turn_back(field, cos, sin):
        front, back = field[:half], field[half:]
        return jnp.concatenate([front * cos + back * sin, back * cos - front * sin], axis=0)

    def flip(field):
        return field.astype(jnp.float32).T.astype(jnp.bfloat16)

    key_t = k_ref[...]
    key = flip(key_t)
    val = flip(v_ref[...])
    q0_t, q1_t = q_ref[:HEAD_SIZE], q_ref[HEAD_SIZE:]
    first_core = place[0] == 0
    early = jnp.where(first_core, keep_ref[...], got_ref[...])
    late = jnp.where(first_core, got_ref[...], keep_ref[...])
    grads = jnp.concatenate([early, late], axis=1)
    g0_t, g1_t = grads[:HEAD_SIZE], grads[HEAD_SIZE:]
    q0, q1, g0, g1 = flip(q0_t), flip(q1_t), flip(g0_t), flip(g1_t)
    dk_acc[...] = jnp.zeros_like(dk_acc)
    dv_acc[...] = jnp.zeros_like(dv_acc)
    rows = lax.broadcasted_iota(jnp.int32, (QB, 2 * QB), 0)
    cols = lax.broadcasted_iota(jnp.int32, (QB, 2 * QB), 1)
    keep = rows <= jnp.where(cols >= QB, cols - QB, cols)
    for b in range(seq // QB):
        lo, n = b * QB, (b + 1) * QB
        q_t = jnp.concatenate([q0_t[:, lo:n], q1_t[:, lo:n]], axis=1)
        g_t = jnp.concatenate([g0_t[:, lo:n], g1_t[:, lo:n]], axis=1)
        q_n = jnp.concatenate([q0[lo:n], q1[lo:n]], axis=0)
        g_n = jnp.concatenate([g0[lo:n], g1[lo:n]], axis=0)
        lse = jnp.concatenate([lse_ref[0, 0:1, lo:n], lse_ref[0, 1:2, lo:n]], axis=1)
        parts = []
        delta = None
        for start, stop in ([(0, lo)] if b > 0 else []) + [(lo, n)]:
            scores = jnp.dot(key[start:stop], q_t, preferred_element_type=jnp.float32) * HEAD_SIZE ** (-0.5)
            prob = jnp.exp(scores - lse)
            if start == lo:
                prob = jnp.where(keep, prob, 0.0)
            d_prob = jnp.dot(val[start:stop], g_t, preferred_element_type=jnp.float32)
            part = jnp.sum(prob * d_prob, axis=0, keepdims=True)
            delta = part if delta is None else delta + part
            dv_acc[start:stop] += jnp.dot(prob.astype(jnp.bfloat16), g_n, preferred_element_type=jnp.float32)
            parts.append((start, stop, prob, d_prob))
        dq_t = None
        for start, stop, prob, d_prob in parts:
            d_score = (prob * (d_prob - delta) * HEAD_SIZE ** (-0.5)).astype(jnp.bfloat16)
            dk_acc[start:stop] += jnp.dot(d_score, q_n, preferred_element_type=jnp.float32)
            part = jnp.dot(key_t[:, start:stop], d_score, preferred_element_type=jnp.float32)
            dq_t = part if dq_t is None else dq_t + part
        cos, sin = cosine[:, lo:n], sine[:, lo:n]
        dq_ref[:HEAD_SIZE, lo:n] = turn_back(dq_t[:, :QB], cos, sin).astype(jnp.bfloat16)
        dq_ref[HEAD_SIZE:, lo:n] = turn_back(dq_t[:, QB:], cos, sin).astype(jnp.bfloat16)
    dk_ref[...] = turn_back(dk_acc[...].T, cosine, sine).astype(jnp.bfloat16)
    dv_ref[...] = dv_acc[...].T.astype(jnp.bfloat16)


def attend_seq_back(place, q_t, k_t, v_t, g_keep, g_got, lse, tables):
    rows, seq = k_t.shape
    kv = rows // HEAD_SIZE
    group = pl.BlockSpec((2 * HEAD_SIZE, seq), lambda j: (j, 0))
    part = pl.BlockSpec((2 * HEAD_SIZE, seq // 2), lambda j: (j, 0))
    head = pl.BlockSpec((HEAD_SIZE, seq), lambda j: (j, 0))
    table = pl.BlockSpec(memory_space=pltpu.VMEM)
    return pl.pallas_call(
        attend_back_kernel,
        grid=(kv,),
        in_specs=[
            pl.BlockSpec(memory_space=pltpu.SMEM), group, head, head, part, part,
            pl.BlockSpec((1, 2, seq), lambda j: (j, 0, 0)), table, table, table, table,
        ],
        out_specs=[group, head, head],
        out_shape=[
            jax.ShapeDtypeStruct((2 * rows, seq), jnp.bfloat16),
            jax.ShapeDtypeStruct((rows, seq), jnp.bfloat16),
            jax.ShapeDtypeStruct((rows, seq), jnp.bfloat16),
        ],
        scratch_shapes=[
            pltpu.VMEM((seq, HEAD_SIZE), jnp.float32),
            pltpu.VMEM((seq, HEAD_SIZE), jnp.float32),
            pltpu.VMEM((HEAD_SIZE // 2, seq), jnp.float32),
            pltpu.VMEM((HEAD_SIZE // 2, seq), jnp.float32),
        ],
        compiler_params=pltpu.CompilerParams(vmem_limit_bytes=VMEM_LIMIT),
        cost_estimate=pl.CostEstimate(
            flops=10 * kv * 2 * seq * seq * HEAD_SIZE, bytes_accessed=20 * rows * seq, transcendentals=kv * seq * seq
        ),
        name="attend_back",
    )(place, q_t, k_t, v_t, g_keep, g_got, lse, *tables)


def fp32(field):
    return field.astype(jnp.float32)


def mm(left, right, dims=((1,), (0,)), out=jnp.float32):
    return lax.dot_general(left, right, (dims, ((), ())), preferred_element_type=out)


ANY = pl.BlockSpec(memory_space=pl.ANY)
SMEM = pl.BlockSpec(memory_space=pltpu.SMEM)
VM = pl.BlockSpec(memory_space=pltpu.VMEM)
PARAMS = pltpu.CompilerParams(vmem_limit_bytes=VMEM_LIMIT)
MESH = pl.DeviceIdType.MESH
TILE = 256


def bf16_like(*dims):
    return jax.ShapeDtypeStruct(dims, jnp.bfloat16)


def f32_like(*dims):
    return jax.ShapeDtypeStruct(dims, jnp.float32)


def cost(flops, moved):
    return pl.CostEstimate(flops=int(flops), bytes_accessed=int(moved), transcendentals=0)


class Spots:
    def __init__(self):
        z, f, g = lax.axis_index("ctx"), lax.axis_index("fsdp"), lax.axis_index("grp")
        self.z, self.f, self.g = z, f, g
        self.parity = z % 2
        self.fx = f + 1 - 2 * (f % 2)
        self.fy = f + 2 - 4 * (f // 2)
        self.fd = 3 - f
        across = z + 1 - 2 * self.parity
        self.x = (z, self.fx, g)
        self.y = (z, self.fy, g)
        self.diag = (z, self.fd, g)
        self.core = (z, f, 1 - g)
        self.across = (across, f, g)
        self.swap = (across, f, 1 - g)


def greet(*partners):
    barrier = pltpu.get_barrier_semaphore()
    for partner in partners:
        pl.semaphore_signal(barrier, inc=1, device_id=partner, device_id_type=MESH)
    pl.semaphore_wait(barrier, len(partners))


def rows_at(start, size):
    return pl.ds(pl.multiple_of(start, size), size)


def gather_kernel(
    tokens, cotangent, wq, wk, wv, wo, gate, up, down, gain,
    qkv_o, out_o, pair_o, down_o, x_o, dy_o, gain_o, xn_o, turned_o,
    send, recv, near, far, qkv_v, out_v, pair_v, down_v, tok_v, gain_v,
    extra, x_v, w_v, gains_v, xn_v, turned_v,
):
    at = Spots()
    g, f, parity = at.g, at.f, at.parity
    greet(at.x, at.y, at.diag, at.core, at.across, at.swap)
    taken = [0, 0]

    def remote(src, dst, device):
        i = taken[0]
        taken[0] += 1
        return pltpu.make_async_remote_copy(
            src_ref=src, dst_ref=dst, send_sem=send.at[i], recv_sem=recv.at[i],
            device_id=device, device_id_type=MESH,
        )

    class Bounce:
        def __init__(self, src, via, dst):
            i = taken[1]
            taken[1] += 1
            self.first = pltpu.make_async_copy(src, via, near.at[i])
            self.second = pltpu.make_async_copy(via, dst, far.at[i])

        def start(self):
            self.first.start()

        def turn(self):
            self.first.wait()
            self.second.start()

        def wait(self):
            self.second.wait()

    def start(copies):
        for copy in copies:
            copy.start()
        return copies

    def arrive(copies):
        for copy in copies:
            copy.wait_recv()

    tok = tokens.shape[1]
    feat = wq.shape[0]
    mid = feat // 2
    nq, nk, nv = (w.shape[1] // 2 for w in (wq, wk, wv))
    nf = gate.shape[1] // 8
    wide = wo.shape[1] // 2
    count = 4
    top, low = slice(0, mid), slice(mid, feat)

    mine = rows_at(g * tok, tok)
    swaps = [
        remote(tokens.at[0], x_o.at[mine], at.swap),
        remote(cotangent.at[0], dy_o.at[mine], at.swap),
    ]
    keeps = [
        Bounce(tokens.at[0], tok_v.at[0], x_o.at[mine]),
        Bounce(cotangent.at[0], tok_v.at[1], dy_o.at[mine]),
    ]
    away = rows_at((1 - g) * tok, tok)
    swaps_out = [
        pltpu.make_async_remote_copy(
            src_ref=array.at[0], dst_ref=into.at[away], send_sem=send.at[i], recv_sem=recv.at[i],
            device_id=at.swap, device_id_type=MESH,
        )
        for i, (array, into) in enumerate(((tokens, x_o), (cotangent, dy_o)))
    ]
    shares = [remote(x_o.at[mine], x_o.at[mine], at.core), remote(dy_o.at[mine], dy_o.at[mine], at.core)]

    @pl.when(g != parity)
    def _():
        start(swaps_out)

    @pl.when(g == parity)
    def _():
        start(keeps)
        for copy in keeps:
            copy.turn()

    own_rows = f * feat
    shared_cols = (count - 1) * nf

    def pair_direct(part, device):
        first = taken[0]
        taken[0] += count + 1
        rows = rows_at(own_rows + part.start, mid)

        def made(array, index, k, i):
            return pltpu.make_async_remote_copy(
                src_ref=array.at[part, rows_at((2 * k + g) * nf, nf)],
                dst_ref=pair_o.at[index, rows, rows_at(k * nf, nf)],
                send_sem=send.at[first + i], recv_sem=recv.at[first + i],
                device_id=device, device_id_type=MESH,
            )

        def some(array):
            return [made(array, parity, k, k) for k in range(count - 1)]

        @pl.when(parity == 0)
        def _():
            start(some(gate))

        @pl.when(parity == 1)
        def _():
            start(some(up))

        last = start([made(gate, 0, count - 1, count - 1), made(up, 1, count - 1, count)])
        return some(gate), last

    pair_xt, last_xt = pair_direct(top, at.x)
    pair_yl, last_yl = pair_direct(low, at.y)
    pair_xl, last_xl = pair_direct(low, at.x)
    pair_yt, last_yt = pair_direct(top, at.y)

    def qkv_direct(part, device):
        copies = []
        for array, width, column in ((wq, nq, 0), (wk, nk, nq), (wv, nv, nq + nk)):
            copies.append(
                remote(
                    array.at[part, rows_at(g * width, width)],
                    qkv_o.at[rows_at(own_rows + part.start, mid), column : column + width],
                    device,
                )
            )
        return start(copies)

    qkv_xt = qkv_direct(top, at.x)
    qkv_yl = qkv_direct(low, at.y)
    qkv_xl = qkv_direct(low, at.x)
    qkv_yt = qkv_direct(top, at.y)

    own = rows_at(own_rows, feat)
    locals_ = [
        Bounce(
            array.at[:, rows_at(g * width, width)],
            qkv_v.at[:, column : column + width],
            qkv_o.at[own, column : column + width],
        )
        for array, width, column in ((wq, nq, 0), (wk, nk, nq), (wv, nv, nq + nk))
    ]
    locals_.append(Bounce(wo, out_v, out_o.at[own]))
    locals_.append(Bounce(down.at[rows_at(g * nf, nf)], down_v, down_o))
    for array, index in ((gate, 0), (up, 1)):
        for k in range(count):
            locals_.append(
                Bounce(
                    array.at[:, rows_at((2 * k + g) * nf, nf)],
                    pair_v.at[index, :, rows_at(k * nf, nf)],
                    pair_o.at[index, own, rows_at(k * nf, nf)],
                )
            )
    gain_place = gain_o.at[pl.ds(f, 1)]
    locals_.append(Bounce(gain, gain_v, gain_place))
    start(locals_)
    for copy in locals_:
        copy.turn()
    gains = start([remote(gain, gain_place, to) for to in (at.x, at.y, at.diag)])

    def forward(array_at, rows_x, rows_y):
        return remote(array_at(rows_x), array_at(rows_x), at.y), remote(
            array_at(rows_y), array_at(rows_y), at.x
        )

    x_top, y_low = rows_at(at.fx * feat, mid), rows_at(at.fy * feat + mid, mid)
    x_low, y_top = rows_at(at.fx * feat + mid, mid), rows_at(at.fy * feat, mid)
    d_top, d_low = rows_at(at.fd * feat, mid), rows_at(at.fd * feat + mid, mid)

    def pair_view(rows):
        return pair_o.at[parity, rows, 0:shared_cols]

    def last_view(rows):
        return pair_o.at[:, rows, shared_cols : shared_cols + nf]

    def out_view(rows):
        return out_o.at[rows, rows_at(g * wide, wide)]

    pair_fy, pair_fx = forward(pair_view, x_top, y_low)
    last_fy, last_fx = forward(last_view, x_top, y_low)
    sends = [pair_fy, pair_fx, last_fy, last_fx]

    def across(rows):
        copy = remote(pair_view(rows), pair_view(rows), at.across)
        copy.start()
        sends.append(copy)
        return copy

    arrive(pair_xt)
    pair_fy.start()
    z_copies = [across(x_top)]
    arrive(pair_yl)
    pair_fx.start()
    z_copies.append(across(y_low))

    def out_direct(part, device):
        copy = remote(
            wo.at[part, rows_at(g * wide, wide)],
            out_o.at[rows_at(own_rows + part.start, mid), rows_at(g * wide, wide)],
            device,
        )
        copy.start()
        return copy

    out_xt, out_yl = out_direct(top, at.x), out_direct(low, at.y)
    out_xl, out_yt = out_direct(low, at.x), out_direct(top, at.y)

    arrive(pair_xl)
    z_copies.append(across(x_low))
    arrive(pair_yt)
    z_copies.append(across(y_top))

    def qkv_view(rows):
        return qkv_o.at[rows]

    qkv_fy, qkv_fx = forward(qkv_view, x_top, y_low)
    arrive(qkv_xt)
    qkv_fy.start()
    arrive(qkv_yl)
    qkv_fx.start()
    arrive(last_xt)
    last_fy.start()
    arrive(last_yl)
    last_fx.start()

    pair_fy.wait_recv()
    z_copies.append(across(d_top))
    pair_fx.wait_recv()
    z_copies.append(across(d_low))

    for i in range(2):

        @pl.when(g != parity)
        def _():
            swaps[i].wait_recv()
            swaps_out[i].wait_send()

        @pl.when(g == parity)
        def _():
            keeps[i].wait()

        shares[i].start()

    out_fy, out_fx = forward(out_view, x_top, y_low)
    out_xt.wait_recv()
    out_fy.start()
    out_yl.wait_recv()
    out_fx.start()
    out_xl.wait_recv()
    out_yt.wait_recv()

    def share(rows):
        copy = remote(out_view(rows), out_view(rows), at.core)
        copy.start()
        return copy

    shared = [share(x_top), share(x_low), share(y_top), share(y_low)]

    arrive(qkv_xl + qkv_yt + [qkv_fy, qkv_fx] + gains + shares[:1])
    for copy in locals_[:3] + locals_[-1:]:
        copy.wait()
    loads = [
        pltpu.make_async_copy(src, dst, extra.at[i])
        for i, (src, dst) in enumerate(((x_o, x_v), (gain_o, gains_v), (qkv_o, w_v)))
    ]
    start(loads)
    for copy in loads:
        copy.wait()
    row = gain_row(gains_v, 0)

    @pl.loop(0, x_v.shape[0] // TILE)
    def _(n):
        part = rows_at(n * TILE, TILE)
        field = fp32(x_v[part, :])
        xn_v[part, :] = (field * norm_scale(field) * row).astype(jnp.bfloat16)

    @pl.loop(0, w_v.shape[1] // TILE)
    def _(n):
        part = rows_at(n * TILE, TILE)
        turned_v[part, :] = mm(w_v[:, part].T, xn_v[...], ((1,), (1,)))

    results = start(
        [pltpu.make_async_copy(xn_v, xn_o, extra.at[3]), pltpu.make_async_copy(turned_v, turned_o, extra.at[4])]
    )

    out_fy.wait_recv()
    shared.append(share(d_top))
    out_fx.wait_recv()
    shared.append(share(d_low))

    arrive([last_fy, last_fx])
    arrive(last_xl + last_yt)
    arrive(shares[1:])
    arrive(shared)
    arrive(z_copies)
    for copy in locals_[3:-1] + results:
        copy.wait()
    for copy in (
        pair_xt + pair_yl + pair_xl + pair_yt + qkv_xt + qkv_yl + qkv_xl + qkv_yt + gains
        + sends + shares + shared
        + [out_xt, out_yl, out_xl, out_yt, out_fy, out_fx, qkv_fy, qkv_fx]
        + last_xt + last_yl + last_xl + last_yt
    ):
        copy.wait_send()


def gather_all(tokens, cotangent, wq, wk, wv, wo, gate, up, down, gain):
    tok, width = tokens.shape[1:]
    nf = gate.shape[1] // 8
    cols = (wq.shape[1] + wk.shape[1] + wv.shape[1]) // 2
    return pl.pallas_call(
        gather_kernel,
        in_specs=[ANY] * 10,
        out_specs=[ANY] * 9,
        out_shape=[
            bf16_like(width, cols),
            bf16_like(4 * wo.shape[0], width),
            bf16_like(2, width, 4 * nf),
            bf16_like(nf, width),
            bf16_like(2 * tok, width),
            bf16_like(2 * tok, width),
            jax.ShapeDtypeStruct((4,) + gain.shape[1:], gain.dtype),
            bf16_like(2 * tok, width),
            f32_like(cols, 2 * tok),
        ],
        scratch_shapes=[
            pltpu.SemaphoreType.DMA((72,)),
            pltpu.SemaphoreType.DMA((72,)),
            pltpu.SemaphoreType.DMA((20,)),
            pltpu.SemaphoreType.DMA((20,)),
            pltpu.VMEM((width // 4, cols), jnp.bfloat16),
            pltpu.VMEM(wo.shape, jnp.bfloat16),
            pltpu.VMEM((2, width // 4, 4 * nf), jnp.bfloat16),
            pltpu.VMEM((nf, width), jnp.bfloat16),
            pltpu.VMEM((2, tok, width), jnp.bfloat16),
            pltpu.VMEM(gain.shape, gain.dtype),
            pltpu.SemaphoreType.DMA((5,)),
            pltpu.VMEM((2 * tok, width), jnp.bfloat16),
            pltpu.VMEM((width, cols), jnp.bfloat16),
            pltpu.VMEM((4,) + gain.shape[1:], gain.dtype),
            pltpu.VMEM((2 * tok, width), jnp.bfloat16),
            pltpu.VMEM((cols, 2 * tok), jnp.float32),
        ],
        compiler_params=pltpu.CompilerParams(
            collective_id=0, has_side_effects=True, vmem_limit_bytes=VMEM_LIMIT
        ),
        cost_estimate=cost(0, 500e6),
        name="gather",
    )(tokens, cotangent, wq, wk, wv, wo, gate, up, down, gain)


def gain_row(gain, which):
    return jnp.concatenate([gain[k, which : which + 1, :] for k in range(gain.shape[0])], axis=1)


def norm_scale(field):
    return lax.rsqrt(jnp.mean(field * field, axis=-1, keepdims=True) + EPS)


def residual_kernel(place, x_ref, attn_keep, attn_got, gain, w_ref, h_ref, xn_ref, attn_ref):
    core = place[0]
    heads = attn_keep.shape[0]
    keep_at, got_at = rows_at(core * heads, heads), rows_at((1 - core) * heads, heads)
    attn_ref[keep_at, :] = attn_keep[...]
    attn_ref[got_at, :] = attn_got[...]
    field = fp32(x_ref[...]) + mm(attn_ref[...].T, w_ref[...])
    h_ref[...] = field
    xn_ref[...] = (field * norm_scale(field) * gain_row(gain, 1)).astype(jnp.bfloat16)


def residual(place, x_seq, attn_keep, attn_got, gains, weight):
    seq, width = x_seq.shape
    tok = seq // 2
    heads = attn_keep.shape[0]
    steps = tok // TILE
    rows = pl.BlockSpec((TILE, width), lambda i, place: (i, 0))
    return pl.pallas_call(
        residual_kernel,
        grid_spec=pltpu.PrefetchScalarGridSpec(
            num_scalar_prefetch=1,
            grid=(steps,),
            in_specs=[
                pl.BlockSpec((TILE, width), lambda i, place: (steps * place[0] + i, 0)),
                pl.BlockSpec((heads, TILE), lambda i, place: (0, i)),
                pl.BlockSpec((heads, TILE), lambda i, place: (0, i)),
                VM,
                VM,
            ],
            out_specs=[rows, rows, pl.BlockSpec((2 * heads, TILE), lambda i, place: (0, i))],
        ),
        out_shape=[f32_like(tok, width), bf16_like(tok, width), bf16_like(2 * heads, tok)],
        compiler_params=PARAMS,
        cost_estimate=cost(2 * tok * width * weight.shape[0], 14e6),
        name="residual",
    )(place, x_seq, attn_keep, attn_got, gains, weight)


def hidden_kernel(place, xn_own, xn_got, gate_w, up_w, hid_ref, for_gate_ref, act_ref, xn_ref):
    @pl.when(pl.program_id(0) == 0)
    def _():
        tok = xn_own.shape[0]
        xn_ref[rows_at(place[0] * tok, tok), :] = xn_own[...]
        xn_ref[rows_at((1 - place[0]) * tok, tok), :] = xn_got[...]

    gate = mm(xn_ref[...], gate_w[0])
    up = mm(xn_ref[...], up_w[0])
    sig = 1.0 / (1.0 + jnp.exp(-gate))
    act = gate * sig
    hid_ref[...] = (act * up).astype(jnp.bfloat16)
    for_gate_ref[...] = (up * (sig + act * (1.0 - sig))).astype(jnp.bfloat16)
    act_ref[...] = act.astype(jnp.bfloat16)


def hidden_step(place, xn_own, xn_got, pair):
    seq, width = 2 * xn_own.shape[0], xn_own.shape[1]
    ff = pair.shape[2]
    block = pl.BlockSpec((seq, TILE), lambda n: (0, n))
    return pl.pallas_call(
        hidden_kernel,
        grid=(ff // TILE,),
        in_specs=[
            SMEM,
            VM,
            VM,
            pl.BlockSpec((1, width, TILE), lambda n: (0, 0, n)),
            pl.BlockSpec((1, width, TILE), lambda n: (1, 0, n)),
        ],
        out_specs=[block] * 3 + [VM],
        out_shape=[bf16_like(seq, ff)] * 3 + [bf16_like(seq, width)],
        compiler_params=PARAMS,
        cost_estimate=cost(4 * seq * width * ff, 30e6),
        name="hidden",
    )(place, xn_own, xn_got, pair, pair)


def hidden_back_kernel(dy_ref, down_w, for_gate_ref, act_ref, dgate_ref, dup_ref):
    d_hidden = mm(dy_ref[...], down_w[...], ((1,), (1,)))
    dgate_ref[...] = (d_hidden * fp32(for_gate_ref[...])).astype(jnp.bfloat16)
    dup_ref[...] = (d_hidden * fp32(act_ref[...])).astype(jnp.bfloat16)


def hidden_back(dy, down, for_gate, act):
    seq, width = dy.shape
    ff = down.shape[0]
    block = pl.BlockSpec((seq, TILE), lambda n: (0, n))
    return pl.pallas_call(
        hidden_back_kernel,
        grid=(ff // TILE,),
        in_specs=[VM, pl.BlockSpec((TILE, width), lambda n: (n, 0)), block, block],
        out_specs=[block] * 2,
        out_shape=[bf16_like(seq, ff)] * 2,
        compiler_params=PARAMS,
        cost_estimate=cost(2 * seq * width * ff, 26e6),
        name="hidden_back",
    )(dy, down, for_gate, act)


def back_kernel(place, dgate_ref, dup_ref, gate_w, up_w, own_ref, send_ref):
    field = mm(dgate_ref[...], gate_w[0], ((1,), (1,)))
    field = field + mm(dup_ref[...], up_w[0], ((1,), (1,)))
    tok = own_ref.shape[0]

    @pl.when(place[0] == 0)
    def _():
        own_ref[...] = field[:tok]
        send_ref[...] = field[tok:].astype(jnp.bfloat16)

    @pl.when(place[0] == 1)
    def _():
        own_ref[...] = field[tok:]
        send_ref[...] = field[:tok].astype(jnp.bfloat16)


def back_step(place, d_gate, d_up, pair):
    seq, ff = d_gate.shape
    width = pair.shape[1]
    out = pl.BlockSpec((seq // 2, TILE), lambda n: (0, n))
    return pl.pallas_call(
        back_kernel,
        grid=(width // TILE,),
        in_specs=[
            SMEM,
            VM,
            VM,
            pl.BlockSpec((1, TILE, ff), lambda n: (0, n, 0)),
            pl.BlockSpec((1, TILE, ff), lambda n: (1, n, 0)),
        ],
        out_specs=[out, out],
        out_shape=[f32_like(seq // 2, width), bf16_like(seq // 2, width)],
        compiler_params=PARAMS,
        cost_estimate=cost(4 * seq * width * ff, 26e6),
        name="back",
    )(place, d_gate, d_up, pair, pair)


def result_kernel(place, hid_ref, h_ref, down_w, own_ref, send_ref):
    field = mm(hid_ref[...], down_w[...])
    tok = own_ref.shape[0]

    @pl.when(place[0] == 0)
    def _():
        own_ref[...] = field[:tok] + h_ref[...]
        send_ref[...] = field[tok:].astype(jnp.bfloat16)

    @pl.when(place[0] == 1)
    def _():
        own_ref[...] = field[tok:] + h_ref[...]
        send_ref[...] = field[:tok].astype(jnp.bfloat16)


def result_step(place, hidden, h_own, down):
    tok, width = h_own.shape
    ff = hidden.shape[1]
    out = pl.BlockSpec((tok, TILE), lambda n: (0, n))
    return pl.pallas_call(
        result_kernel,
        grid=(width // TILE,),
        in_specs=[SMEM, VM, out, pl.BlockSpec((ff, TILE), lambda n: (0, n))],
        out_specs=[out, out],
        out_shape=[f32_like(tok, width), bf16_like(tok, width)],
        compiler_params=PARAMS,
        cost_estimate=cost(4 * tok * width * ff, 20e6),
        name="result",
    )(place, hidden, h_own, down)


def entry_kernel(place, dn_own, dn_got, h_ref, dy_ref, gain, w_ref, dh_ref, da_ref, keep_ref, send_ref, part_ref):
    core = place[0]

    @pl.when(pl.program_id(0) == 0)
    def _():
        part_ref[...] = jnp.zeros_like(part_ref)

    field = h_ref[...]
    scale = norm_scale(field)
    hat = field * scale
    grad = dn_own[...] + fp32(dn_got[...])
    part_ref[...] += jnp.sum(grad * hat, axis=0, keepdims=True)
    total = fp32(dy_ref[...]) + rms_back(grad * gain_row(gain, 1), hat, scale)
    dh_ref[...] = total
    da_ref[...] = total.astype(jnp.bfloat16)
    heads = keep_ref.shape[0]
    for ref, at in ((send_ref, 1 - core), (keep_ref, core)):
        ref[...] = mm(w_ref[rows_at(at * heads, heads), :], da_ref[...], ((1,), (1,))).astype(jnp.bfloat16)


def entry_step(place, dn_own, dn_got, h_own, dy_all, gains, weight):
    tok, width = h_own.shape
    heads = weight.shape[0] // 2
    steps = tok // TILE
    rows = pl.BlockSpec((TILE, width), lambda i, place: (i, 0))
    cols = pl.BlockSpec((heads, TILE), lambda i, place: (0, i))
    return pl.pallas_call(
        entry_kernel,
        grid_spec=pltpu.PrefetchScalarGridSpec(
            num_scalar_prefetch=1,
            grid=(steps,),
            in_specs=[
                rows,
                rows,
                rows,
                pl.BlockSpec((TILE, width), lambda i, place: (steps * place[0] + i, 0)),
                VM,
                VM,
            ],
            out_specs=[rows, rows, cols, cols, VM],
        ),
        out_shape=[
            f32_like(tok, width),
            bf16_like(tok, width),
            bf16_like(heads, tok),
            bf16_like(heads, tok),
            f32_like(1, width),
        ],
        compiler_params=PARAMS,
        cost_estimate=cost(2 * tok * width * weight.shape[0], 20e6),
        name="entry",
    )(place, dn_own, dn_got, h_own, dy_all, gains, weight)


def inputs_kernel(place, dq_ref, dk_ref, dv_ref, w_ref, own_ref, send_ref, d_ref):
    @pl.when(pl.program_id(0) == 0)
    def _():
        nq, nk = dq_ref.shape[0], dk_ref.shape[0]
        d_ref[:, :nq] = dq_ref[...].T
        d_ref[:, nq : nq + nk] = dk_ref[...].T
        d_ref[:, nq + nk :] = dv_ref[...].T

    field = mm(d_ref[...], w_ref[...], ((1,), (1,)))
    tok = own_ref.shape[0]

    @pl.when(place[0] == 0)
    def _():
        own_ref[...] = field[:tok]
        send_ref[...] = field[tok:].astype(jnp.bfloat16)

    @pl.when(place[0] == 1)
    def _():
        own_ref[...] = field[tok:]
        send_ref[...] = field[:tok].astype(jnp.bfloat16)


def inputs_step(place, dq_t, dk_t, dv_t, weight):
    width, cols = weight.shape
    tok = dq_t.shape[1] // 2
    out = pl.BlockSpec((tok, TILE), lambda n: (0, n))
    return pl.pallas_call(
        inputs_kernel,
        grid=(width // TILE,),
        in_specs=[SMEM] + [VM] * 3 + [pl.BlockSpec((TILE, cols), lambda n: (n, 0))],
        out_specs=[out, out, VM],
        out_shape=[f32_like(tok, width), bf16_like(tok, width), bf16_like(2 * tok, cols)],
        compiler_params=PARAMS,
        cost_estimate=cost(4 * tok * width * cols, 14e6),
        name="inputs",
    )(place, dq_t, dk_t, dv_t, weight)


def last_kernel(place, d1_own, d1_got, x_ref, dh_ref, gain, dx_ref, part_ref):
    @pl.when(pl.program_id(0) == 0)
    def _():
        part_ref[...] = jnp.zeros_like(part_ref)

    field = fp32(x_ref[...])
    scale = norm_scale(field)
    hat = field * scale
    grad = d1_own[...] + fp32(d1_got[...])
    part_ref[...] += jnp.sum(grad * hat, axis=0, keepdims=True)
    dx_ref[...] = (dh_ref[...] + rms_back(grad * gain_row(gain, 0), hat, scale)).astype(jnp.bfloat16)


def last_step(place, d1_own, d1_got, x_seq, dh_own, gains):
    tok, width = dh_own.shape
    tile = TILE // 2
    steps = tok // tile
    rows = pl.BlockSpec((tile, width), lambda i, place: (i, 0))
    return pl.pallas_call(
        last_kernel,
        grid_spec=pltpu.PrefetchScalarGridSpec(
            num_scalar_prefetch=1,
            grid=(steps,),
            in_specs=[
                rows,
                rows,
                pl.BlockSpec((tile, width), lambda i, place: (steps * place[0] + i, 0)),
                rows,
                VM,
            ],
            out_specs=[rows, VM],
        ),
        out_shape=[bf16_like(tok, width), f32_like(1, width)],
        compiler_params=PARAMS,
        cost_estimate=cost(0, 14e6),
        name="last",
    )(place, d1_own, d1_got, x_seq, dh_own, gains)


class Group:
    def __init__(self, source, rows, put):
        self.source, self.rows, self.put = source, rows, put
        mid = rows // 2
        self.top, self.low = pl.ds(0, mid), pl.ds(mid, mid)


def add_rows(dst, left, right):
    rows = dst.shape[0]

    @pl.loop(0, rows // 64)
    def _(i):
        at = rows_at(i * 64, 64)
        dst[at] = (fp32(left[at]) + fp32(right[at])).astype(dst.dtype)


ORDER = (
    "gie", "b1u", "s1", "b0u", "end", "b1v", "h1u", "ene", "jod", "gwe", "kee", "sed", "zad",
    "gq", "b1r", "b0v", "joe", "see", "zae", "h1v", "h0u", "s2", "wad", "go", "plu", "b0r",
    "giu", "fid", "enu", "zbd", "ao", "wae", "h1r", "gwu", "kwe", "h0v", "keu", "jou", "plv",
    "giv", "b1q", "h0r", "s3", "env", "fie", "zbe", "b1o", "seu", "b0o", "zau", "plr", "gwv",
    "gir", "kev", "h1o", "h0o", "gwr", "jov", "sev", "zav", "b0q", "enr", "h1q", "dee", "ker",
    "plo", "s4", "gio", "fiu", "fiv", "h0q", "wau", "zbu", "kwr", "kwu", "wav", "zbv", "plq",
    "kwv", "giq", "gwo", "jor", "ser", "gwq", "deu", "keo", "eno", "enq", "keq", "zar", "joo",
    "seo", "s5", "dev", "kwq", "zao", "fir", "war", "joq", "seq", "zaq", "fio", "kwo", "zbr",
    "waq", "fiq", "wao", "zbq", "ded", "der", "zbo", "deq", "deo",
)


def collect_kernel(
    down, down_in, gate, up, xn, d_qkv, attn, da, sums, lse,
    down_o, gate_o, up_o, query_o, key_o, value_o, out_o, sums_o, lse_o,
    send, recv, near, lse_send, lse_recv, lse_near, out_mine, out_got, sums_got,
    out_away, qkv, xn_v, d_qkv_v, attn_v, da_v, *buffers,
):
    at = Spots()
    z, f, g, parity = at.z, at.f, at.g, at.parity
    is_inner = (z == 1) | (z == 2)
    is_outer = (z == 0) | (z == 3)
    toward = (1 + z // 2, f, g)
    outward = (3 * (z // 2), f, g)
    other = (3 - z, f, g)
    chips = 4
    barrier = pltpu.get_barrier_semaphore()
    for partner in (at.x, at.y):
        pl.semaphore_signal(barrier, inc=1, device_id=partner, device_id_type=MESH)
    for level in range(chips):
        for core in range(2):

            @pl.when((z != level) | (g != core))
            def _():
                pl.semaphore_signal(barrier, inc=1, device_id=(level, f, core), device_id_type=MESH)

    pl.semaphore_wait(barrier, 2 * chips + 1)

    taken = [0, 0]

    def between(index, src, dst, device):
        return pltpu.make_async_remote_copy(
            src_ref=src, dst_ref=dst, send_sem=send.at[index], recv_sem=recv.at[index],
            device_id=device, device_id_type=MESH,
        )

    def remote(src, dst, device):
        taken[0] += 1
        return between(taken[0] - 1, src, dst, device)

    def local(src, dst):
        i = taken[1]
        taken[1] += 1
        return pltpu.make_async_copy(src, dst, near.at[i])

    nf = down.shape[0]
    feat = gate.shape[0]
    nq, nk = query_o.shape[1] // 2, key_o.shape[1] // 2
    wide = out_o.shape[1] // 2

    def put_down(done):
        return [(done, down_o.at[rows_at(g * nf, nf)])]

    def put_pair(into, first, count):
        def put(done):
            return [
                (
                    done.at[:, rows_at(k * nf, nf)],
                    into.at[:, rows_at((2 * (first + k) + g) * nf, nf)],
                )
                for k in range(count)
            ]

        return put

    def put_query(done):
        return [(done, query_o.at[:, rows_at(g * nq, nq)])]

    def put_key_value(done):
        return [
            (done.at[:, 0:nk], key_o.at[:, rows_at(g * nk, nk)]),
            (done.at[:, nk : 2 * nk], value_o.at[:, rows_at(g * nk, nk)]),
        ]

    def put_out(done):
        return [(done, out_o.at[:, rows_at(g * wide, wide)])]

    lse_place = lse_o.at[2 * (z // 2) + g]
    for level in range(chips):
        copy = pltpu.make_async_remote_copy(
            src_ref=lse, dst_ref=lse_place, send_sem=lse_send.at[level],
            recv_sem=lse_recv.at[2 * (z // 2) + g],
            device_id=(level, f, parity), device_id_type=MESH,
        )

        @pl.when((z != level) | (g != parity))
        def _():
            copy.start()

    lse_keep = pltpu.make_async_copy(lse, lse_place, lse_near)

    @pl.when(g == parity)
    def _():
        lse_keep.start()

    out_send = remote(out_away, out_got, at.core)
    operands = [local(xn, xn_v), local(d_qkv, d_qkv_v), local(attn, attn_v), local(da, da_v)]
    sums_send = remote(sums, sums_got.at[0], at.core)

    groups = []
    used = 0
    for source, rows, put, ready in (
        (down, nf, put_down, True),
        (gate, feat, put_pair(gate_o, 0, 4), True),
        (up.at[:, 0 : 2 * nf], feat, put_pair(up_o, 0, 2), False),
        (up.at[:, 2 * nf : 4 * nf], feat, put_pair(up_o, 2, 2), False),
        (qkv.at[:, 0:nq], feat, put_query, False),
        (qkv.at[:, nq : nq + 2 * nk], feat, put_key_value, False),
        (out_mine, feat, put_out, False),
    ):
        group = Group(source, rows, put)
        groups.append(group)
        mid = rows // 2
        group.acc, group.outer, group.inner, group.done = buffers[used : used + 4]
        used += 4
        if ready:
            group.load = local(source, group.acc)
            if source is down:
                group.load_in = local(down_in, group.outer)
        else:
            group.mid, group.got, group.late = buffers[used : used + 3]
            used += 3
            group.sends = [
                remote(source.at[rows_at(at.fd * rows, mid)], group.got.at[1], at.x),
                remote(source.at[rows_at(at.fd * rows + mid, mid)], group.got.at[3], at.y),
                remote(source.at[rows_at(at.fx * rows, mid)], group.got.at[0], at.x),
                remote(source.at[rows_at(at.fy * rows + mid, mid)], group.got.at[2], at.y),
            ]
            group.loads = [
                local(source.at[rows_at(at.fy * rows, mid)], group.mid.at[0]),
                local(source.at[rows_at(at.fx * rows + mid, mid)], group.mid.at[1]),
                local(source.at[rows_at(f * rows, rows)], group.acc),
            ]
            group.second = [
                remote(group.mid.at[0], group.late.at[0], at.y),
                remote(group.mid.at[1], group.late.at[1], at.x),
            ]
        i = taken[0]
        taken[0] += 6
        group.first = i

        def inward(part, slot, group=group, i=i):
            return between(i + slot, group.acc.at[part], group.outer.at[part], toward)

        group.inward = inward

        def crossing(keep, give, i=i, group=group):
            return (
                between(i + 2, group.acc.at[give], group.inner, other),
                between(i + 3, group.done.at[keep], group.done.at[keep], other),
                between(i + 4, group.done.at[keep], group.done.at[keep], outward),
                between(i + 5, group.done.at[give], group.done.at[give], outward),
            )

        group.crossing = crossing
        pairs = group.put(group.done)
        group.shares = [remote(src_ref, dst_ref, at.core) for src_ref, dst_ref in pairs]
        group.stores = [local(src_ref, dst_ref) for src_ref, dst_ref in pairs]

    def by_end(group, step):
        @pl.when(z == 0)
        def _():
            step(group.low, group.top)

        @pl.when(z == 3)
        def _():
            step(group.top, group.low)

    def by_side(group, step):
        @pl.when(z == 1)
        def _():
            step(group.top, group.low, group.crossing(group.top, group.low))

        @pl.when(z == 2)
        def _():
            step(group.low, group.top, group.crossing(group.low, group.top))

    def b1(group):
        for copy in group.sends[:2] + group.loads:
            copy.start()

    def b0(group):
        for copy in group.sends[2:]:
            copy.start()

    def h1(group):
        for i, which in ((0, 1), (1, 3)):
            group.sends[i].wait_recv()
            group.loads[i].wait()
            add_rows(group.mid.at[i], group.mid.at[i], group.got.at[which])
            group.second[i].start()

    def h0(group):
        group.loads[2].wait()
        for i, part, which in ((2, group.top, 0), (3, group.low, 2)):
            group.sends[i].wait_recv()
            add_rows(group.acc.at[part], group.acc.at[part], group.got.at[which])

    def pl_(group):
        for i, part in ((0, group.top), (1, group.low)):
            group.second[i].wait_recv()
            add_rows(group.acc.at[part], group.acc.at[part], group.late.at[i])

    def gi(group):
        if group is e:
            e.load.wait()
        by_end(group, lambda give, keep: group.inward(give, 0).start())

    def gw(group):
        by_end(group, lambda give, keep: group.inward(give, 0).wait_send())

    def ke(group):
        by_end(group, lambda give, keep: group.inward(keep, 1).start())

    def kw(group):
        by_end(group, lambda give, keep: group.inward(keep, 1).wait_send())

    def en(group):
        if group is d:
            d.load.wait()
            d.load_in.wait()

        def step(keep, give, copies):
            if group is not d:
                group.inward(give, 0).wait_recv()
            add_rows(group.acc.at[give], group.acc.at[give], group.outer.at[give])
            copies[0].start()

        by_side(group, step)

    def jo(group):
        def step(keep, give, copies):
            if group is not d:
                group.inward(keep, 1).wait_recv()
            add_rows(group.acc.at[keep], group.acc.at[keep], group.outer.at[keep])

        by_side(group, step)

    def se(group):
        def step(keep, give, copies):
            copies[0].wait_recv()
            add_rows(group.done.at[keep], group.acc.at[keep], group.inner)
            copies[1].start()

        by_side(group, step)

    def za(group):
        by_side(group, lambda keep, give, copies: copies[2].start())

    def fi(group):
        by_side(group, lambda keep, give, copies: copies[1].wait_recv())

    def wa(group):
        by_side(group, lambda keep, give, copies: copies[2].wait_send())

    def zb(group):
        by_side(group, lambda keep, give, copies: copies[3].start())

    def de(group):
        def end(give, keep):
            copies = group.crossing(keep, give)
            copies[2].wait_recv()
            copies[3].wait_recv()

        by_end(group, end)

        def step(keep, give, copies):
            for i in (0, 1, 3):
                copies[i].wait_send()

        by_side(group, step)
        for copy in group.shares + group.stores:
            copy.start()

    d, e, u, v, q, r, o = groups
    for copy in [e.load, d.load, d.load_in, sums_send] + operands:
        copy.start()
    steps = {
        "b1": b1, "b0": b0, "h1": h1, "h0": h0, "pl": pl_, "gi": gi, "gw": gw, "ke": ke, "kw": kw,
        "en": en, "jo": jo, "se": se, "za": za, "fi": fi, "wa": wa, "zb": zb, "de": de,
    }
    named = {"d": d, "e": e, "u": u, "v": v, "q": q, "r": r, "o": o}

    over_x = remote(sums_o, sums_got.at[1], at.x)
    over_y = remote(sums_o, sums_got.at[2], at.y)
    sums_in = remote(sums_o, sums_got.at[3], toward)
    sums_mid = remote(sums_o, sums_got.at[4], other)
    sums_out = remote(sums_o, sums_got.at[5], outward)

    def sums_1():
        sums_send.wait_recv()
        sums_o[...] = sums[...] + sums_got[0]
        over_x.start()

    def sums_2():
        over_x.wait()
        sums_o[...] += sums_got[1]
        over_y.start()

    def sums_3():
        over_y.wait()
        sums_o[...] += sums_got[2]

        @pl.when(is_outer)
        def _():
            sums_in.start()

    def sums_4():
        @pl.when(is_inner)
        def _():
            sums_in.wait_recv()
            sums_o[...] += sums_got[3]
            sums_mid.start()

    def sums_5():
        @pl.when(is_inner)
        def _():
            sums_mid.wait()
            sums_o[...] += sums_got[4]
            sums_out.start()

    def out_gradient():
        for copy in operands[2:]:
            copy.wait()
        tile = wide // 2
        for ref, core in ((out_away, 1 - g), (out_mine, g)):


            @pl.loop(0, 2)
            def _(n):
                cols = rows_at(core * wide + n * tile, tile)
                ref[:, rows_at(n * tile, tile)] = mm(attn_v[...], da_v[:, cols]).astype(ref.dtype)

            if ref is out_away:
                out_send.start()

    def qkv_gradient():
        for copy in operands[:2]:
            copy.wait()
        tile = 2 * TILE

        @pl.loop(0, qkv.shape[1] // tile)
        def _(n):
            cols = rows_at(n * tile, tile)
            qkv[:, cols] = mm(xn_v[...], d_qkv_v[:, cols], ((0,), (0,))).astype(qkv.dtype)

    def out_sum():
        out_send.wait_recv()
        add_rows(out_mine, out_mine, out_got)

    single = {
        "s1": sums_1, "s2": sums_2, "s3": sums_3, "s4": sums_4, "s5": sums_5,
        "go": out_gradient, "gq": qkv_gradient, "ao": out_sum,
    }
    for name in ORDER:
        if len(name) == 2:
            single[name]()
        else:
            steps[name[:2]](named[name[2]])

    @pl.when(is_outer)
    def _():
        sums_in.wait_send()
        sums_out.wait_recv()
        sums_o[...] = sums_got[5]

    @pl.when(is_inner)
    def _():
        sums_out.wait_send()

    sums_send.wait_send()
    out_send.wait_send()
    for group in (u, v, q, r, o):
        for copy in group.sends + group.second:
            copy.wait_send()
    for group in groups:
        for copy in group.stores:
            copy.wait()
        for copy in group.shares:
            copy.wait_send()
            copy.wait_recv()
    for level in range(chips):
        copy = pltpu.make_async_remote_copy(
            src_ref=lse, dst_ref=lse_place, send_sem=lse_send.at[level], recv_sem=lse_recv.at[level],
            device_id=(level, f, parity), device_id_type=MESH,
        )

        @pl.when((z != level) | (g != parity))
        def _():
            copy.wait_send()

        @pl.when((z != 2 * (level // 2) + g) | (g != level % 2))
        def _():
            copy.wait_recv()

    @pl.when(g == parity)
    def _():
        lse_keep.wait()


def collect(down, down_in, gate, up, xn, d_qkv, attn, da, sums, lse, nq, nk):
    bf = jnp.bfloat16
    buffers = []
    wide = da.shape[1] // 2
    feat = gate.shape[0]
    for rows, cols, ready in (
        (down.shape[0], down.shape[1], True),
        (gate.shape[0], gate.shape[1], True),
        (feat, up.shape[1] // 2, False),
        (feat, up.shape[1] // 2, False),
        (feat, nq, False),
        (feat, 2 * nk, False),
        (attn.shape[0] // 4, wide, False),
    ):
        mid = rows // 2
        buffers += [
            pltpu.VMEM((rows, cols), bf),
            pltpu.VMEM((rows, cols), bf),
            pltpu.VMEM((mid, cols), bf),
            pltpu.VMEM((rows, cols), bf),
        ]
        if not ready:
            buffers += [
                pltpu.VMEM((2, mid, cols), bf),
                pltpu.VMEM((4, mid, cols), bf),
                pltpu.VMEM((2, mid, cols), bf),
            ]
    return pl.pallas_call(
        collect_kernel,
        in_specs=[ANY] * 8 + [VM, VM],
        out_specs=[ANY] * 7 + [VM, VM],
        out_shape=[
            bf16_like(2 * down.shape[0], down.shape[1]),
            bf16_like(feat, 2 * gate.shape[1]),
            bf16_like(feat, 2 * up.shape[1]),
            bf16_like(feat, 2 * nq),
            bf16_like(feat, 2 * nk),
            bf16_like(feat, 2 * nk),
            bf16_like(feat, da.shape[1]),
            f32_like(*sums.shape),
            f32_like(4, *lse.shape),
        ],
        scratch_shapes=[
            pltpu.SemaphoreType.DMA((96,)),
            pltpu.SemaphoreType.DMA((96,)),
            pltpu.SemaphoreType.DMA((48,)),
            pltpu.SemaphoreType.DMA((4,)),
            pltpu.SemaphoreType.DMA((4,)),
            pltpu.SemaphoreType.DMA,
            pltpu.VMEM((attn.shape[0], wide), bf),
            pltpu.VMEM((attn.shape[0], wide), bf),
            pltpu.VMEM((6,) + sums.shape, jnp.float32),
            pltpu.VMEM((attn.shape[0], wide), bf),
            pltpu.VMEM((xn.shape[1], d_qkv.shape[1]), bf),
            pltpu.VMEM(xn.shape, bf),
            pltpu.VMEM(d_qkv.shape, bf),
            pltpu.VMEM(attn.shape, bf),
            pltpu.VMEM(da.shape, bf),
        ]
        + buffers,
        compiler_params=pltpu.CompilerParams(
            collective_id=1, has_side_effects=True, vmem_limit_bytes=62 * 1024 * 1024
        ),
        cost_estimate=cost(0, 500e6),
        name="collect",
    )(down, down_in, gate, up, xn, d_qkv, attn, da, sums, lse)


def widen_kernel(spot, dealing, lse, sums, *refs):
    totals, first, second = refs[-3:]
    half = (len(refs) - 3) // 2
    for narrow, wide in zip(refs[:half], refs[half:-3]):
        wide[...] = fp32(narrow[...])

    @pl.when(pl.program_id(0) == 0)
    def _():
        shard = rows_at(spot[1] * first.shape[0], first.shape[0])
        first[...] = sums[0, shard]
        second[...] = sums[1, shard]
        heads = lse.shape[1]
        for r in range(4):
            for i in range(4):

                @pl.when(dealing[r, i] == spot[0])
                def _():
                    col = (4 * r + i) % 8 * BLK
                    for core in range(2):
                        totals[core * heads : (core + 1) * heads, r * BLK : (r + 1) * BLK] = lse[
                            2 * (r // 2) + core, :, col : col + BLK
                        ]


def widen(spot, dealing, lse, sums, arrays, steps=8):
    specs = [pl.BlockSpec((a.shape[0] // steps, a.shape[1]), lambda n: (n, 0)) for a in arrays]
    shard = sums.shape[1] // 4
    return pl.pallas_call(
        widen_kernel,
        grid=(steps,),
        in_specs=[SMEM, SMEM, VM, VM] + specs,
        out_specs=specs + [VM] * 3,
        out_shape=[f32_like(*a.shape) for a in arrays]
        + [f32_like(2 * lse.shape[1], 4 * BLK), f32_like(shard), f32_like(shard)],
        compiler_params=PARAMS,
        cost_estimate=cost(0, 40e6),
        name="widen",
    )(spot, dealing, lse, sums, *arrays)


def turning_tables(seq):
    half = HEAD_SIZE // 2
    frequency = ROPE_BASE ** (-2.0 * np.arange(half) / (2 * half))
    low = frequency[:, None] * np.arange(BLK)[None, :]
    high = frequency[:, None] * (BLK * np.arange(seq // BLK))[None, :]
    return tuple(part.astype(np.float32) for part in (np.cos(low), np.sin(low), np.cos(high), np.sin(high)))


def chip_local(
    tokens,
    seq_lengths,
    dealing,
    first_gain,
    query_weight,
    key_matrix,
    value_matrix,
    out_weight,
    second_gain,
    gate_weight,
    up_weight,
    down_weight,
    cotangent,
):
    ctx = lax.axis_size("ctx")
    z = lax.axis_index("ctx")
    f = lax.axis_index("fsdp")
    g = lax.axis_index("grp")
    parity = z % 2
    parity_core = g == parity
    width = tokens.shape[2]
    tok = tokens.shape[1]
    seq = 2 * tok
    place = jnp.stack([g, parity]).astype(jnp.int32)

    def over_x(field):
        return lax.ppermute(field, "fsdp", [(i, i ^ 1) for i in range(4)])

    def over_y(field):
        return lax.ppermute(field, "fsdp", [(i, i ^ 2) for i in range(4)])

    def over_core(field):
        return lax.ppermute(field, "grp", [(0, 1), (1, 0)])

    swap_pairs = [(2 * i + (1 - i % 2), 2 * (i ^ 1) + i % 2) for i in range(ctx)]

    def swap(field):
        got = lax.ppermute(field, ("ctx", "grp"), swap_pairs)
        return jnp.where(parity_core, field, got)

    def along(field, pairs):
        return lax.ppermute(field, "ctx", pairs)

    def cut(field, start, size, axis):
        return lax.dynamic_slice_in_dim(field, start, size, axis)

    def in_order(mine, other, axis=0):
        first = jnp.where(g == 0, mine, other)
        second = jnp.where(g == 0, other, mine)
        return jnp.concatenate([first, second], axis=axis)

    heads_q = query_weight.shape[1] // 2
    heads_k = key_matrix.shape[1] // 2
    part_ff = down_weight.shape[0] // 2
    rows_in = gate_weight.shape[0]

    row = lax.broadcasted_iota(jnp.int32, (1, 8, first_gain.shape[0]), 1)
    gain_own = jnp.where(row == 0, fp32(first_gain), jnp.where(row == 1, fp32(second_gain), 0.0))
    qkv_w, out_w, pair_w, down_own, x_seq, dy_all, gain_all, xn_one, qkv_t = gather_all(
        tokens, cotangent, query_weight, key_matrix, value_matrix, out_weight,
        gate_weight, up_weight, down_weight, gain_own,
    )
    down_w = lax.all_gather(down_own, "fsdp", axis=0, tiled=True)

    tables = turning_tables(seq)

    attn_keep, attn_send, lse, q_t, k_t, v_t = attend_seq(place, qkv_t, tables)
    attn_got = over_core(attn_send)
    h_own, xn_own, attn_mine = residual(place, x_seq, attn_keep, attn_got, gain_all, out_w)
    hidden, for_gate, act, xn_two = hidden_step(place, xn_own, over_core(xn_own), pair_w)
    d_gate, d_up = hidden_back(dy_all, down_w, for_gate, act)
    bf = jnp.bfloat16
    tokens_in = ((0,), (0,))
    down_grad = mm(hidden, dy_all, tokens_in, bf)
    gate_grad = mm(xn_two, d_gate, tokens_in, bf)
    down_plane = lax.psum_scatter(down_grad, "fsdp", scatter_dimension=0, tiled=True)
    down_in = along(down_plane, [(0, 1), (3, 2)])
    gate_plane = lax.psum_scatter(gate_grad, "fsdp", scatter_dimension=0, tiled=True)
    d_gate, d_up, hidden, _, _ = lax.optimization_barrier((d_gate, d_up, hidden, down_grad, gate_grad))
    dn_own, dn_send = back_step(place, d_gate, d_up, pair_w)
    dn_got = over_core(dn_send)
    res_own, res_send = result_step(place, hidden, h_own, down_w)
    up_grad = mm(xn_two, d_up, tokens_in, bf)
    layer_out = swap((res_own + fp32(over_core(res_send))).astype(bf))

    dh_own, da, dattn_keep, dattn_send, gain_two_part = entry_step(
        place, dn_own, dn_got, h_own, dy_all, gain_all, out_w
    )
    dattn_got = over_core(dattn_send)
    q_t, _ = lax.optimization_barrier((q_t, down_plane))
    dq_t, dk_t, dv_t = attend_seq_back(
        place, q_t, k_t, v_t, dattn_keep, dattn_got, lse, tables
    )
    half_width = width // 2
    d1_own, d1_send, d_qkv = inputs_step(place, dq_t, dk_t, dv_t, qkv_w)
    dh_own, down_in = lax.optimization_barrier((dh_own, down_in))
    dx, gain_one_part = last_step(place, d1_own, over_core(d1_send), x_seq, dh_own, gain_all)
    tokens_grad = swap(dx)

    parts = jnp.concatenate([gain_one_part, gain_two_part])
    down_sum, gate_sum, up_sum, query_sum, key_sum, value_sum, out_sum, sums, all_lse = collect(
        down_plane, down_in, gate_plane, up_grad, xn_one, d_qkv, attn_mine, da,
        jnp.pad(parts, ((0, 6), (0, 0))), lse.reshape(-1, seq), heads_q, heads_k,
    )
    query_out, key_out, value_out, out_out, gate_out, up_out, down_out, totals, gain_one, gain_two = widen(
        jnp.stack([z, f]).astype(jnp.int32), dealing[0], all_lse, sums,
        (query_sum, key_sum, value_sum, out_sum, gate_sum, up_sum, down_sum),
    )

    return (
        layer_out[None],
        tokens_grad[None],
        totals[None],
        gain_one,
        query_out,
        key_out,
        value_out,
        out_out,
        gain_two,
        gate_out,
        up_out,
        down_out,
    )


def chip_holds_sequence(mesh, tokens, seq_lengths):
    sizes = dict(mesh.shape)
    packs, length, _ = tokens.shape
    count = seq_lengths.shape[1]
    return (
        sizes["fsdp"] == 4
        and sizes["grp"] == 2
        and sizes["ctx"] == 4
        and packs == sizes["fsdp"] * sizes["grp"]
        and length == count * MINLEN
        and 2 * length == sizes["ctx"] * MINLEN
    )


def solution(mesh):
    placed = (
        P(("fsdp", "grp"), "ctx", None),
        P(("fsdp", "grp"), None),
        P(("fsdp", "grp"), None, None),
        P("fsdp"),
        P("fsdp", None),
        P("fsdp", None),
        P("fsdp", None),
        P("fsdp", None),
        P("fsdp"),
        P("fsdp", None),
        P("fsdp", None),
        P("fsdp", None),
        P(("fsdp", "grp"), "ctx", None),
    )
    results = (
        P(("fsdp", "grp"), "ctx", None),
        P(("fsdp", "grp"), "ctx", None),
        P(("fsdp", "grp"), None, "ctx"),
        P("fsdp"),
        P("fsdp", None),
        P("fsdp", None),
        P("fsdp", None),
        P("fsdp", None),
        P("fsdp"),
        P("fsdp", None),
        P("fsdp", None),
        P("fsdp", None),
    )

    def program(*arrays):
        body = chip_local if chip_holds_sequence(mesh, arrays[0], arrays[1]) else local
        return jax.shard_map(
            body, mesh=mesh, in_specs=placed, out_specs=results, check_vma=False
        )(*arrays)

    return program
```

```python
import jax
import jax.numpy as jnp
import numpy as np
from jax import lax
from jax.experimental import pallas as pl
from jax.experimental.pallas import tpu as pltpu
from jax.sharding import PartitionSpec as P

QUERY_HEADS = 16
KEY_VALUE_HEADS = 8
HEAD_SIZE = 96
BLK = 128


EPS = 1e-05
ROPE_BASE = 100000.0
MASKED = -1e30


def place_rows(positions, lengths):
    ends = jnp.cumsum(lengths, axis=-1)
    before = positions[..., :, None] >= ends[..., None, :]
    segment = jnp.sum(before.astype(jnp.int32), axis=-1)
    offset = jnp.sum(jnp.where(before, lengths[..., None, :], 0), axis=-1)
    return (segment, positions - offset)


def rotation(relative, half_size):
    frequency = ROPE_BASE ** (-(2.0 * jnp.arange(half_size, dtype=jnp.float32)) / (2 * half_size))
    angles = relative.astype(jnp.float32)[:, None] * frequency[None, :]
    return (jnp.cos(angles), jnp.sin(angles))


def rotate(field, cosine, sine_part):
    row_count = field.shape[0]
    half_size = cosine.shape[-1]
    split_heads = field.reshape(row_count, -1, 2 * half_size)
    front_half = split_heads[..., :half_size]
    back_half = split_heads[..., half_size:]
    cos_rows = cosine[:, None, :]
    sin_rows = sine_part[:, None, :]
    turned = jnp.concatenate(
        [
            front_half * cos_rows - back_half * sin_rows,
            back_half * cos_rows + front_half * sin_rows,
        ],
        axis=-1,
    )
    return turned.reshape(row_count, -1)


def rms_back(d_normed, normed, scale):
    return scale * (d_normed - normed * jnp.mean(d_normed * normed, axis=-1, keepdims=True))


def score_block(query_part, key_part, visible):
    scores = jnp.einsum(
        "rgd,kd->grk", query_part, key_part, preferred_element_type=jnp.float32
    ) * HEAD_SIZE ** (-0.5)
    return jnp.where(visible[None], scores, MASKED)


def attend_pack(query_pack, key_pack, value_pack, visible_list):
    token_count = query_pack.shape[0]
    rounds = len(visible_list)
    query_group_width = QUERY_HEADS // KEY_VALUE_HEADS
    context_count = key_pack.shape[0] // token_count

    def width_per_head(head_index, carry):
        out_buf, total_buf = carry
        query_head = lax.dynamic_slice_in_dim(
            query_pack, head_index * query_group_width * HEAD_SIZE, query_group_width * HEAD_SIZE, 1
        ).reshape(token_count, query_group_width, HEAD_SIZE)
        key_head = lax.dynamic_slice_in_dim(key_pack, head_index * HEAD_SIZE, HEAD_SIZE, 1).reshape(
            context_count, rounds, BLK, HEAD_SIZE
        )
        value_head = lax.dynamic_slice_in_dim(
            value_pack, head_index * HEAD_SIZE, HEAD_SIZE, 1
        ).reshape(context_count, rounds, BLK, HEAD_SIZE)
        running_top = jnp.full((query_group_width, token_count), MASKED, jnp.float32)
        running_sum = jnp.zeros((query_group_width, token_count), jnp.float32)
        for round_index in range(rounds):
            first_row = round_index * BLK
            scores = score_block(
                query_head[first_row:],
                key_head[:, round_index].reshape(-1, HEAD_SIZE),
                visible_list[round_index],
            )
            new_top = jnp.maximum(running_top[:, first_row:], jnp.max(scores, axis=-1))
            weights = jnp.where(
                visible_list[round_index][None], jnp.exp(scores - new_top[..., None]), 0.0
            )
            new_sum = running_sum[:, first_row:] * jnp.exp(
                running_top[:, first_row:] - new_top
            ) + jnp.sum(weights, axis=-1)
            running_top = running_top.at[:, first_row:].set(new_top)
            running_sum = running_sum.at[:, first_row:].set(new_sum)
        log_totals = running_top + jnp.log(running_sum)
        mixture = jnp.zeros((token_count, query_group_width, HEAD_SIZE), jnp.float32)
        for round_index in range(rounds):
            first_row = round_index * BLK
            scores = score_block(
                query_head[first_row:],
                key_head[:, round_index].reshape(-1, HEAD_SIZE),
                visible_list[round_index],
            )
            prob_bf = jnp.where(
                visible_list[round_index][None],
                jnp.exp(scores - log_totals[:, first_row:, None]),
                0.0,
            ).astype(jnp.bfloat16)
            mixture = mixture.at[first_row:].add(
                jnp.einsum(
                    "grk,kd->rgd",
                    prob_bf,
                    value_head[:, round_index].reshape(-1, HEAD_SIZE),
                    preferred_element_type=jnp.float32,
                )
            )
        out_buf = lax.dynamic_update_slice_in_dim(
            out_buf,
            mixture.astype(jnp.bfloat16).reshape(token_count, -1),
            head_index * query_group_width * HEAD_SIZE,
            1,
        )
        total_buf = lax.dynamic_update_slice_in_dim(
            total_buf, log_totals, head_index * query_group_width, 0
        )
        return (out_buf, total_buf)

    start_offsets = (
        jnp.zeros((token_count, QUERY_HEADS * HEAD_SIZE), jnp.bfloat16),
        jnp.zeros((QUERY_HEADS, token_count), jnp.float32),
    )
    return lax.fori_loop(0, KEY_VALUE_HEADS, width_per_head, start_offsets)


def attend_back(
    query_pack, key_pack, value_pack, grad_pack, attended_pack, total_pack, visible_list
):
    token_count = query_pack.shape[0]
    rounds = len(visible_list)
    query_group_width = QUERY_HEADS // KEY_VALUE_HEADS
    context_count = key_pack.shape[0] // token_count

    def width_per_head(head_index, carry):
        query_buf, key_buf, value_buf = carry
        query_head = lax.dynamic_slice_in_dim(
            query_pack, head_index * query_group_width * HEAD_SIZE, query_group_width * HEAD_SIZE, 1
        ).reshape(token_count, query_group_width, HEAD_SIZE)
        grad_head = lax.dynamic_slice_in_dim(
            grad_pack, head_index * query_group_width * HEAD_SIZE, query_group_width * HEAD_SIZE, 1
        ).reshape(token_count, query_group_width, HEAD_SIZE)
        output_head = lax.dynamic_slice_in_dim(
            attended_pack,
            head_index * query_group_width * HEAD_SIZE,
            query_group_width * HEAD_SIZE,
            1,
        ).reshape(token_count, query_group_width, HEAD_SIZE)
        key_head = lax.dynamic_slice_in_dim(key_pack, head_index * HEAD_SIZE, HEAD_SIZE, 1).reshape(
            context_count, rounds, BLK, HEAD_SIZE
        )
        value_head = lax.dynamic_slice_in_dim(
            value_pack, head_index * HEAD_SIZE, HEAD_SIZE, 1
        ).reshape(context_count, rounds, BLK, HEAD_SIZE)
        log_totals = lax.dynamic_slice_in_dim(
            total_pack, head_index * query_group_width, query_group_width, 0
        )
        delta = jnp.sum(grad_head.astype(jnp.float32) * output_head.astype(jnp.float32), axis=-1).T
        query_grad = jnp.zeros((token_count, query_group_width, HEAD_SIZE), jnp.float32)
        key_parts = []
        value_parts = []
        for round_index in range(rounds):
            first_row = round_index * BLK
            key_round = key_head[:, round_index].reshape(-1, HEAD_SIZE)
            value_round = value_head[:, round_index].reshape(-1, HEAD_SIZE)
            scores = score_block(query_head[first_row:], key_round, visible_list[round_index])
            probs_full = jnp.where(
                visible_list[round_index][None],
                jnp.exp(scores - log_totals[:, first_row:, None]),
                0.0,
            )
            d_probs = jnp.einsum(
                "rgd,kd->grk",
                grad_head[first_row:],
                value_round,
                preferred_element_type=jnp.float32,
            )
            d_scores = (
                HEAD_SIZE ** (-0.5) * probs_full * (d_probs - delta[:, first_row:, None])
            ).astype(jnp.bfloat16)
            value_parts.append(
                jnp.einsum(
                    "grk,rgd->kd",
                    probs_full.astype(jnp.bfloat16),
                    grad_head[first_row:],
                    preferred_element_type=jnp.float32,
                )
            )
            key_parts.append(
                jnp.einsum(
                    "grk,rgd->kd",
                    d_scores,
                    query_head[first_row:],
                    preferred_element_type=jnp.float32,
                )
            )
            query_grad = query_grad.at[first_row:].add(
                jnp.einsum("grk,kd->rgd", d_scores, key_round, preferred_element_type=jnp.float32)
            )
        key_block = jnp.stack(
            [part.reshape(context_count, BLK, HEAD_SIZE) for part in key_parts], axis=1
        ).reshape(-1, HEAD_SIZE)
        value_block = jnp.stack(
            [part.reshape(context_count, BLK, HEAD_SIZE) for part in value_parts], axis=1
        ).reshape(-1, HEAD_SIZE)
        query_buf = lax.dynamic_update_slice_in_dim(
            query_buf,
            query_grad.reshape(token_count, -1),
            head_index * query_group_width * HEAD_SIZE,
            1,
        )
        key_buf = lax.dynamic_update_slice_in_dim(key_buf, key_block, head_index * HEAD_SIZE, 1)
        value_buf = lax.dynamic_update_slice_in_dim(
            value_buf, value_block, head_index * HEAD_SIZE, 1
        )
        return (query_buf, key_buf, value_buf)

    start_offsets = (
        jnp.zeros((token_count, QUERY_HEADS * HEAD_SIZE), jnp.float32),
        jnp.zeros((context_count * token_count, KEY_VALUE_HEADS * HEAD_SIZE), jnp.float32),
        jnp.zeros((context_count * token_count, KEY_VALUE_HEADS * HEAD_SIZE), jnp.float32),
    )
    return lax.fori_loop(0, KEY_VALUE_HEADS, width_per_head, start_offsets)


def local(
    tokens,
    seq_lengths,
    dealing,
    first_gain,
    query_weight,
    key_matrix,
    value_matrix,
    out_weight,
    second_gain,
    gate_weight,
    up_weight,
    down_weight,
    cotangent,
):
    context_count = lax.axis_size("ctx")
    my_index = lax.axis_index("ctx")
    pack_count, token_count, model_dim = tokens.shape
    rounds = token_count // BLK
    spread = context_count // rounds
    ctx_range = jnp.arange(context_count, dtype=jnp.int32)
    matches = (dealing[..., None] == ctx_range).astype(jnp.int32)
    slot_of = jnp.sum(matches * ctx_range[:, None], axis=2)
    block_of = jnp.arange(rounds, dtype=jnp.int32)[None, :, None] * context_count + slot_of
    key_pos = (
        jnp.transpose(block_of, (0, 2, 1))[..., None] * BLK + jnp.arange(BLK, dtype=jnp.int32)
    ).reshape(pack_count, -1)
    key_seg = place_rows(key_pos, seq_lengths)[0]
    query_pos = lax.dynamic_slice_in_dim(key_pos, my_index * token_count, token_count, 1)
    query_seg, query_rel = place_rows(query_pos, seq_lengths)
    home_row = lax.dynamic_index_in_dim(dealing, my_index // spread, 1, False)
    targets = lax.dynamic_slice_in_dim(home_row, my_index % spread * rounds, rounds, 1)
    picker = (targets[:, None, :] == ctx_range[None, :, None]).astype(jnp.bfloat16)
    my_slots = lax.dynamic_index_in_dim(slot_of, my_index, 2, False)
    owner_index = (
        jnp.arange(rounds, dtype=jnp.int32)[None, :] * context_count + my_slots
    ) // rounds
    keep_slot = jnp.repeat(owner_index, spread, axis=1) == ctx_range[None, :]

    def spread_out(field):
        blocks = field.reshape(pack_count, rounds, BLK, model_dim)
        return jnp.einsum(
            "pkj,pjtd->pktd", picker, blocks, preferred_element_type=jnp.float32
        ).astype(jnp.bfloat16)

    def collect(received):
        grouped = received.reshape(pack_count, rounds, spread, BLK, model_dim)
        return (
            jnp.sum(grouped, axis=2, dtype=jnp.float32)
            .astype(jnp.bfloat16)
            .reshape(pack_count * token_count, model_dim)
        )

    def send_home(field):
        blocks = jnp.repeat(field.reshape(pack_count, rounds, BLK, model_dim), spread, axis=1)
        return jnp.where(keep_slot[:, :, None, None], blocks, jnp.zeros_like(blocks))

    def restore(returned):
        placed = jnp.einsum("pkj,pktd->pjtd", picker, returned, preferred_element_type=jnp.float32)
        return placed.astype(jnp.bfloat16).reshape(pack_count, token_count, model_dim)

    dealt_tokens, dealt_upstream = (
        lax.all_to_all(spread_out(tokens), "ctx", split_axis=1, concat_axis=1, tiled=True),
        lax.all_to_all(spread_out(cotangent), "ctx", split_axis=1, concat_axis=1, tiled=True),
    )
    inputs = collect(dealt_tokens)
    upstream = collect(dealt_upstream)
    gain_one, query_full, key_full, value_full, out_full = (
        lax.all_gather(first_gain, "fsdp", axis=0, tiled=True),
        lax.all_gather(query_weight, "fsdp", axis=0, tiled=True),
        lax.all_gather(key_matrix, "fsdp", axis=0, tiled=True),
        lax.all_gather(value_matrix, "fsdp", axis=0, tiled=True),
        lax.all_gather(out_weight, "fsdp", axis=0, tiled=True),
    )
    gain_two, gate_full, up_full, down_full = (
        lax.all_gather(second_gain, "fsdp", axis=0, tiled=True),
        lax.all_gather(gate_weight, "fsdp", axis=0, tiled=True),
        lax.all_gather(up_weight, "fsdp", axis=0, tiled=True),
        lax.all_gather(down_weight, "fsdp", axis=0, tiled=True),
    )
    gain_one32 = gain_one.astype(jnp.float32)
    gain_two32 = gain_two.astype(jnp.float32)
    cosine, sine_part = rotation(query_rel.reshape(-1), HEAD_SIZE // 2)
    inputs32 = inputs.astype(jnp.float32)
    scale_one = lax.rsqrt(jnp.mean(inputs32 * inputs32, axis=-1, keepdims=True) + EPS)
    normed_one = inputs32 * scale_one
    xn_one = (normed_one * gain_one32).astype(jnp.bfloat16)
    query_rot = rotate(
        jnp.dot(xn_one, query_full, preferred_element_type=jnp.float32), cosine, sine_part
    ).astype(jnp.bfloat16)
    key_rot = rotate(
        jnp.dot(xn_one, key_full, preferred_element_type=jnp.float32), cosine, sine_part
    ).astype(jnp.bfloat16)
    rows_of_values = jnp.dot(xn_one, value_full, preferred_element_type=jnp.float32).astype(
        jnp.bfloat16
    )
    key_local = key_rot.reshape(pack_count, token_count, -1)
    value_local = rows_of_values.reshape(pack_count, token_count, -1)
    gathered_keys, gathered_values = (
        lax.all_gather(key_local, "ctx", axis=1, tiled=True),
        lax.all_gather(value_local, "ctx", axis=1, tiled=True),
    )
    key_pos_rounds = key_pos.reshape(pack_count, context_count, rounds, BLK)
    key_seg_rounds = key_seg.reshape(pack_count, context_count, rounds, BLK)
    visible = []
    for round_index in range(rounds):
        first_row = round_index * BLK
        round_pos = key_pos_rounds[:, :, round_index].reshape(pack_count, -1)
        round_seg = key_seg_rounds[:, :, round_index].reshape(pack_count, -1)
        same_seq = query_seg[:, first_row:, None] == round_seg[:, None, :]
        earlier = round_pos[:, None, :] <= query_pos[:, first_row:, None]
        visible.append(same_seq & earlier)
    query_packs = query_rot.reshape(pack_count, token_count, -1)
    pack_index = 0
    pack_visible = [mask[pack_index] for mask in visible]
    attended_pack, total_pack = attend_pack(
        query_packs[pack_index],
        gathered_keys[pack_index],
        gathered_values[pack_index],
        pack_visible,
    )
    total_list = [total_pack]
    softmax_totals = jnp.stack(total_list, axis=0)
    hidden_in = inputs32 + jnp.dot(attended_pack, out_full, preferred_element_type=jnp.float32)
    scale_two = lax.rsqrt(jnp.mean(hidden_in * hidden_in, axis=-1, keepdims=True) + EPS)
    normed_two = hidden_in * scale_two
    xn_two = (normed_two * gain_two32).astype(jnp.bfloat16)
    gate_val = jnp.dot(xn_two, gate_full, preferred_element_type=jnp.float32)
    up_val = jnp.dot(xn_two, up_full, preferred_element_type=jnp.float32)
    activated = jax.nn.silu(gate_val)
    hidden = (activated * up_val).astype(jnp.bfloat16)
    result = (hidden_in + jnp.dot(hidden, down_full, preferred_element_type=jnp.float32)).astype(
        jnp.bfloat16
    )
    down_grad = jnp.dot(hidden.T, upstream, preferred_element_type=jnp.float32)
    d_hidden = jnp.dot(upstream, down_full.T, preferred_element_type=jnp.float32)
    sigmoid_gate = jax.nn.sigmoid(gate_val)
    d_gate = (d_hidden * up_val * sigmoid_gate * (1.0 + gate_val * (1.0 - sigmoid_gate))).astype(
        jnp.bfloat16
    )
    d_up = (d_hidden * activated).astype(jnp.bfloat16)
    gate_grad = jnp.dot(xn_two.T, d_gate, preferred_element_type=jnp.float32)
    up_grad = jnp.dot(xn_two.T, d_up, preferred_element_type=jnp.float32)
    d_norm_two = jnp.dot(d_gate, gate_full.T, preferred_element_type=jnp.float32) + jnp.dot(
        d_up, up_full.T, preferred_element_type=jnp.float32
    )
    gain_two_grad = jnp.sum(d_norm_two * normed_two, axis=0)
    d_hidden_in = upstream.astype(jnp.float32) + rms_back(
        d_norm_two * gain_two32, normed_two, scale_two
    )
    mlp_parts = (
        lax.psum_scatter(
            gain_two_grad.astype(jnp.bfloat16), "fsdp", scatter_dimension=0, tiled=True
        ).astype(jnp.float32),
        lax.psum_scatter(
            gate_grad.astype(jnp.bfloat16), "fsdp", scatter_dimension=0, tiled=True
        ).astype(jnp.float32),
        lax.psum_scatter(
            up_grad.astype(jnp.bfloat16), "fsdp", scatter_dimension=0, tiled=True
        ).astype(jnp.float32),
        lax.psum_scatter(
            down_grad.astype(jnp.bfloat16), "fsdp", scatter_dimension=0, tiled=True
        ).astype(jnp.float32),
    )
    d_branch = d_hidden_in.astype(jnp.bfloat16)
    out_grad = jnp.dot(attended_pack.T, d_branch, preferred_element_type=jnp.float32)
    d_attended = jnp.dot(d_branch, out_full.T, preferred_element_type=jnp.float32).astype(
        jnp.bfloat16
    )
    back_keys, back_values = (gathered_keys, gathered_values)
    grad_packs = d_attended.reshape(pack_count, token_count, -1)
    out_packs = attended_pack.reshape(pack_count, token_count, -1)
    pack_index = 0
    pack_visible = [mask[pack_index] for mask in visible]
    query_part, key_part, value_part = attend_back(
        query_packs[pack_index],
        back_keys[pack_index],
        back_values[pack_index],
        grad_packs[pack_index],
        out_packs[pack_index],
        softmax_totals[pack_index],
        pack_visible,
    )
    key_list = [key_part]
    value_list = [value_part]
    d_keys, d_values = (
        lax.psum_scatter(
            jnp.stack(key_list, axis=0).astype(jnp.bfloat16), "ctx", scatter_dimension=1, tiled=True
        ).astype(jnp.float32),
        lax.psum_scatter(
            jnp.stack(value_list, axis=0).astype(jnp.bfloat16),
            "ctx",
            scatter_dimension=1,
            tiled=True,
        ).astype(jnp.float32),
    )
    d_query = rotate(query_part, cosine, -sine_part).astype(jnp.bfloat16)
    d_key = rotate(d_keys.reshape(pack_count * token_count, -1), cosine, -sine_part).astype(
        jnp.bfloat16
    )
    d_value = d_values.reshape(pack_count * token_count, -1).astype(jnp.bfloat16)
    query_grad = jnp.dot(xn_one.T, d_query, preferred_element_type=jnp.float32)
    key_grad = jnp.dot(xn_one.T, d_key, preferred_element_type=jnp.float32)
    value_grad = jnp.dot(xn_one.T, d_value, preferred_element_type=jnp.float32)
    d_norm_one = (
        jnp.dot(d_query, query_full.T, preferred_element_type=jnp.float32)
        + jnp.dot(d_key, key_full.T, preferred_element_type=jnp.float32)
        + jnp.dot(d_value, value_full.T, preferred_element_type=jnp.float32)
    )
    gain_one_grad = jnp.sum(d_norm_one * normed_one, axis=0)
    d_inputs = d_hidden_in + rms_back(d_norm_one * gain_one32, normed_one, scale_one)
    attn_parts = (
        lax.psum_scatter(
            gain_one_grad.astype(jnp.bfloat16), "fsdp", scatter_dimension=0, tiled=True
        ).astype(jnp.float32),
        lax.psum_scatter(
            query_grad.astype(jnp.bfloat16), "fsdp", scatter_dimension=0, tiled=True
        ).astype(jnp.float32),
        lax.psum_scatter(
            key_grad.astype(jnp.bfloat16), "fsdp", scatter_dimension=0, tiled=True
        ).astype(jnp.float32),
        lax.psum_scatter(
            value_grad.astype(jnp.bfloat16), "fsdp", scatter_dimension=0, tiled=True
        ).astype(jnp.float32),
        lax.psum_scatter(
            out_grad.astype(jnp.bfloat16), "fsdp", scatter_dimension=0, tiled=True
        ).astype(jnp.float32),
    )
    finished = (
        lax.psum(attn_parts[0].astype(jnp.bfloat16), ("ctx", "grp")).astype(jnp.float32),
        lax.psum(attn_parts[1].astype(jnp.bfloat16), ("ctx", "grp")).astype(jnp.float32),
        lax.psum(attn_parts[2].astype(jnp.bfloat16), ("ctx", "grp")).astype(jnp.float32),
        lax.psum(attn_parts[3].astype(jnp.bfloat16), ("ctx", "grp")).astype(jnp.float32),
        lax.psum(attn_parts[4].astype(jnp.bfloat16), ("ctx", "grp")).astype(jnp.float32),
        lax.psum(mlp_parts[0].astype(jnp.bfloat16), ("ctx", "grp")).astype(jnp.float32),
        lax.psum(mlp_parts[1].astype(jnp.bfloat16), ("ctx", "grp")).astype(jnp.float32),
        lax.psum(mlp_parts[2].astype(jnp.bfloat16), ("ctx", "grp")).astype(jnp.float32),
        lax.psum(mlp_parts[3].astype(jnp.bfloat16), ("ctx", "grp")).astype(jnp.float32),
    )
    home_out, home_grad = (
        lax.all_to_all(send_home(result), "ctx", split_axis=1, concat_axis=1, tiled=True),
        lax.all_to_all(
            send_home(d_inputs.astype(jnp.bfloat16)), "ctx", split_axis=1, concat_axis=1, tiled=True
        ),
    )
    return (
        restore(home_out),
        restore(home_grad),
        softmax_totals,
        finished[0],
        finished[1],
        finished[2],
        finished[3],
        finished[4],
        finished[5],
        finished[6],
        finished[7],
        finished[8],
    )


MINLEN = 1024
QB = 256
VMEM_LIMIT = 56 * 1024 * 1024


def fill_tables(cl_ref, sl_ref, ch_ref, sh_ref, c_ref, s_ref):
    @pl.when(pl.program_id(0) == 0)
    def _():
        cos_low, sin_low = cl_ref[...], sl_ref[...]
        for i in range(c_ref.shape[1] // BLK):
            at = slice(i * BLK, (i + 1) * BLK)
            cos_high, sin_high = ch_ref[:, i : i + 1], sh_ref[:, i : i + 1]
            c_ref[:, at] = cos_high * cos_low - sin_high * sin_low
            s_ref[:, at] = sin_high * cos_low + cos_high * sin_low


def attend_kernel(
    place, q_ref, k_ref, v_ref, cl_ref, sl_ref, ch_ref, sh_ref,
    keep_ref, send_ref, lse_ref, qr_ref, kr_ref, vr_ref, held, c_ref, s_ref,
):
    fill_tables(cl_ref, sl_ref, ch_ref, sh_ref, c_ref, s_ref)
    cosine = c_ref[...]
    sine = s_ref[...]
    half = HEAD_SIZE // 2
    seq = cosine.shape[1]

    def turn(field):
        front, back = field[:half], field[half:]
        return jnp.concatenate(
            [front * cosine - back * sine, back * cosine + front * sine], axis=0
        )

    k_rot = turn(k_ref[...])
    kr_ref[...] = k_rot.astype(jnp.bfloat16)
    key = k_rot.T.astype(jnp.bfloat16)
    val_t = v_ref[...].astype(jnp.bfloat16)
    vr_ref[...] = val_t
    q0 = turn(q_ref[:HEAD_SIZE]).astype(jnp.bfloat16)
    q1 = turn(q_ref[HEAD_SIZE:]).astype(jnp.bfloat16)
    qr_ref[:HEAD_SIZE] = q0
    qr_ref[HEAD_SIZE:] = q1
    rows = lax.broadcasted_iota(jnp.int32, (QB, 2 * QB), 0)
    cols = lax.broadcasted_iota(jnp.int32, (QB, 2 * QB), 1)
    keep = rows <= jnp.where(cols >= QB, cols - QB, cols)
    for b in range(seq // QB):
        lo, n = b * QB, (b + 1) * QB
        q_t = jnp.concatenate([q0[:, lo:n], q1[:, lo:n]], axis=1)
        scores = jnp.dot(key[:n], q_t, preferred_element_type=jnp.float32) * HEAD_SIZE ** (-0.5)
        diag = jnp.where(keep, scores[lo:], MASKED)
        top = jnp.max(diag, axis=0, keepdims=True)
        if b > 0:
            top = jnp.maximum(top, jnp.max(scores[:lo], axis=0, keepdims=True))
        e_diag = jnp.exp(diag - top)
        total = jnp.sum(e_diag, axis=0, keepdims=True)
        out = jnp.dot(val_t[:, lo:n], e_diag.astype(jnp.bfloat16), preferred_element_type=jnp.float32)
        if b > 0:
            e_rest = jnp.exp(scores[:lo] - top)
            total = total + jnp.sum(e_rest, axis=0, keepdims=True)
            out = out + jnp.dot(
                val_t[:, :lo], e_rest.astype(jnp.bfloat16), preferred_element_type=jnp.float32
            )
        out = (out / total).astype(jnp.bfloat16)
        held[:HEAD_SIZE, lo:n] = out[:, :QB]
        held[HEAD_SIZE:, lo:n] = out[:, QB:]
        lse = top + jnp.log(total)
        lse_ref[0, 0:1, lo:n] = lse[:, :QB]
        lse_ref[0, 1:2, lo:n] = lse[:, QB:]
    tok = seq // 2
    for core in range(2):

        @pl.when(place[0] == core)
        def _():
            keep_ref[...] = held[:, core * tok : (core + 1) * tok]
            send_ref[...] = held[:, (1 - core) * tok : (2 - core) * tok]


def attend_seq(place, qkv_t, tables):
    rows, seq = qkv_t.shape
    kv = rows // (4 * HEAD_SIZE)
    group = pl.BlockSpec((2 * HEAD_SIZE, seq), lambda j: (j, 0))

    def head(base):
        return pl.BlockSpec((HEAD_SIZE, seq), lambda j: (base + j, 0))

    table = pl.BlockSpec(memory_space=pltpu.VMEM)
    return pl.pallas_call(
        attend_kernel,
        grid=(kv,),
        in_specs=[pl.BlockSpec(memory_space=pltpu.SMEM), group, head(2 * kv), head(3 * kv), table, table, table, table],
        out_specs=[
            pl.BlockSpec((2 * HEAD_SIZE, seq // 2), lambda j: (j, 0)),
            pl.BlockSpec((2 * HEAD_SIZE, seq // 2), lambda j: (j, 0)),
            pl.BlockSpec((1, 2, seq), lambda j: (j, 0, 0)),
            group,
            head(0),
            head(0),
        ],
        out_shape=[
            jax.ShapeDtypeStruct((2 * kv * HEAD_SIZE, seq // 2), jnp.bfloat16),
            jax.ShapeDtypeStruct((2 * kv * HEAD_SIZE, seq // 2), jnp.bfloat16),
            jax.ShapeDtypeStruct((kv, 2, seq), jnp.float32),
            jax.ShapeDtypeStruct((2 * kv * HEAD_SIZE, seq), jnp.bfloat16),
            jax.ShapeDtypeStruct((kv * HEAD_SIZE, seq), jnp.bfloat16),
            jax.ShapeDtypeStruct((kv * HEAD_SIZE, seq), jnp.bfloat16),
        ],
        scratch_shapes=[
            pltpu.VMEM((2 * HEAD_SIZE, seq), jnp.bfloat16),
            pltpu.VMEM((HEAD_SIZE // 2, seq), jnp.float32),
            pltpu.VMEM((HEAD_SIZE // 2, seq), jnp.float32),
        ],
        compiler_params=pltpu.CompilerParams(vmem_limit_bytes=VMEM_LIMIT),
        cost_estimate=pl.CostEstimate(
            flops=4 * kv * 2 * seq * seq * HEAD_SIZE, bytes_accessed=10 * rows * seq, transcendentals=kv * seq * seq
        ),
        name="attend",
    )(place, qkv_t, qkv_t, qkv_t, *tables)


def attend_back_kernel(
    place, q_ref, k_ref, v_ref, keep_ref, got_ref, lse_ref, cl_ref, sl_ref, ch_ref, sh_ref,
    dq_ref, dk_ref, dv_ref, dk_acc, dv_acc, c_ref, s_ref,
):
    fill_tables(cl_ref, sl_ref, ch_ref, sh_ref, c_ref, s_ref)
    half = HEAD_SIZE // 2
    cosine = c_ref[...]
    sine = s_ref[...]
    seq = cosine.shape[1]

    def turn_back(field, cos, sin):
        front, back = field[:half], field[half:]
        return jnp.concatenate([front * cos + back * sin, back * cos - front * sin], axis=0)

    def flip(field):
        return field.astype(jnp.float32).T.astype(jnp.bfloat16)

    key_t = k_ref[...]
    key = flip(key_t)
    val = flip(v_ref[...])
    q0_t, q1_t = q_ref[:HEAD_SIZE], q_ref[HEAD_SIZE:]
    first_core = place[0] == 0
    early = jnp.where(first_core, keep_ref[...], got_ref[...])
    late = jnp.where(first_core, got_ref[...], keep_ref[...])
    grads = jnp.concatenate([early, late], axis=1)
    g0_t, g1_t = grads[:HEAD_SIZE], grads[HEAD_SIZE:]
    q0, q1, g0, g1 = flip(q0_t), flip(q1_t), flip(g0_t), flip(g1_t)
    dk_acc[...] = jnp.zeros_like(dk_acc)
    dv_acc[...] = jnp.zeros_like(dv_acc)
    rows = lax.broadcasted_iota(jnp.int32, (QB, 2 * QB), 0)
    cols = lax.broadcasted_iota(jnp.int32, (QB, 2 * QB), 1)
    keep = rows <= jnp.where(cols >= QB, cols - QB, cols)
    for b in range(seq // QB):
        lo, n = b * QB, (b + 1) * QB
        q_t = jnp.concatenate([q0_t[:, lo:n], q1_t[:, lo:n]], axis=1)
        g_t = jnp.concatenate([g0_t[:, lo:n], g1_t[:, lo:n]], axis=1)
        q_n = jnp.concatenate([q0[lo:n], q1[lo:n]], axis=0)
        g_n = jnp.concatenate([g0[lo:n], g1[lo:n]], axis=0)
        lse = jnp.concatenate([lse_ref[0, 0:1, lo:n], lse_ref[0, 1:2, lo:n]], axis=1)
        parts = []
        delta = None
        for start, stop in ([(0, lo)] if b > 0 else []) + [(lo, n)]:
            scores = jnp.dot(key[start:stop], q_t, preferred_element_type=jnp.float32) * HEAD_SIZE ** (-0.5)
            prob = jnp.exp(scores - lse)
            if start == lo:
                prob = jnp.where(keep, prob, 0.0)
            d_prob = jnp.dot(val[start:stop], g_t, preferred_element_type=jnp.float32)
            part = jnp.sum(prob * d_prob, axis=0, keepdims=True)
            delta = part if delta is None else delta + part
            dv_acc[start:stop] += jnp.dot(prob.astype(jnp.bfloat16), g_n, preferred_element_type=jnp.float32)
            parts.append((start, stop, prob, d_prob))
        dq_t = None
        for start, stop, prob, d_prob in parts:
            d_score = (prob * (d_prob - delta) * HEAD_SIZE ** (-0.5)).astype(jnp.bfloat16)
            dk_acc[start:stop] += jnp.dot(d_score, q_n, preferred_element_type=jnp.float32)
            part = jnp.dot(key_t[:, start:stop], d_score, preferred_element_type=jnp.float32)
            dq_t = part if dq_t is None else dq_t + part
        cos, sin = cosine[:, lo:n], sine[:, lo:n]
        dq_ref[:HEAD_SIZE, lo:n] = turn_back(dq_t[:, :QB], cos, sin).astype(jnp.bfloat16)
        dq_ref[HEAD_SIZE:, lo:n] = turn_back(dq_t[:, QB:], cos, sin).astype(jnp.bfloat16)
    dk_ref[...] = turn_back(dk_acc[...].T, cosine, sine).astype(jnp.bfloat16)
    dv_ref[...] = dv_acc[...].T.astype(jnp.bfloat16)


def attend_seq_back(place, q_t, k_t, v_t, g_keep, g_got, lse, tables):
    rows, seq = k_t.shape
    kv = rows // HEAD_SIZE
    group = pl.BlockSpec((2 * HEAD_SIZE, seq), lambda j: (j, 0))
    part = pl.BlockSpec((2 * HEAD_SIZE, seq // 2), lambda j: (j, 0))
    head = pl.BlockSpec((HEAD_SIZE, seq), lambda j: (j, 0))
    table = pl.BlockSpec(memory_space=pltpu.VMEM)
    return pl.pallas_call(
        attend_back_kernel,
        grid=(kv,),
        in_specs=[
            pl.BlockSpec(memory_space=pltpu.SMEM), group, head, head, part, part,
            pl.BlockSpec((1, 2, seq), lambda j: (j, 0, 0)), table, table, table, table,
        ],
        out_specs=[group, head, head],
        out_shape=[
            jax.ShapeDtypeStruct((2 * rows, seq), jnp.bfloat16),
            jax.ShapeDtypeStruct((rows, seq), jnp.bfloat16),
            jax.ShapeDtypeStruct((rows, seq), jnp.bfloat16),
        ],
        scratch_shapes=[
            pltpu.VMEM((seq, HEAD_SIZE), jnp.float32),
            pltpu.VMEM((seq, HEAD_SIZE), jnp.float32),
            pltpu.VMEM((HEAD_SIZE // 2, seq), jnp.float32),
            pltpu.VMEM((HEAD_SIZE // 2, seq), jnp.float32),
        ],
        compiler_params=pltpu.CompilerParams(vmem_limit_bytes=VMEM_LIMIT),
        cost_estimate=pl.CostEstimate(
            flops=10 * kv * 2 * seq * seq * HEAD_SIZE, bytes_accessed=20 * rows * seq, transcendentals=kv * seq * seq
        ),
        name="attend_back",
    )(place, q_t, k_t, v_t, g_keep, g_got, lse, *tables)


def fp32(field):
    return field.astype(jnp.float32)


def mm(left, right, dims=((1,), (0,)), out=jnp.float32):
    return lax.dot_general(left, right, (dims, ((), ())), preferred_element_type=out)


ANY = pl.BlockSpec(memory_space=pl.ANY)
SMEM = pl.BlockSpec(memory_space=pltpu.SMEM)
VM = pl.BlockSpec(memory_space=pltpu.VMEM)
PARAMS = pltpu.CompilerParams(vmem_limit_bytes=VMEM_LIMIT)
MESH = pl.DeviceIdType.MESH
TILE = 256
WIDE = 512


def bf16_like(*dims):
    return jax.ShapeDtypeStruct(dims, jnp.bfloat16)


def f32_like(*dims):
    return jax.ShapeDtypeStruct(dims, jnp.float32)


def cost(flops, moved):
    return pl.CostEstimate(flops=int(flops), bytes_accessed=int(moved), transcendentals=0)


class Spots:
    def __init__(self):
        z, f, g = lax.axis_index("ctx"), lax.axis_index("fsdp"), lax.axis_index("grp")
        self.z, self.f, self.g = z, f, g
        self.parity = z % 2
        self.fx = f + 1 - 2 * (f % 2)
        self.fy = f + 2 - 4 * (f // 2)
        self.fd = 3 - f
        across = z + 1 - 2 * self.parity
        self.x = (z, self.fx, g)
        self.y = (z, self.fy, g)
        self.diag = (z, self.fd, g)
        self.core = (z, f, 1 - g)
        self.across = (across, f, g)
        self.swap = (across, f, 1 - g)


def greet(*partners):
    barrier = pltpu.get_barrier_semaphore()
    for partner in partners:
        pl.semaphore_signal(barrier, inc=1, device_id=partner, device_id_type=MESH)
    pl.semaphore_wait(barrier, len(partners))


def rows_at(start, size):
    return pl.ds(pl.multiple_of(start, size), size)


def gather_kernel(
    tokens, cotangent, wq, wk, wv, wo, gate, up, down, gain,
    qkv_o, out_o, pair_o, down_o, x_o, dy_o, gain_o, xn_o, turned_o,
    send, recv, near, far, qkv_v, out_v, pair_v, down_v, tok_v, gain_v,
    extra, x_v, w_v, gains_v, xn_v, turned_v,
):
    at = Spots()
    g, f, parity = at.g, at.f, at.parity
    greet(at.x, at.y, at.diag, at.core, at.across, at.swap)
    taken = [0, 0]

    def remote(src, dst, device):
        i = taken[0]
        taken[0] += 1
        return pltpu.make_async_remote_copy(
            src_ref=src, dst_ref=dst, send_sem=send.at[i], recv_sem=recv.at[i],
            device_id=device, device_id_type=MESH,
        )

    class Bounce:
        def __init__(self, src, via, dst):
            i = taken[1]
            taken[1] += 1
            self.first = pltpu.make_async_copy(src, via, near.at[i])
            self.second = pltpu.make_async_copy(via, dst, far.at[i])

        def start(self):
            self.first.start()

        def turn(self):
            self.first.wait()
            self.second.start()

        def wait(self):
            self.second.wait()

    def start(copies):
        for copy in copies:
            copy.start()
        return copies

    def arrive(copies):
        for copy in copies:
            copy.wait_recv()

    tok = tokens.shape[1]
    feat = wq.shape[0]
    mid = feat // 2
    nq, nk, nv = (w.shape[1] // 2 for w in (wq, wk, wv))
    nf = gate.shape[1] // 8
    wide = wo.shape[1] // 2
    count = 4
    top, low = slice(0, mid), slice(mid, feat)

    mine = rows_at(g * tok, tok)
    swaps = [
        remote(tokens.at[0], x_o.at[mine], at.swap),
        remote(cotangent.at[0], dy_o.at[mine], at.swap),
    ]
    keeps = [
        Bounce(tokens.at[0], tok_v.at[0], x_o.at[mine]),
        Bounce(cotangent.at[0], tok_v.at[1], dy_o.at[mine]),
    ]
    away = rows_at((1 - g) * tok, tok)
    swaps_out = [
        pltpu.make_async_remote_copy(
            src_ref=array.at[0], dst_ref=into.at[away], send_sem=send.at[i], recv_sem=recv.at[i],
            device_id=at.swap, device_id_type=MESH,
        )
        for i, (array, into) in enumerate(((tokens, x_o), (cotangent, dy_o)))
    ]
    shares = [remote(x_o.at[mine], x_o.at[mine], at.core), remote(dy_o.at[mine], dy_o.at[mine], at.core)]

    @pl.when(g != parity)
    def _():
        start(swaps_out)

    @pl.when(g == parity)
    def _():
        start(keeps)
        for copy in keeps:
            copy.turn()

    own_rows = f * feat
    shared_cols = (count - 1) * nf

    def pair_direct(part, device):
        first = taken[0]
        taken[0] += count + 1
        rows = rows_at(own_rows + part.start, mid)

        def made(array, index, k, i):
            return pltpu.make_async_remote_copy(
                src_ref=array.at[part, rows_at((2 * k + g) * nf, nf)],
                dst_ref=pair_o.at[index, rows, rows_at(k * nf, nf)],
                send_sem=send.at[first + i], recv_sem=recv.at[first + i],
                device_id=device, device_id_type=MESH,
            )

        def some(array):
            return [made(array, parity, k, k) for k in range(count - 1)]

        @pl.when(parity == 0)
        def _():
            start(some(gate))

        @pl.when(parity == 1)
        def _():
            start(some(up))

        last = start([made(gate, 0, count - 1, count - 1), made(up, 1, count - 1, count)])
        return some(gate), last

    pair_xt, last_xt = pair_direct(top, at.x)
    pair_yl, last_yl = pair_direct(low, at.y)
    pair_xl, last_xl = pair_direct(low, at.x)
    pair_yt, last_yt = pair_direct(top, at.y)

    def qkv_direct(part, device):
        copies = []
        for array, width, column in ((wq, nq, 0), (wk, nk, nq), (wv, nv, nq + nk)):
            copies.append(
                remote(
                    array.at[part, rows_at(g * width, width)],
                    qkv_o.at[rows_at(own_rows + part.start, mid), column : column + width],
                    device,
                )
            )
        return start(copies)

    qkv_xt = qkv_direct(top, at.x)
    qkv_yl = qkv_direct(low, at.y)
    qkv_xl = qkv_direct(low, at.x)
    qkv_yt = qkv_direct(top, at.y)

    own = rows_at(own_rows, feat)
    locals_ = [
        Bounce(
            array.at[:, rows_at(g * width, width)],
            qkv_v.at[:, column : column + width],
            qkv_o.at[own, column : column + width],
        )
        for array, width, column in ((wq, nq, 0), (wk, nk, nq), (wv, nv, nq + nk))
    ]
    locals_.append(Bounce(wo, out_v, out_o.at[own]))
    locals_.append(Bounce(down.at[rows_at(g * nf, nf)], down_v, down_o))
    for array, index in ((gate, 0), (up, 1)):
        for k in range(count):
            locals_.append(
                Bounce(
                    array.at[:, rows_at((2 * k + g) * nf, nf)],
                    pair_v.at[index, :, rows_at(k * nf, nf)],
                    pair_o.at[index, own, rows_at(k * nf, nf)],
                )
            )
    gain_place = gain_o.at[pl.ds(f, 1)]
    locals_.append(Bounce(gain, gain_v, gain_place))
    start(locals_)
    for copy in locals_:
        copy.turn()
    gains = start([remote(gain, gain_place, to) for to in (at.x, at.y, at.diag)])

    def forward(array_at, rows_x, rows_y):
        return remote(array_at(rows_x), array_at(rows_x), at.y), remote(
            array_at(rows_y), array_at(rows_y), at.x
        )

    x_top, y_low = rows_at(at.fx * feat, mid), rows_at(at.fy * feat + mid, mid)
    x_low, y_top = rows_at(at.fx * feat + mid, mid), rows_at(at.fy * feat, mid)
    d_top, d_low = rows_at(at.fd * feat, mid), rows_at(at.fd * feat + mid, mid)

    def pair_view(rows):
        return pair_o.at[parity, rows, 0:shared_cols]

    def last_view(rows):
        return pair_o.at[:, rows, shared_cols : shared_cols + nf]

    def out_view(rows):
        return out_o.at[rows, rows_at(g * wide, wide)]

    pair_fy, pair_fx = forward(pair_view, x_top, y_low)
    last_fy, last_fx = forward(last_view, x_top, y_low)
    sends = [pair_fy, pair_fx, last_fy, last_fx]

    def across(rows):
        copy = remote(pair_view(rows), pair_view(rows), at.across)
        copy.start()
        sends.append(copy)
        return copy

    arrive(pair_xt)
    pair_fy.start()
    z_copies = [across(x_top)]
    arrive(pair_yl)
    pair_fx.start()
    z_copies.append(across(y_low))

    def out_direct(part, device):
        copy = remote(
            wo.at[part, rows_at(g * wide, wide)],
            out_o.at[rows_at(own_rows + part.start, mid), rows_at(g * wide, wide)],
            device,
        )
        copy.start()
        return copy

    out_xt, out_yl = out_direct(top, at.x), out_direct(low, at.y)
    out_xl, out_yt = out_direct(low, at.x), out_direct(top, at.y)

    arrive(pair_xl)
    z_copies.append(across(x_low))
    arrive(pair_yt)
    z_copies.append(across(y_top))

    def qkv_view(rows):
        return qkv_o.at[rows]

    qkv_fy, qkv_fx = forward(qkv_view, x_top, y_low)
    arrive(qkv_xt)
    qkv_fy.start()
    arrive(qkv_yl)
    qkv_fx.start()
    arrive(last_xt)
    last_fy.start()
    arrive(last_yl)
    last_fx.start()

    pair_fy.wait_recv()
    z_copies.append(across(d_top))
    pair_fx.wait_recv()
    z_copies.append(across(d_low))

    for i in range(2):

        @pl.when(g != parity)
        def _():
            swaps[i].wait_recv()
            swaps_out[i].wait_send()

        @pl.when(g == parity)
        def _():
            keeps[i].wait()

        shares[i].start()

    out_fy, out_fx = forward(out_view, x_top, y_low)
    out_xt.wait_recv()
    out_fy.start()
    out_yl.wait_recv()
    out_fx.start()
    out_xl.wait_recv()
    out_yt.wait_recv()

    def share(rows):
        copy = remote(out_view(rows), out_view(rows), at.core)
        copy.start()
        return copy

    shared = [share(x_top), share(x_low), share(y_top), share(y_low)]

    arrive(qkv_xl + qkv_yt + [qkv_fy, qkv_fx] + gains + shares[:1])
    for copy in locals_[:3] + locals_[-1:]:
        copy.wait()
    loads = [
        pltpu.make_async_copy(src, dst, extra.at[i])
        for i, (src, dst) in enumerate(((x_o, x_v), (gain_o, gains_v), (qkv_o, w_v)))
    ]
    start(loads)
    for copy in loads:
        copy.wait()
    row = gain_row(gains_v, 0)

    @pl.loop(0, x_v.shape[0] // TILE)
    def _(n):
        part = rows_at(n * TILE, TILE)
        field = fp32(x_v[part, :])
        xn_v[part, :] = (field * norm_scale(field) * row).astype(jnp.bfloat16)

    @pl.loop(0, w_v.shape[1] // TILE)
    def _(n):
        part = rows_at(n * TILE, TILE)
        turned_v[part, :] = mm(w_v[:, part].T, xn_v[...], ((1,), (1,)))

    results = start(
        [pltpu.make_async_copy(xn_v, xn_o, extra.at[3]), pltpu.make_async_copy(turned_v, turned_o, extra.at[4])]
    )

    out_fy.wait_recv()
    shared.append(share(d_top))
    out_fx.wait_recv()
    shared.append(share(d_low))

    arrive([last_fy, last_fx])
    arrive(last_xl + last_yt)
    arrive(shares[1:])
    arrive(shared)
    arrive(z_copies)
    for copy in locals_[3:-1] + results:
        copy.wait()
    for copy in (
        pair_xt + pair_yl + pair_xl + pair_yt + qkv_xt + qkv_yl + qkv_xl + qkv_yt + gains
        + sends + shares + shared
        + [out_xt, out_yl, out_xl, out_yt, out_fy, out_fx, qkv_fy, qkv_fx]
        + last_xt + last_yl + last_xl + last_yt
    ):
        copy.wait_send()


def gather_all(tokens, cotangent, wq, wk, wv, wo, gate, up, down, gain):
    tok, width = tokens.shape[1:]
    nf = gate.shape[1] // 8
    cols = (wq.shape[1] + wk.shape[1] + wv.shape[1]) // 2
    return pl.pallas_call(
        gather_kernel,
        in_specs=[ANY] * 10,
        out_specs=[ANY] * 9,
        out_shape=[
            bf16_like(width, cols),
            bf16_like(4 * wo.shape[0], width),
            bf16_like(2, width, 4 * nf),
            bf16_like(nf, width),
            bf16_like(2 * tok, width),
            bf16_like(2 * tok, width),
            jax.ShapeDtypeStruct((4,) + gain.shape[1:], gain.dtype),
            bf16_like(2 * tok, width),
            f32_like(cols, 2 * tok),
        ],
        scratch_shapes=[
            pltpu.SemaphoreType.DMA((72,)),
            pltpu.SemaphoreType.DMA((72,)),
            pltpu.SemaphoreType.DMA((20,)),
            pltpu.SemaphoreType.DMA((20,)),
            pltpu.VMEM((width // 4, cols), jnp.bfloat16),
            pltpu.VMEM(wo.shape, jnp.bfloat16),
            pltpu.VMEM((2, width // 4, 4 * nf), jnp.bfloat16),
            pltpu.VMEM((nf, width), jnp.bfloat16),
            pltpu.VMEM((2, tok, width), jnp.bfloat16),
            pltpu.VMEM(gain.shape, gain.dtype),
            pltpu.SemaphoreType.DMA((5,)),
            pltpu.VMEM((2 * tok, width), jnp.bfloat16),
            pltpu.VMEM((width, cols), jnp.bfloat16),
            pltpu.VMEM((4,) + gain.shape[1:], gain.dtype),
            pltpu.VMEM((2 * tok, width), jnp.bfloat16),
            pltpu.VMEM((cols, 2 * tok), jnp.float32),
        ],
        compiler_params=pltpu.CompilerParams(
            collective_id=0, has_side_effects=True, vmem_limit_bytes=VMEM_LIMIT
        ),
        cost_estimate=cost(0, 500e6),
        name="gather",
    )(tokens, cotangent, wq, wk, wv, wo, gate, up, down, gain)


def gain_row(gain, which):
    return jnp.concatenate([gain[k, which : which + 1, :] for k in range(gain.shape[0])], axis=1)


def norm_scale(field):
    return lax.rsqrt(jnp.mean(field * field, axis=-1, keepdims=True) + EPS)


def residual_kernel(place, x_ref, attn_keep, attn_got, gain, w_ref, h_ref, xn_ref, attn_ref):
    core = place[0]
    heads = attn_keep.shape[0]
    keep_at, got_at = rows_at(core * heads, heads), rows_at((1 - core) * heads, heads)
    attn_ref[keep_at, :] = attn_keep[...]
    attn_ref[got_at, :] = attn_got[...]
    field = fp32(x_ref[...]) + mm(attn_ref[...].T, w_ref[...])
    h_ref[...] = field
    xn_ref[...] = (field * norm_scale(field) * gain_row(gain, 1)).astype(jnp.bfloat16)


def residual(place, x_seq, attn_keep, attn_got, gains, weight):
    seq, width = x_seq.shape
    tok = seq // 2
    heads = attn_keep.shape[0]
    steps = tok // TILE
    rows = pl.BlockSpec((TILE, width), lambda i, place: (i, 0))
    return pl.pallas_call(
        residual_kernel,
        grid_spec=pltpu.PrefetchScalarGridSpec(
            num_scalar_prefetch=1,
            grid=(steps,),
            in_specs=[
                pl.BlockSpec((TILE, width), lambda i, place: (steps * place[0] + i, 0)),
                pl.BlockSpec((heads, TILE), lambda i, place: (0, i)),
                pl.BlockSpec((heads, TILE), lambda i, place: (0, i)),
                VM,
                VM,
            ],
            out_specs=[rows, rows, pl.BlockSpec((2 * heads, TILE), lambda i, place: (0, i))],
        ),
        out_shape=[f32_like(tok, width), bf16_like(tok, width), bf16_like(2 * heads, tok)],
        compiler_params=PARAMS,
        cost_estimate=cost(2 * tok * width * weight.shape[0], 14e6),
        name="residual",
    )(place, x_seq, attn_keep, attn_got, gains, weight)


def hidden_kernel(place, xn_own, xn_got, gate_w, up_w, hid_ref, for_gate_ref, act_ref, xn_ref):
    @pl.when(pl.program_id(0) == 0)
    def _():
        tok = xn_own.shape[0]
        xn_ref[rows_at(place[0] * tok, tok), :] = xn_own[...]
        xn_ref[rows_at((1 - place[0]) * tok, tok), :] = xn_got[...]

    gate = mm(xn_ref[...], gate_w[0])
    up = mm(xn_ref[...], up_w[0])
    sig = 1.0 / (1.0 + jnp.exp(-gate))
    act = gate * sig
    hid_ref[...] = (act * up).astype(jnp.bfloat16)
    for_gate_ref[...] = (up * (sig + act * (1.0 - sig))).astype(jnp.bfloat16)
    act_ref[...] = act.astype(jnp.bfloat16)


def hidden_step(place, xn_own, xn_got, pair):
    seq, width = 2 * xn_own.shape[0], xn_own.shape[1]
    ff = pair.shape[2]
    block = pl.BlockSpec((seq, TILE), lambda n: (0, n))
    return pl.pallas_call(
        hidden_kernel,
        grid=(ff // TILE,),
        in_specs=[
            SMEM,
            VM,
            VM,
            pl.BlockSpec((1, width, TILE), lambda n: (0, 0, n)),
            pl.BlockSpec((1, width, TILE), lambda n: (1, 0, n)),
        ],
        out_specs=[block] * 3 + [VM],
        out_shape=[bf16_like(seq, ff)] * 3 + [bf16_like(seq, width)],
        compiler_params=PARAMS,
        cost_estimate=cost(4 * seq * width * ff, 30e6),
        name="hidden",
    )(place, xn_own, xn_got, pair, pair)


def hidden_back_kernel(dy_ref, down_w, for_gate_ref, act_ref, dgate_ref, dup_ref):
    d_hidden = mm(dy_ref[...], down_w[...], ((1,), (1,)))
    dgate_ref[...] = (d_hidden * fp32(for_gate_ref[...])).astype(jnp.bfloat16)
    dup_ref[...] = (d_hidden * fp32(act_ref[...])).astype(jnp.bfloat16)


def hidden_back(dy, down, for_gate, act):
    seq, width = dy.shape
    ff = down.shape[0]
    block = pl.BlockSpec((seq, WIDE), lambda n: (0, n))
    return pl.pallas_call(
        hidden_back_kernel,
        grid=(ff // WIDE,),
        in_specs=[VM, pl.BlockSpec((WIDE, width), lambda n: (n, 0)), block, block],
        out_specs=[block] * 2,
        out_shape=[bf16_like(seq, ff)] * 2,
        compiler_params=PARAMS,
        cost_estimate=cost(2 * seq * width * ff, 26e6),
        name="hidden_back",
    )(dy, down, for_gate, act)


def back_kernel(place, dgate_ref, dup_ref, gate_w, up_w, own_ref, send_ref):
    field = mm(dgate_ref[...], gate_w[0], ((1,), (1,)))
    field = field + mm(dup_ref[...], up_w[0], ((1,), (1,)))
    tok = own_ref.shape[0]

    @pl.when(place[0] == 0)
    def _():
        own_ref[...] = field[:tok]
        send_ref[...] = field[tok:].astype(jnp.bfloat16)

    @pl.when(place[0] == 1)
    def _():
        own_ref[...] = field[tok:]
        send_ref[...] = field[:tok].astype(jnp.bfloat16)


def back_step(place, d_gate, d_up, pair):
    seq, ff = d_gate.shape
    width = pair.shape[1]
    out = pl.BlockSpec((seq // 2, WIDE), lambda n: (0, n))
    return pl.pallas_call(
        back_kernel,
        grid=(width // WIDE,),
        in_specs=[
            SMEM,
            VM,
            VM,
            pl.BlockSpec((1, WIDE, ff), lambda n: (0, n, 0)),
            pl.BlockSpec((1, WIDE, ff), lambda n: (1, n, 0)),
        ],
        out_specs=[out, out],
        out_shape=[f32_like(seq // 2, width), bf16_like(seq // 2, width)],
        compiler_params=PARAMS,
        cost_estimate=cost(4 * seq * width * ff, 26e6),
        name="back",
    )(place, d_gate, d_up, pair, pair)


def result_kernel(place, hid_ref, h_ref, down_w, own_ref, send_ref):
    field = mm(hid_ref[...], down_w[...])
    tok = own_ref.shape[0]

    @pl.when(place[0] == 0)
    def _():
        own_ref[...] = field[:tok] + h_ref[...]
        send_ref[...] = field[tok:].astype(jnp.bfloat16)

    @pl.when(place[0] == 1)
    def _():
        own_ref[...] = field[tok:] + h_ref[...]
        send_ref[...] = field[:tok].astype(jnp.bfloat16)


def result_step(place, hidden, h_own, down):
    tok, width = h_own.shape
    ff = hidden.shape[1]
    out = pl.BlockSpec((tok, WIDE), lambda n: (0, n))
    return pl.pallas_call(
        result_kernel,
        grid=(width // WIDE,),
        in_specs=[SMEM, VM, out, pl.BlockSpec((ff, WIDE), lambda n: (0, n))],
        out_specs=[out, out],
        out_shape=[f32_like(tok, width), bf16_like(tok, width)],
        compiler_params=PARAMS,
        cost_estimate=cost(4 * tok * width * ff, 20e6),
        name="result",
    )(place, hidden, h_own, down)


def entry_kernel(place, dn_own, dn_got, h_ref, dy_ref, gain, w_ref, dh_ref, da_ref, keep_ref, send_ref, part_ref):
    core = place[0]

    @pl.when(pl.program_id(0) == 0)
    def _():
        part_ref[...] = jnp.zeros_like(part_ref)

    field = h_ref[...]
    scale = norm_scale(field)
    hat = field * scale
    grad = dn_own[...] + fp32(dn_got[...])
    part_ref[...] += jnp.sum(grad * hat, axis=0, keepdims=True)
    total = fp32(dy_ref[...]) + rms_back(grad * gain_row(gain, 1), hat, scale)
    dh_ref[...] = total
    da_ref[...] = total.astype(jnp.bfloat16)
    heads = keep_ref.shape[0]
    for ref, at in ((send_ref, 1 - core), (keep_ref, core)):
        ref[...] = mm(w_ref[rows_at(at * heads, heads), :], da_ref[...], ((1,), (1,))).astype(jnp.bfloat16)


def entry_step(place, dn_own, dn_got, h_own, dy_all, gains, weight):
    tok, width = h_own.shape
    heads = weight.shape[0] // 2
    steps = tok // TILE
    rows = pl.BlockSpec((TILE, width), lambda i, place: (i, 0))
    cols = pl.BlockSpec((heads, TILE), lambda i, place: (0, i))
    return pl.pallas_call(
        entry_kernel,
        grid_spec=pltpu.PrefetchScalarGridSpec(
            num_scalar_prefetch=1,
            grid=(steps,),
            in_specs=[
                rows,
                rows,
                rows,
                pl.BlockSpec((TILE, width), lambda i, place: (steps * place[0] + i, 0)),
                VM,
                VM,
            ],
            out_specs=[rows, rows, cols, cols, VM],
        ),
        out_shape=[
            f32_like(tok, width),
            bf16_like(tok, width),
            bf16_like(heads, tok),
            bf16_like(heads, tok),
            f32_like(1, width),
        ],
        compiler_params=PARAMS,
        cost_estimate=cost(2 * tok * width * weight.shape[0], 20e6),
        name="entry",
    )(place, dn_own, dn_got, h_own, dy_all, gains, weight)


def inputs_kernel(place, dq_ref, dk_ref, dv_ref, w_ref, own_ref, send_ref, d_ref):
    @pl.when(pl.program_id(0) == 0)
    def _():
        nq, nk = dq_ref.shape[0], dk_ref.shape[0]
        d_ref[:, :nq] = dq_ref[...].T
        d_ref[:, nq : nq + nk] = dk_ref[...].T
        d_ref[:, nq + nk :] = dv_ref[...].T

    field = mm(d_ref[...], w_ref[...], ((1,), (1,)))
    tok = own_ref.shape[0]

    @pl.when(place[0] == 0)
    def _():
        own_ref[...] = field[:tok]
        send_ref[...] = field[tok:].astype(jnp.bfloat16)

    @pl.when(place[0] == 1)
    def _():
        own_ref[...] = field[tok:]
        send_ref[...] = field[:tok].astype(jnp.bfloat16)


def inputs_step(place, dq_t, dk_t, dv_t, weight):
    width, cols = weight.shape
    tok = dq_t.shape[1] // 2
    out = pl.BlockSpec((tok, WIDE), lambda n: (0, n))
    return pl.pallas_call(
        inputs_kernel,
        grid=(width // WIDE,),
        in_specs=[SMEM] + [VM] * 3 + [pl.BlockSpec((WIDE, cols), lambda n: (n, 0))],
        out_specs=[out, out, VM],
        out_shape=[f32_like(tok, width), bf16_like(tok, width), bf16_like(2 * tok, cols)],
        compiler_params=PARAMS,
        cost_estimate=cost(4 * tok * width * cols, 14e6),
        name="inputs",
    )(place, dq_t, dk_t, dv_t, weight)


def last_kernel(place, d1_own, d1_got, x_ref, dh_ref, gain, dx_ref, part_ref):
    @pl.when(pl.program_id(0) == 0)
    def _():
        part_ref[...] = jnp.zeros_like(part_ref)

    field = fp32(x_ref[...])
    scale = norm_scale(field)
    hat = field * scale
    grad = d1_own[...] + fp32(d1_got[...])
    part_ref[...] += jnp.sum(grad * hat, axis=0, keepdims=True)
    dx_ref[...] = (dh_ref[...] + rms_back(grad * gain_row(gain, 0), hat, scale)).astype(jnp.bfloat16)


def last_step(place, d1_own, d1_got, x_seq, dh_own, gains):
    tok, width = dh_own.shape
    tile = TILE // 2
    steps = tok // tile
    rows = pl.BlockSpec((tile, width), lambda i, place: (i, 0))
    return pl.pallas_call(
        last_kernel,
        grid_spec=pltpu.PrefetchScalarGridSpec(
            num_scalar_prefetch=1,
            grid=(steps,),
            in_specs=[
                rows,
                rows,
                pl.BlockSpec((tile, width), lambda i, place: (steps * place[0] + i, 0)),
                rows,
                VM,
            ],
            out_specs=[rows, VM],
        ),
        out_shape=[bf16_like(tok, width), f32_like(1, width)],
        compiler_params=PARAMS,
        cost_estimate=cost(0, 14e6),
        name="last",
    )(place, d1_own, d1_got, x_seq, dh_own, gains)


class Group:
    def __init__(self, source, rows, put):
        self.source, self.rows, self.put = source, rows, put
        mid = rows // 2
        self.top, self.low = pl.ds(0, mid), pl.ds(mid, mid)


def add_rows(dst, left, right):
    rows = dst.shape[0]

    @pl.loop(0, rows // 64)
    def _(i):
        at = rows_at(i * 64, 64)
        dst[at] = (fp32(left[at]) + fp32(right[at])).astype(dst.dtype)


ORDER = (
    "end", "b1u", "s1", "gie", "b1f", "b0u", "gwe", "h1u", "jod", "ene", "h1f", "b1v", "sed",
    "kee", "zad", "gq", "joe", "b0f", "kwe", "h0u", "s2", "see", "zae", "plu", "wad", "giu",
    "b0v", "fid", "gwu", "zbd", "enu", "h0f", "plf", "gif", "h1v", "go", "keu", "b1q", "fie",
    "gwf", "wae", "b1r", "enf", "b0q", "zbe", "jou", "kef", "seu", "h0v", "s3", "zau", "plv",
    "giv", "gwv", "kwu", "kev", "env", "h1q", "ao", "ded", "b0r", "jof", "sef", "h1r", "dee",
    "zaf", "h0q", "jov", "sev", "zav", "plq", "wau", "fif", "b1o", "b0o", "giq", "kwf", "kwv",
    "fiu", "zbu", "gwq", "enq", "keq", "h0r", "plr", "wav", "joq", "gir", "fiv", "zbv", "h1o",
    "seq", "gwr", "zaq", "fiq", "h0o", "waf", "ker", "zbf", "enr", "waq", "plo", "gio", "s4",
    "zbq", "eno", "deu", "jor", "kwr", "dev", "gwo", "keo", "ser", "kwq", "zar", "joo", "seo",
    "s5", "zao", "fir", "war", "def", "zbr", "wao", "fio", "zbo", "kwo", "der", "deq", "deo",
)


def collect_kernel(
    down, down_in, gate, gate_last, up, xn, d_qkv, attn, da, sums, lse,
    down_o, gate_o, up_o, query_o, key_o, value_o, out_o, sums_o, lse_o,
    send, recv, near, lse_send, lse_recv, lse_near, out_mine, out_got, sums_got,
    out_away, qkv, xn_v, d_qkv_v, attn_v, da_v, *buffers,
):
    at = Spots()
    z, f, g, parity = at.z, at.f, at.g, at.parity
    is_inner = (z == 1) | (z == 2)
    is_outer = (z == 0) | (z == 3)
    toward = (1 + z // 2, f, g)
    outward = (3 * (z // 2), f, g)
    other = (3 - z, f, g)
    chips = 4
    barrier = pltpu.get_barrier_semaphore()
    for partner in (at.x, at.y):
        pl.semaphore_signal(barrier, inc=1, device_id=partner, device_id_type=MESH)
    for level in range(chips):
        for core in range(2):

            @pl.when((z != level) | (g != core))
            def _():
                pl.semaphore_signal(barrier, inc=1, device_id=(level, f, core), device_id_type=MESH)

    pl.semaphore_wait(barrier, 2 * chips + 1)

    taken = [0, 0]

    def between(index, src, dst, device):
        return pltpu.make_async_remote_copy(
            src_ref=src, dst_ref=dst, send_sem=send.at[index], recv_sem=recv.at[index],
            device_id=device, device_id_type=MESH,
        )

    def remote(src, dst, device):
        taken[0] += 1
        return between(taken[0] - 1, src, dst, device)

    def local(src, dst):
        i = taken[1]
        taken[1] += 1
        return pltpu.make_async_copy(src, dst, near.at[i])

    nf = down.shape[0]
    feat = gate.shape[0]
    nq, nk = query_o.shape[1] // 2, key_o.shape[1] // 2
    wide = out_o.shape[1] // 2

    def put_down(done):
        return [(done, down_o.at[rows_at(g * nf, nf)])]

    def put_pair(into, first, count):
        def put(done):
            return [
                (
                    done.at[:, rows_at(k * nf, nf)],
                    into.at[:, rows_at((2 * (first + k) + g) * nf, nf)],
                )
                for k in range(count)
            ]

        return put

    def put_query(done):
        return [(done, query_o.at[:, rows_at(g * nq, nq)])]

    def put_key_value(done):
        return [
            (done.at[:, 0:nk], key_o.at[:, rows_at(g * nk, nk)]),
            (done.at[:, nk : 2 * nk], value_o.at[:, rows_at(g * nk, nk)]),
        ]

    def put_out(done):
        return [(done, out_o.at[:, rows_at(g * wide, wide)])]

    lse_place = lse_o.at[2 * (z // 2) + g]
    for level in range(chips):
        copy = pltpu.make_async_remote_copy(
            src_ref=lse, dst_ref=lse_place, send_sem=lse_send.at[level],
            recv_sem=lse_recv.at[2 * (z // 2) + g],
            device_id=(level, f, parity), device_id_type=MESH,
        )

        @pl.when((z != level) | (g != parity))
        def _():
            copy.start()

    lse_keep = pltpu.make_async_copy(lse, lse_place, lse_near)

    @pl.when(g == parity)
    def _():
        lse_keep.start()

    out_send = remote(out_away, out_got, at.core)
    operands = [local(xn, xn_v), local(d_qkv, d_qkv_v), local(attn, attn_v), local(da, da_v)]
    sums_send = remote(sums, sums_got.at[0], at.core)

    groups = []
    used = 0
    for source, rows, put, ready in (
        (down, nf, put_down, True),
        (gate, feat, put_pair(gate_o, 0, 3), True),
        (gate_last, feat, put_pair(gate_o, 3, 1), False),
        (up.at[:, 0 : 2 * nf], feat, put_pair(up_o, 0, 2), False),
        (up.at[:, 2 * nf : 4 * nf], feat, put_pair(up_o, 2, 2), False),
        (qkv.at[:, 0:nq], feat, put_query, False),
        (qkv.at[:, nq : nq + 2 * nk], feat, put_key_value, False),
        (out_mine, feat, put_out, False),
    ):
        group = Group(source, rows, put)
        groups.append(group)
        mid = rows // 2
        group.acc, group.outer, group.inner, group.done = buffers[used : used + 4]
        used += 4
        if ready:
            group.load = local(source, group.acc)
            if source is down:
                group.load_in = local(down_in, group.outer)
        else:
            group.mid, group.got, group.late = buffers[used : used + 3]
            used += 3
            group.sends = [
                remote(source.at[rows_at(at.fd * rows, mid)], group.got.at[1], at.x),
                remote(source.at[rows_at(at.fd * rows + mid, mid)], group.got.at[3], at.y),
                remote(source.at[rows_at(at.fx * rows, mid)], group.got.at[0], at.x),
                remote(source.at[rows_at(at.fy * rows + mid, mid)], group.got.at[2], at.y),
            ]
            group.loads = [
                local(source.at[rows_at(at.fy * rows, mid)], group.mid.at[0]),
                local(source.at[rows_at(at.fx * rows + mid, mid)], group.mid.at[1]),
                local(source.at[rows_at(f * rows, rows)], group.acc),
            ]
            group.second = [
                remote(group.mid.at[0], group.late.at[0], at.y),
                remote(group.mid.at[1], group.late.at[1], at.x),
            ]
        i = taken[0]
        taken[0] += 6
        group.first = i

        def inward(part, slot, group=group, i=i):
            return between(i + slot, group.acc.at[part], group.outer.at[part], toward)

        group.inward = inward

        def crossing(keep, give, i=i, group=group):
            return (
                between(i + 2, group.acc.at[give], group.inner, other),
                between(i + 3, group.done.at[keep], group.done.at[keep], other),
                between(i + 4, group.done.at[keep], group.done.at[keep], outward),
                between(i + 5, group.done.at[give], group.done.at[give], outward),
            )

        group.crossing = crossing
        pairs = group.put(group.done)
        group.shares = [remote(src_ref, dst_ref, at.core) for src_ref, dst_ref in pairs]
        group.stores = [local(src_ref, dst_ref) for src_ref, dst_ref in pairs]

    def by_end(group, step):
        @pl.when(z == 0)
        def _():
            step(group.low, group.top)

        @pl.when(z == 3)
        def _():
            step(group.top, group.low)

    def by_side(group, step):
        @pl.when(z == 1)
        def _():
            step(group.top, group.low, group.crossing(group.top, group.low))

        @pl.when(z == 2)
        def _():
            step(group.low, group.top, group.crossing(group.low, group.top))

    def b1(group):
        for copy in group.sends[:2] + group.loads:
            copy.start()

    def b0(group):
        for copy in group.sends[2:]:
            copy.start()

    def h1(group):
        for i, which in ((0, 1), (1, 3)):
            group.sends[i].wait_recv()
            group.loads[i].wait()
            add_rows(group.mid.at[i], group.mid.at[i], group.got.at[which])
            group.second[i].start()

    def h0(group):
        group.loads[2].wait()
        for i, part, which in ((2, group.top, 0), (3, group.low, 2)):
            group.sends[i].wait_recv()
            add_rows(group.acc.at[part], group.acc.at[part], group.got.at[which])

    def pl_(group):
        for i, part in ((0, group.top), (1, group.low)):
            group.second[i].wait_recv()
            add_rows(group.acc.at[part], group.acc.at[part], group.late.at[i])

    def gi(group):
        if group is e:
            e.load.wait()
        by_end(group, lambda give, keep: group.inward(give, 0).start())

    def gw(group):
        by_end(group, lambda give, keep: group.inward(give, 0).wait_send())

    def ke(group):
        by_end(group, lambda give, keep: group.inward(keep, 1).start())

    def kw(group):
        by_end(group, lambda give, keep: group.inward(keep, 1).wait_send())

    def en(group):
        if group is d:
            d.load.wait()
            d.load_in.wait()

        def step(keep, give, copies):
            if group is not d:
                group.inward(give, 0).wait_recv()
            add_rows(group.acc.at[give], group.acc.at[give], group.outer.at[give])
            copies[0].start()

        by_side(group, step)

    def jo(group):
        def step(keep, give, copies):
            if group is not d:
                group.inward(keep, 1).wait_recv()
            add_rows(group.acc.at[keep], group.acc.at[keep], group.outer.at[keep])

        by_side(group, step)

    def se(group):
        def step(keep, give, copies):
            copies[0].wait_recv()
            add_rows(group.done.at[keep], group.acc.at[keep], group.inner)
            copies[1].start()

        by_side(group, step)

    def za(group):
        by_side(group, lambda keep, give, copies: copies[2].start())

    def fi(group):
        by_side(group, lambda keep, give, copies: copies[1].wait_recv())

    def wa(group):
        by_side(group, lambda keep, give, copies: copies[2].wait_send())

    def zb(group):
        by_side(group, lambda keep, give, copies: copies[3].start())

    def de(group):
        def end(give, keep):
            copies = group.crossing(keep, give)
            copies[2].wait_recv()
            copies[3].wait_recv()

        by_end(group, end)

        def step(keep, give, copies):
            for i in (0, 1, 3):
                copies[i].wait_send()

        by_side(group, step)
        for copy in group.shares + group.stores:
            copy.start()

    d, e, last, u, v, q, r, o = groups
    for copy in [e.load, d.load, d.load_in, sums_send] + operands:
        copy.start()
    steps = {
        "b1": b1, "b0": b0, "h1": h1, "h0": h0, "pl": pl_, "gi": gi, "gw": gw, "ke": ke, "kw": kw,
        "en": en, "jo": jo, "se": se, "za": za, "fi": fi, "wa": wa, "zb": zb, "de": de,
    }
    named = {"d": d, "e": e, "f": last, "u": u, "v": v, "q": q, "r": r, "o": o}

    over_x = remote(sums_o, sums_got.at[1], at.x)
    over_y = remote(sums_o, sums_got.at[2], at.y)
    sums_in = remote(sums_o, sums_got.at[3], toward)
    sums_mid = remote(sums_o, sums_got.at[4], other)
    sums_out = remote(sums_o, sums_got.at[5], outward)

    def sums_1():
        sums_send.wait_recv()
        sums_o[...] = sums[...] + sums_got[0]
        over_x.start()

    def sums_2():
        over_x.wait()
        sums_o[...] += sums_got[1]
        over_y.start()

    def sums_3():
        over_y.wait()
        sums_o[...] += sums_got[2]

        @pl.when(is_outer)
        def _():
            sums_in.start()

    def sums_4():
        @pl.when(is_inner)
        def _():
            sums_in.wait_recv()
            sums_o[...] += sums_got[3]
            sums_mid.start()

    def sums_5():
        @pl.when(is_inner)
        def _():
            sums_mid.wait()
            sums_o[...] += sums_got[4]
            sums_out.start()

    def out_gradient():
        for copy in operands[2:]:
            copy.wait()
        tile = wide // 2
        for ref, core in ((out_away, 1 - g), (out_mine, g)):


            @pl.loop(0, 2)
            def _(n):
                cols = rows_at(core * wide + n * tile, tile)
                ref[:, rows_at(n * tile, tile)] = mm(attn_v[...], da_v[:, cols]).astype(ref.dtype)

            if ref is out_away:
                out_send.start()

    def qkv_gradient():
        for copy in operands[:2]:
            copy.wait()
        tile = 2 * TILE

        @pl.loop(0, qkv.shape[1] // tile)
        def _(n):
            cols = rows_at(n * tile, tile)
            qkv[:, cols] = mm(xn_v[...], d_qkv_v[:, cols], ((0,), (0,))).astype(qkv.dtype)

    def out_sum():
        out_send.wait_recv()
        add_rows(out_mine, out_mine, out_got)

    single = {
        "s1": sums_1, "s2": sums_2, "s3": sums_3, "s4": sums_4, "s5": sums_5,
        "go": out_gradient, "gq": qkv_gradient, "ao": out_sum,
    }
    for name in ORDER:
        if len(name) == 2:
            single[name]()
        else:
            steps[name[:2]](named[name[2]])

    @pl.when(is_outer)
    def _():
        sums_in.wait_send()
        sums_out.wait_recv()
        sums_o[...] = sums_got[5]

    @pl.when(is_inner)
    def _():
        sums_out.wait_send()

    sums_send.wait_send()
    out_send.wait_send()
    for group in (last, u, v, q, r, o):
        for copy in group.sends + group.second:
            copy.wait_send()
    for group in groups:
        for copy in group.stores:
            copy.wait()
        for copy in group.shares:
            copy.wait_send()
            copy.wait_recv()
    for level in range(chips):
        copy = pltpu.make_async_remote_copy(
            src_ref=lse, dst_ref=lse_place, send_sem=lse_send.at[level], recv_sem=lse_recv.at[level],
            device_id=(level, f, parity), device_id_type=MESH,
        )

        @pl.when((z != level) | (g != parity))
        def _():
            copy.wait_send()

        @pl.when((z != 2 * (level // 2) + g) | (g != level % 2))
        def _():
            copy.wait_recv()

    @pl.when(g == parity)
    def _():
        lse_keep.wait()


def collect(down, down_in, gate, gate_last, up, xn, d_qkv, attn, da, sums, lse, nq, nk):
    bf = jnp.bfloat16
    buffers = []
    wide = da.shape[1] // 2
    feat = gate.shape[0]
    for rows, cols, ready in (
        (down.shape[0], down.shape[1], True),
        (gate.shape[0], gate.shape[1], True),
        (feat, gate_last.shape[1], False),
        (feat, up.shape[1] // 2, False),
        (feat, up.shape[1] // 2, False),
        (feat, nq, False),
        (feat, 2 * nk, False),
        (attn.shape[0] // 4, wide, False),
    ):
        mid = rows // 2
        buffers += [
            pltpu.VMEM((rows, cols), bf),
            pltpu.VMEM((rows, cols), bf),
            pltpu.VMEM((mid, cols), bf),
            pltpu.VMEM((rows, cols), bf),
        ]
        if not ready:
            buffers += [
                pltpu.VMEM((2, mid, cols), bf),
                pltpu.VMEM((4, mid, cols), bf),
                pltpu.VMEM((2, mid, cols), bf),
            ]
    return pl.pallas_call(
        collect_kernel,
        in_specs=[ANY] * 9 + [VM, VM],
        out_specs=[ANY] * 7 + [VM, VM],
        out_shape=[
            bf16_like(2 * down.shape[0], down.shape[1]),
            bf16_like(feat, 2 * up.shape[1]),
            bf16_like(feat, 2 * up.shape[1]),
            bf16_like(feat, 2 * nq),
            bf16_like(feat, 2 * nk),
            bf16_like(feat, 2 * nk),
            bf16_like(feat, da.shape[1]),
            f32_like(*sums.shape),
            f32_like(4, *lse.shape),
        ],
        scratch_shapes=[
            pltpu.SemaphoreType.DMA((112,)),
            pltpu.SemaphoreType.DMA((112,)),
            pltpu.SemaphoreType.DMA((48,)),
            pltpu.SemaphoreType.DMA((4,)),
            pltpu.SemaphoreType.DMA((4,)),
            pltpu.SemaphoreType.DMA,
            pltpu.VMEM((attn.shape[0], wide), bf),
            pltpu.VMEM((attn.shape[0], wide), bf),
            pltpu.VMEM((6,) + sums.shape, jnp.float32),
            pltpu.VMEM((attn.shape[0], wide), bf),
            pltpu.VMEM((xn.shape[1], d_qkv.shape[1]), bf),
            pltpu.VMEM(xn.shape, bf),
            pltpu.VMEM(d_qkv.shape, bf),
            pltpu.VMEM(attn.shape, bf),
            pltpu.VMEM(da.shape, bf),
        ]
        + buffers,
        compiler_params=pltpu.CompilerParams(
            collective_id=1, has_side_effects=True, vmem_limit_bytes=62 * 1024 * 1024
        ),
        cost_estimate=cost(0, 500e6),
        name="collect",
    )(down, down_in, gate, gate_last, up, xn, d_qkv, attn, da, sums, lse)


def widen_kernel(spot, dealing, lse, sums, *refs):
    totals, first, second = refs[-3:]
    half = (len(refs) - 3) // 2
    for narrow, wide in zip(refs[:half], refs[half:-3]):
        wide[...] = fp32(narrow[...])

    @pl.when(pl.program_id(0) == 0)
    def _():
        shard = rows_at(spot[1] * first.shape[0], first.shape[0])
        first[...] = sums[0, shard]
        second[...] = sums[1, shard]
        heads = lse.shape[1]
        for r in range(4):
            for i in range(4):

                @pl.when(dealing[r, i] == spot[0])
                def _():
                    col = (4 * r + i) % 8 * BLK
                    for core in range(2):
                        totals[core * heads : (core + 1) * heads, r * BLK : (r + 1) * BLK] = lse[
                            2 * (r // 2) + core, :, col : col + BLK
                        ]


def widen(spot, dealing, lse, sums, arrays, steps=8):
    specs = [pl.BlockSpec((a.shape[0] // steps, a.shape[1]), lambda n: (n, 0)) for a in arrays]
    shard = sums.shape[1] // 4
    return pl.pallas_call(
        widen_kernel,
        grid=(steps,),
        in_specs=[SMEM, SMEM, VM, VM] + specs,
        out_specs=specs + [VM] * 3,
        out_shape=[f32_like(*a.shape) for a in arrays]
        + [f32_like(2 * lse.shape[1], 4 * BLK), f32_like(shard), f32_like(shard)],
        compiler_params=PARAMS,
        cost_estimate=cost(0, 40e6),
        name="widen",
    )(spot, dealing, lse, sums, *arrays)


def turning_tables(seq):
    half = HEAD_SIZE // 2
    frequency = ROPE_BASE ** (-2.0 * np.arange(half) / (2 * half))
    low = frequency[:, None] * np.arange(BLK)[None, :]
    high = frequency[:, None] * (BLK * np.arange(seq // BLK))[None, :]
    return tuple(part.astype(np.float32) for part in (np.cos(low), np.sin(low), np.cos(high), np.sin(high)))


def chip_local(
    tokens,
    seq_lengths,
    dealing,
    first_gain,
    query_weight,
    key_matrix,
    value_matrix,
    out_weight,
    second_gain,
    gate_weight,
    up_weight,
    down_weight,
    cotangent,
):
    ctx = lax.axis_size("ctx")
    z = lax.axis_index("ctx")
    f = lax.axis_index("fsdp")
    g = lax.axis_index("grp")
    parity = z % 2
    parity_core = g == parity
    width = tokens.shape[2]
    tok = tokens.shape[1]
    seq = 2 * tok
    place = jnp.stack([g, parity]).astype(jnp.int32)

    def over_x(field):
        return lax.ppermute(field, "fsdp", [(i, i ^ 1) for i in range(4)])

    def over_y(field):
        return lax.ppermute(field, "fsdp", [(i, i ^ 2) for i in range(4)])

    def over_core(field):
        return lax.ppermute(field, "grp", [(0, 1), (1, 0)])

    swap_pairs = [(2 * i + (1 - i % 2), 2 * (i ^ 1) + i % 2) for i in range(ctx)]

    def swap(field):
        got = lax.ppermute(field, ("ctx", "grp"), swap_pairs)
        return jnp.where(parity_core, field, got)

    def along(field, pairs):
        return lax.ppermute(field, "ctx", pairs)

    def cut(field, start, size, axis):
        return lax.dynamic_slice_in_dim(field, start, size, axis)

    def in_order(mine, other, axis=0):
        first = jnp.where(g == 0, mine, other)
        second = jnp.where(g == 0, other, mine)
        return jnp.concatenate([first, second], axis=axis)

    heads_q = query_weight.shape[1] // 2
    heads_k = key_matrix.shape[1] // 2
    part_ff = down_weight.shape[0] // 2
    rows_in = gate_weight.shape[0]

    row = lax.broadcasted_iota(jnp.int32, (1, 8, first_gain.shape[0]), 1)
    gain_own = jnp.where(row == 0, fp32(first_gain), jnp.where(row == 1, fp32(second_gain), 0.0))
    qkv_w, out_w, pair_w, down_own, x_seq, dy_all, gain_all, xn_one, qkv_t = gather_all(
        tokens, cotangent, query_weight, key_matrix, value_matrix, out_weight,
        gate_weight, up_weight, down_weight, gain_own,
    )
    down_w = lax.all_gather(down_own, "fsdp", axis=0, tiled=True)

    tables = turning_tables(seq)

    attn_keep, attn_send, lse, q_t, k_t, v_t = attend_seq(place, qkv_t, tables)
    attn_got = over_core(attn_send)
    h_own, xn_own, attn_mine = residual(place, x_seq, attn_keep, attn_got, gain_all, out_w)
    hidden, for_gate, act, xn_two = hidden_step(place, xn_own, over_core(xn_own), pair_w)
    d_gate, d_up = hidden_back(dy_all, down_w, for_gate, act)
    bf = jnp.bfloat16
    tokens_in = ((0,), (0,))
    down_grad = mm(hidden, dy_all, tokens_in, bf)
    most = 3 * part_ff
    gate_grad = mm(xn_two, d_gate[:, :most], tokens_in, bf)
    down_plane = lax.psum_scatter(down_grad, "fsdp", scatter_dimension=0, tiled=True)
    down_in = along(down_plane, [(0, 1), (3, 2)])
    gate_plane = lax.psum_scatter(gate_grad, "fsdp", scatter_dimension=0, tiled=True)
    d_gate, d_up, hidden, _, _ = lax.optimization_barrier((d_gate, d_up, hidden, down_grad, gate_grad))
    dn_own, dn_send = back_step(place, d_gate, d_up, pair_w)
    dn_got = over_core(dn_send)
    res_own, res_send = result_step(place, hidden, h_own, down_w)
    up_grad = mm(xn_two, d_up, tokens_in, bf)
    gate_last = mm(xn_two, d_gate[:, most:], tokens_in, bf)
    layer_out = swap((res_own + fp32(over_core(res_send))).astype(bf))

    dh_own, da, dattn_keep, dattn_send, gain_two_part = entry_step(
        place, dn_own, dn_got, h_own, dy_all, gain_all, out_w
    )
    dattn_got = over_core(dattn_send)
    q_t, _, up_grad = lax.optimization_barrier((q_t, down_plane, up_grad))
    dq_t, dk_t, dv_t = attend_seq_back(
        place, q_t, k_t, v_t, dattn_keep, dattn_got, lse, tables
    )
    half_width = width // 2
    d1_own, d1_send, d_qkv = inputs_step(place, dq_t, dk_t, dv_t, qkv_w)
    dh_own, down_in = lax.optimization_barrier((dh_own, down_in))
    dx, gain_one_part = last_step(place, d1_own, over_core(d1_send), x_seq, dh_own, gain_all)
    tokens_grad = swap(dx)

    parts = jnp.concatenate([gain_one_part, gain_two_part])
    down_sum, gate_sum, up_sum, query_sum, key_sum, value_sum, out_sum, sums, all_lse = collect(
        down_plane, down_in, gate_plane, gate_last, up_grad, xn_one, d_qkv, attn_mine, da,
        jnp.pad(parts, ((0, 6), (0, 0))), lse.reshape(-1, seq), heads_q, heads_k,
    )
    query_out, key_out, value_out, out_out, gate_out, up_out, down_out, totals, gain_one, gain_two = widen(
        jnp.stack([z, f]).astype(jnp.int32), dealing[0], all_lse, sums,
        (query_sum, key_sum, value_sum, out_sum, gate_sum, up_sum, down_sum),
    )

    return (
        layer_out[None],
        tokens_grad[None],
        totals[None],
        gain_one,
        query_out,
        key_out,
        value_out,
        out_out,
        gain_two,
        gate_out,
        up_out,
        down_out,
    )


def chip_holds_sequence(mesh, tokens, seq_lengths):
    sizes = dict(mesh.shape)
    packs, length, _ = tokens.shape
    count = seq_lengths.shape[1]
    return (
        sizes["fsdp"] == 4
        and sizes["grp"] == 2
        and sizes["ctx"] == 4
        and packs == sizes["fsdp"] * sizes["grp"]
        and length == count * MINLEN
        and 2 * length == sizes["ctx"] * MINLEN
    )


def solution(mesh):
    placed = (
        P(("fsdp", "grp"), "ctx", None),
        P(("fsdp", "grp"), None),
        P(("fsdp", "grp"), None, None),
        P("fsdp"),
        P("fsdp", None),
        P("fsdp", None),
        P("fsdp", None),
        P("fsdp", None),
        P("fsdp"),
        P("fsdp", None),
        P("fsdp", None),
        P("fsdp", None),
        P(("fsdp", "grp"), "ctx", None),
    )
    results = (
        P(("fsdp", "grp"), "ctx", None),
        P(("fsdp", "grp"), "ctx", None),
        P(("fsdp", "grp"), None, "ctx"),
        P("fsdp"),
        P("fsdp", None),
        P("fsdp", None),
        P("fsdp", None),
        P("fsdp", None),
        P("fsdp"),
        P("fsdp", None),
        P("fsdp", None),
        P("fsdp", None),
    )

    def program(*arrays):
        body = chip_local if chip_holds_sequence(mesh, arrays[0], arrays[1]) else local
        return jax.shard_map(
            body, mesh=mesh, in_specs=placed, out_specs=results, check_vma=False
        )(*arrays)

    return program
```

```python
import jax
import jax.numpy as jnp
import numpy as np
from jax import lax
from jax.experimental import pallas as pl
from jax.experimental.pallas import tpu as pltpu
from jax.sharding import PartitionSpec as P

QUERY_HEADS = 16
KEY_VALUE_HEADS = 8
HEAD_SIZE = 96
BLK = 128


EPS = 1e-05
ROPE_BASE = 100000.0
MASKED = -1e30


def place_rows(positions, lengths):
    ends = jnp.cumsum(lengths, axis=-1)
    before = positions[..., :, None] >= ends[..., None, :]
    segment = jnp.sum(before.astype(jnp.int32), axis=-1)
    offset = jnp.sum(jnp.where(before, lengths[..., None, :], 0), axis=-1)
    return (segment, positions - offset)


def rotation(relative, half_size):
    frequency = ROPE_BASE ** (-(2.0 * jnp.arange(half_size, dtype=jnp.float32)) / (2 * half_size))
    angles = relative.astype(jnp.float32)[:, None] * frequency[None, :]
    return (jnp.cos(angles), jnp.sin(angles))


def rotate(field, cosine, sine_part):
    row_count = field.shape[0]
    half_size = cosine.shape[-1]
    split_heads = field.reshape(row_count, -1, 2 * half_size)
    front_half = split_heads[..., :half_size]
    back_half = split_heads[..., half_size:]
    cos_rows = cosine[:, None, :]
    sin_rows = sine_part[:, None, :]
    turned = jnp.concatenate(
        [
            front_half * cos_rows - back_half * sin_rows,
            back_half * cos_rows + front_half * sin_rows,
        ],
        axis=-1,
    )
    return turned.reshape(row_count, -1)


def rms_back(d_normed, normed, scale):
    return scale * (d_normed - normed * jnp.mean(d_normed * normed, axis=-1, keepdims=True))


def score_block(query_part, key_part, visible):
    scores = jnp.einsum(
        "rgd,kd->grk", query_part, key_part, preferred_element_type=jnp.float32
    ) * HEAD_SIZE ** (-0.5)
    return jnp.where(visible[None], scores, MASKED)


def attend_pack(query_pack, key_pack, value_pack, visible_list):
    token_count = query_pack.shape[0]
    rounds = len(visible_list)
    query_group_width = QUERY_HEADS // KEY_VALUE_HEADS
    context_count = key_pack.shape[0] // token_count

    def width_per_head(head_index, carry):
        out_buf, total_buf = carry
        query_head = lax.dynamic_slice_in_dim(
            query_pack, head_index * query_group_width * HEAD_SIZE, query_group_width * HEAD_SIZE, 1
        ).reshape(token_count, query_group_width, HEAD_SIZE)
        key_head = lax.dynamic_slice_in_dim(key_pack, head_index * HEAD_SIZE, HEAD_SIZE, 1).reshape(
            context_count, rounds, BLK, HEAD_SIZE
        )
        value_head = lax.dynamic_slice_in_dim(
            value_pack, head_index * HEAD_SIZE, HEAD_SIZE, 1
        ).reshape(context_count, rounds, BLK, HEAD_SIZE)
        running_top = jnp.full((query_group_width, token_count), MASKED, jnp.float32)
        running_sum = jnp.zeros((query_group_width, token_count), jnp.float32)
        for round_index in range(rounds):
            first_row = round_index * BLK
            scores = score_block(
                query_head[first_row:],
                key_head[:, round_index].reshape(-1, HEAD_SIZE),
                visible_list[round_index],
            )
            new_top = jnp.maximum(running_top[:, first_row:], jnp.max(scores, axis=-1))
            weights = jnp.where(
                visible_list[round_index][None], jnp.exp(scores - new_top[..., None]), 0.0
            )
            new_sum = running_sum[:, first_row:] * jnp.exp(
                running_top[:, first_row:] - new_top
            ) + jnp.sum(weights, axis=-1)
            running_top = running_top.at[:, first_row:].set(new_top)
            running_sum = running_sum.at[:, first_row:].set(new_sum)
        log_totals = running_top + jnp.log(running_sum)
        mixture = jnp.zeros((token_count, query_group_width, HEAD_SIZE), jnp.float32)
        for round_index in range(rounds):
            first_row = round_index * BLK
            scores = score_block(
                query_head[first_row:],
                key_head[:, round_index].reshape(-1, HEAD_SIZE),
                visible_list[round_index],
            )
            prob_bf = jnp.where(
                visible_list[round_index][None],
                jnp.exp(scores - log_totals[:, first_row:, None]),
                0.0,
            ).astype(jnp.bfloat16)
            mixture = mixture.at[first_row:].add(
                jnp.einsum(
                    "grk,kd->rgd",
                    prob_bf,
                    value_head[:, round_index].reshape(-1, HEAD_SIZE),
                    preferred_element_type=jnp.float32,
                )
            )
        out_buf = lax.dynamic_update_slice_in_dim(
            out_buf,
            mixture.astype(jnp.bfloat16).reshape(token_count, -1),
            head_index * query_group_width * HEAD_SIZE,
            1,
        )
        total_buf = lax.dynamic_update_slice_in_dim(
            total_buf, log_totals, head_index * query_group_width, 0
        )
        return (out_buf, total_buf)

    start_offsets = (
        jnp.zeros((token_count, QUERY_HEADS * HEAD_SIZE), jnp.bfloat16),
        jnp.zeros((QUERY_HEADS, token_count), jnp.float32),
    )
    return lax.fori_loop(0, KEY_VALUE_HEADS, width_per_head, start_offsets)


def attend_back(
    query_pack, key_pack, value_pack, grad_pack, attended_pack, total_pack, visible_list
):
    token_count = query_pack.shape[0]
    rounds = len(visible_list)
    query_group_width = QUERY_HEADS // KEY_VALUE_HEADS
    context_count = key_pack.shape[0] // token_count

    def width_per_head(head_index, carry):
        query_buf, key_buf, value_buf = carry
        query_head = lax.dynamic_slice_in_dim(
            query_pack, head_index * query_group_width * HEAD_SIZE, query_group_width * HEAD_SIZE, 1
        ).reshape(token_count, query_group_width, HEAD_SIZE)
        grad_head = lax.dynamic_slice_in_dim(
            grad_pack, head_index * query_group_width * HEAD_SIZE, query_group_width * HEAD_SIZE, 1
        ).reshape(token_count, query_group_width, HEAD_SIZE)
        output_head = lax.dynamic_slice_in_dim(
            attended_pack,
            head_index * query_group_width * HEAD_SIZE,
            query_group_width * HEAD_SIZE,
            1,
        ).reshape(token_count, query_group_width, HEAD_SIZE)
        key_head = lax.dynamic_slice_in_dim(key_pack, head_index * HEAD_SIZE, HEAD_SIZE, 1).reshape(
            context_count, rounds, BLK, HEAD_SIZE
        )
        value_head = lax.dynamic_slice_in_dim(
            value_pack, head_index * HEAD_SIZE, HEAD_SIZE, 1
        ).reshape(context_count, rounds, BLK, HEAD_SIZE)
        log_totals = lax.dynamic_slice_in_dim(
            total_pack, head_index * query_group_width, query_group_width, 0
        )
        delta = jnp.sum(grad_head.astype(jnp.float32) * output_head.astype(jnp.float32), axis=-1).T
        query_grad = jnp.zeros((token_count, query_group_width, HEAD_SIZE), jnp.float32)
        key_parts = []
        value_parts = []
        for round_index in range(rounds):
            first_row = round_index * BLK
            key_round = key_head[:, round_index].reshape(-1, HEAD_SIZE)
            value_round = value_head[:, round_index].reshape(-1, HEAD_SIZE)
            scores = score_block(query_head[first_row:], key_round, visible_list[round_index])
            probs_full = jnp.where(
                visible_list[round_index][None],
                jnp.exp(scores - log_totals[:, first_row:, None]),
                0.0,
            )
            d_probs = jnp.einsum(
                "rgd,kd->grk",
                grad_head[first_row:],
                value_round,
                preferred_element_type=jnp.float32,
            )
            d_scores = (
                HEAD_SIZE ** (-0.5) * probs_full * (d_probs - delta[:, first_row:, None])
            ).astype(jnp.bfloat16)
            value_parts.append(
                jnp.einsum(
                    "grk,rgd->kd",
                    probs_full.astype(jnp.bfloat16),
                    grad_head[first_row:],
                    preferred_element_type=jnp.float32,
                )
            )
            key_parts.append(
                jnp.einsum(
                    "grk,rgd->kd",
                    d_scores,
                    query_head[first_row:],
                    preferred_element_type=jnp.float32,
                )
            )
            query_grad = query_grad.at[first_row:].add(
                jnp.einsum("grk,kd->rgd", d_scores, key_round, preferred_element_type=jnp.float32)
            )
        key_block = jnp.stack(
            [part.reshape(context_count, BLK, HEAD_SIZE) for part in key_parts], axis=1
        ).reshape(-1, HEAD_SIZE)
        value_block = jnp.stack(
            [part.reshape(context_count, BLK, HEAD_SIZE) for part in value_parts], axis=1
        ).reshape(-1, HEAD_SIZE)
        query_buf = lax.dynamic_update_slice_in_dim(
            query_buf,
            query_grad.reshape(token_count, -1),
            head_index * query_group_width * HEAD_SIZE,
            1,
        )
        key_buf = lax.dynamic_update_slice_in_dim(key_buf, key_block, head_index * HEAD_SIZE, 1)
        value_buf = lax.dynamic_update_slice_in_dim(
            value_buf, value_block, head_index * HEAD_SIZE, 1
        )
        return (query_buf, key_buf, value_buf)

    start_offsets = (
        jnp.zeros((token_count, QUERY_HEADS * HEAD_SIZE), jnp.float32),
        jnp.zeros((context_count * token_count, KEY_VALUE_HEADS * HEAD_SIZE), jnp.float32),
        jnp.zeros((context_count * token_count, KEY_VALUE_HEADS * HEAD_SIZE), jnp.float32),
    )
    return lax.fori_loop(0, KEY_VALUE_HEADS, width_per_head, start_offsets)


def local(
    tokens,
    seq_lengths,
    dealing,
    first_gain,
    query_weight,
    key_matrix,
    value_matrix,
    out_weight,
    second_gain,
    gate_weight,
    up_weight,
    down_weight,
    cotangent,
):
    context_count = lax.axis_size("ctx")
    my_index = lax.axis_index("ctx")
    pack_count, token_count, model_dim = tokens.shape
    rounds = token_count // BLK
    spread = context_count // rounds
    ctx_range = jnp.arange(context_count, dtype=jnp.int32)
    matches = (dealing[..., None] == ctx_range).astype(jnp.int32)
    slot_of = jnp.sum(matches * ctx_range[:, None], axis=2)
    block_of = jnp.arange(rounds, dtype=jnp.int32)[None, :, None] * context_count + slot_of
    key_pos = (
        jnp.transpose(block_of, (0, 2, 1))[..., None] * BLK + jnp.arange(BLK, dtype=jnp.int32)
    ).reshape(pack_count, -1)
    key_seg = place_rows(key_pos, seq_lengths)[0]
    query_pos = lax.dynamic_slice_in_dim(key_pos, my_index * token_count, token_count, 1)
    query_seg, query_rel = place_rows(query_pos, seq_lengths)
    home_row = lax.dynamic_index_in_dim(dealing, my_index // spread, 1, False)
    targets = lax.dynamic_slice_in_dim(home_row, my_index % spread * rounds, rounds, 1)
    picker = (targets[:, None, :] == ctx_range[None, :, None]).astype(jnp.bfloat16)
    my_slots = lax.dynamic_index_in_dim(slot_of, my_index, 2, False)
    owner_index = (
        jnp.arange(rounds, dtype=jnp.int32)[None, :] * context_count + my_slots
    ) // rounds
    keep_slot = jnp.repeat(owner_index, spread, axis=1) == ctx_range[None, :]

    def spread_out(field):
        blocks = field.reshape(pack_count, rounds, BLK, model_dim)
        return jnp.einsum(
            "pkj,pjtd->pktd", picker, blocks, preferred_element_type=jnp.float32
        ).astype(jnp.bfloat16)

    def collect(received):
        grouped = received.reshape(pack_count, rounds, spread, BLK, model_dim)
        return (
            jnp.sum(grouped, axis=2, dtype=jnp.float32)
            .astype(jnp.bfloat16)
            .reshape(pack_count * token_count, model_dim)
        )

    def send_home(field):
        blocks = jnp.repeat(field.reshape(pack_count, rounds, BLK, model_dim), spread, axis=1)
        return jnp.where(keep_slot[:, :, None, None], blocks, jnp.zeros_like(blocks))

    def restore(returned):
        placed = jnp.einsum("pkj,pktd->pjtd", picker, returned, preferred_element_type=jnp.float32)
        return placed.astype(jnp.bfloat16).reshape(pack_count, token_count, model_dim)

    dealt_tokens, dealt_upstream = (
        lax.all_to_all(spread_out(tokens), "ctx", split_axis=1, concat_axis=1, tiled=True),
        lax.all_to_all(spread_out(cotangent), "ctx", split_axis=1, concat_axis=1, tiled=True),
    )
    inputs = collect(dealt_tokens)
    upstream = collect(dealt_upstream)
    gain_one, query_full, key_full, value_full, out_full = (
        lax.all_gather(first_gain, "fsdp", axis=0, tiled=True),
        lax.all_gather(query_weight, "fsdp", axis=0, tiled=True),
        lax.all_gather(key_matrix, "fsdp", axis=0, tiled=True),
        lax.all_gather(value_matrix, "fsdp", axis=0, tiled=True),
        lax.all_gather(out_weight, "fsdp", axis=0, tiled=True),
    )
    gain_two, gate_full, up_full, down_full = (
        lax.all_gather(second_gain, "fsdp", axis=0, tiled=True),
        lax.all_gather(gate_weight, "fsdp", axis=0, tiled=True),
        lax.all_gather(up_weight, "fsdp", axis=0, tiled=True),
        lax.all_gather(down_weight, "fsdp", axis=0, tiled=True),
    )
    gain_one32 = gain_one.astype(jnp.float32)
    gain_two32 = gain_two.astype(jnp.float32)
    cosine, sine_part = rotation(query_rel.reshape(-1), HEAD_SIZE // 2)
    inputs32 = inputs.astype(jnp.float32)
    scale_one = lax.rsqrt(jnp.mean(inputs32 * inputs32, axis=-1, keepdims=True) + EPS)
    normed_one = inputs32 * scale_one
    xn_one = (normed_one * gain_one32).astype(jnp.bfloat16)
    query_rot = rotate(
        jnp.dot(xn_one, query_full, preferred_element_type=jnp.float32), cosine, sine_part
    ).astype(jnp.bfloat16)
    key_rot = rotate(
        jnp.dot(xn_one, key_full, preferred_element_type=jnp.float32), cosine, sine_part
    ).astype(jnp.bfloat16)
    rows_of_values = jnp.dot(xn_one, value_full, preferred_element_type=jnp.float32).astype(
        jnp.bfloat16
    )
    key_local = key_rot.reshape(pack_count, token_count, -1)
    value_local = rows_of_values.reshape(pack_count, token_count, -1)
    gathered_keys, gathered_values = (
        lax.all_gather(key_local, "ctx", axis=1, tiled=True),
        lax.all_gather(value_local, "ctx", axis=1, tiled=True),
    )
    key_pos_rounds = key_pos.reshape(pack_count, context_count, rounds, BLK)
    key_seg_rounds = key_seg.reshape(pack_count, context_count, rounds, BLK)
    visible = []
    for round_index in range(rounds):
        first_row = round_index * BLK
        round_pos = key_pos_rounds[:, :, round_index].reshape(pack_count, -1)
        round_seg = key_seg_rounds[:, :, round_index].reshape(pack_count, -1)
        same_seq = query_seg[:, first_row:, None] == round_seg[:, None, :]
        earlier = round_pos[:, None, :] <= query_pos[:, first_row:, None]
        visible.append(same_seq & earlier)
    query_packs = query_rot.reshape(pack_count, token_count, -1)
    pack_index = 0
    pack_visible = [mask[pack_index] for mask in visible]
    attended_pack, total_pack = attend_pack(
        query_packs[pack_index],
        gathered_keys[pack_index],
        gathered_values[pack_index],
        pack_visible,
    )
    total_list = [total_pack]
    softmax_totals = jnp.stack(total_list, axis=0)
    hidden_in = inputs32 + jnp.dot(attended_pack, out_full, preferred_element_type=jnp.float32)
    scale_two = lax.rsqrt(jnp.mean(hidden_in * hidden_in, axis=-1, keepdims=True) + EPS)
    normed_two = hidden_in * scale_two
    xn_two = (normed_two * gain_two32).astype(jnp.bfloat16)
    gate_val = jnp.dot(xn_two, gate_full, preferred_element_type=jnp.float32)
    up_val = jnp.dot(xn_two, up_full, preferred_element_type=jnp.float32)
    activated = jax.nn.silu(gate_val)
    hidden = (activated * up_val).astype(jnp.bfloat16)
    result = (hidden_in + jnp.dot(hidden, down_full, preferred_element_type=jnp.float32)).astype(
        jnp.bfloat16
    )
    down_grad = jnp.dot(hidden.T, upstream, preferred_element_type=jnp.float32)
    d_hidden = jnp.dot(upstream, down_full.T, preferred_element_type=jnp.float32)
    sigmoid_gate = jax.nn.sigmoid(gate_val)
    d_gate = (d_hidden * up_val * sigmoid_gate * (1.0 + gate_val * (1.0 - sigmoid_gate))).astype(
        jnp.bfloat16
    )
    d_up = (d_hidden * activated).astype(jnp.bfloat16)
    gate_grad = jnp.dot(xn_two.T, d_gate, preferred_element_type=jnp.float32)
    up_grad = jnp.dot(xn_two.T, d_up, preferred_element_type=jnp.float32)
    d_norm_two = jnp.dot(d_gate, gate_full.T, preferred_element_type=jnp.float32) + jnp.dot(
        d_up, up_full.T, preferred_element_type=jnp.float32
    )
    gain_two_grad = jnp.sum(d_norm_two * normed_two, axis=0)
    d_hidden_in = upstream.astype(jnp.float32) + rms_back(
        d_norm_two * gain_two32, normed_two, scale_two
    )
    mlp_parts = (
        lax.psum_scatter(
            gain_two_grad.astype(jnp.bfloat16), "fsdp", scatter_dimension=0, tiled=True
        ).astype(jnp.float32),
        lax.psum_scatter(
            gate_grad.astype(jnp.bfloat16), "fsdp", scatter_dimension=0, tiled=True
        ).astype(jnp.float32),
        lax.psum_scatter(
            up_grad.astype(jnp.bfloat16), "fsdp", scatter_dimension=0, tiled=True
        ).astype(jnp.float32),
        lax.psum_scatter(
            down_grad.astype(jnp.bfloat16), "fsdp", scatter_dimension=0, tiled=True
        ).astype(jnp.float32),
    )
    d_branch = d_hidden_in.astype(jnp.bfloat16)
    out_grad = jnp.dot(attended_pack.T, d_branch, preferred_element_type=jnp.float32)
    d_attended = jnp.dot(d_branch, out_full.T, preferred_element_type=jnp.float32).astype(
        jnp.bfloat16
    )
    back_keys, back_values = (gathered_keys, gathered_values)
    grad_packs = d_attended.reshape(pack_count, token_count, -1)
    out_packs = attended_pack.reshape(pack_count, token_count, -1)
    pack_index = 0
    pack_visible = [mask[pack_index] for mask in visible]
    query_part, key_part, value_part = attend_back(
        query_packs[pack_index],
        back_keys[pack_index],
        back_values[pack_index],
        grad_packs[pack_index],
        out_packs[pack_index],
        softmax_totals[pack_index],
        pack_visible,
    )
    key_list = [key_part]
    value_list = [value_part]
    d_keys, d_values = (
        lax.psum_scatter(
            jnp.stack(key_list, axis=0).astype(jnp.bfloat16), "ctx", scatter_dimension=1, tiled=True
        ).astype(jnp.float32),
        lax.psum_scatter(
            jnp.stack(value_list, axis=0).astype(jnp.bfloat16),
            "ctx",
            scatter_dimension=1,
            tiled=True,
        ).astype(jnp.float32),
    )
    d_query = rotate(query_part, cosine, -sine_part).astype(jnp.bfloat16)
    d_key = rotate(d_keys.reshape(pack_count * token_count, -1), cosine, -sine_part).astype(
        jnp.bfloat16
    )
    d_value = d_values.reshape(pack_count * token_count, -1).astype(jnp.bfloat16)
    query_grad = jnp.dot(xn_one.T, d_query, preferred_element_type=jnp.float32)
    key_grad = jnp.dot(xn_one.T, d_key, preferred_element_type=jnp.float32)
    value_grad = jnp.dot(xn_one.T, d_value, preferred_element_type=jnp.float32)
    d_norm_one = (
        jnp.dot(d_query, query_full.T, preferred_element_type=jnp.float32)
        + jnp.dot(d_key, key_full.T, preferred_element_type=jnp.float32)
        + jnp.dot(d_value, value_full.T, preferred_element_type=jnp.float32)
    )
    gain_one_grad = jnp.sum(d_norm_one * normed_one, axis=0)
    d_inputs = d_hidden_in + rms_back(d_norm_one * gain_one32, normed_one, scale_one)
    attn_parts = (
        lax.psum_scatter(
            gain_one_grad.astype(jnp.bfloat16), "fsdp", scatter_dimension=0, tiled=True
        ).astype(jnp.float32),
        lax.psum_scatter(
            query_grad.astype(jnp.bfloat16), "fsdp", scatter_dimension=0, tiled=True
        ).astype(jnp.float32),
        lax.psum_scatter(
            key_grad.astype(jnp.bfloat16), "fsdp", scatter_dimension=0, tiled=True
        ).astype(jnp.float32),
        lax.psum_scatter(
            value_grad.astype(jnp.bfloat16), "fsdp", scatter_dimension=0, tiled=True
        ).astype(jnp.float32),
        lax.psum_scatter(
            out_grad.astype(jnp.bfloat16), "fsdp", scatter_dimension=0, tiled=True
        ).astype(jnp.float32),
    )
    finished = (
        lax.psum(attn_parts[0].astype(jnp.bfloat16), ("ctx", "grp")).astype(jnp.float32),
        lax.psum(attn_parts[1].astype(jnp.bfloat16), ("ctx", "grp")).astype(jnp.float32),
        lax.psum(attn_parts[2].astype(jnp.bfloat16), ("ctx", "grp")).astype(jnp.float32),
        lax.psum(attn_parts[3].astype(jnp.bfloat16), ("ctx", "grp")).astype(jnp.float32),
        lax.psum(attn_parts[4].astype(jnp.bfloat16), ("ctx", "grp")).astype(jnp.float32),
        lax.psum(mlp_parts[0].astype(jnp.bfloat16), ("ctx", "grp")).astype(jnp.float32),
        lax.psum(mlp_parts[1].astype(jnp.bfloat16), ("ctx", "grp")).astype(jnp.float32),
        lax.psum(mlp_parts[2].astype(jnp.bfloat16), ("ctx", "grp")).astype(jnp.float32),
        lax.psum(mlp_parts[3].astype(jnp.bfloat16), ("ctx", "grp")).astype(jnp.float32),
    )
    home_out, home_grad = (
        lax.all_to_all(send_home(result), "ctx", split_axis=1, concat_axis=1, tiled=True),
        lax.all_to_all(
            send_home(d_inputs.astype(jnp.bfloat16)), "ctx", split_axis=1, concat_axis=1, tiled=True
        ),
    )
    return (
        restore(home_out),
        restore(home_grad),
        softmax_totals,
        finished[0],
        finished[1],
        finished[2],
        finished[3],
        finished[4],
        finished[5],
        finished[6],
        finished[7],
        finished[8],
    )


MINLEN = 1024
QB = 256
VMEM_LIMIT = 56 * 1024 * 1024


def fill_tables(cl_ref, sl_ref, ch_ref, sh_ref, c_ref, s_ref):
    @pl.when(pl.program_id(0) == 0)
    def _():
        cos_low, sin_low = cl_ref[...], sl_ref[...]
        for i in range(c_ref.shape[1] // BLK):
            at = slice(i * BLK, (i + 1) * BLK)
            cos_high, sin_high = ch_ref[:, i : i + 1], sh_ref[:, i : i + 1]
            c_ref[:, at] = cos_high * cos_low - sin_high * sin_low
            s_ref[:, at] = sin_high * cos_low + cos_high * sin_low


def attend_kernel(
    place, q_ref, k_ref, v_ref, cl_ref, sl_ref, ch_ref, sh_ref,
    keep_ref, send_ref, lse_ref, qr_ref, kr_ref, vr_ref, held, c_ref, s_ref,
):
    fill_tables(cl_ref, sl_ref, ch_ref, sh_ref, c_ref, s_ref)
    cosine = c_ref[...]
    sine = s_ref[...]
    half = HEAD_SIZE // 2
    seq = cosine.shape[1]

    def turn(field):
        front, back = field[:half], field[half:]
        return jnp.concatenate(
            [front * cosine - back * sine, back * cosine + front * sine], axis=0
        )

    k_rot = turn(k_ref[...])
    kr_ref[...] = k_rot.astype(jnp.bfloat16)
    key = k_rot.T.astype(jnp.bfloat16)
    val_t = v_ref[...].astype(jnp.bfloat16)
    vr_ref[...] = val_t
    q0 = turn(q_ref[:HEAD_SIZE]).astype(jnp.bfloat16)
    q1 = turn(q_ref[HEAD_SIZE:]).astype(jnp.bfloat16)
    qr_ref[:HEAD_SIZE] = q0
    qr_ref[HEAD_SIZE:] = q1
    rows = lax.broadcasted_iota(jnp.int32, (QB, 2 * QB), 0)
    cols = lax.broadcasted_iota(jnp.int32, (QB, 2 * QB), 1)
    keep = rows <= jnp.where(cols >= QB, cols - QB, cols)
    for b in range(seq // QB):
        lo, n = b * QB, (b + 1) * QB
        q_t = jnp.concatenate([q0[:, lo:n], q1[:, lo:n]], axis=1)
        scores = jnp.dot(key[:n], q_t, preferred_element_type=jnp.float32) * HEAD_SIZE ** (-0.5)
        diag = jnp.where(keep, scores[lo:], MASKED)
        top = jnp.max(diag, axis=0, keepdims=True)
        if b > 0:
            top = jnp.maximum(top, jnp.max(scores[:lo], axis=0, keepdims=True))
        e_diag = jnp.exp(diag - top)
        total = jnp.sum(e_diag, axis=0, keepdims=True)
        out = jnp.dot(val_t[:, lo:n], e_diag.astype(jnp.bfloat16), preferred_element_type=jnp.float32)
        if b > 0:
            e_rest = jnp.exp(scores[:lo] - top)
            total = total + jnp.sum(e_rest, axis=0, keepdims=True)
            out = out + jnp.dot(
                val_t[:, :lo], e_rest.astype(jnp.bfloat16), preferred_element_type=jnp.float32
            )
        out = (out / total).astype(jnp.bfloat16)
        held[:HEAD_SIZE, lo:n] = out[:, :QB]
        held[HEAD_SIZE:, lo:n] = out[:, QB:]
        lse = top + jnp.log(total)
        lse_ref[0, 0:1, lo:n] = lse[:, :QB]
        lse_ref[0, 1:2, lo:n] = lse[:, QB:]
    tok = seq // 2
    for core in range(2):

        @pl.when(place[0] == core)
        def _():
            keep_ref[...] = held[:, core * tok : (core + 1) * tok]
            send_ref[...] = held[:, (1 - core) * tok : (2 - core) * tok]


def attend_seq(place, qkv_t, tables):
    rows, seq = qkv_t.shape
    kv = rows // (4 * HEAD_SIZE)
    group = pl.BlockSpec((2 * HEAD_SIZE, seq), lambda j: (j, 0))

    def head(base):
        return pl.BlockSpec((HEAD_SIZE, seq), lambda j: (base + j, 0))

    table = pl.BlockSpec(memory_space=pltpu.VMEM)
    return pl.pallas_call(
        attend_kernel,
        grid=(kv,),
        in_specs=[pl.BlockSpec(memory_space=pltpu.SMEM), group, head(2 * kv), head(3 * kv), table, table, table, table],
        out_specs=[
            pl.BlockSpec((2 * HEAD_SIZE, seq // 2), lambda j: (j, 0)),
            pl.BlockSpec((2 * HEAD_SIZE, seq // 2), lambda j: (j, 0)),
            pl.BlockSpec((1, 2, seq), lambda j: (j, 0, 0)),
            group,
            head(0),
            head(0),
        ],
        out_shape=[
            jax.ShapeDtypeStruct((2 * kv * HEAD_SIZE, seq // 2), jnp.bfloat16),
            jax.ShapeDtypeStruct((2 * kv * HEAD_SIZE, seq // 2), jnp.bfloat16),
            jax.ShapeDtypeStruct((kv, 2, seq), jnp.float32),
            jax.ShapeDtypeStruct((2 * kv * HEAD_SIZE, seq), jnp.bfloat16),
            jax.ShapeDtypeStruct((kv * HEAD_SIZE, seq), jnp.bfloat16),
            jax.ShapeDtypeStruct((kv * HEAD_SIZE, seq), jnp.bfloat16),
        ],
        scratch_shapes=[
            pltpu.VMEM((2 * HEAD_SIZE, seq), jnp.bfloat16),
            pltpu.VMEM((HEAD_SIZE // 2, seq), jnp.float32),
            pltpu.VMEM((HEAD_SIZE // 2, seq), jnp.float32),
        ],
        compiler_params=pltpu.CompilerParams(vmem_limit_bytes=VMEM_LIMIT),
        cost_estimate=pl.CostEstimate(
            flops=4 * kv * 2 * seq * seq * HEAD_SIZE, bytes_accessed=10 * rows * seq, transcendentals=kv * seq * seq
        ),
        name="attend",
    )(place, qkv_t, qkv_t, qkv_t, *tables)


def attend_back_kernel(
    place, q_ref, k_ref, v_ref, keep_ref, got_ref, lse_ref, cl_ref, sl_ref, ch_ref, sh_ref,
    dq_ref, dk_ref, dv_ref, dk_acc, dv_acc, c_ref, s_ref,
):
    fill_tables(cl_ref, sl_ref, ch_ref, sh_ref, c_ref, s_ref)
    half = HEAD_SIZE // 2
    cosine = c_ref[...]
    sine = s_ref[...]
    seq = cosine.shape[1]

    def turn_back(field, cos, sin):
        front, back = field[:half], field[half:]
        return jnp.concatenate([front * cos + back * sin, back * cos - front * sin], axis=0)

    def flip(field):
        return field.astype(jnp.float32).T.astype(jnp.bfloat16)

    key_t = k_ref[...]
    key = flip(key_t)
    val = flip(v_ref[...])
    q0_t, q1_t = q_ref[:HEAD_SIZE], q_ref[HEAD_SIZE:]
    first_core = place[0] == 0
    early = jnp.where(first_core, keep_ref[...], got_ref[...])
    late = jnp.where(first_core, got_ref[...], keep_ref[...])
    grads = jnp.concatenate([early, late], axis=1)
    g0_t, g1_t = grads[:HEAD_SIZE], grads[HEAD_SIZE:]
    q0, q1, g0, g1 = flip(q0_t), flip(q1_t), flip(g0_t), flip(g1_t)
    dk_acc[...] = jnp.zeros_like(dk_acc)
    dv_acc[...] = jnp.zeros_like(dv_acc)
    rows = lax.broadcasted_iota(jnp.int32, (QB, 2 * QB), 0)
    cols = lax.broadcasted_iota(jnp.int32, (QB, 2 * QB), 1)
    keep = rows <= jnp.where(cols >= QB, cols - QB, cols)
    for b in range(seq // QB):
        lo, n = b * QB, (b + 1) * QB
        q_t = jnp.concatenate([q0_t[:, lo:n], q1_t[:, lo:n]], axis=1)
        g_t = jnp.concatenate([g0_t[:, lo:n], g1_t[:, lo:n]], axis=1)
        q_n = jnp.concatenate([q0[lo:n], q1[lo:n]], axis=0)
        g_n = jnp.concatenate([g0[lo:n], g1[lo:n]], axis=0)
        lse = jnp.concatenate([lse_ref[0, 0:1, lo:n], lse_ref[0, 1:2, lo:n]], axis=1)
        parts = []
        delta = None
        for start, stop in ([(0, lo)] if b > 0 else []) + [(lo, n)]:
            scores = jnp.dot(key[start:stop], q_t, preferred_element_type=jnp.float32) * HEAD_SIZE ** (-0.5)
            prob = jnp.exp(scores - lse)
            if start == lo:
                prob = jnp.where(keep, prob, 0.0)
            d_prob = jnp.dot(val[start:stop], g_t, preferred_element_type=jnp.float32)
            part = jnp.sum(prob * d_prob, axis=0, keepdims=True)
            delta = part if delta is None else delta + part
            dv_acc[start:stop] += jnp.dot(prob.astype(jnp.bfloat16), g_n, preferred_element_type=jnp.float32)
            parts.append((start, stop, prob, d_prob))
        dq_t = None
        for start, stop, prob, d_prob in parts:
            d_score = (prob * (d_prob - delta) * HEAD_SIZE ** (-0.5)).astype(jnp.bfloat16)
            dk_acc[start:stop] += jnp.dot(d_score, q_n, preferred_element_type=jnp.float32)
            part = jnp.dot(key_t[:, start:stop], d_score, preferred_element_type=jnp.float32)
            dq_t = part if dq_t is None else dq_t + part
        cos, sin = cosine[:, lo:n], sine[:, lo:n]
        dq_ref[:HEAD_SIZE, lo:n] = turn_back(dq_t[:, :QB], cos, sin).astype(jnp.bfloat16)
        dq_ref[HEAD_SIZE:, lo:n] = turn_back(dq_t[:, QB:], cos, sin).astype(jnp.bfloat16)
    dk_ref[...] = turn_back(dk_acc[...].T, cosine, sine).astype(jnp.bfloat16)
    dv_ref[...] = dv_acc[...].T.astype(jnp.bfloat16)


def attend_seq_back(place, q_t, k_t, v_t, g_keep, g_got, lse, tables):
    rows, seq = k_t.shape
    kv = rows // HEAD_SIZE
    group = pl.BlockSpec((2 * HEAD_SIZE, seq), lambda j: (j, 0))
    part = pl.BlockSpec((2 * HEAD_SIZE, seq // 2), lambda j: (j, 0))
    head = pl.BlockSpec((HEAD_SIZE, seq), lambda j: (j, 0))
    table = pl.BlockSpec(memory_space=pltpu.VMEM)
    return pl.pallas_call(
        attend_back_kernel,
        grid=(kv,),
        in_specs=[
            pl.BlockSpec(memory_space=pltpu.SMEM), group, head, head, part, part,
            pl.BlockSpec((1, 2, seq), lambda j: (j, 0, 0)), table, table, table, table,
        ],
        out_specs=[group, head, head],
        out_shape=[
            jax.ShapeDtypeStruct((2 * rows, seq), jnp.bfloat16),
            jax.ShapeDtypeStruct((rows, seq), jnp.bfloat16),
            jax.ShapeDtypeStruct((rows, seq), jnp.bfloat16),
        ],
        scratch_shapes=[
            pltpu.VMEM((seq, HEAD_SIZE), jnp.float32),
            pltpu.VMEM((seq, HEAD_SIZE), jnp.float32),
            pltpu.VMEM((HEAD_SIZE // 2, seq), jnp.float32),
            pltpu.VMEM((HEAD_SIZE // 2, seq), jnp.float32),
        ],
        compiler_params=pltpu.CompilerParams(vmem_limit_bytes=VMEM_LIMIT),
        cost_estimate=pl.CostEstimate(
            flops=10 * kv * 2 * seq * seq * HEAD_SIZE, bytes_accessed=20 * rows * seq, transcendentals=kv * seq * seq
        ),
        name="attend_back",
    )(place, q_t, k_t, v_t, g_keep, g_got, lse, *tables)


def fp32(field):
    return field.astype(jnp.float32)


def mm(left, right, dims=((1,), (0,)), out=jnp.float32):
    return lax.dot_general(left, right, (dims, ((), ())), preferred_element_type=out)


ANY = pl.BlockSpec(memory_space=pl.ANY)
SMEM = pl.BlockSpec(memory_space=pltpu.SMEM)
VM = pl.BlockSpec(memory_space=pltpu.VMEM)
PARAMS = pltpu.CompilerParams(vmem_limit_bytes=VMEM_LIMIT)
MESH = pl.DeviceIdType.MESH
TILE = 256
WIDE = 512


def bf16_like(*dims):
    return jax.ShapeDtypeStruct(dims, jnp.bfloat16)


def f32_like(*dims):
    return jax.ShapeDtypeStruct(dims, jnp.float32)


def cost(flops, moved):
    return pl.CostEstimate(flops=int(flops), bytes_accessed=int(moved), transcendentals=0)


class Spots:
    def __init__(self):
        z, f, g = lax.axis_index("ctx"), lax.axis_index("fsdp"), lax.axis_index("grp")
        self.z, self.f, self.g = z, f, g
        self.parity = z % 2
        self.fx = f + 1 - 2 * (f % 2)
        self.fy = f + 2 - 4 * (f // 2)
        self.fd = 3 - f
        across = z + 1 - 2 * self.parity
        self.x = (z, self.fx, g)
        self.y = (z, self.fy, g)
        self.diag = (z, self.fd, g)
        self.core = (z, f, 1 - g)
        self.across = (across, f, g)
        self.swap = (across, f, 1 - g)


def greet(*partners):
    barrier = pltpu.get_barrier_semaphore()
    for partner in partners:
        pl.semaphore_signal(barrier, inc=1, device_id=partner, device_id_type=MESH)
    pl.semaphore_wait(barrier, len(partners))


def rows_at(start, size):
    return pl.ds(pl.multiple_of(start, size), size)


def gather_kernel(
    tokens, cotangent, wq, wk, wv, wo, gate, up, down, gain,
    qkv_o, out_o, pair_o, down_o, x_o, dy_o, gain_o, xn_o, turned_o,
    send, recv, near, far, qkv_v, out_v, pair_v, down_v, tok_v, gain_v,
    extra, x_v, w_v, gains_v, xn_v, turned_v,
):
    at = Spots()
    g, f, parity = at.g, at.f, at.parity
    greet(at.x, at.y, at.diag, at.core, at.across, at.swap)
    taken = [0, 0]

    def remote(src, dst, device):
        i = taken[0]
        taken[0] += 1
        return pltpu.make_async_remote_copy(
            src_ref=src, dst_ref=dst, send_sem=send.at[i], recv_sem=recv.at[i],
            device_id=device, device_id_type=MESH,
        )

    class Bounce:
        def __init__(self, src, via, dst):
            i = taken[1]
            taken[1] += 1
            self.first = pltpu.make_async_copy(src, via, near.at[i])
            self.second = pltpu.make_async_copy(via, dst, far.at[i])

        def start(self):
            self.first.start()

        def turn(self):
            self.first.wait()
            self.second.start()

        def wait(self):
            self.second.wait()

    def start(copies):
        for copy in copies:
            copy.start()
        return copies

    def arrive(copies):
        for copy in copies:
            copy.wait_recv()

    tok = tokens.shape[1]
    feat = wq.shape[0]
    mid = feat // 2
    nq, nk, nv = (w.shape[1] // 2 for w in (wq, wk, wv))
    nf = gate.shape[1] // 8
    wide = wo.shape[1] // 2
    count = 4
    top, low = slice(0, mid), slice(mid, feat)

    mine = rows_at(g * tok, tok)
    swaps = [
        remote(tokens.at[0], x_o.at[mine], at.swap),
        remote(cotangent.at[0], dy_o.at[mine], at.swap),
    ]
    keeps = [
        Bounce(tokens.at[0], tok_v.at[0], x_o.at[mine]),
        Bounce(cotangent.at[0], tok_v.at[1], dy_o.at[mine]),
    ]
    away = rows_at((1 - g) * tok, tok)
    swaps_out = [
        pltpu.make_async_remote_copy(
            src_ref=array.at[0], dst_ref=into.at[away], send_sem=send.at[i], recv_sem=recv.at[i],
            device_id=at.swap, device_id_type=MESH,
        )
        for i, (array, into) in enumerate(((tokens, x_o), (cotangent, dy_o)))
    ]
    shares = [remote(x_o.at[mine], x_o.at[mine], at.core), remote(dy_o.at[mine], dy_o.at[mine], at.core)]

    @pl.when(g != parity)
    def _():
        start(swaps_out)

    @pl.when(g == parity)
    def _():
        start(keeps)
        for copy in keeps:
            copy.turn()

    own_rows = f * feat
    shared_cols = (count - 1) * nf

    def pair_direct(part, device):
        first = taken[0]
        taken[0] += count + 1
        rows = rows_at(own_rows + part.start, mid)

        def made(array, index, k, i):
            return pltpu.make_async_remote_copy(
                src_ref=array.at[part, rows_at((2 * k + g) * nf, nf)],
                dst_ref=pair_o.at[index, rows, rows_at(k * nf, nf)],
                send_sem=send.at[first + i], recv_sem=recv.at[first + i],
                device_id=device, device_id_type=MESH,
            )

        def some(array):
            return [made(array, parity, k, k) for k in range(count - 1)]

        @pl.when(parity == 0)
        def _():
            start(some(gate))

        @pl.when(parity == 1)
        def _():
            start(some(up))

        last = start([made(gate, 0, count - 1, count - 1), made(up, 1, count - 1, count)])
        return some(gate), last

    pair_xt, last_xt = pair_direct(top, at.x)
    pair_yl, last_yl = pair_direct(low, at.y)
    pair_xl, last_xl = pair_direct(low, at.x)
    pair_yt, last_yt = pair_direct(top, at.y)

    def qkv_direct(part, device):
        copies = []
        for array, width, column in ((wq, nq, 0), (wk, nk, nq), (wv, nv, nq + nk)):
            copies.append(
                remote(
                    array.at[part, rows_at(g * width, width)],
                    qkv_o.at[rows_at(own_rows + part.start, mid), column : column + width],
                    device,
                )
            )
        return start(copies)

    qkv_xt = qkv_direct(top, at.x)
    qkv_yl = qkv_direct(low, at.y)
    qkv_xl = qkv_direct(low, at.x)
    qkv_yt = qkv_direct(top, at.y)

    own = rows_at(own_rows, feat)
    locals_ = [
        Bounce(
            array.at[:, rows_at(g * width, width)],
            qkv_v.at[:, column : column + width],
            qkv_o.at[own, column : column + width],
        )
        for array, width, column in ((wq, nq, 0), (wk, nk, nq), (wv, nv, nq + nk))
    ]
    locals_.append(Bounce(wo, out_v, out_o.at[own]))
    locals_.append(Bounce(down.at[rows_at(g * nf, nf)], down_v, down_o))
    for array, index in ((gate, 0), (up, 1)):
        for k in range(count):
            locals_.append(
                Bounce(
                    array.at[:, rows_at((2 * k + g) * nf, nf)],
                    pair_v.at[index, :, rows_at(k * nf, nf)],
                    pair_o.at[index, own, rows_at(k * nf, nf)],
                )
            )
    gain_place = gain_o.at[pl.ds(f, 1)]
    locals_.append(Bounce(gain, gain_v, gain_place))
    start(locals_)
    for copy in locals_:
        copy.turn()
    gains = start([remote(gain, gain_place, to) for to in (at.x, at.y, at.diag)])

    def forward(array_at, rows_x, rows_y):
        return remote(array_at(rows_x), array_at(rows_x), at.y), remote(
            array_at(rows_y), array_at(rows_y), at.x
        )

    x_top, y_low = rows_at(at.fx * feat, mid), rows_at(at.fy * feat + mid, mid)
    x_low, y_top = rows_at(at.fx * feat + mid, mid), rows_at(at.fy * feat, mid)
    d_top, d_low = rows_at(at.fd * feat, mid), rows_at(at.fd * feat + mid, mid)

    def pair_view(rows):
        return pair_o.at[parity, rows, 0:shared_cols]

    def last_view(rows):
        return pair_o.at[:, rows, shared_cols : shared_cols + nf]

    def out_view(rows):
        return out_o.at[rows, rows_at(g * wide, wide)]

    pair_fy, pair_fx = forward(pair_view, x_top, y_low)
    last_fy, last_fx = forward(last_view, x_top, y_low)
    sends = [pair_fy, pair_fx, last_fy, last_fx]

    def across(rows):
        copy = remote(pair_view(rows), pair_view(rows), at.across)
        copy.start()
        sends.append(copy)
        return copy

    arrive(pair_xt)
    pair_fy.start()
    z_copies = [across(x_top)]
    arrive(pair_yl)
    pair_fx.start()
    z_copies.append(across(y_low))

    def out_direct(part, device):
        copy = remote(
            wo.at[part, rows_at(g * wide, wide)],
            out_o.at[rows_at(own_rows + part.start, mid), rows_at(g * wide, wide)],
            device,
        )
        copy.start()
        return copy

    out_xt, out_yl = out_direct(top, at.x), out_direct(low, at.y)
    out_xl, out_yt = out_direct(low, at.x), out_direct(top, at.y)

    arrive(pair_xl)
    z_copies.append(across(x_low))
    arrive(pair_yt)
    z_copies.append(across(y_top))

    def qkv_view(rows):
        return qkv_o.at[rows]

    qkv_fy, qkv_fx = forward(qkv_view, x_top, y_low)
    arrive(qkv_xt)
    qkv_fy.start()
    arrive(qkv_yl)
    qkv_fx.start()
    arrive(last_xt)
    last_fy.start()
    arrive(last_yl)
    last_fx.start()

    pair_fy.wait_recv()
    z_copies.append(across(d_top))
    pair_fx.wait_recv()
    z_copies.append(across(d_low))

    for i in range(2):

        @pl.when(g != parity)
        def _():
            swaps[i].wait_recv()
            swaps_out[i].wait_send()

        @pl.when(g == parity)
        def _():
            keeps[i].wait()

        shares[i].start()

    out_fy, out_fx = forward(out_view, x_top, y_low)
    out_xt.wait_recv()
    out_fy.start()
    out_yl.wait_recv()
    out_fx.start()
    out_xl.wait_recv()
    out_yt.wait_recv()

    def share(rows):
        copy = remote(out_view(rows), out_view(rows), at.core)
        copy.start()
        return copy

    shared = [share(x_top), share(x_low), share(y_top), share(y_low)]

    arrive(qkv_xl + qkv_yt + [qkv_fy, qkv_fx] + gains + shares[:1])
    for copy in locals_[:3] + locals_[-1:]:
        copy.wait()
    loads = [
        pltpu.make_async_copy(src, dst, extra.at[i])
        for i, (src, dst) in enumerate(((x_o, x_v), (gain_o, gains_v), (qkv_o, w_v)))
    ]
    start(loads)
    for copy in loads:
        copy.wait()
    row = gain_row(gains_v, 0)

    @pl.loop(0, x_v.shape[0] // TILE)
    def _(n):
        part = rows_at(n * TILE, TILE)
        field = fp32(x_v[part, :])
        xn_v[part, :] = (field * norm_scale(field) * row).astype(jnp.bfloat16)

    @pl.loop(0, w_v.shape[1] // TILE)
    def _(n):
        part = rows_at(n * TILE, TILE)
        turned_v[part, :] = mm(w_v[:, part].T, xn_v[...], ((1,), (1,)))

    results = start(
        [pltpu.make_async_copy(xn_v, xn_o, extra.at[3]), pltpu.make_async_copy(turned_v, turned_o, extra.at[4])]
    )

    out_fy.wait_recv()
    shared.append(share(d_top))
    out_fx.wait_recv()
    shared.append(share(d_low))

    arrive([last_fy, last_fx])
    arrive(last_xl + last_yt)
    arrive(shares[1:])
    arrive(shared)
    arrive(z_copies)
    for copy in locals_[3:-1] + results:
        copy.wait()
    for copy in (
        pair_xt + pair_yl + pair_xl + pair_yt + qkv_xt + qkv_yl + qkv_xl + qkv_yt + gains
        + sends + shares + shared
        + [out_xt, out_yl, out_xl, out_yt, out_fy, out_fx, qkv_fy, qkv_fx]
        + last_xt + last_yl + last_xl + last_yt
    ):
        copy.wait_send()


def gather_all(tokens, cotangent, wq, wk, wv, wo, gate, up, down, gain):
    tok, width = tokens.shape[1:]
    nf = gate.shape[1] // 8
    cols = (wq.shape[1] + wk.shape[1] + wv.shape[1]) // 2
    return pl.pallas_call(
        gather_kernel,
        in_specs=[ANY] * 10,
        out_specs=[ANY] * 9,
        out_shape=[
            bf16_like(width, cols),
            bf16_like(4 * wo.shape[0], width),
            bf16_like(2, width, 4 * nf),
            bf16_like(nf, width),
            bf16_like(2 * tok, width),
            bf16_like(2 * tok, width),
            jax.ShapeDtypeStruct((4,) + gain.shape[1:], gain.dtype),
            bf16_like(2 * tok, width),
            f32_like(cols, 2 * tok),
        ],
        scratch_shapes=[
            pltpu.SemaphoreType.DMA((72,)),
            pltpu.SemaphoreType.DMA((72,)),
            pltpu.SemaphoreType.DMA((20,)),
            pltpu.SemaphoreType.DMA((20,)),
            pltpu.VMEM((width // 4, cols), jnp.bfloat16),
            pltpu.VMEM(wo.shape, jnp.bfloat16),
            pltpu.VMEM((2, width // 4, 4 * nf), jnp.bfloat16),
            pltpu.VMEM((nf, width), jnp.bfloat16),
            pltpu.VMEM((2, tok, width), jnp.bfloat16),
            pltpu.VMEM(gain.shape, gain.dtype),
            pltpu.SemaphoreType.DMA((5,)),
            pltpu.VMEM((2 * tok, width), jnp.bfloat16),
            pltpu.VMEM((width, cols), jnp.bfloat16),
            pltpu.VMEM((4,) + gain.shape[1:], gain.dtype),
            pltpu.VMEM((2 * tok, width), jnp.bfloat16),
            pltpu.VMEM((cols, 2 * tok), jnp.float32),
        ],
        compiler_params=pltpu.CompilerParams(
            collective_id=0, has_side_effects=True, vmem_limit_bytes=VMEM_LIMIT
        ),
        cost_estimate=cost(0, 500e6),
        name="gather",
    )(tokens, cotangent, wq, wk, wv, wo, gate, up, down, gain)


def gain_row(gain, which):
    return jnp.concatenate([gain[k, which : which + 1, :] for k in range(gain.shape[0])], axis=1)


def norm_scale(field):
    return lax.rsqrt(jnp.mean(field * field, axis=-1, keepdims=True) + EPS)


def residual_kernel(place, x_ref, attn_keep, attn_got, gain, w_ref, h_ref, xn_ref, attn_ref):
    core = place[0]
    heads = attn_keep.shape[0]
    keep_at, got_at = rows_at(core * heads, heads), rows_at((1 - core) * heads, heads)
    attn_ref[keep_at, :] = attn_keep[...]
    attn_ref[got_at, :] = attn_got[...]
    field = fp32(x_ref[...]) + mm(attn_ref[...].T, w_ref[...])
    h_ref[...] = field
    xn_ref[...] = (field * norm_scale(field) * gain_row(gain, 1)).astype(jnp.bfloat16)


def residual(place, x_seq, attn_keep, attn_got, gains, weight):
    seq, width = x_seq.shape
    tok = seq // 2
    heads = attn_keep.shape[0]
    steps = tok // TILE
    rows = pl.BlockSpec((TILE, width), lambda i, place: (i, 0))
    return pl.pallas_call(
        residual_kernel,
        grid_spec=pltpu.PrefetchScalarGridSpec(
            num_scalar_prefetch=1,
            grid=(steps,),
            in_specs=[
                pl.BlockSpec((TILE, width), lambda i, place: (steps * place[0] + i, 0)),
                pl.BlockSpec((heads, TILE), lambda i, place: (0, i)),
                pl.BlockSpec((heads, TILE), lambda i, place: (0, i)),
                VM,
                VM,
            ],
            out_specs=[rows, rows, pl.BlockSpec((2 * heads, TILE), lambda i, place: (0, i))],
        ),
        out_shape=[f32_like(tok, width), bf16_like(tok, width), bf16_like(2 * heads, tok)],
        compiler_params=PARAMS,
        cost_estimate=cost(2 * tok * width * weight.shape[0], 14e6),
        name="residual",
    )(place, x_seq, attn_keep, attn_got, gains, weight)


def hidden_kernel(place, xn_own, xn_got, gate_w, up_w, hid_ref, for_gate_ref, act_ref, xn_ref):
    @pl.when(pl.program_id(0) == 0)
    def _():
        tok = xn_own.shape[0]
        xn_ref[rows_at(place[0] * tok, tok), :] = xn_own[...]
        xn_ref[rows_at((1 - place[0]) * tok, tok), :] = xn_got[...]

    gate = mm(xn_ref[...], gate_w[0])
    up = mm(xn_ref[...], up_w[0])
    sig = 1.0 / (1.0 + jnp.exp(-gate))
    act = gate * sig
    hid_ref[...] = (act * up).astype(jnp.bfloat16)
    for_gate_ref[...] = (up * (sig + act * (1.0 - sig))).astype(jnp.bfloat16)
    act_ref[...] = act.astype(jnp.bfloat16)


def hidden_step(place, xn_own, xn_got, pair):
    seq, width = 2 * xn_own.shape[0], xn_own.shape[1]
    ff = pair.shape[2]
    block = pl.BlockSpec((seq, TILE), lambda n: (0, n))
    return pl.pallas_call(
        hidden_kernel,
        grid=(ff // TILE,),
        in_specs=[
            SMEM,
            VM,
            VM,
            pl.BlockSpec((1, width, TILE), lambda n: (0, 0, n)),
            pl.BlockSpec((1, width, TILE), lambda n: (1, 0, n)),
        ],
        out_specs=[block] * 3 + [VM],
        out_shape=[bf16_like(seq, ff)] * 3 + [bf16_like(seq, width)],
        compiler_params=PARAMS,
        cost_estimate=cost(4 * seq * width * ff, 30e6),
        name="hidden",
    )(place, xn_own, xn_got, pair, pair)


def hidden_back_kernel(dy_ref, down_w, for_gate_ref, act_ref, dgate_ref, dup_ref):
    d_hidden = mm(dy_ref[...], down_w[...], ((1,), (1,)))
    dgate_ref[...] = (d_hidden * fp32(for_gate_ref[...])).astype(jnp.bfloat16)
    dup_ref[...] = (d_hidden * fp32(act_ref[...])).astype(jnp.bfloat16)


def hidden_back(dy, down, for_gate, act):
    seq, width = dy.shape
    ff = down.shape[0]
    block = pl.BlockSpec((seq, WIDE), lambda n: (0, n))
    return pl.pallas_call(
        hidden_back_kernel,
        grid=(ff // WIDE,),
        in_specs=[VM, pl.BlockSpec((WIDE, width), lambda n: (n, 0)), block, block],
        out_specs=[block] * 2,
        out_shape=[bf16_like(seq, ff)] * 2,
        compiler_params=PARAMS,
        cost_estimate=cost(2 * seq * width * ff, 26e6),
        name="hidden_back",
    )(dy, down, for_gate, act)


def back_kernel(place, dgate_ref, dup_ref, gate_w, up_w, own_ref, send_ref):
    field = mm(dgate_ref[...], gate_w[0], ((1,), (1,)))
    field = field + mm(dup_ref[...], up_w[0], ((1,), (1,)))
    tok = own_ref.shape[0]

    @pl.when(place[0] == 0)
    def _():
        own_ref[...] = field[:tok]
        send_ref[...] = field[tok:].astype(jnp.bfloat16)

    @pl.when(place[0] == 1)
    def _():
        own_ref[...] = field[tok:]
        send_ref[...] = field[:tok].astype(jnp.bfloat16)


def back_step(place, d_gate, d_up, pair):
    seq, ff = d_gate.shape
    width = pair.shape[1]
    out = pl.BlockSpec((seq // 2, WIDE), lambda n: (0, n))
    return pl.pallas_call(
        back_kernel,
        grid=(width // WIDE,),
        in_specs=[
            SMEM,
            VM,
            VM,
            pl.BlockSpec((1, WIDE, ff), lambda n: (0, n, 0)),
            pl.BlockSpec((1, WIDE, ff), lambda n: (1, n, 0)),
        ],
        out_specs=[out, out],
        out_shape=[f32_like(seq // 2, width), bf16_like(seq // 2, width)],
        compiler_params=PARAMS,
        cost_estimate=cost(4 * seq * width * ff, 26e6),
        name="back",
    )(place, d_gate, d_up, pair, pair)


def result_kernel(place, hid_ref, h_ref, down_w, own_ref, send_ref):
    field = mm(hid_ref[...], down_w[...])
    tok = own_ref.shape[0]

    @pl.when(place[0] == 0)
    def _():
        own_ref[...] = field[:tok] + h_ref[...]
        send_ref[...] = field[tok:].astype(jnp.bfloat16)

    @pl.when(place[0] == 1)
    def _():
        own_ref[...] = field[tok:] + h_ref[...]
        send_ref[...] = field[:tok].astype(jnp.bfloat16)


def result_step(place, hidden, h_own, down):
    tok, width = h_own.shape
    ff = hidden.shape[1]
    out = pl.BlockSpec((tok, WIDE), lambda n: (0, n))
    return pl.pallas_call(
        result_kernel,
        grid=(width // WIDE,),
        in_specs=[SMEM, VM, out, pl.BlockSpec((ff, WIDE), lambda n: (0, n))],
        out_specs=[out, out],
        out_shape=[f32_like(tok, width), bf16_like(tok, width)],
        compiler_params=PARAMS,
        cost_estimate=cost(4 * tok * width * ff, 20e6),
        name="result",
    )(place, hidden, h_own, down)


def entry_kernel(place, dn_own, dn_got, h_ref, dy_ref, gain, w_ref, dh_ref, da_ref, keep_ref, send_ref, part_ref):
    core = place[0]

    @pl.when(pl.program_id(0) == 0)
    def _():
        part_ref[...] = jnp.zeros_like(part_ref)

    field = h_ref[...]
    scale = norm_scale(field)
    hat = field * scale
    grad = dn_own[...] + fp32(dn_got[...])
    part_ref[...] += jnp.sum(grad * hat, axis=0, keepdims=True)
    total = fp32(dy_ref[...]) + rms_back(grad * gain_row(gain, 1), hat, scale)
    dh_ref[...] = total
    da_ref[...] = total.astype(jnp.bfloat16)
    heads = keep_ref.shape[0]
    for ref, at in ((send_ref, 1 - core), (keep_ref, core)):
        ref[...] = mm(w_ref[rows_at(at * heads, heads), :], da_ref[...], ((1,), (1,))).astype(jnp.bfloat16)


def entry_step(place, dn_own, dn_got, h_own, dy_all, gains, weight):
    tok, width = h_own.shape
    heads = weight.shape[0] // 2
    steps = tok // TILE
    rows = pl.BlockSpec((TILE, width), lambda i, place: (i, 0))
    cols = pl.BlockSpec((heads, TILE), lambda i, place: (0, i))
    return pl.pallas_call(
        entry_kernel,
        grid_spec=pltpu.PrefetchScalarGridSpec(
            num_scalar_prefetch=1,
            grid=(steps,),
            in_specs=[
                rows,
                rows,
                rows,
                pl.BlockSpec((TILE, width), lambda i, place: (steps * place[0] + i, 0)),
                VM,
                VM,
            ],
            out_specs=[rows, rows, cols, cols, VM],
        ),
        out_shape=[
            f32_like(tok, width),
            bf16_like(tok, width),
            bf16_like(heads, tok),
            bf16_like(heads, tok),
            f32_like(1, width),
        ],
        compiler_params=PARAMS,
        cost_estimate=cost(2 * tok * width * weight.shape[0], 20e6),
        name="entry",
    )(place, dn_own, dn_got, h_own, dy_all, gains, weight)


def inputs_kernel(place, dq_ref, dk_ref, dv_ref, w_ref, own_ref, send_ref, d_ref):
    @pl.when(pl.program_id(0) == 0)
    def _():
        nq, nk = dq_ref.shape[0], dk_ref.shape[0]
        d_ref[:, :nq] = dq_ref[...].T
        d_ref[:, nq : nq + nk] = dk_ref[...].T
        d_ref[:, nq + nk :] = dv_ref[...].T

    field = mm(d_ref[...], w_ref[...], ((1,), (1,)))
    tok = own_ref.shape[0]

    @pl.when(place[0] == 0)
    def _():
        own_ref[...] = field[:tok]
        send_ref[...] = field[tok:].astype(jnp.bfloat16)

    @pl.when(place[0] == 1)
    def _():
        own_ref[...] = field[tok:]
        send_ref[...] = field[:tok].astype(jnp.bfloat16)


def inputs_step(place, dq_t, dk_t, dv_t, weight):
    width, cols = weight.shape
    tok = dq_t.shape[1] // 2
    out = pl.BlockSpec((tok, WIDE), lambda n: (0, n))
    return pl.pallas_call(
        inputs_kernel,
        grid=(width // WIDE,),
        in_specs=[SMEM] + [VM] * 3 + [pl.BlockSpec((WIDE, cols), lambda n: (n, 0))],
        out_specs=[out, out, VM],
        out_shape=[f32_like(tok, width), bf16_like(tok, width), bf16_like(2 * tok, cols)],
        compiler_params=PARAMS,
        cost_estimate=cost(4 * tok * width * cols, 14e6),
        name="inputs",
    )(place, dq_t, dk_t, dv_t, weight)


def last_kernel(place, d1_own, d1_got, x_ref, dh_ref, gain, dx_ref, part_ref):
    @pl.when(pl.program_id(0) == 0)
    def _():
        part_ref[...] = jnp.zeros_like(part_ref)

    field = fp32(x_ref[...])
    scale = norm_scale(field)
    hat = field * scale
    grad = d1_own[...] + fp32(d1_got[...])
    part_ref[...] += jnp.sum(grad * hat, axis=0, keepdims=True)
    dx_ref[...] = (dh_ref[...] + rms_back(grad * gain_row(gain, 0), hat, scale)).astype(jnp.bfloat16)


def last_step(place, d1_own, d1_got, x_seq, dh_own, gains):
    tok, width = dh_own.shape
    tile = TILE // 2
    steps = tok // tile
    rows = pl.BlockSpec((tile, width), lambda i, place: (i, 0))
    return pl.pallas_call(
        last_kernel,
        grid_spec=pltpu.PrefetchScalarGridSpec(
            num_scalar_prefetch=1,
            grid=(steps,),
            in_specs=[
                rows,
                rows,
                pl.BlockSpec((tile, width), lambda i, place: (steps * place[0] + i, 0)),
                rows,
                VM,
            ],
            out_specs=[rows, VM],
        ),
        out_shape=[bf16_like(tok, width), f32_like(1, width)],
        compiler_params=PARAMS,
        cost_estimate=cost(0, 14e6),
        name="last",
    )(place, d1_own, d1_got, x_seq, dh_own, gains)


class Group:
    def __init__(self, source, rows, put):
        self.source, self.rows, self.put = source, rows, put
        mid = rows // 2
        self.top, self.low = pl.ds(0, mid), pl.ds(mid, mid)


def add_rows(dst, left, right):
    rows = dst.shape[0]

    @pl.loop(0, rows // 64)
    def _(i):
        at = rows_at(i * 64, 64)
        dst[at] = (fp32(left[at]) + fp32(right[at])).astype(dst.dtype)


ORDER = (
    "end", "b1u", "s1", "gie", "b1f", "b0u", "gwe", "h1u", "jod", "ene", "h1f", "b1v", "sed",
    "kee", "zad", "gq", "joe", "b0f", "kwe", "h0u", "s2", "see", "zae", "plu", "wad", "giu",
    "b0v", "fid", "gwu", "zbd", "enu", "h0f", "plf", "gif", "h1v", "go", "keu", "b1q", "fie",
    "gwf", "wae", "b1r", "enf", "b0q", "zbe", "jou", "kef", "seu", "h0v", "s3", "zau", "plv",
    "giv", "gwv", "kwu", "kev", "env", "h1q", "ao", "ded", "b0r", "jof", "sef", "h1r", "dee",
    "zaf", "h0q", "jov", "sev", "zav", "plq", "wau", "fif", "b1o", "b0o", "giq", "kwf", "kwv",
    "fiu", "zbu", "gwq", "enq", "keq", "h0r", "plr", "wav", "joq", "gir", "fiv", "zbv", "h1o",
    "seq", "gwr", "zaq", "fiq", "h0o", "waf", "ker", "zbf", "enr", "waq", "plo", "gio", "s4",
    "zbq", "eno", "deu", "jor", "kwr", "dev", "gwo", "keo", "ser", "kwq", "zar", "joo", "seo",
    "s5", "zao", "fir", "war", "def", "zbr", "wao", "fio", "zbo", "kwo", "der", "deq", "deo",
)


def collect_kernel(
    down, down_in, gate, gate_last, up, xn, d_qkv, attn, da, sums, lse,
    down_o, gate_o, up_o, query_o, key_o, value_o, out_o, sums_o, lse_o,
    send, recv, near, lse_send, lse_recv, lse_near, out_mine, out_got, sums_got,
    out_away, qkv, xn_v, d_qkv_v, attn_v, da_v, *buffers,
):
    at = Spots()
    z, f, g, parity = at.z, at.f, at.g, at.parity
    is_inner = (z == 1) | (z == 2)
    is_outer = (z == 0) | (z == 3)
    toward = (1 + z // 2, f, g)
    outward = (3 * (z // 2), f, g)
    other = (3 - z, f, g)
    chips = 4
    barrier = pltpu.get_barrier_semaphore()
    for partner in (at.x, at.y):
        pl.semaphore_signal(barrier, inc=1, device_id=partner, device_id_type=MESH)
    for level in range(chips):
        for core in range(2):

            @pl.when((z != level) | (g != core))
            def _():
                pl.semaphore_signal(barrier, inc=1, device_id=(level, f, core), device_id_type=MESH)

    pl.semaphore_wait(barrier, 2 * chips + 1)

    taken = [0, 0]

    def between(index, src, dst, device):
        return pltpu.make_async_remote_copy(
            src_ref=src, dst_ref=dst, send_sem=send.at[index], recv_sem=recv.at[index],
            device_id=device, device_id_type=MESH,
        )

    def remote(src, dst, device):
        taken[0] += 1
        return between(taken[0] - 1, src, dst, device)

    def local(src, dst):
        i = taken[1]
        taken[1] += 1
        return pltpu.make_async_copy(src, dst, near.at[i])

    nf = down.shape[0]
    feat = gate.shape[0]
    nq, nk = query_o.shape[1] // 2, key_o.shape[1] // 2
    wide = out_o.shape[1] // 2

    def put_down(done):
        return [(done, down_o.at[rows_at(g * nf, nf)])]

    def put_pair(into, first, count):
        def put(done):
            return [
                (
                    done.at[:, rows_at(k * nf, nf)],
                    into.at[:, rows_at((2 * (first + k) + g) * nf, nf)],
                )
                for k in range(count)
            ]

        return put

    def put_query(done):
        return [(done, query_o.at[:, rows_at(g * nq, nq)])]

    def put_key_value(done):
        return [
            (done.at[:, 0:nk], key_o.at[:, rows_at(g * nk, nk)]),
            (done.at[:, nk : 2 * nk], value_o.at[:, rows_at(g * nk, nk)]),
        ]

    def put_out(done):
        return [(done, out_o.at[:, rows_at(g * wide, wide)])]

    lse_place = lse_o.at[2 * (z // 2) + g]
    for level in range(chips):
        copy = pltpu.make_async_remote_copy(
            src_ref=lse, dst_ref=lse_place, send_sem=lse_send.at[level],
            recv_sem=lse_recv.at[2 * (z // 2) + g],
            device_id=(level, f, parity), device_id_type=MESH,
        )

        @pl.when((z != level) | (g != parity))
        def _():
            copy.start()

    lse_keep = pltpu.make_async_copy(lse, lse_place, lse_near)

    @pl.when(g == parity)
    def _():
        lse_keep.start()

    out_send = remote(out_away, out_got, at.core)
    operands = [local(xn, xn_v), local(d_qkv, d_qkv_v), local(attn, attn_v), local(da, da_v)]
    sums_send = remote(sums, sums_got.at[0], at.core)

    groups = []
    used = 0
    for source, rows, put, ready in (
        (down, nf, put_down, True),
        (gate, feat, put_pair(gate_o, 0, 3), True),
        (gate_last, feat, put_pair(gate_o, 3, 1), False),
        (up.at[:, 0 : 2 * nf], feat, put_pair(up_o, 0, 2), False),
        (up.at[:, 2 * nf : 4 * nf], feat, put_pair(up_o, 2, 2), False),
        (qkv.at[:, 0:nq], feat, put_query, False),
        (qkv.at[:, nq : nq + 2 * nk], feat, put_key_value, False),
        (out_mine, feat, put_out, False),
    ):
        group = Group(source, rows, put)
        groups.append(group)
        mid = rows // 2
        group.acc, group.outer, group.inner, group.done = buffers[used : used + 4]
        used += 4
        if ready:
            group.load = local(source, group.acc)
            if source is down:
                group.load_in = local(down_in, group.outer)
        else:
            group.mid, group.got, group.late = buffers[used : used + 3]
            used += 3
            group.sends = [
                remote(source.at[rows_at(at.fd * rows, mid)], group.got.at[1], at.x),
                remote(source.at[rows_at(at.fd * rows + mid, mid)], group.got.at[3], at.y),
                remote(source.at[rows_at(at.fx * rows, mid)], group.got.at[0], at.x),
                remote(source.at[rows_at(at.fy * rows + mid, mid)], group.got.at[2], at.y),
            ]
            group.loads = [
                local(source.at[rows_at(at.fy * rows, mid)], group.mid.at[0]),
                local(source.at[rows_at(at.fx * rows + mid, mid)], group.mid.at[1]),
                local(source.at[rows_at(f * rows, rows)], group.acc),
            ]
            group.second = [
                remote(group.mid.at[0], group.late.at[0], at.y),
                remote(group.mid.at[1], group.late.at[1], at.x),
            ]
        i = taken[0]
        taken[0] += 6
        group.first = i

        def inward(part, slot, group=group, i=i):
            return between(i + slot, group.acc.at[part], group.outer.at[part], toward)

        group.inward = inward

        def crossing(keep, give, i=i, group=group):
            return (
                between(i + 2, group.acc.at[give], group.inner, other),
                between(i + 3, group.done.at[keep], group.done.at[keep], other),
                between(i + 4, group.done.at[keep], group.done.at[keep], outward),
                between(i + 5, group.done.at[give], group.done.at[give], outward),
            )

        group.crossing = crossing
        pairs = group.put(group.done)
        group.shares = [remote(src_ref, dst_ref, at.core) for src_ref, dst_ref in pairs]
        group.stores = [local(src_ref, dst_ref) for src_ref, dst_ref in pairs]

    def by_end(group, step):
        @pl.when(z == 0)
        def _():
            step(group.low, group.top)

        @pl.when(z == 3)
        def _():
            step(group.top, group.low)

    def by_side(group, step):
        @pl.when(z == 1)
        def _():
            step(group.top, group.low, group.crossing(group.top, group.low))

        @pl.when(z == 2)
        def _():
            step(group.low, group.top, group.crossing(group.low, group.top))

    def b1(group):
        for copy in group.sends[:2] + group.loads:
            copy.start()

    def b0(group):
        for copy in group.sends[2:]:
            copy.start()

    def h1(group):
        for i, which in ((0, 1), (1, 3)):
            group.sends[i].wait_recv()
            group.loads[i].wait()
            add_rows(group.mid.at[i], group.mid.at[i], group.got.at[which])
            group.second[i].start()

    def h0(group):
        group.loads[2].wait()
        for i, part, which in ((2, group.top, 0), (3, group.low, 2)):
            group.sends[i].wait_recv()
            add_rows(group.acc.at[part], group.acc.at[part], group.got.at[which])

    def pl_(group):
        for i, part in ((0, group.top), (1, group.low)):
            group.second[i].wait_recv()
            add_rows(group.acc.at[part], group.acc.at[part], group.late.at[i])

    def gi(group):
        if group is e:
            e.load.wait()
        by_end(group, lambda give, keep: group.inward(give, 0).start())

    def gw(group):
        by_end(group, lambda give, keep: group.inward(give, 0).wait_send())

    def ke(group):
        by_end(group, lambda give, keep: group.inward(keep, 1).start())

    def kw(group):
        by_end(group, lambda give, keep: group.inward(keep, 1).wait_send())

    def en(group):
        if group is d:
            d.load.wait()
            d.load_in.wait()

        def step(keep, give, copies):
            if group is not d:
                group.inward(give, 0).wait_recv()
            add_rows(group.acc.at[give], group.acc.at[give], group.outer.at[give])
            copies[0].start()

        by_side(group, step)

    def jo(group):
        def step(keep, give, copies):
            if group is not d:
                group.inward(keep, 1).wait_recv()
            add_rows(group.acc.at[keep], group.acc.at[keep], group.outer.at[keep])

        by_side(group, step)

    def se(group):
        def step(keep, give, copies):
            copies[0].wait_recv()
            add_rows(group.done.at[keep], group.acc.at[keep], group.inner)
            copies[1].start()

        by_side(group, step)

    def za(group):
        by_side(group, lambda keep, give, copies: copies[2].start())

    def fi(group):
        by_side(group, lambda keep, give, copies: copies[1].wait_recv())

    def wa(group):
        by_side(group, lambda keep, give, copies: copies[2].wait_send())

    def zb(group):
        by_side(group, lambda keep, give, copies: copies[3].start())

    def de(group):
        def end(give, keep):
            copies = group.crossing(keep, give)
            copies[2].wait_recv()
            copies[3].wait_recv()

        by_end(group, end)

        def step(keep, give, copies):
            for i in (0, 1, 3):
                copies[i].wait_send()

        by_side(group, step)
        for copy in group.shares + group.stores:
            copy.start()

    d, e, last, u, v, q, r, o = groups
    for copy in [e.load, d.load, d.load_in, sums_send] + operands:
        copy.start()
    steps = {
        "b1": b1, "b0": b0, "h1": h1, "h0": h0, "pl": pl_, "gi": gi, "gw": gw, "ke": ke, "kw": kw,
        "en": en, "jo": jo, "se": se, "za": za, "fi": fi, "wa": wa, "zb": zb, "de": de,
    }
    named = {"d": d, "e": e, "f": last, "u": u, "v": v, "q": q, "r": r, "o": o}

    over_x = remote(sums_o, sums_got.at[1], at.x)
    over_y = remote(sums_o, sums_got.at[2], at.y)
    sums_in = remote(sums_o, sums_got.at[3], toward)
    sums_mid = remote(sums_o, sums_got.at[4], other)
    sums_out = remote(sums_o, sums_got.at[5], outward)

    def sums_1():
        sums_send.wait_recv()
        sums_o[...] = sums[...] + sums_got[0]
        over_x.start()

    def sums_2():
        over_x.wait()
        sums_o[...] += sums_got[1]
        over_y.start()

    def sums_3():
        over_y.wait()
        sums_o[...] += sums_got[2]

        @pl.when(is_outer)
        def _():
            sums_in.start()

    def sums_4():
        @pl.when(is_inner)
        def _():
            sums_in.wait_recv()
            sums_o[...] += sums_got[3]
            sums_mid.start()

    def sums_5():
        @pl.when(is_inner)
        def _():
            sums_mid.wait()
            sums_o[...] += sums_got[4]
            sums_out.start()

    def out_gradient():
        for copy in operands[2:]:
            copy.wait()
        tile = wide // 2
        for ref, core in ((out_away, 1 - g), (out_mine, g)):


            @pl.loop(0, 2)
            def _(n):
                cols = rows_at(core * wide + n * tile, tile)
                ref[:, rows_at(n * tile, tile)] = mm(attn_v[...], da_v[:, cols]).astype(ref.dtype)

            if ref is out_away:
                out_send.start()

    def qkv_gradient():
        for copy in operands[:2]:
            copy.wait()
        tile = 2 * TILE

        @pl.loop(0, qkv.shape[1] // tile)
        def _(n):
            cols = rows_at(n * tile, tile)
            qkv[:, cols] = mm(xn_v[...], d_qkv_v[:, cols], ((0,), (0,))).astype(qkv.dtype)

    def out_sum():
        out_send.wait_recv()
        add_rows(out_mine, out_mine, out_got)

    single = {
        "s1": sums_1, "s2": sums_2, "s3": sums_3, "s4": sums_4, "s5": sums_5,
        "go": out_gradient, "gq": qkv_gradient, "ao": out_sum,
    }
    for name in ORDER:
        if len(name) == 2:
            single[name]()
        else:
            steps[name[:2]](named[name[2]])

    @pl.when(is_outer)
    def _():
        sums_in.wait_send()
        sums_out.wait_recv()
        sums_o[...] = sums_got[5]

    @pl.when(is_inner)
    def _():
        sums_out.wait_send()

    sums_send.wait_send()
    out_send.wait_send()
    for group in (last, u, v, q, r, o):
        for copy in group.sends + group.second:
            copy.wait_send()
    for group in groups:
        for copy in group.stores:
            copy.wait()
        for copy in group.shares:
            copy.wait_send()
            copy.wait_recv()
    for level in range(chips):
        copy = pltpu.make_async_remote_copy(
            src_ref=lse, dst_ref=lse_place, send_sem=lse_send.at[level], recv_sem=lse_recv.at[level],
            device_id=(level, f, parity), device_id_type=MESH,
        )

        @pl.when((z != level) | (g != parity))
        def _():
            copy.wait_send()

        @pl.when((z != 2 * (level // 2) + g) | (g != level % 2))
        def _():
            copy.wait_recv()

    @pl.when(g == parity)
    def _():
        lse_keep.wait()


def collect(down, down_in, gate, gate_last, up, xn, d_qkv, attn, da, sums, lse, nq, nk):
    bf = jnp.bfloat16
    buffers = []
    wide = da.shape[1] // 2
    feat = gate.shape[0]
    for rows, cols, ready in (
        (down.shape[0], down.shape[1], True),
        (gate.shape[0], gate.shape[1], True),
        (feat, gate_last.shape[1], False),
        (feat, up.shape[1] // 2, False),
        (feat, up.shape[1] // 2, False),
        (feat, nq, False),
        (feat, 2 * nk, False),
        (attn.shape[0] // 4, wide, False),
    ):
        mid = rows // 2
        buffers += [
            pltpu.VMEM((rows, cols), bf),
            pltpu.VMEM((rows, cols), bf),
            pltpu.VMEM((mid, cols), bf),
            pltpu.VMEM((rows, cols), bf),
        ]
        if not ready:
            buffers += [
                pltpu.VMEM((2, mid, cols), bf),
                pltpu.VMEM((4, mid, cols), bf),
                pltpu.VMEM((2, mid, cols), bf),
            ]
    return pl.pallas_call(
        collect_kernel,
        in_specs=[ANY] * 9 + [VM, VM],
        out_specs=[ANY] * 7 + [VM, VM],
        out_shape=[
            bf16_like(2 * down.shape[0], down.shape[1]),
            bf16_like(feat, 2 * up.shape[1]),
            bf16_like(feat, 2 * up.shape[1]),
            bf16_like(feat, 2 * nq),
            bf16_like(feat, 2 * nk),
            bf16_like(feat, 2 * nk),
            bf16_like(feat, da.shape[1]),
            f32_like(*sums.shape),
            f32_like(4, *lse.shape),
        ],
        scratch_shapes=[
            pltpu.SemaphoreType.DMA((112,)),
            pltpu.SemaphoreType.DMA((112,)),
            pltpu.SemaphoreType.DMA((48,)),
            pltpu.SemaphoreType.DMA((4,)),
            pltpu.SemaphoreType.DMA((4,)),
            pltpu.SemaphoreType.DMA,
            pltpu.VMEM((attn.shape[0], wide), bf),
            pltpu.VMEM((attn.shape[0], wide), bf),
            pltpu.VMEM((6,) + sums.shape, jnp.float32),
            pltpu.VMEM((attn.shape[0], wide), bf),
            pltpu.VMEM((xn.shape[1], d_qkv.shape[1]), bf),
            pltpu.VMEM(xn.shape, bf),
            pltpu.VMEM(d_qkv.shape, bf),
            pltpu.VMEM(attn.shape, bf),
            pltpu.VMEM(da.shape, bf),
        ]
        + buffers,
        compiler_params=pltpu.CompilerParams(
            collective_id=1, has_side_effects=True, vmem_limit_bytes=62 * 1024 * 1024
        ),
        cost_estimate=cost(0, 500e6),
        name="collect",
    )(down, down_in, gate, gate_last, up, xn, d_qkv, attn, da, sums, lse)


def widen_kernel(spot, dealing, lse, sums, *refs):
    totals, first, second = refs[-3:]
    half = (len(refs) - 3) // 2
    for narrow, wide in zip(refs[:half], refs[half:-3]):
        wide[...] = fp32(narrow[...])

    @pl.when(pl.program_id(0) == 0)
    def _():
        shard = rows_at(spot[1] * first.shape[0], first.shape[0])
        first[...] = sums[0, shard]
        second[...] = sums[1, shard]
        heads = lse.shape[1]
        for r in range(4):
            for i in range(4):

                @pl.when(dealing[r, i] == spot[0])
                def _():
                    col = (4 * r + i) % 8 * BLK
                    for core in range(2):
                        totals[core * heads : (core + 1) * heads, r * BLK : (r + 1) * BLK] = lse[
                            2 * (r // 2) + core, :, col : col + BLK
                        ]


def widen(spot, dealing, lse, sums, arrays, steps=8):
    specs = [pl.BlockSpec((a.shape[0] // steps, a.shape[1]), lambda n: (n, 0)) for a in arrays]
    shard = sums.shape[1] // 4
    return pl.pallas_call(
        widen_kernel,
        grid=(steps,),
        in_specs=[SMEM, SMEM, VM, VM] + specs,
        out_specs=specs + [VM] * 3,
        out_shape=[f32_like(*a.shape) for a in arrays]
        + [f32_like(2 * lse.shape[1], 4 * BLK), f32_like(shard), f32_like(shard)],
        compiler_params=PARAMS,
        cost_estimate=cost(0, 40e6),
        name="widen",
    )(spot, dealing, lse, sums, *arrays)


def turning_tables(seq):
    half = HEAD_SIZE // 2
    frequency = ROPE_BASE ** (-2.0 * np.arange(half) / (2 * half))
    low = frequency[:, None] * np.arange(BLK)[None, :]
    high = frequency[:, None] * (BLK * np.arange(seq // BLK))[None, :]
    return tuple(part.astype(np.float32) for part in (np.cos(low), np.sin(low), np.cos(high), np.sin(high)))


def chip_local(
    tokens,
    seq_lengths,
    dealing,
    first_gain,
    query_weight,
    key_matrix,
    value_matrix,
    out_weight,
    second_gain,
    gate_weight,
    up_weight,
    down_weight,
    cotangent,
):
    ctx = lax.axis_size("ctx")
    z = lax.axis_index("ctx")
    f = lax.axis_index("fsdp")
    g = lax.axis_index("grp")
    parity = z % 2
    parity_core = g == parity
    width = tokens.shape[2]
    tok = tokens.shape[1]
    seq = 2 * tok
    place = jnp.stack([g, parity]).astype(jnp.int32)

    def over_x(field):
        return lax.ppermute(field, "fsdp", [(i, i ^ 1) for i in range(4)])

    def over_y(field):
        return lax.ppermute(field, "fsdp", [(i, i ^ 2) for i in range(4)])

    def over_core(field):
        return lax.ppermute(field, "grp", [(0, 1), (1, 0)])

    swap_pairs = [(2 * i + (1 - i % 2), 2 * (i ^ 1) + i % 2) for i in range(ctx)]

    def swap(field):
        got = lax.ppermute(field, ("ctx", "grp"), swap_pairs)
        return jnp.where(parity_core, field, got)

    def along(field, pairs):
        return lax.ppermute(field, "ctx", pairs)

    def cut(field, start, size, axis):
        return lax.dynamic_slice_in_dim(field, start, size, axis)

    def in_order(mine, other, axis=0):
        first = jnp.where(g == 0, mine, other)
        second = jnp.where(g == 0, other, mine)
        return jnp.concatenate([first, second], axis=axis)

    heads_q = query_weight.shape[1] // 2
    heads_k = key_matrix.shape[1] // 2
    part_ff = down_weight.shape[0] // 2
    rows_in = gate_weight.shape[0]

    row = lax.broadcasted_iota(jnp.int32, (1, 8, first_gain.shape[0]), 1)
    gain_own = jnp.where(row == 0, fp32(first_gain), jnp.where(row == 1, fp32(second_gain), 0.0))
    qkv_w, out_w, pair_w, down_own, x_seq, dy_all, gain_all, xn_one, qkv_t = gather_all(
        tokens, cotangent, query_weight, key_matrix, value_matrix, out_weight,
        gate_weight, up_weight, down_weight, gain_own,
    )
    down_w = lax.all_gather(down_own, "fsdp", axis=0, tiled=True)

    tables = turning_tables(seq)

    attn_keep, attn_send, lse, q_t, k_t, v_t = attend_seq(place, qkv_t, tables)
    attn_got = over_core(attn_send)
    h_own, xn_own, attn_mine = residual(place, x_seq, attn_keep, attn_got, gain_all, out_w)
    hidden, for_gate, act, xn_two = hidden_step(place, xn_own, over_core(xn_own), pair_w)
    d_gate, d_up = hidden_back(dy_all, down_w, for_gate, act)
    bf = jnp.bfloat16
    tokens_in = ((0,), (0,))
    down_grad = mm(hidden, dy_all, tokens_in, bf)
    most = 3 * part_ff
    gate_grad = mm(xn_two, d_gate[:, :most], tokens_in, bf)
    down_plane = lax.psum_scatter(down_grad, "fsdp", scatter_dimension=0, tiled=True)
    down_in = along(down_plane, [(0, 1), (3, 2)])
    gate_plane = lax.psum_scatter(gate_grad, "fsdp", scatter_dimension=0, tiled=True)
    d_gate, d_up, hidden, _, _ = lax.optimization_barrier((d_gate, d_up, hidden, down_grad, gate_grad))
    dn_own, dn_send = back_step(place, d_gate, d_up, pair_w)
    dn_got = over_core(dn_send)
    res_own, res_send = result_step(place, hidden, h_own, down_w)
    up_grad = mm(xn_two, d_up, tokens_in, bf)
    gate_last = mm(xn_two, d_gate[:, most:], tokens_in, bf)
    layer_out = swap((res_own + fp32(over_core(res_send))).astype(bf))

    dh_own, da, dattn_keep, dattn_send, gain_two_part = entry_step(
        place, dn_own, dn_got, h_own, dy_all, gain_all, out_w
    )
    dattn_got = over_core(dattn_send)
    q_t, _, up_grad = lax.optimization_barrier((q_t, down_plane, up_grad))
    dq_t, dk_t, dv_t = attend_seq_back(
        place, q_t, k_t, v_t, dattn_keep, dattn_got, lse, tables
    )
    half_width = width // 2
    d1_own, d1_send, d_qkv = inputs_step(place, dq_t, dk_t, dv_t, qkv_w)
    dh_own, down_in = lax.optimization_barrier((dh_own, down_in))
    dx, gain_one_part = last_step(place, d1_own, over_core(d1_send), x_seq, dh_own, gain_all)

    parts = jnp.concatenate([gain_one_part, gain_two_part])
    down_sum, gate_sum, up_sum, query_sum, key_sum, value_sum, out_sum, sums, all_lse = collect(
        down_plane, down_in, gate_plane, gate_last, up_grad, xn_one, d_qkv, attn_mine, da,
        jnp.pad(parts, ((0, 6), (0, 0))), lse.reshape(-1, seq), heads_q, heads_k,
    )
    dx, sums = lax.optimization_barrier((dx, sums))
    tokens_grad = swap(dx)
    query_out, key_out, value_out, out_out, gate_out, up_out, down_out, totals, gain_one, gain_two = widen(
        jnp.stack([z, f]).astype(jnp.int32), dealing[0], all_lse, sums,
        (query_sum, key_sum, value_sum, out_sum, gate_sum, up_sum, down_sum),
    )

    return (
        layer_out[None],
        tokens_grad[None],
        totals[None],
        gain_one,
        query_out,
        key_out,
        value_out,
        out_out,
        gain_two,
        gate_out,
        up_out,
        down_out,
    )


def chip_holds_sequence(mesh, tokens, seq_lengths):
    sizes = dict(mesh.shape)
    packs, length, _ = tokens.shape
    count = seq_lengths.shape[1]
    return (
        sizes["fsdp"] == 4
        and sizes["grp"] == 2
        and sizes["ctx"] == 4
        and packs == sizes["fsdp"] * sizes["grp"]
        and length == count * MINLEN
        and 2 * length == sizes["ctx"] * MINLEN
    )


def solution(mesh):
    placed = (
        P(("fsdp", "grp"), "ctx", None),
        P(("fsdp", "grp"), None),
        P(("fsdp", "grp"), None, None),
        P("fsdp"),
        P("fsdp", None),
        P("fsdp", None),
        P("fsdp", None),
        P("fsdp", None),
        P("fsdp"),
        P("fsdp", None),
        P("fsdp", None),
        P("fsdp", None),
        P(("fsdp", "grp"), "ctx", None),
    )
    results = (
        P(("fsdp", "grp"), "ctx", None),
        P(("fsdp", "grp"), "ctx", None),
        P(("fsdp", "grp"), None, "ctx"),
        P("fsdp"),
        P("fsdp", None),
        P("fsdp", None),
        P("fsdp", None),
        P("fsdp", None),
        P("fsdp"),
        P("fsdp", None),
        P("fsdp", None),
        P("fsdp", None),
    )

    def program(*arrays):
        body = chip_local if chip_holds_sequence(mesh, arrays[0], arrays[1]) else local
        return jax.shard_map(
            body, mesh=mesh, in_specs=placed, out_specs=results, check_vma=False
        )(*arrays)

    return program
```
